32 devices in a mesh: dp: 8 (over z, y), seq: 4 (over x, core).
Axes of the slice: x: 2, y: 2, z: 4, core: 2. Of those that a mesh axis runs over, the one named last changes fastest.
Arguments:
- layer_input: bfloat16 [16, 1024, 1536], P('dp', 'seq'), may hold values from -6 to 6
- document_index: int32 [16, 1024], P('dp', 'seq'), may hold values from 0 to 7, never falling along the last dimension, each value on 1 to 512 neighbouring positions
- adapter_index: int32 [16], P('dp'), may hold values from 0 to 7
- input_norm_gain: bfloat16 [1536], P(('dp', 'seq')), may hold values from 0.5 to 1.5
- input_projection: bfloat16 [1536, 6400], P(('dp', 'seq')), may hold values from -0.15625 to 0.15625
- step_projection: bfloat16 [1536, 48], P(('dp', 'seq')), may hold values from -0.15625 to 0.15625
- convolution_weight: bfloat16 [3328, 4], P(('dp', 'seq')), may hold values from -3 to 3
- convolution_bias: bfloat16 [3328], P(('dp', 'seq')), may hold values from -1.5 to 1.5
- head_step_bias: float32 [48], replicated, may hold values from -7 to -2.5
- log_decay_rate: float32 [48], replicated, may hold values from 0 to 1.5
- head_skip_gain: float32 [48], replicated, may hold values from 0.5 to 1.5
- gated_norm_gain: bfloat16 [3072], P(('dp', 'seq')), may hold values from 0.5 to 1.5
- output_projection: bfloat16 [3072, 1536], P(('dp', 'seq')), may hold values from -0.109375 to 0.109375
- adapter_input_down: bfloat16 [8, 16, 1536], P(None, None, ('dp', 'seq')), may hold values from -0.15625 to 0.15625
- adapter_input_up: bfloat16 [8, 16, 6400], P(None, None, ('dp', 'seq')), may hold values from -0.75 to 0.75
- adapter_output_down: bfloat16 [8, 16, 3072], P(None, None, ('dp', 'seq')), may hold values from -0.109375 to 0.109375
- adapter_output_up: bfloat16 [8, 16, 1536], P(None, None, ('dp', 'seq')), may hold values from -0.75 to 0.75
- output_gradient: bfloat16 [16, 1024, 1536], P('dp', 'seq'), may hold values from -6 to 6
Outputs:
- output: bfloat16 [16, 1024, 1536], P('dp', 'seq')
- grad_in: float32 [16, 1024, 1536], P('dp', 'seq')
- grad_lora_in_down: float32 [8, 16, 1536], P(None, None, ('dp', 'seq'))
- grad_lora_in_up: float32 [8, 16, 6400], P(None, None, ('dp', 'seq'))
- grad_lora_out_down: float32 [8, 16, 3072], P(None, None, ('dp', 'seq'))
- grad_lora_out_up: float32 [8, 16, 1536], P(None, None, ('dp', 'seq'))
The draws below stay inside these ranges and needn't reach their ends.
Inputs may be any that keep to these rules, and one draw needn't show every extreme that they name: `document_index`: in each sequence the numbers start at 0, never fall, and each of the 8 segments has 1 to 512 tokens, one exactly 512.
All inputs are finite; a program needn't handle non-finite values.
Results may differ from the reference program's by a relative error of at most 0.0086.
Values may be sent and summed in bfloat16 or wider, within the bound.
No kernel may reach another device: no remote copies, remote signals or barrier semaphores. Data moves between devices by JAX's collectives and lax.ppermute only.
A program may use at most 192 MiB of HBM per device.

```python
import math
import jax
import jax.numpy as jnp
import numpy as np
from jax import lax

MODEL_DIM = 1536
INNER_DIM = 3072
HDIM = 64
NSTATE = 128
CONV = 4
HEADS = 48
PROJECTION_COLS = 6400
CONVCH = 3328
ADAPTER_COUNT = 8
ADAPTER_RANK = 16
LENGTH = 1024
SEGMENTS = 8
LOC = 256
SEQS = 16


def set_ends(entries, key, least, largest):
    index_at = [jax.random.randint(jax.random.fold_in(key, axis), (), 0, length) for axis, length in enumerate(entries.shape)]
    widest = entries.shape.index(max(entries.shape))
    next_to = index_at[:widest] + [(index_at[widest] + 1) % entries.shape[widest]] + index_at[widest + 1:]
    return entries.at[tuple(index_at)].set(least).at[tuple(next_to)].set(largest)


def shard_levels(stream_key, dims, cuts, least, high):
    def one(dim, shards_of):
        draws = jax.random.uniform(jax.random.fold_in(jax.random.fold_in(stream_key, 6), dim), (shards_of,), jnp.float32, least / len(cuts), high / len(cuts))
        return jnp.repeat(jnp.exp(draws), dims[dim] // shards_of).reshape((-1,) + (1,) * (len(dims) - dim - 1))

    loudness = one(*cuts[0])
    for cut in cuts[1:]:
        loudness = loudness * one(*cut)
    return loudness


def split_up(amount, total, bound, lean):
    portions = [(1 << 20) // math.isqrt(standing ** lean) + 1 for standing in range(2, amount + 1)]
    surplus, holding = total - bound - (amount - 1), [1] * (amount - 1)
    while surplus > 0:
        movable = [i for i in range(amount - 1) if holding[i] < bound]
        mass, budget = sum([portions[i] for i in movable]), surplus
        for i in movable:
            addition = min(bound - holding[i], max(1, budget * portions[i] // mass), surplus)
            holding[i] = holding[i] + addition
            surplus = surplus - addition
    return np.array([bound] + holding)


def ragged_sizes(rng, amount, total, most, skew):
    if amount == 2:
        one = jax.random.randint(rng, (), max(1, total - most), min(most, total - 1) + 1)
        return jnp.stack([one, total - one])
    lengths = jnp.asarray(split_up(amount, total, most, skew), jnp.int32)
    twos = (amount - 1) // 2
    source_of, receiver = lengths[1:1 + 2 * twos:2], lengths[2:2 + 2 * twos:2]
    margin = jnp.minimum(source_of - 1, most - receiver)
    shifted = jax.random.randint(jax.random.fold_in(rng, 1), (twos,), 0, 1 << 20) % (margin + 1)
    lengths = lengths.at[1:1 + 2 * twos:2].set(source_of - shifted).at[2:2 + 2 * twos:2].set(receiver + shifted)
    return lengths[jax.random.permutation(jax.random.fold_in(rng, 2), amount)]


def gaussian(stream_key, dims, scale, reach, cuts=(), held_as=jnp.bfloat16):
    loudness = shard_levels(stream_key, dims, cuts, -0.22, 0.18) if cuts else 1.0
    drawn = jax.random.normal(stream_key, dims, jnp.float32) * scale * loudness
    return jnp.minimum(jnp.maximum(drawn, -reach), reach).astype(held_as)


def setup_inputs(seed: int = 0) -> dict:
    streams_of = jax.random.split(jax.random.key(seed), 19)
    return {
        "layer_input": gaussian(streams_of[0], (SEQS, LENGTH, MODEL_DIM), 1.0, 6.0, ((0, 8), (1, 4))),
        "document_index": jax.vmap(lambda own: jnp.searchsorted(jnp.cumsum(ragged_sizes(own, SEGMENTS, LENGTH, LENGTH // 2, 2)), jnp.arange(LENGTH), side="right"))(jax.random.split(streams_of[1], SEQS)).reshape((SEQS, LENGTH)).astype(jnp.int32),
        "adapter_index": set_ends(jax.random.randint(streams_of[2], (SEQS,), 0, ADAPTER_COUNT), jax.random.fold_in(streams_of[2], 1), 0, ADAPTER_COUNT - 1).astype(jnp.int32),
        "input_norm_gain": jnp.clip(1.0 + 0.1 * jax.random.normal(streams_of[3], (MODEL_DIM,), jnp.float32), 0.5, 1.5).astype(jnp.bfloat16),
        "input_projection": gaussian(streams_of[4], (MODEL_DIM, PROJECTION_COLS), MODEL_DIM ** -0.5, 0.15625, ((0, 32),)),
        "step_projection": gaussian(streams_of[5], (MODEL_DIM, HEADS), MODEL_DIM ** -0.5, 0.15625, ((0, 32),)),
        "convolution_weight": gaussian(streams_of[6], (CONVCH, CONV), CONV ** -0.5, 3.0, ((0, 32),)),
        "convolution_bias": gaussian(streams_of[7], (CONVCH,), 0.3, 1.5, ((0, 32),)),
        "head_step_bias": jnp.clip(jax.random.uniform(streams_of[8], (HEADS,), jnp.float32, -7.0, -2.5), -7.0, -2.5),
        "log_decay_rate": jnp.clip(jax.random.uniform(streams_of[9], (HEADS,), jnp.float32, 0.0, 1.5), 0.0, 1.5),
        "head_skip_gain": jnp.clip(jax.random.uniform(streams_of[10], (HEADS,), jnp.float32, 0.5, 1.5), 0.5, 1.5),
        "gated_norm_gain": jnp.clip(1.0 + 0.1 * jax.random.normal(streams_of[11], (INNER_DIM,), jnp.float32), 0.5, 1.5).astype(jnp.bfloat16),
        "output_projection": gaussian(streams_of[12], (INNER_DIM, MODEL_DIM), INNER_DIM ** -0.5, 0.109375, ((0, 32),)),
        "adapter_input_down": gaussian(streams_of[13], (ADAPTER_COUNT, ADAPTER_RANK, MODEL_DIM), MODEL_DIM ** -0.5, 0.15625, ((2, 32),)),
        "adapter_input_up": gaussian(streams_of[14], (ADAPTER_COUNT, ADAPTER_RANK, PROJECTION_COLS), (4 * ADAPTER_RANK) ** -0.5, 0.75, ((2, 32),)),
        "adapter_output_down": gaussian(streams_of[15], (ADAPTER_COUNT, ADAPTER_RANK, INNER_DIM), INNER_DIM ** -0.5, 0.109375, ((2, 32),)),
        "adapter_output_up": gaussian(streams_of[16], (ADAPTER_COUNT, ADAPTER_RANK, MODEL_DIM), (4 * ADAPTER_RANK) ** -0.5, 0.75, ((2, 32),)),
        "output_gradient": gaussian(streams_of[17], (SEQS, LENGTH, MODEL_DIM), 1.0, 6.0, ((0, 8), (1, 4))),
    }


EPS = 1e-05
HIGH = lax.Precision.HIGHEST

@jax.custom_vjp
def narrow_value(v):
    return lax.optimization_barrier(v.astype(jnp.bfloat16)).astype(jnp.float32)

@jax.custom_vjp
def narrow_backward(v):
    return v

def low_keep(v):
    return (narrow_value(v), None)

def low_pass(kept, grad):
    return (grad,)

def back_keep(v):
    return (v, None)

def back_low(kept, grad):
    return (narrow_value(grad),)
narrow_value.defvjp(low_keep, low_pass)
narrow_backward.defvjp(back_keep, back_low)

def product_value(form, left, right):
    return jnp.einsum(form, left, right, precision=HIGH)

def block_step(carried, pieces):
    states, last_segment = carried
    values, in_state, out_state, log_decay, step_size, document_segments = pieces
    cumulative = jnp.cumsum(log_decay, axis=1)
    positions = jnp.arange(document_segments.shape[1])
    same_mask = (document_segments[:, :, None] == document_segments[:, None, :]) & (positions[:, None] >= positions[None, :])[None]
    same_mask = same_mask[..., None]
    log_gaps = cumulative[:, :, None, :] - cumulative[:, None, :, :]
    decays = jnp.where(same_mask, jnp.exp(jnp.where(same_mask, log_gaps, 0.0)), 0.0)
    contact = narrow_backward(product_value('gtn,gun->gtu', out_state, in_state))
    weights_low = narrow_value(contact[..., None] * decays * step_size[:, None, :, :])
    within = product_value('gtuh,guhp->gthp', weights_low, values)
    keep_mask = (document_segments == last_segment[:, None]).astype(jnp.float32)
    entry_decay = keep_mask[..., None] * jnp.exp(cumulative)
    readout = narrow_backward(product_value('gtn,ghpn->gthp', out_state, narrow_value(states)))
    carried_in = readout * entry_decay[..., None]
    ssm_sum = narrow_backward(within + carried_in)
    end_mask = (document_segments == document_segments[:, -1:]).astype(jnp.float32)
    state_weight = end_mask[..., None] * jnp.exp(cumulative[:, -1:, :] - cumulative) * step_size
    scaled_low = narrow_value(state_weight[..., None] * values)
    local_state = narrow_backward(product_value('guhp,gun->ghpn', scaled_low, in_state))
    states = entry_decay[:, -1, :, None, None] * states + local_state
    return ((states, document_segments[:, -1]), ssm_sum)

def layer_apply(hidden_rows, document_segments, adapter_selector, frozen_params, adapter_input_down, adapter_input_up, adapter_output_down, adapter_output_up):
    input_norm_gain, input_projection, step_projection, convolution_weight, convolution_bias, head_step_bias, log_decay_rate, head_skip_gain, gated_norm_gain, output_projection = frozen_params
    per_group = hidden_rows.shape[0]
    seq_len = hidden_rows.shape[1]
    normed = hidden_rows * lax.rsqrt(lax.optimization_barrier(jnp.mean(hidden_rows * hidden_rows, -1, keepdims=True)) + EPS) * input_norm_gain
    normed_narrow = narrow_value(normed)
    input_down_map = product_value('mc,cuw->muw', adapter_selector, adapter_input_down)
    input_up_map = product_value('es,saf->eaf', adapter_selector, adapter_input_up)
    input_rank_rows = narrow_backward(narrow_value(product_value('gld,grd->glr', normed_narrow, input_down_map)))
    projected_rows = narrow_backward(product_value('tqa,aj->tqj', normed_narrow, input_projection) + product_value('ibh,ihw->ibw', input_rank_rows, input_up_map))
    step_raw = narrow_backward(product_value('gld,dh->glh', normed_narrow, step_projection))
    gate_pre = projected_rows[..., :INNER_DIM]
    conv_in = narrow_value(projected_rows[..., INNER_DIM:])
    padded = jnp.pad(conv_in, ((0, 0), (CONV - 1, 0), (0, 0)))
    seg_padded = jnp.pad(document_segments, ((0, 0), (CONV - 1, 0)), constant_values=-1)
    conv_pre = jnp.zeros(conv_in.shape, jnp.float32) + convolution_bias
    for tap_index in range(CONV):
        matching = (seg_padded[:, tap_index:tap_index + seq_len] == document_segments).astype(jnp.float32)
        conv_pre = conv_pre + convolution_weight[:, tap_index] * padded[:, tap_index:tap_index + seq_len] * matching[..., None]
    conv_out = jax.nn.silu(conv_pre)
    values = narrow_value(conv_out[..., :INNER_DIM]).reshape(per_group, seq_len, HEADS, HDIM)
    in_state = narrow_value(conv_out[..., INNER_DIM:INNER_DIM + NSTATE])
    out_state = narrow_value(conv_out[..., INNER_DIM + NSTATE:])
    step_size = jax.nn.softplus(step_raw + head_step_bias)
    log_decay = -jnp.exp(log_decay_rate) * step_size
    blocks = seq_len // LOC

    def to_blocks(array):
        return jnp.moveaxis(array.reshape((per_group, blocks, LOC) + array.shape[2:]), 1, 0)
    initial = (jnp.zeros((per_group, HEADS, HDIM, NSTATE), jnp.float32), document_segments[:, 0])
    final_carry, mixed_out = lax.scan(jax.checkpoint(block_step), initial, (to_blocks(values), to_blocks(in_state), to_blocks(out_state), to_blocks(log_decay), to_blocks(step_size), to_blocks(document_segments)))
    ssm_out = jnp.moveaxis(mixed_out, 0, 1).reshape(per_group, seq_len, HEADS, HDIM)
    ssm_out = (ssm_out + head_skip_gain[:, None] * values).reshape(per_group, seq_len, INNER_DIM)
    gated = ssm_out * jax.nn.silu(gate_pre)
    gated_norm = gated * lax.rsqrt(lax.optimization_barrier(jnp.mean(gated * gated, -1, keepdims=True)) + EPS) * gated_norm_gain
    gated_narrow = narrow_value(gated_norm)
    output_down_map = product_value('es,saf->eaf', adapter_selector, adapter_output_down)
    output_up_map = product_value('mc,cuw->muw', adapter_selector, adapter_output_up)
    output_rank_rows = narrow_backward(narrow_value(product_value('nws,njs->nwj', gated_narrow, output_down_map)))
    branch_value = product_value('skj,jz->skz', gated_narrow, output_projection) + product_value('isf,ifh->ish', output_rank_rows, output_up_map)
    return hidden_rows + branch_value

def reference(layer_input, document_index, adapter_index, input_norm_gain, input_projection, step_projection, convolution_weight, convolution_bias, head_step_bias, log_decay_rate, head_skip_gain, gated_norm_gain, output_projection, adapter_input_down, adapter_input_up, adapter_output_down, adapter_output_up, output_gradient):
    per_group = math.gcd(SEQS, max(1, 4096 // LENGTH))
    count_groups = SEQS // per_group
    frozen_params = tuple((element_item.astype(jnp.float32) for element_item in (input_norm_gain, input_projection, step_projection, convolution_weight, convolution_bias, head_step_bias, log_decay_rate, head_skip_gain, gated_norm_gain, output_projection)))
    adapter_stack = tuple((element_item.astype(jnp.float32) for element_item in (adapter_input_down, adapter_input_up, adapter_output_down, adapter_output_up)))
    hidden_all = layer_input.astype(jnp.float32).reshape(count_groups, per_group, LENGTH, MODEL_DIM)
    segments_all = document_index.reshape(count_groups, per_group, LENGTH)
    chosen_all = adapter_index.reshape(count_groups, per_group)
    cotangent_all = output_gradient.astype(jnp.float32).reshape(count_groups, per_group, LENGTH, MODEL_DIM)

    def one_group(totals, pieces):
        hidden_rows, document_segments, chosen, cotangent = pieces
        adapter_selector = (chosen[:, None] == jnp.arange(ADAPTER_COUNT, dtype=jnp.int32)[None, :]).astype(jnp.float32)

        def execute_layer(hidden_f, first, second, third, fourth):
            return layer_apply(hidden_f, document_segments, adapter_selector, frozen_params, first, second, third, fourth)
        result_value, pullback_function = jax.vjp(execute_layer, hidden_rows, *adapter_stack)
        gradients = pullback_function(cotangent)
        totals = tuple((total + grad_part for total, grad_part in zip(totals, gradients[1:])))
        return (totals, (result_value.astype(jnp.bfloat16), gradients[0]))
    empty_gradients = tuple((jnp.zeros_like(element_item) for element_item in adapter_stack))
    totals, stacked = lax.scan(one_group, empty_gradients, (hidden_all, segments_all, chosen_all, cotangent_all))
    outputs, grad_hidden = stacked
    return (outputs.reshape(SEQS, LENGTH, MODEL_DIM), grad_hidden.reshape(SEQS, LENGTH, MODEL_DIM), totals[0], totals[1], totals[2], totals[3])
```

```python
import jax
import jax.numpy as jnp
from jax import lax
from jax.sharding import PartitionSpec as P

EPS = 1e-05
f32 = jnp.float32
bf16 = jnp.bfloat16
BLOCK = 256


def mm(form, a, b):
    return jnp.einsum(form, a, b, preferred_element_type=f32)


def silu_slope(v):
    s = jax.nn.sigmoid(v)
    return s * (1.0 + v * (1.0 - s))


def shift_down(v, by):
    return v if by == 0 else jnp.pad(v, ((0, 0), (by, 0), (0, 0)))[:, : v.shape[1]]


def shift_up(v, by):
    return v if by == 0 else jnp.pad(v, ((0, 0), (0, by), (0, 0)))[:, by:]


def per_device(
    layer_input,
    document_index,
    adapter_index,
    input_norm_gain,
    input_projection,
    step_projection,
    convolution_weight,
    convolution_bias,
    head_step_bias,
    log_decay_rate,
    head_skip_gain,
    gated_norm_gain,
    output_projection,
    adapter_input_down,
    adapter_input_up,
    adapter_output_down,
    adapter_output_up,
    output_gradient,
):
    both = ("dp", "seq")
    dps, n = lax.axis_size("dp"), lax.axis_size("seq")
    here = lax.axis_index("seq")
    seqs, own_len, width = layer_input.shape
    adapters, rank, _ = adapter_input_down.shape
    ranks = adapters * rank
    heads = head_step_bias.shape[0]
    inner = output_projection.shape[0] * dps * n
    cols = input_projection.shape[1]
    state2 = cols - 2 * inner
    state = state2 // 2
    taps = convolution_weight.shape[1]
    hn = heads // n
    hc = inner // n
    hd = inner // heads
    length = own_len * n
    nb = length // BLOCK

    x_all = lax.all_gather(layer_input, "seq", axis=1, tiled=True)
    og_all = lax.all_gather(output_gradient, "seq", axis=1, tiled=True)
    docs = lax.all_gather(document_index, "seq", axis=1, tiled=True)

    rows = input_projection.shape[0]
    down_rows = adapter_input_down.reshape(ranks, rows).T
    step_pad = 128 - hn
    per_target = []
    for t in range(n):
        per_target.append(
            jnp.concatenate(
                [
                    input_projection[:, inner + t * hc : inner + (t + 1) * hc],
                    input_projection[:, 2 * inner :],
                    down_rows,
                    jnp.pad(step_projection[:, t * hn : (t + 1) * hn], ((0, 0), (0, step_pad))),
                    input_projection[:, t * hc : (t + 1) * hc],
                ],
                1,
            )
        )
    w_mine = lax.all_to_all(jnp.stack(per_target), "seq", 0, 0, tiled=True)
    w_mine = w_mine.reshape(n * rows, -1)
    w_in = lax.all_gather(w_mine, "dp", axis=0, tiled=True)
    conv_cols = hc + state2
    wa_cols = conv_cols + ranks + 128
    wa, wb = w_in[:, :wa_cols], w_in[:, wa_cols:]

    out_rows = output_projection.shape[0]
    w_o = jnp.concatenate(
        [
            output_projection,
            adapter_output_down.reshape(ranks, out_rows).T,
            jnp.pad(gated_norm_gain[:, None], ((0, 0), (0, 127))),
        ],
        1,
    )
    w_o = lax.ppermute(
        w_o, both, [(dps * s + d, n * d + s) for d in range(dps) for s in range(n)]
    )
    w_o = lax.all_gather(w_o, "dp", axis=0, tiled=True)
    w_out = w_o[:, :width]
    down_out = w_o[:, width : width + ranks]
    gate_gain = w_o[:, width + ranks].astype(f32)

    up_rows = adapter_input_up.shape[2]
    conv_rows = convolution_weight.shape[0]

    wide = -(-conv_rows // 128) * 128

    def as_row(v):
        return jnp.pad(v, ((0, 0), (0, wide - v.shape[1])))

    misc = jnp.concatenate(
        [
            as_row(convolution_weight.T),
            as_row(convolution_bias[None]),
            as_row(input_norm_gain[None]),
            as_row(adapter_index.astype(bf16)[None]),
        ],
        0,
    )
    misc_rows = misc.shape[0]
    small = jnp.concatenate(
        [
            adapter_input_up.reshape(ranks, up_rows).T,
            adapter_output_up.reshape(ranks, rows).T,
            misc.reshape(-1, 128),
        ],
        0,
    )
    small = lax.all_gather(small, both, axis=0)
    up_full = small[:, :up_rows].reshape(cols, ranks)
    up_out = small[:, up_rows : up_rows + rows].reshape(width, ranks)
    misc = small[:, up_rows + rows :].reshape(dps * n, misc_rows, wide)
    conv_w = jnp.moveaxis(misc[:, :taps, :conv_rows], 1, 0).reshape(taps, -1).astype(f32)
    conv_b = misc[:, taps, :conv_rows].reshape(-1).astype(f32)
    gain = misc[:, taps + 1, :rows].reshape(-1).astype(f32)
    every_index = misc[:, taps + 2, :seqs].reshape(dps, n, seqs)[:, 0].astype(jnp.int32)

    def mine(v, size, base=0):
        return lax.dynamic_slice_in_dim(v, base + here * size, size, 0)

    up_gate = mine(up_full, hc)
    up_conv = jnp.concatenate([mine(up_full, hc, inner), up_full[2 * inner :]], 0)
    conv_w = jnp.concatenate([mine(conv_w.T, hc), conv_w.T[inner:]], 0).T
    conv_b = jnp.concatenate([mine(conv_b, hc), conv_b[inner:]], 0)
    step_bias = mine(head_step_bias, hn)
    decay_rate = -jnp.exp(mine(log_decay_rate, hn))
    skip = mine(head_skip_gain, hn)

    chosen = (adapter_index[:, None] == jnp.arange(adapters, dtype=jnp.int32)[None, :]).astype(f32)
    mask = jnp.repeat(chosen, rank, axis=1)[:, None, :]

    hidden = x_all.astype(f32)
    inv_hidden = lax.rsqrt(jnp.mean(hidden * hidden, -1, keepdims=True) + EPS)
    normed = (hidden * inv_hidden * gain).astype(bf16)
    pa = mm("std,dc->stc", normed, wa)
    rank_in = (pa[..., conv_cols : conv_cols + ranks] * mask).astype(bf16)
    step_raw = pa[..., conv_cols + ranks : conv_cols + ranks + hn]
    conv_in = (pa[..., :conv_cols] + mm("str,cr->stc", rank_in, up_conv)).astype(bf16).astype(f32)
    gate_pre = mm("std,dc->stc", normed, wb) + mm("str,cr->stc", rank_in, up_gate)
    same = [
        (shift_down((docs + 1)[..., None], taps - 1 - j) == (docs + 1)[..., None]).astype(f32)
        for j in range(taps)
    ]
    conv_pre = conv_b + sum(
        conv_w[j] * shift_down(conv_in, taps - 1 - j) * same[j] for j in range(taps)
    )
    conv_out = jax.nn.silu(conv_pre).astype(bf16)
    values = conv_out[..., :hc].reshape(seqs, nb, BLOCK, hn, hd)
    in_state = conv_out[..., hc : hc + state].reshape(seqs, nb, BLOCK, state)
    out_state = conv_out[..., hc + state :].reshape(seqs, nb, BLOCK, state)
    step_arg = (step_raw + step_bias).reshape(seqs, nb, BLOCK, hn)
    dt = jax.nn.softplus(step_arg)
    cum = jnp.cumsum(decay_rate * dt, 2)
    doc = docs.reshape(seqs, nb, BLOCK)
    pos = jnp.arange(BLOCK)
    ok = (
        (doc[:, :, :, None] == doc[:, :, None, :]) & (pos[:, None] >= pos[None, :])[None, None]
    )[..., None]
    decays = jnp.where(
        ok, jnp.exp(jnp.where(ok, cum[:, :, :, None] - cum[:, :, None], 0.0)), 0.0
    )
    contact = mm("sbtn,sbun->sbtu", out_state, in_state)
    w_pre = contact[..., None] * decays * dt[:, :, None]
    w_low = w_pre.astype(bf16)
    within = mm("sbtuh,sbuhp->sbthp", w_low, values)
    prior = jnp.concatenate([doc[:, :1, 0], doc[:, :-1, -1]], 1)
    keep = (doc == prior[:, :, None]).astype(f32)
    entry = keep[..., None] * jnp.exp(cum)
    ends = (doc == doc[:, :, -1:]).astype(f32)
    end_decay = ends[..., None] * jnp.exp(cum[:, :, -1:] - cum)
    weight = end_decay * dt
    values_f = values.astype(f32)
    scaled = (weight[..., None] * values_f).astype(bf16)
    local = mm("sbuhp,sbun->sbhpn", scaled, in_state)
    passing = entry[:, :, -1]
    states = [jnp.zeros_like(local[:, 0])]
    for b in range(nb - 1):
        states.append(passing[:, b, :, None, None] * states[-1] + local[:, b])
    states = jnp.stack(states, 1)
    states_low = states.astype(bf16)
    readout = mm("sbtn,sbhpn->sbthp", out_state, states_low)
    mixed = within + readout * entry[..., None] + skip[:, None] * values_f
    mixed = mixed.reshape(seqs, length, hc)
    act = jax.nn.silu(gate_pre)
    gated = mixed * act

    grad_rank_out = (mm("std,dr->str", og_all, up_out) * mask).astype(bf16)
    scaled_grad = gate_gain * (
        mm("std,cd->stc", og_all, w_out) + mm("str,cr->stc", grad_rank_out, down_out)
    )
    stats = lax.psum(
        jnp.stack([jnp.sum(gated * gated, -1), jnp.sum(scaled_grad * gated, -1)], -1), "seq"
    )
    inv_gated = lax.rsqrt(stats[..., :1] / inner + EPS)
    mean_grad = stats[..., 1:] / inner
    gated_low = (gated * inv_gated * gate_gain).astype(bf16)
    branch = mm("stc,cd->std", gated_low, w_o[:, : width + ranks])
    branch = lax.psum_scatter(branch, "seq", scatter_dimension=1, tiled=True)
    rank_out = (branch[..., width:] * mask).astype(bf16)
    output = (
        layer_input.astype(f32) + branch[..., :width] + mm("str,dr->std", rank_out, up_out)
    ).astype(bf16)

    def compact(v):
        return v.reshape(seqs, adapters, rank, -1).sum(1)

    g_out_up = compact(mm("str,std->srd", rank_out, output_gradient))
    g_out_down = compact(mm("str,stc->src", grad_rank_out, gated_low))

    grad_gated = inv_gated * scaled_grad - gated * inv_gated**3 * mean_grad
    grad_mixed = grad_gated * act
    grad_gate = grad_gated * mixed * silu_slope(gate_pre)
    grad_mixed = grad_mixed.reshape(seqs, nb, BLOCK, hn, hd)
    grad_values = skip[:, None] * grad_mixed
    gsum = grad_mixed.astype(bf16)
    gw = mm("sbthp,sbuhp->sbtuh", gsum, values)
    grad_values = grad_values + mm("sbtuh,sbthp->sbuhp", w_low, gsum)
    through = gw * w_pre
    grad_cum = jnp.sum(through, 3) - jnp.sum(through, 2)
    grad_dt = jnp.sum(gw * contact[..., None] * decays, 2)
    g_contact = jnp.sum(gw * decays * dt[:, :, None], -1).astype(bf16)
    g_out_state = mm("sbtu,sbun->sbtn", g_contact, in_state)
    g_in_state = mm("sbtu,sbtn->sbun", g_contact, out_state)
    gsum_f = gsum.astype(f32)
    weighted = (gsum_f * entry[..., None]).astype(bf16)
    direct = mm("sbthp,sbtn->sbhpn", weighted, out_state)
    g_out_state = g_out_state + mm("sbthp,sbhpn->sbtn", weighted, states_low)
    grad_cum = grad_cum + jnp.sum(gsum_f * readout, -1) * entry
    later = [jnp.zeros_like(direct[:, 0])]
    for b in range(nb - 1, 0, -1):
        later.append(direct[:, b] + passing[:, b, :, None, None] * later[-1])
    later = jnp.stack(later[::-1], 1)
    later_low = later.astype(bf16)
    grad_passing = jnp.sum(later * states, (3, 4))
    grad_scaled = mm("sbhpn,sbun->sbuhp", later_low, in_state)
    g_in_state = g_in_state + mm("sbuhp,sbhpn->sbun", scaled, later_low)
    grad_values = grad_values + grad_scaled * weight[..., None]
    grad_weight = jnp.sum(grad_scaled * values_f, -1)
    grad_dt = grad_dt + grad_weight * end_decay
    spread = grad_weight * weight
    last = jnp.sum(spread, 2) + grad_passing * passing
    grad_cum = grad_cum - spread
    grad_cum = grad_cum.at[:, :, -1].add(last)
    grad_log = jnp.flip(jnp.cumsum(jnp.flip(grad_cum, 2), 2), 2)
    grad_dt = grad_dt + decay_rate * grad_log
    g_step = (grad_dt * jax.nn.sigmoid(step_arg)).astype(bf16).reshape(seqs, length, hn)
    grad_conv = jnp.concatenate(
        [
            grad_values.reshape(seqs, length, hc),
            g_in_state.reshape(seqs, length, state),
            g_out_state.reshape(seqs, length, state),
        ],
        -1,
    ) * silu_slope(conv_pre)
    grad_conv_in = sum(
        shift_up(conv_w[j] * grad_conv * same[j], taps - 1 - j) for j in range(taps)
    )
    gp_gate = grad_gate.astype(bf16)
    gp_conv = grad_conv_in.astype(bf16)
    g_in_up_gate = compact(mm("str,stc->src", rank_in, gp_gate))
    g_in_up_conv = compact(mm("str,stc->src", rank_in, gp_conv))
    partial = jnp.concatenate(
        [
            mm("stc,dc->std", gp_gate, wb)
            + mm("stc,dc->std", gp_conv, wa[:, :conv_cols])
            + mm("sth,dh->std", g_step, wa[:, conv_cols + ranks : conv_cols + ranks + hn]),
            mm("stc,cr->str", gp_gate, up_gate) + mm("stc,cr->str", gp_conv, up_conv),
        ],
        -1,
    )
    partial = lax.psum_scatter(partial, "seq", scatter_dimension=1, tiled=True)
    grad_rank_in = (partial[..., width:] * mask).astype(bf16)
    down_in = wa[:, conv_cols : conv_cols + ranks]
    grad_normed = partial[..., :width] + mm("str,dr->std", grad_rank_in, down_in)
    own = layer_input.astype(f32)
    inv_own = lax.rsqrt(jnp.mean(own * own, -1, keepdims=True) + EPS)
    normed_own = (own * inv_own * gain).astype(bf16)
    g_in_down = compact(mm("str,std->srd", grad_rank_in, normed_own))
    scaled_in = grad_normed * gain
    grad_in = (
        inv_own * scaled_in
        - own * inv_own**3 * jnp.mean(scaled_in * own, -1, keepdims=True)
        + output_gradient.astype(f32)
    )

    def placed(parts, total):
        full = jnp.zeros((seqs, rank, total), f32)
        for part, start in parts:
            full = lax.dynamic_update_slice_in_dim(full, part, start, 2)
        return full

    everything = [
        g_in_down,
        placed(
            [
                (g_in_up_gate, here * hc),
                (g_in_up_conv[..., :hc], inner + here * hc),
                (g_in_up_conv[..., hc:], 2 * inner),
            ],
            cols,
        ),
        placed([(g_out_down, here * hc)], inner),
        g_out_up,
    ]
    owners = dps * n
    widths = [v.shape[-1] // owners for v in everything]
    packed = jnp.concatenate(
        [v.reshape(seqs, rank, owners, -1) for v in everything], -1
    ).transpose(2, 0, 1, 3)
    got = lax.all_to_all(packed, both, 0, 0, tiled=True)
    got = got.reshape(dps, n, seqs, rank, -1).sum(1)
    all_chosen = (every_index[..., None] == jnp.arange(adapters)).astype(f32)
    table = jnp.einsum("dsk,dsrc->krc", all_chosen, got, precision=lax.Precision.HIGHEST)
    cuts = [sum(widths[:i]) for i in range(len(widths) + 1)]
    grads = [table[..., cuts[i] : cuts[i + 1]] for i in range(len(widths))]
    return (output, grad_in, grads[0], grads[1], grads[2], grads[3])


def solution(mesh):
    return jax.shard_map(
        per_device,
        mesh=mesh,
        in_specs=(
            P("dp", "seq", None),
            P("dp", "seq"),
            P("dp"),
            P(("dp", "seq")),
            P(("dp", "seq"), None),
            P(("dp", "seq"), None),
            P(("dp", "seq"), None),
            P(("dp", "seq")),
            P(),
            P(),
            P(),
            P(("dp", "seq")),
            P(("dp", "seq"), None),
            P(None, None, ("dp", "seq")),
            P(None, None, ("dp", "seq")),
            P(None, None, ("dp", "seq")),
            P(None, None, ("dp", "seq")),
            P("dp", "seq", None),
        ),
        out_specs=(
            P("dp", "seq", None),
            P("dp", "seq", None),
            P(None, None, ("dp", "seq")),
            P(None, None, ("dp", "seq")),
            P(None, None, ("dp", "seq")),
            P(None, None, ("dp", "seq")),
        ),
        check_vma=False,
    )
```

```python
import functools

import jax
import jax.numpy as jnp
from jax import lax
from jax.experimental import pallas as pl
from jax.experimental.pallas import tpu as pltpu
from jax.sharding import PartitionSpec as P

EPS = 1e-05
f32 = jnp.float32
bf16 = jnp.bfloat16
BLOCK = 256


def mm(form, a, b):
    return jnp.einsum(form, a, b, preferred_element_type=f32)


LOG2E = 1.4426950408889634
VMEM_BYTES = 66_000_000


def dot_nn(a, b):
    return lax.dot_general(a, b, (((1,), (0,)), ((), ())), preferred_element_type=f32)


def dot_nt(a, b):
    return lax.dot_general(a, b, (((1,), (1,)), ((), ())), preferred_element_type=f32)


def dot_tn(a, b):
    return lax.dot_general(a, b, (((0,), (0,)), ((), ())), preferred_element_type=f32)


def dot_exact(a, b):
    return lax.dot_general(
        a, b, (((1,), (0,)), ((), ())), preferred_element_type=f32, precision=lax.Precision.HIGHEST
    )


def sigmoid(v):
    return 0.5 * jnp.tanh(0.5 * v) + 0.5


def spread_pair(cols, j):
    rows = cols.shape[0]
    lane = lax.broadcasted_iota(jnp.int32, (rows, 128), 1)
    return jnp.where(lane < 64, cols[:, 2 * j : 2 * j + 1], cols[:, 2 * j + 1 : 2 * j + 2])


def spread_all(cols, pairs):
    return jnp.concatenate([spread_pair(cols, j) for j in range(pairs)], 1)


def per_head(v, select):
    hi = v.astype(bf16)
    lo = (v - hi.astype(f32)).astype(bf16)
    return dot_nn(hi, select) + dot_nn(lo, select)


def forward_kernel(
    x_ref, meta_ref, doc_ref, wa_ref, up_ref, conv_ref, gain_ref, head_ref, mask_ref, half_ref,
    normed_ref, rank_ref, vbc_ref, pre_ref, ssm_ref, state_ref, tok_ref,
    buf, carry,
    *, hn, hc,
):
    pairs = hn // 2
    cc = hc + 256

    @pl.when(pl.program_id(1) == 0)
    def _():
        carry[...] = jnp.zeros_like(carry)
        buf[0:8, :] = jnp.zeros((8, cc), f32)

    x = x_ref[0].astype(f32)
    inv = lax.rsqrt(jnp.mean(x * x, -1, keepdims=True) + EPS)
    normed = (x * inv * gain_ref[0:1, :]).astype(bf16)
    normed_ref[0] = normed
    pa = dot_nn(normed, wa_ref[...])
    rank = (pa[:, cc : cc + 128] * mask_ref[0, 0:1, :]).astype(bf16)
    rank_ref[0] = rank
    conv_in = (pa[:, :cc] + dot_nt(rank, up_ref[...])).astype(bf16).astype(f32)
    buf[8:, :] = conv_in
    meta = meta_ref[0]
    pre = conv_ref[4:5, :] + conv_ref[3:4, :] * conv_in
    for k in (1, 2, 3):
        pre = pre + conv_ref[3 - k : 4 - k, :] * (buf[8 - k : 8 - k + BLOCK, :] * meta[:, k - 1 : k])
    buf[0:8, :] = buf[BLOCK : BLOCK + 8, :]
    pre_ref[0] = pre
    vbc = (pre * sigmoid(pre)).astype(bf16)
    vbc_ref[0] = vbc
    values = vbc[:, :hc]
    in_state = vbc[:, hc : hc + 128]
    out_state = vbc[:, hc + 128 :]
    arg = pa[:, cc + 128 : cc + 256] + head_ref[0:1, :]
    dt = jnp.maximum(arg, 0.0) + jnp.log1p(jnp.exp(-jnp.abs(arg)))
    row = lax.broadcasted_iota(jnp.int32, (BLOCK, BLOCK), 0)
    col = lax.broadcasted_iota(jnp.int32, (BLOCK, BLOCK), 1)
    cum = dot_exact((row >= col).astype(f32), dt * head_ref[1:2, :])
    tok_ref[0, :, 0:128] = dt
    tok_ref[0, :, 128:256] = cum
    tok_ref[0, :, 256:384] = arg
    left = cum * LOG2E
    right = (left - jnp.log(jnp.maximum(dt, 1e-37)) * LOG2E).T
    ok = (row >= col) & (meta[:, 5:6] == doc_ref[0, 0])
    bias = jnp.where(ok, 0.0, -1e30)
    contact = dot_nt(out_state, in_state)
    entry = jnp.exp(cum) * meta[:, 3:4]
    weight = jnp.exp(cum[BLOCK - 1 :, :] - cum) * dt * meta[:, 4:5]
    state = carry[...]
    state_low = state.astype(bf16)
    state_ref[0, 0] = state_low
    readout = dot_nt(out_state, state_low)
    half = BLOCK // 2
    scaled = []
    for j in range(pairs):
        at = slice(128 * j, 128 * j + 128)
        v = values[:, at]
        ys = []
        for r0, c1 in ((0, half), (half, BLOCK)):
            ws = []
            for h in (2 * j, 2 * j + 1):
                e = jnp.exp2(
                    (left[r0 : r0 + half, h : h + 1] - right[h : h + 1, :c1])
                    + bias[r0 : r0 + half, :c1]
                )
                ws.append((contact[r0 : r0 + half, :c1] * e).astype(bf16))
            vv = jnp.concatenate([v[:c1] * half_ref[0:1, :], v[:c1] * half_ref[1:2, :]], 0)
            ys.append(dot_nn(jnp.concatenate(ws, 1), vv))
        y = jnp.concatenate(ys, 0)
        ssm_ref[0, :, at] = y + readout[:, at] * spread_pair(entry, j)
        scaled.append((v.astype(f32) * spread_pair(weight, j)).astype(bf16))
    local = dot_tn(jnp.concatenate(scaled, 1), in_state)
    passing = entry[BLOCK - 1 :, :]
    for h in range(hn):
        at = slice(64 * h, 64 * h + 64)
        carry[at, :] = passing[:, h : h + 1] * state[at] + local[at]


def middle_kernel(
    normed_ref, rank_ref, vbc_ref, ssm_ref, og_ref, wb_ref, up_ref, wo_ref, upo_ref, row_ref, mask_ref,
    g_ref, q_ref, gro_ref, part_ref, stat_ref,
    *, hc, width,
):
    gate = dot_nn(normed_ref[0], wb_ref[...]) + dot_nt(rank_ref[0], up_ref[...])
    g_ref[0] = gate
    mixed = ssm_ref[0] + row_ref[0:1, :] * vbc_ref[0, :, :hc].astype(f32)
    gated = mixed * (gate * sigmoid(gate))
    og = og_ref[0]
    gro = (dot_nt(og, upo_ref[...]) * mask_ref[0, 0:1, :]).astype(bf16)
    gro_ref[0] = gro
    q = dot_nt(og, wo_ref[:, :width]) + dot_nt(gro, wo_ref[:, width : width + 128])
    q = q * row_ref[1:2, :]
    q_ref[0] = q
    lane = lax.broadcasted_iota(jnp.int32, (BLOCK, 128), 1)
    s0 = jnp.sum(gated * gated, -1, keepdims=True)
    s1 = jnp.sum(q * gated, -1, keepdims=True)
    stat_ref[0] = jnp.where(lane == 0, s0, s1).T[:8]
    part_ref[0] = dot_nn((gated * row_ref[1:2, :]).astype(bf16), wo_ref[:, : width + 128]).astype(
        part_ref.dtype
    )


def backward_kernel(
    q_ref, g_ref, ssm_ref, vbc_ref, pre_ref, tok_ref, rm_ref, meta_ref, doc_ref, state_ref, next_ref,
    rank_ref, gro_ref, conv_ref, head_ref, row_ref, half_ref, select_ref,
    gpg_ref, gpc_ref, gs_ref, up_ref, down_ref,
    buf, carry,
    *, hn, hc,
):
    pairs = hn // 2
    cc = hc + 256
    first = pl.program_id(1) == 0

    @pl.when(first)
    def _():
        carry[...] = jnp.zeros_like(carry)
        buf[BLOCK:, :] = jnp.zeros((8, cc), f32)
        up_ref[...] = jnp.zeros_like(up_ref)
        down_ref[...] = jnp.zeros_like(down_ref)

    rm = jnp.concatenate([rm_ref[0]] * 16, 0).T
    inv = rm[:, 0:1]
    mean = rm[:, 1:2]
    meta = meta_ref[0]
    gate = g_ref[0]
    ssm = ssm_ref[0]
    q = q_ref[0]
    vbc = vbc_ref[0]
    values = vbc[:, :hc]
    values_f = values.astype(f32)
    in_state = vbc[:, hc : hc + 128]
    out_state = vbc[:, hc + 128 :]
    skip = row_ref[0:1, :]
    mixed = ssm + skip * values_f
    sg = sigmoid(gate)
    act = gate * sg
    gated = mixed * act
    gated_r = gated * inv
    grad_gated = inv * (q - gated_r * (inv * mean))
    gated_low = (gated_r * row_ref[1:2, :]).astype(bf16)
    down_ref[0] = down_ref[0] + dot_tn(gro_ref[0], gated_low)
    grad_mixed = grad_gated * act
    gp_gate = (grad_gated * mixed * (sg + act * (1.0 - sg))).astype(bf16)
    gpg_ref[0] = gp_gate
    gsum = grad_mixed.astype(bf16)
    gsum_f = gsum.astype(f32)

    dt = tok_ref[0, :, 0:128]
    cum = tok_ref[0, :, 128:256]
    arg = tok_ref[0, :, 256:384]
    scaled_cum = cum * LOG2E
    down = scaled_cum - jnp.log(jnp.maximum(dt, 1e-37)) * LOG2E
    across = scaled_cum.T
    row = lax.broadcasted_iota(jnp.int32, (BLOCK, BLOCK), 0)
    col = lax.broadcasted_iota(jnp.int32, (BLOCK, BLOCK), 1)
    ok = (col >= row) & (meta[:, 5:6] == doc_ref[0, 0])
    bias = jnp.where(ok, 0.0, -1e30)
    contact = dot_nt(in_state, out_state)
    entry = jnp.exp(cum) * meta[:, 3:4]
    weight = jnp.exp(cum[BLOCK - 1 :, :] - cum) * dt * meta[:, 4:5]
    later = carry[...]
    later_low = later.astype(bf16)
    grad_scaled = dot_nt(in_state, later_low)
    weight_wide = spread_all(weight, pairs)
    entry_wide = spread_all(entry, pairs)
    scaled = (values_f * weight_wide).astype(bf16)
    weighted = (gsum_f * entry_wide).astype(bf16)
    half = BLOCK // 2
    g_con = [jnp.zeros((half, BLOCK), f32), jnp.zeros((half, half), f32)]
    g_val = []
    for j in range(pairs):
        at = slice(128 * j, 128 * j + 128)
        v = values[:, at]
        gs = gsum[:, at]
        tops = []
        for i, (r0, c0) in enumerate(((0, 0), (half, half))):
            ws = []
            for side in (0, 1):
                h = 2 * j + side
                gw = dot_nt(v[r0 : r0 + half] * half_ref[side : side + 1, :], gs[c0:])
                e = jnp.exp2(
                    (across[h : h + 1, c0:] - down[r0 : r0 + half, h : h + 1])
                    + bias[r0 : r0 + half, c0:]
                )
                ws.append((contact[r0 : r0 + half, c0:] * e).astype(bf16))
                g_con[i] = g_con[i] + gw * e
            gg = jnp.concatenate([gs[c0:] * half_ref[0:1, :], gs[c0:] * half_ref[1:2, :]], 0)
            tops.append(dot_nn(jnp.concatenate(ws, 1), gg))
        g_val.append(jnp.concatenate(tops, 0))
    g_val = jnp.concatenate(g_val, 1) + grad_scaled * weight_wide
    con_low = jnp.concatenate(
        [g_con[0], jnp.concatenate([jnp.zeros((half, half), f32), g_con[1]], 1)], 0
    ).astype(bf16)
    g_in = dot_nn(con_low, out_state) + dot_nn(scaled, later_low)
    g_out = dot_tn(con_low, in_state) + dot_nn(weighted, state_ref[0, 0])
    select = select_ref[...]
    spent = per_head(values_f * g_val, select)
    gained = per_head(gsum_f * ssm, select)
    ends = later * next_ref[0, 0].astype(f32)
    parts = [jnp.sum(ends[64 * h : 64 * h + 64], 0, keepdims=True) for h in range(hn)]
    parts.append(jnp.zeros((128 - hn, 128), f32))
    last = jnp.sum(jnp.concatenate(parts, 0).T, 0, keepdims=True)
    where_last = lax.broadcasted_iota(jnp.int32, (BLOCK, 128), 0) == BLOCK - 1
    grad_cum = gained - spent + jnp.where(where_last, last, 0.0)
    grad_log = dot_exact((col >= row).astype(f32), grad_cum)
    sig = sigmoid(arg)
    gs_ref[0] = (
        spent * (sig / jnp.maximum(dt, 1e-37)) + head_ref[1:2, :] * grad_log * sig
    ).astype(bf16)
    passing = entry[BLOCK - 1 :, :]
    direct = dot_tn(weighted, out_state)
    for h in range(hn):
        at = slice(64 * h, 64 * h + 64)
        carry[at, :] = passing[:, h : h + 1] * later[at] + direct[at]

    pre = pre_ref[0]
    sp = sigmoid(pre)
    grad_out = jnp.concatenate([skip * grad_mixed + g_val, g_in, g_out], 1)
    grad_pre = grad_out * (sp + pre * sp * (1.0 - sp))
    buf[:BLOCK, :] = grad_pre
    total = conv_ref[3:4, :] * grad_pre
    for k in (1, 2, 3):
        total = total + conv_ref[3 - k : 4 - k, :] * (buf[k : k + BLOCK, :] * meta[:, 5 + k : 6 + k])
    buf[BLOCK:, :] = grad_pre[:8]
    gp_conv = total.astype(bf16)
    gpc_ref[0] = gp_conv
    rank = rank_ref[0]
    up_ref[0, :, :hc] = up_ref[0, :, :hc] + dot_tn(rank, gp_gate)
    up_ref[0, :, hc:] = up_ref[0, :, hc:] + dot_tn(rank, gp_conv)


def per_device(
    layer_input,
    document_index,
    adapter_index,
    input_norm_gain,
    input_projection,
    step_projection,
    convolution_weight,
    convolution_bias,
    head_step_bias,
    log_decay_rate,
    head_skip_gain,
    gated_norm_gain,
    output_projection,
    adapter_input_down,
    adapter_input_up,
    adapter_output_down,
    adapter_output_up,
    output_gradient,
):
    both = ("dp", "seq")
    dps, n = lax.axis_size("dp"), lax.axis_size("seq")
    here = lax.axis_index("seq")
    seqs, own_len, width = layer_input.shape
    adapters, rank, _ = adapter_input_down.shape
    ranks = adapters * rank
    heads = head_step_bias.shape[0]
    inner = output_projection.shape[0] * dps * n
    cols = input_projection.shape[1]
    state2 = cols - 2 * inner
    state = state2 // 2
    taps = convolution_weight.shape[1]
    hn = heads // n
    hc = inner // n
    hd = inner // heads
    length = own_len * n
    nb = length // BLOCK

    x_all = lax.all_gather(layer_input, "seq", axis=1, tiled=True)
    og_all = lax.all_gather(output_gradient, "seq", axis=1, tiled=True)
    docs = lax.all_gather(document_index, "seq", axis=1, tiled=True)

    rows = input_projection.shape[0]
    down_rows = adapter_input_down.reshape(ranks, rows).T
    step_pad = 128 - hn
    per_target = []
    for t in range(n):
        per_target.append(
            jnp.concatenate(
                [
                    input_projection[:, inner + t * hc : inner + (t + 1) * hc],
                    input_projection[:, 2 * inner :],
                    down_rows,
                    jnp.pad(step_projection[:, t * hn : (t + 1) * hn], ((0, 0), (0, step_pad))),
                    input_projection[:, t * hc : (t + 1) * hc],
                ],
                1,
            )
        )
    w_mine = lax.all_to_all(jnp.stack(per_target), "seq", 0, 0, tiled=True)
    w_mine = w_mine.reshape(n * rows, -1)
    w_in = lax.all_gather(w_mine, "dp", axis=0, tiled=True)
    conv_cols = hc + state2
    wa_cols = conv_cols + ranks + 128
    wa, wb = w_in[:, :wa_cols], w_in[:, wa_cols:]

    out_rows = output_projection.shape[0]
    w_o = jnp.concatenate(
        [
            output_projection,
            adapter_output_down.reshape(ranks, out_rows).T,
            jnp.pad(gated_norm_gain[:, None], ((0, 0), (0, 127))),
        ],
        1,
    )
    w_o = lax.ppermute(
        w_o, both, [(dps * s + d, n * d + s) for d in range(dps) for s in range(n)]
    )
    w_o = lax.all_gather(w_o, "dp", axis=0, tiled=True)
    gate_gain = w_o[:, width + ranks].astype(f32)

    up_rows = adapter_input_up.shape[2]
    conv_rows = convolution_weight.shape[0]

    wide = -(-conv_rows // 128) * 128

    def as_row(v):
        return jnp.pad(v, ((0, 0), (0, wide - v.shape[1])))

    misc = jnp.concatenate(
        [
            as_row(convolution_weight.T),
            as_row(convolution_bias[None]),
            as_row(input_norm_gain[None]),
            as_row(adapter_index.astype(bf16)[None]),
        ],
        0,
    )
    misc_rows = misc.shape[0]
    small = jnp.concatenate(
        [
            adapter_input_up.reshape(ranks, up_rows).T,
            adapter_output_up.reshape(ranks, rows).T,
            misc.reshape(-1, 128),
        ],
        0,
    )
    small = lax.all_gather(small, both, axis=0)
    up_full = small[:, :up_rows].reshape(cols, ranks)
    up_out = small[:, up_rows : up_rows + rows].reshape(width, ranks)
    misc = small[:, up_rows + rows :].reshape(dps * n, misc_rows, wide)
    conv_w = jnp.moveaxis(misc[:, :taps, :conv_rows], 1, 0).reshape(taps, -1).astype(f32)
    conv_b = misc[:, taps, :conv_rows].reshape(-1).astype(f32)
    gain = misc[:, taps + 1, :rows].reshape(-1).astype(f32)
    every_index = misc[:, taps + 2, :seqs].reshape(dps, n, seqs)[:, 0].astype(jnp.int32)

    def mine(v, size, base=0):
        return lax.dynamic_slice_in_dim(v, base + here * size, size, 0)

    up_gate = mine(up_full, hc)
    up_conv = jnp.concatenate([mine(up_full, hc, inner), up_full[2 * inner :]], 0)
    conv_w = jnp.concatenate([mine(conv_w.T, hc), conv_w.T[inner:]], 0).T
    conv_b = jnp.concatenate([mine(conv_b, hc), conv_b[inner:]], 0)
    step_bias = mine(head_step_bias, hn)
    decay_rate = -jnp.exp(mine(log_decay_rate, hn))
    skip = mine(head_skip_gain, hn)

    chosen = (adapter_index[:, None] == jnp.arange(adapters, dtype=jnp.int32)[None, :]).astype(f32)
    mask = jnp.repeat(chosen, rank, axis=1)[:, None, :]

    doc_f = docs.astype(f32)

    def before(k):
        return jnp.pad(doc_f, ((0, 0), (k, 0)), constant_values=-1.0)[:, :length] == doc_f

    def after(k):
        return jnp.pad(doc_f, ((0, 0), (0, k)), constant_values=-1.0)[:, k:] == doc_f

    blocks = doc_f.reshape(seqs, nb, BLOCK)
    prior = jnp.concatenate([blocks[:, :1, 0], blocks[:, :-1, -1]], 1)
    keep = (blocks == prior[:, :, None]).reshape(seqs, length)
    ends = (blocks == blocks[:, :, -1:]).reshape(seqs, length)
    flags = [before(1), before(2), before(3), keep, ends, doc_f, after(1), after(2), after(3)]
    meta = jnp.stack([v.astype(f32) for v in flags], -1)
    meta = jnp.pad(meta, ((0, 0), (0, 0), (0, 128 - len(flags))))
    doc_rows = blocks[:, :, None, :]

    def rows8(*vs):
        return jnp.pad(jnp.stack(vs), ((0, 8 - len(vs)), (0, 0)))

    conv_rows8 = rows8(conv_w[0], conv_w[1], conv_w[2], conv_w[3], conv_b)
    head_rows = rows8(
        jnp.pad(step_bias, (0, 128 - hn)), jnp.pad(decay_rate, (0, 128 - hn))
    )
    wide_rows = rows8(jnp.repeat(skip, hd), gate_gain)
    gain_rows = rows8(gain)
    halves = jnp.pad(
        (jnp.arange(128)[None, :] // 64 == jnp.arange(2)[:, None]).astype(bf16), ((0, 14), (0, 0))
    )
    select = (jnp.arange(hc)[:, None] // hd == jnp.arange(128)[None, :]).astype(bf16)
    mask8 = jnp.broadcast_to(mask, (seqs, 8, ranks))
    grid = (seqs, nb)

    def tile(w, flip=False):
        return pl.BlockSpec(
            (1, BLOCK, w), (lambda s, b: (s, nb - 1 - b, 0)) if flip else (lambda s, b: (s, b, 0))
        )

    def fixed(v):
        return pl.BlockSpec(v.shape, lambda s, b: (0,) * v.ndim, pipeline_mode=pl.Buffered(1))

    def by_seq(v):
        return pl.BlockSpec((1,) + v.shape[1:], lambda s, b: (s, 0, 0))

    def shape(w, dtype):
        return jax.ShapeDtypeStruct((seqs, length, w), dtype)

    params = pltpu.CompilerParams(
        dimension_semantics=("arbitrary", "arbitrary"), vmem_limit_bytes=VMEM_BYTES
    )
    cc = conv_cols
    tokens = seqs * length
    state_shape = jax.ShapeDtypeStruct((seqs, nb, hc, state), bf16)
    normed, rank_in, vbc, pre, ssm, states_low, tok = pl.pallas_call(
        functools.partial(forward_kernel, hn=hn, hc=hc),
        grid=grid,
        in_specs=[
            tile(width), tile(128), pl.BlockSpec((1, 1, 1, BLOCK), lambda s, b: (s, b, 0, 0)),
            fixed(wa), fixed(up_conv), fixed(conv_rows8), fixed(gain_rows), fixed(head_rows),
            by_seq(mask8), fixed(halves),
        ],
        out_specs=[
            tile(width), tile(128), tile(cc), tile(cc), tile(hc),
            pl.BlockSpec((1, 1, hc, state), lambda s, b: (s, b, 0, 0)), tile(384),
        ],
        out_shape=[
            shape(width, bf16), shape(128, bf16), shape(cc, bf16), shape(cc, f32), shape(hc, f32),
            state_shape, shape(384, f32),
        ],
        scratch_shapes=[pltpu.VMEM((BLOCK + 8, cc), f32), pltpu.VMEM((hc, state), f32)],
        compiler_params=params,
        name="ssm_forward",
        cost_estimate=pl.CostEstimate(
            flops=2 * tokens * (width * wa_cols + 3 * BLOCK * hc), bytes_accessed=40 << 20, transcendentals=0
        ),
    )(x_all, meta, doc_rows, wa, up_conv, conv_rows8, gain_rows, head_rows, mask8, halves)

    w_ext = w_o[:, : width + ranks]
    gate, q, grad_rank_out, branch, stats = pl.pallas_call(
        functools.partial(middle_kernel, hc=hc, width=width),
        grid=grid,
        in_specs=[
            tile(width), tile(128), tile(cc), tile(hc), tile(width), fixed(wb), fixed(up_gate),
            fixed(w_ext), fixed(up_out.T), fixed(wide_rows), by_seq(mask8),
        ],
        out_specs=[
            tile(hc), tile(hc), tile(128), tile(width + ranks),
            pl.BlockSpec((1, 8, BLOCK), lambda s, b: (s, 0, b)),
        ],
        out_shape=[
            shape(hc, f32), shape(hc, f32), shape(128, bf16), shape(width + ranks, f32),
            jax.ShapeDtypeStruct((seqs, 8, length), f32),
        ],
        compiler_params=params,
        name="gate_and_output",
        cost_estimate=pl.CostEstimate(
            flops=2 * tokens * width * hc * 3, bytes_accessed=50 << 20, transcendentals=0
        ),
    )(normed, rank_in, vbc, ssm, og_all, wb, up_gate, w_ext, up_out.T, wide_rows, mask8)

    stats = lax.psum(stats[:, :2], "seq")
    inv_gated = lax.rsqrt(stats[:, :1] / inner + EPS)
    rm = jnp.concatenate([inv_gated, stats[:, 1:] / inner], 1)
    rm = jnp.pad(rm, ((0, 0), (0, 6), (0, 0)))
    branch = lax.psum_scatter(branch, "seq", scatter_dimension=1, tiled=True)
    inv_mine = lax.dynamic_slice_in_dim(inv_gated[:, 0], here * own_len, own_len, 1)[..., None]
    branch = branch * inv_mine
    rank_out = (branch[..., width:] * mask).astype(bf16)
    output = (
        layer_input.astype(f32) + branch[..., :width] + mm("str,dr->std", rank_out, up_out)
    ).astype(bf16)

    def compact(v):
        return v.reshape(seqs, adapters, rank, -1).sum(1)

    g_out_up = compact(mm("str,std->srd", rank_out, output_gradient))

    def back_state(at):
        return pl.BlockSpec((1, 1, hc, state), lambda s, b: (s, at(nb - 1 - b), 0, 0))

    gp_gate, gp_conv, g_step, g_in_up, g_out_down = pl.pallas_call(
        functools.partial(backward_kernel, hn=hn, hc=hc),
        grid=grid,
        in_specs=[
            tile(hc, True), tile(hc, True), tile(hc, True), tile(cc, True), tile(cc, True),
            tile(384, True), pl.BlockSpec((1, 8, BLOCK), lambda s, b: (s, 0, nb - 1 - b)),
            tile(128, True), pl.BlockSpec((1, 1, 1, BLOCK), lambda s, b: (s, nb - 1 - b, 0, 0)),
            back_state(lambda b: b), back_state(lambda b: jnp.minimum(b + 1, nb - 1)),
            tile(128, True), tile(128, True), fixed(conv_rows8), fixed(head_rows), fixed(wide_rows),
            fixed(halves), fixed(select),
        ],
        out_specs=[
            tile(hc, True), tile(cc, True), tile(128, True),
            pl.BlockSpec((1, ranks, hc + cc), lambda s, b: (s, 0, 0)),
            pl.BlockSpec((1, ranks, hc), lambda s, b: (s, 0, 0)),
        ],
        out_shape=[
            shape(hc, bf16), shape(cc, bf16), shape(128, bf16),
            jax.ShapeDtypeStruct((seqs, ranks, hc + cc), f32),
            jax.ShapeDtypeStruct((seqs, ranks, hc), f32),
        ],
        scratch_shapes=[pltpu.VMEM((BLOCK + 8, cc), f32), pltpu.VMEM((hc, state), f32)],
        compiler_params=params,
        name="ssm_backward",
        cost_estimate=pl.CostEstimate(
            flops=2 * tokens * 8 * BLOCK * hc, bytes_accessed=50 << 20, transcendentals=0
        ),
    )(
        q, gate, ssm, vbc, pre, tok, rm, meta, doc_rows, states_low, states_low, rank_in,
        grad_rank_out, conv_rows8, head_rows, wide_rows, halves, select,
    )
    g_in_up = compact(g_in_up)
    g_in_up_gate, g_in_up_conv = g_in_up[..., :hc], g_in_up[..., hc:]
    g_out_down = compact(g_out_down)
    partial = jnp.concatenate(
        [
            mm("stc,dc->std", gp_gate, wb)
            + mm("stc,dc->std", gp_conv, wa[:, :conv_cols])
            + mm("sth,dh->std", g_step, wa[:, conv_cols + ranks :]),
            mm("stc,cr->str", gp_gate, up_gate) + mm("stc,cr->str", gp_conv, up_conv),
        ],
        -1,
    )
    partial = lax.psum_scatter(partial, "seq", scatter_dimension=1, tiled=True)
    grad_rank_in = (partial[..., width:] * mask).astype(bf16)
    down_in = wa[:, conv_cols : conv_cols + ranks]
    grad_normed = partial[..., :width] + mm("str,dr->std", grad_rank_in, down_in)
    own = layer_input.astype(f32)
    inv_own = lax.rsqrt(jnp.mean(own * own, -1, keepdims=True) + EPS)
    normed_own = (own * inv_own * gain).astype(bf16)
    g_in_down = compact(mm("str,std->srd", grad_rank_in, normed_own))
    scaled_in = grad_normed * gain
    grad_in = (
        inv_own * scaled_in
        - own * inv_own**3 * jnp.mean(scaled_in * own, -1, keepdims=True)
        + output_gradient.astype(f32)
    )

    def placed(parts, total):
        full = jnp.zeros((seqs, rank, total), f32)
        for part, start in parts:
            full = lax.dynamic_update_slice_in_dim(full, part, start, 2)
        return full

    everything = [
        g_in_down,
        placed(
            [
                (g_in_up_gate, here * hc),
                (g_in_up_conv[..., :hc], inner + here * hc),
                (g_in_up_conv[..., hc:], 2 * inner),
            ],
            cols,
        ),
        placed([(g_out_down, here * hc)], inner),
        g_out_up,
    ]
    owners = dps * n
    widths = [v.shape[-1] // owners for v in everything]
    packed = jnp.concatenate(
        [v.reshape(seqs, rank, owners, -1) for v in everything], -1
    ).transpose(2, 0, 1, 3)
    got = lax.all_to_all(packed, both, 0, 0, tiled=True)
    got = got.reshape(dps, n, seqs, rank, -1).sum(1)
    all_chosen = (every_index[..., None] == jnp.arange(adapters)).astype(f32)
    table = jnp.einsum("dsk,dsrc->krc", all_chosen, got, precision=lax.Precision.HIGHEST)
    cuts = [sum(widths[:i]) for i in range(len(widths) + 1)]
    grads = [table[..., cuts[i] : cuts[i + 1]] for i in range(len(widths))]
    return (output, grad_in, grads[0], grads[1], grads[2], grads[3])


def solution(mesh):
    return jax.shard_map(
        per_device,
        mesh=mesh,
        in_specs=(
            P("dp", "seq", None),
            P("dp", "seq"),
            P("dp"),
            P(("dp", "seq")),
            P(("dp", "seq"), None),
            P(("dp", "seq"), None),
            P(("dp", "seq"), None),
            P(("dp", "seq")),
            P(),
            P(),
            P(),
            P(("dp", "seq")),
            P(("dp", "seq"), None),
            P(None, None, ("dp", "seq")),
            P(None, None, ("dp", "seq")),
            P(None, None, ("dp", "seq")),
            P(None, None, ("dp", "seq")),
            P("dp", "seq", None),
        ),
        out_specs=(
            P("dp", "seq", None),
            P("dp", "seq", None),
            P(None, None, ("dp", "seq")),
            P(None, None, ("dp", "seq")),
            P(None, None, ("dp", "seq")),
            P(None, None, ("dp", "seq")),
        ),
        check_vma=False,
    )
```

```python
import functools

import jax
import jax.numpy as jnp
from jax import lax
from jax.experimental import pallas as pl
from jax.experimental.pallas import tpu as pltpu
from jax.sharding import PartitionSpec as P

EPS = 1e-05
f32 = jnp.float32
bf16 = jnp.bfloat16
BLOCK = 256


def mm(form, a, b):
    return jnp.einsum(form, a, b, preferred_element_type=f32)


LOG2E = 1.4426950408889634
VMEM_BYTES = 66_000_000


def dot_nn(a, b):
    return lax.dot_general(a, b, (((1,), (0,)), ((), ())), preferred_element_type=f32)


def dot_nt(a, b):
    return lax.dot_general(a, b, (((1,), (1,)), ((), ())), preferred_element_type=f32)


def dot_tn(a, b):
    return lax.dot_general(a, b, (((0,), (0,)), ((), ())), preferred_element_type=f32)


def dot_exact(a, b):
    return lax.dot_general(
        a, b, (((1,), (0,)), ((), ())), preferred_element_type=f32, precision=lax.Precision.HIGHEST
    )


def sigmoid(v):
    return 0.5 * jnp.tanh(0.5 * v) + 0.5


def spread_pair(cols, j):
    rows = cols.shape[0]
    lane = lax.broadcasted_iota(jnp.int32, (rows, 128), 1)
    return jnp.where(lane < 64, cols[:, 2 * j : 2 * j + 1], cols[:, 2 * j + 1 : 2 * j + 2])


def spread_all(cols, pairs):
    return jnp.concatenate([spread_pair(cols, j) for j in range(pairs)], 1)


def per_head(v, select):
    hi = v.astype(bf16)
    lo = (v - hi.astype(f32)).astype(bf16)
    return dot_nn(hi, select) + dot_nn(lo, select)


def by_rank(t, rank):
    out = t[:rank]
    for k in range(rank, 128, rank):
        out = out + t[k : k + rank]
    return out


def fold(v, rank):
    return by_rank(v.T, rank)


def assemble(order_ref, base, pieces, target, sems):
    copies = []
    for i, piece in enumerate(pieces):
        size = piece.shape[0]
        at = pl.multiple_of(order_ref[base + i] * size, 16)
        copies.append(pltpu.make_async_copy(piece, target.at[pl.ds(at, size)], sems.at[i]))
    for copy in copies:
        copy.start()
    for copy in copies:
        copy.wait()


def choose(order_ref, b, blocks, target):
    for i, block in enumerate(blocks):

        @pl.when(order_ref[b] == i)
        def _(block=block):
            target[...] = block[0]


def forward_kernel(order_ref, *refs, hn, hc, count, base, total):
    (x0, x1, x2, x3, meta_ref, doc_ref, up_ref, conv_ref, head_ref, mask_ref, half_ref) = refs[:11]
    pieces = refs[11 : 11 + count]
    rest = refs[11 + count :]
    if base:
        carry_in, rest = rest[0], rest[8:]
    else:
        full_ref, rest = rest[0], rest[1:]
    normed_ref, rank_ref, vbc_ref, pre_ref, ssm_ref, state_ref, tok_ref, *rest = rest
    if base + 2 < total:
        carry_out, rest = rest[0], rest[1:]
    buf, carry, x_buf, wa_ref, gain_ref, sems, full_sem = rest
    pairs = hn // 2
    cc = hc + 256
    b = pl.program_id(0)
    last = b == pl.num_programs(0) - 1

    @pl.when(b == 0)
    def _():
        assemble(order_ref, 4, pieces, wa_ref, sems)
        gain_ref[...] = wa_ref[:, cc + 128 :].astype(f32).T[120:, :]
        if base:
            carry[...] = carry_in[0:hc, 0:128]
            for i in range(cc // 128):
                buf[0:8, 128 * i : 128 * i + 128] = carry_in[hc + 8 * i : hc + 8 * i + 8, :]
        else:
            pltpu.make_async_copy(wa_ref, full_ref, full_sem).start()
            carry[...] = jnp.zeros_like(carry)
            buf[0:8, :] = jnp.zeros((8, cc), f32)

    choose(order_ref, b + base, (x0, x1, x2, x3), x_buf)
    x = x_buf[...].astype(f32)
    inv = lax.rsqrt(jnp.mean(x * x, -1, keepdims=True) + EPS)
    normed = (x * inv * gain_ref[7:8, :]).astype(bf16)
    normed_ref[0] = normed
    pa = dot_nn(normed, wa_ref[...])
    rank = (pa[:, cc : cc + 128] * mask_ref[0, 0:1, :]).astype(bf16)
    rank_ref[0] = rank
    conv_in = (pa[:, :cc] + dot_nt(rank, up_ref[...])).astype(bf16).astype(f32)
    buf[8:, :] = conv_in
    meta = meta_ref[0]
    pre = conv_ref[4:5, :] + conv_ref[3:4, :] * conv_in
    for k in (1, 2, 3):
        pre = pre + conv_ref[3 - k : 4 - k, :] * (buf[8 - k : 8 - k + BLOCK, :] * meta[:, k - 1 : k])
    buf[0:8, :] = buf[BLOCK : BLOCK + 8, :]
    pre_ref[0] = pre
    vbc = (pre * sigmoid(pre)).astype(bf16)
    vbc_ref[0] = vbc
    values = vbc[:, :hc]
    in_state = vbc[:, hc : hc + 128]
    out_state = vbc[:, hc + 128 :]
    arg = pa[:, cc + 128 : cc + 256] + head_ref[0:1, :]
    dt = jnp.maximum(arg, 0.0) + jnp.log1p(jnp.exp(-jnp.abs(arg)))
    row = lax.broadcasted_iota(jnp.int32, (BLOCK, BLOCK), 0)
    col = lax.broadcasted_iota(jnp.int32, (BLOCK, BLOCK), 1)
    cum = dot_exact((row >= col).astype(f32), dt * head_ref[1:2, :])
    tok_ref[0, :, 0:128] = dt
    tok_ref[0, :, 128:256] = cum
    tok_ref[0, :, 256:384] = arg
    left = cum * LOG2E
    right = (left - jnp.log(jnp.maximum(dt, 1e-37)) * LOG2E).T
    ok = (row >= col) & (meta[:, 5:6] == doc_ref[0, 0])
    bias = jnp.where(ok, 0.0, -1e30)
    contact = dot_nt(out_state, in_state)
    entry = jnp.exp(cum) * meta[:, 3:4]
    weight = jnp.exp(cum[BLOCK - 1 :, :] - cum) * dt * meta[:, 4:5]
    state = carry[...]
    state_low = state.astype(bf16)
    state_ref[0, 0] = state_low
    readout = dot_nt(out_state, state_low)
    half = BLOCK // 2
    scaled = []
    for j in range(pairs):
        at = slice(128 * j, 128 * j + 128)
        v = values[:, at]
        ys = []
        for r0, c1 in ((0, half), (half, BLOCK)):
            ws = []
            for h in (2 * j, 2 * j + 1):
                e = jnp.exp2(
                    (left[r0 : r0 + half, h : h + 1] - right[h : h + 1, :c1])
                    + bias[r0 : r0 + half, :c1]
                )
                ws.append((contact[r0 : r0 + half, :c1] * e).astype(bf16))
            vv = jnp.concatenate([v[:c1] * half_ref[0:1, :], v[:c1] * half_ref[1:2, :]], 0)
            ys.append(dot_nn(jnp.concatenate(ws, 1), vv))
        y = jnp.concatenate(ys, 0)
        ssm_ref[0, :, at] = y + readout[:, at] * spread_pair(entry, j)
        scaled.append((v.astype(f32) * spread_pair(weight, j)).astype(bf16))
    local = dot_tn(jnp.concatenate(scaled, 1), in_state)
    passing = entry[BLOCK - 1 :, :]
    for h in range(hn):
        at = slice(64 * h, 64 * h + 64)
        carry[at, :] = passing[:, h : h + 1] * state[at] + local[at]

    @pl.when(last)
    def _():
        if base + 2 < total:
            carry_out[0:hc, :] = carry[...]
            for i in range(cc // 128):
                carry_out[hc + 8 * i : hc + 8 * i + 8, :] = buf[0:8, 128 * i : 128 * i + 128]
        if not base:
            pltpu.make_async_copy(wa_ref, full_ref, full_sem).wait()


def gate_kernel(order_ref, normed_ref, rank_ref, up_ref, *refs, hc, count):
    pieces = refs[:count]
    g_ref, full_ref, wb_ref, sems, full_sem = refs[count:]
    b = pl.program_id(0)
    full_copy = pltpu.make_async_copy(wb_ref, full_ref, full_sem)

    @pl.when(b == 0)
    def _():
        assemble(order_ref, 4, pieces, wb_ref, sems)
        full_copy.start()

    g_ref[0] = dot_nn(normed_ref[0], wb_ref[:, :hc]) + dot_nt(rank_ref[0], up_ref[...])

    @pl.when(b == pl.num_programs(0) - 1)
    def _():
        full_copy.wait()


def middle_kernel(order_ref, *refs, hc, width, rank, count):
    g_ref, vbc_ref, ssm_ref, og0, og1, og2, og3, upo_ref, row_ref, mask_ref = refs[:10]
    pieces = refs[10 : 10 + count]
    q_ref, gro_ref, *part_refs, stat_ref, og_buf, wo_ref, sems = refs[10 + count :]
    b = pl.program_id(0)

    @pl.when(b == 0)
    def _():
        assemble(order_ref, 4, pieces, wo_ref, sems)

    choose(order_ref, b, (og0, og1, og2, og3), og_buf)
    gate = g_ref[0]
    mixed = ssm_ref[0] + row_ref[0:1, :] * vbc_ref[0, :, :hc].astype(f32)
    gated = mixed * (gate * sigmoid(gate))
    og = og_buf[...]
    gro = (dot_nn(og, upo_ref[...]) * mask_ref[0, 0:1, :]).astype(bf16)
    gro_ref[0] = gro
    q = dot_nt(og, wo_ref[:, :width]) + dot_nt(gro, wo_ref[:, width : width + 128])
    q = q * row_ref[1:2, :]
    q_ref[0] = q
    lane = lax.broadcasted_iota(jnp.int32, (BLOCK, 128), 1)
    s0 = jnp.sum(gated * gated, -1, keepdims=True)
    s1 = jnp.sum(q * gated, -1, keepdims=True)
    stat_ref[0, 0:8, :] = jnp.where(lane == 0, s0, s1).T[:8]
    low = (gated * row_ref[1:2, :]).astype(bf16)
    part = dot_nn(low, wo_ref[:, :width]).astype(bf16)
    for i, part_ref in enumerate(part_refs):

        @pl.when(order_ref[b] == i)
        def _(part_ref=part_ref):
            part_ref[...] = part

    stat_ref[0, 8:, :] = fold(dot_nn(low, wo_ref[:, width : width + 128]) * mask_ref[0, 0:1, :], rank)


def backward_kernel(
    q_ref, g_ref, ssm_ref, vbc_ref, pre_ref, tok_ref, rm_ref, meta_ref, doc_ref, state_ref, next_ref,
    rank_ref, gro_ref, conv_ref, head_ref, row_ref, half_ref, select_ref, upg_ref, upc_ref, mask_ref,
    gpg_ref, gpc_ref, gs_ref, grads_ref, gri_ref,
    buf, carry,
    *, hn, hc, rank,
):
    pairs = hn // 2
    cc = hc + 256
    first = pl.program_id(0) == 0

    @pl.when(first)
    def _():
        carry[...] = jnp.zeros_like(carry)
        buf[BLOCK:, :] = jnp.zeros((8, cc), f32)
        grads_ref[...] = jnp.zeros_like(grads_ref)

    rm = jnp.concatenate([rm_ref[0]] * 16, 0).T
    inv = rm[:, 0:1]
    mean = rm[:, 1:2]
    meta = meta_ref[0]
    gate = g_ref[0]
    ssm = ssm_ref[0]
    q = q_ref[0]
    vbc = vbc_ref[0]
    values = vbc[:, :hc]
    values_f = values.astype(f32)
    in_state = vbc[:, hc : hc + 128]
    out_state = vbc[:, hc + 128 :]
    skip = row_ref[0:1, :]
    mixed = ssm + skip * values_f
    sg = sigmoid(gate)
    act = gate * sg
    gated = mixed * act
    gated_r = gated * inv
    grad_gated = inv * (q - gated_r * (inv * mean))
    gated_low = (gated_r * row_ref[1:2, :]).astype(bf16)
    grads_ref[0, :, hc + cc :] = grads_ref[0, :, hc + cc :] + by_rank(
        dot_tn(gro_ref[0], gated_low), rank
    )
    grad_mixed = grad_gated * act
    gp_gate = (grad_gated * mixed * (sg + act * (1.0 - sg))).astype(bf16)
    gpg_ref[0] = gp_gate
    gsum = grad_mixed.astype(bf16)
    gsum_f = gsum.astype(f32)

    dt = tok_ref[0, :, 0:128]
    cum = tok_ref[0, :, 128:256]
    arg = tok_ref[0, :, 256:384]
    scaled_cum = cum * LOG2E
    down = scaled_cum - jnp.log(jnp.maximum(dt, 1e-37)) * LOG2E
    across = scaled_cum.T
    row = lax.broadcasted_iota(jnp.int32, (BLOCK, BLOCK), 0)
    col = lax.broadcasted_iota(jnp.int32, (BLOCK, BLOCK), 1)
    ok = (col >= row) & (meta[:, 5:6] == doc_ref[0, 0])
    bias = jnp.where(ok, 0.0, -1e30)
    contact = dot_nt(in_state, out_state)
    entry = jnp.exp(cum) * meta[:, 3:4]
    weight = jnp.exp(cum[BLOCK - 1 :, :] - cum) * dt * meta[:, 4:5]
    later = carry[...]
    later_low = later.astype(bf16)
    grad_scaled = dot_nt(in_state, later_low)
    weight_wide = spread_all(weight, pairs)
    entry_wide = spread_all(entry, pairs)
    scaled = (values_f * weight_wide).astype(bf16)
    weighted = (gsum_f * entry_wide).astype(bf16)
    half = BLOCK // 2
    g_con = [jnp.zeros((half, BLOCK), f32), jnp.zeros((half, half), f32)]
    g_val = []
    for j in range(pairs):
        at = slice(128 * j, 128 * j + 128)
        v = values[:, at]
        gs = gsum[:, at]
        tops = []
        for i, (r0, c0) in enumerate(((0, 0), (half, half))):
            ws = []
            for side in (0, 1):
                h = 2 * j + side
                gw = dot_nt(v[r0 : r0 + half] * half_ref[side : side + 1, :], gs[c0:])
                e = jnp.exp2(
                    (across[h : h + 1, c0:] - down[r0 : r0 + half, h : h + 1])
                    + bias[r0 : r0 + half, c0:]
                )
                ws.append((contact[r0 : r0 + half, c0:] * e).astype(bf16))
                g_con[i] = g_con[i] + gw * e
            gg = jnp.concatenate([gs[c0:] * half_ref[0:1, :], gs[c0:] * half_ref[1:2, :]], 0)
            tops.append(dot_nn(jnp.concatenate(ws, 1), gg))
        g_val.append(jnp.concatenate(tops, 0))
    g_val = jnp.concatenate(g_val, 1) + grad_scaled * weight_wide
    con_low = jnp.concatenate(
        [g_con[0], jnp.concatenate([jnp.zeros((half, half), f32), g_con[1]], 1)], 0
    ).astype(bf16)
    g_in = dot_nn(con_low, out_state) + dot_nn(scaled, later_low)
    g_out = dot_tn(con_low, in_state) + dot_nn(weighted, state_ref[0, 0])
    select = select_ref[...]
    spent = per_head(values_f * g_val, select)
    gained = per_head(gsum_f * ssm, select)
    ends = later * next_ref[0, 0].astype(f32)
    parts = [jnp.sum(ends[64 * h : 64 * h + 64], 0, keepdims=True) for h in range(hn)]
    parts.append(jnp.zeros((128 - hn, 128), f32))
    last = jnp.sum(jnp.concatenate(parts, 0).T, 0, keepdims=True)
    where_last = lax.broadcasted_iota(jnp.int32, (BLOCK, 128), 0) == BLOCK - 1
    grad_cum = gained - spent + jnp.where(where_last, last, 0.0)
    grad_log = dot_exact((col >= row).astype(f32), grad_cum)
    sig = sigmoid(arg)
    gs_ref[0] = (
        spent * (sig / jnp.maximum(dt, 1e-37)) + head_ref[1:2, :] * grad_log * sig
    ).astype(bf16)
    passing = entry[BLOCK - 1 :, :]
    direct = dot_tn(weighted, out_state)
    for h in range(hn):
        at = slice(64 * h, 64 * h + 64)
        carry[at, :] = passing[:, h : h + 1] * later[at] + direct[at]

    pre = pre_ref[0]
    sp = sigmoid(pre)
    grad_out = jnp.concatenate([skip * grad_mixed + g_val, g_in, g_out], 1)
    grad_pre = grad_out * (sp + pre * sp * (1.0 - sp))
    buf[:BLOCK, :] = grad_pre
    total = conv_ref[3:4, :] * grad_pre
    for k in (1, 2, 3):
        total = total + conv_ref[3 - k : 4 - k, :] * (buf[k : k + BLOCK, :] * meta[:, 5 + k : 6 + k])
    buf[BLOCK:, :] = grad_pre[:8]
    gp_conv = total.astype(bf16)
    gpc_ref[0] = gp_conv
    rows = rank_ref[0]
    grads_ref[0, :, :hc] = grads_ref[0, :, :hc] + by_rank(dot_tn(rows, gp_gate), rank)
    grads_ref[0, :, hc : hc + cc] = grads_ref[0, :, hc : hc + cc] + by_rank(
        dot_tn(rows, gp_conv), rank
    )
    gri_ref[0] = fold(
        (dot_nn(gp_gate, upg_ref[...]) + dot_nn(gp_conv, upc_ref[...])) * mask_ref[0, 0:1, :], rank
    )


def input_gradient_kernel(order_ref, gpg_ref, gpc_ref, gs_ref, wa_ref, wb_ref, *outs, hc, cc):
    out = (
        dot_nt(gpg_ref[0], wb_ref[:, :hc])
        + dot_nt(gpc_ref[0], wa_ref[:, :cc])
        + dot_nt(gs_ref[0], wa_ref[:, cc + 128 :])
    ).astype(bf16)
    for i, out_ref in enumerate(outs):

        @pl.when(pl.program_id(0) == i)
        def _(out_ref=out_ref):
            out_ref[...] = out


def swap(v, axis, bit):
    size = lax.axis_size(axis)
    return lax.ppermute(v, axis, [(i, i ^ bit) for i in range(size)])


def put(pieces):
    rows = pieces[0][0].shape[0]
    out = jnp.zeros((len(pieces) * rows, pieces[0][0].shape[1]), pieces[0][0].dtype)
    for piece, slot in pieces:
        out = lax.dynamic_update_slice_in_dim(out, piece, slot * rows, 0)
    return out


def rotate(v, r):
    size = lax.axis_size("dp")
    return lax.ppermute(v, "dp", [(i, (i + 2 * r) % size) for i in range(size)])


def after(v, *others):
    return lax.optimization_barrier((v, others))[0]


def gather_seq(v):
    if lax.axis_size("seq") != 4:
        return lax.all_gather(v, "seq", axis=0, tiled=True)
    s = lax.axis_index("seq")
    far = swap(v, "seq", 2)
    return put([(v, s), (swap(v, "seq", 1), s ^ 1), (far, s ^ 2), (swap(far, "seq", 1), s ^ 3)])


def fence(*values):
    return lax.optimization_barrier(values)


def others(v):
    return [swap(v, "seq", k) for k in (1, 2, 3)]


def total_of(v, got):
    return (v + got[0]) + (got[1] + got[2])


def near_sums(k0, k1, k2, k3, r1, r3):
    return k0.astype(f32) + r1.astype(f32), (k2.astype(f32) + r3.astype(f32)).astype(bf16)


def scatter_plain(parts):
    v = jnp.concatenate(parts, 0).astype(f32)
    return lax.psum_scatter(v, "seq", scatter_dimension=0, tiled=True)


def per_device(
    layer_input,
    document_index,
    adapter_index,
    input_norm_gain,
    input_projection,
    step_projection,
    convolution_weight,
    convolution_bias,
    head_step_bias,
    log_decay_rate,
    head_skip_gain,
    gated_norm_gain,
    output_projection,
    adapter_input_down,
    adapter_input_up,
    adapter_output_down,
    adapter_output_up,
    output_gradient,
):
    both = ("dp", "seq")
    dps, n = lax.axis_size("dp"), lax.axis_size("seq")
    here = lax.axis_index("seq")
    seqs, own_len, width = layer_input.shape
    adapters, rank, _ = adapter_input_down.shape
    ranks = adapters * rank
    heads = head_step_bias.shape[0]
    inner = output_projection.shape[0] * dps * n
    cols = input_projection.shape[1]
    state2 = cols - 2 * inner
    state = state2 // 2
    taps = convolution_weight.shape[1]
    hn = heads // n
    hc = inner // n
    hd = inner // heads
    length = own_len * n
    nb = length // BLOCK

    staged = n == 4 and dps == 8
    rows = input_projection.shape[0]
    conv_cols = hc + state2
    wa_cols = conv_cols + ranks + 128
    shared = jnp.concatenate(
        [input_projection[:, 2 * inner :], adapter_input_down.reshape(ranks, rows).T], 1
    )
    late = adapter_output_up.reshape(ranks, rows).T
    doc_cols = -(-seqs * own_len // rows)
    doc_block = document_index.astype(bf16).reshape(-1)
    doc_block = jnp.pad(doc_block, (0, rows * doc_cols - doc_block.shape[0])).reshape(rows, -1)
    gap = jnp.zeros((rows, 127 - hn - doc_cols), bf16)
    payload = jnp.concatenate(
        [
            jnp.concatenate(
                [
                    input_projection[:, inner + t * hc : inner + (t + 1) * hc],
                    shared,
                    step_projection[:, t * hn : (t + 1) * hn],
                    gap,
                    doc_block,
                    input_norm_gain[:, None],
                ],
                1,
            )
            for t in range(n)
        ],
        0,
    )
    w_a = lax.all_to_all(payload, "seq", 0, 0, tiled=True)
    payload = jnp.concatenate(
        [
            jnp.concatenate([input_projection[:, t * hc : (t + 1) * hc], late], 1)
            for t in range(n)
        ],
        0,
    )

    up_rows = adapter_input_up.shape[2]
    conv_rows = convolution_weight.shape[0]
    wide = -(-conv_rows // 128) * 128

    def as_row(v):
        return jnp.pad(v, ((0, 0), (0, wide - v.shape[1])))

    misc = jnp.concatenate(
        [
            as_row(convolution_weight.T),
            as_row(convolution_bias[None]),
            as_row(adapter_index.astype(bf16)[None]),
            as_row(gated_norm_gain[None]),
        ],
        0,
    )
    misc_rows = misc.shape[0]
    small = jnp.concatenate([adapter_input_up.reshape(ranks, up_rows).T, misc.reshape(-1, 128)], 0)
    small = jnp.pad(small, ((0, -small.shape[0] % 16), (0, 0)))
    small_rows = small.shape[0]
    out_rows = output_projection.shape[0]
    w_o = jnp.concatenate([output_projection, adapter_output_down.reshape(ranks, out_rows).T], 1)
    to_head = [(dps * s + d, n * d + s) for d in range(dps) for s in range(n)]

    if staged:
        d = lax.axis_index("dp")
        y, z = d % 2, d // 2
        pair = put([(small, y), (swap(small, "dp", 1), 1 - y)])
        small = put(
            [(pair, z)] + [(rotate(pair, r), lax.rem(z + 4 - r, 4)) for r in (1, 2, 3)]
        )
        x_near = swap(layer_input, "seq", 1)
        w_a, payload, x_near = fence(w_a, payload, x_near)
        a1, a3, a0y = rotate(w_a, 1), rotate(w_a, 3), swap(w_a, "dp", 1)
        w_b = lax.all_to_all(payload, "seq", 0, 0, tiled=True)
        small_far = swap(small, "seq", 2)
        a1, a3, a0y, w_a, w_b, small, small_far, x0, x1, w_o = fence(
            a1, a3, a0y, w_a, w_b, small, small_far, layer_input[:1], layer_input[1:], w_o
        )
        a2 = rotate(w_a, 2)
        a1y, a3y = swap(a1, "dp", 1), swap(a3, "dp", 1)
        x_far0 = swap(x0, "seq", 2)
        small_near = swap(small, "seq", 1)
        small_both = swap(small_far, "seq", 1)
        a2, a1y, a3y, x_far0, small_near, small_both, w_b, x1 = fence(
            a2, a1y, a3y, x_far0, small_near, small_both, w_b, x1
        )
        small = put(
            [(small, here), (small_near, here ^ 1), (small_far, here ^ 2), (small_both, here ^ 3)]
        )
        a2y = swap(a2, "dp", 1)
        x_both0 = swap(x_far0, "seq", 1)
        wa_pieces = [w_a, a0y, a1, a1y, a2, a2y, a3, a3y]
        slots = []
        for r in (0, 1, 2, 3):
            at = 2 * lax.rem(z + 4 - r, 4) + y
            slots += [at, at ^ 1]
        slots = jnp.stack(slots).astype(jnp.int32)
        x_order = jnp.arange(4, dtype=jnp.int32) ^ here
        xs = [[layer_input, x_near, x_far0, x_both0]]
    else:
        w_b = lax.all_to_all(payload, "seq", 0, 0, tiled=True)
        w_o = lax.ppermute(w_o, both, to_head)
        small = lax.all_gather(lax.all_gather(small, "dp", tiled=True), "seq", tiled=True)
        wa_pieces = [lax.all_gather(w_a, "dp", tiled=True)]
        slots = jnp.zeros((1,), jnp.int32)
        x_order = jnp.arange(nb, dtype=jnp.int32)
        xs = [jnp.split(lax.all_gather(layer_input, "seq", axis=1, tiled=True), nb, axis=1)] * seqs
    docs = w_a[:, wa_cols - 1 - doc_cols : wa_cols - 1].reshape(n, -1)[:, : seqs * own_len]
    docs = jnp.moveaxis(docs.reshape(n, seqs, own_len), 0, 1).reshape(seqs, length)
    order = jnp.concatenate([x_order, slots])
    order_whole = jnp.concatenate([x_order, jnp.zeros((1,), jnp.int32)])

    small = small.reshape(n, dps, small_rows, 128)
    small = jnp.moveaxis(small, 0, 1).reshape(dps * n, small_rows, 128)
    up_full = small[:, :up_rows].reshape(cols, ranks)
    misc = small[:, up_rows : up_rows + misc_rows * wide // 128].reshape(dps * n, misc_rows, wide)
    conv_w = jnp.moveaxis(misc[:, :taps, :conv_rows], 1, 0).reshape(taps, -1).astype(f32)
    conv_b = misc[:, taps, :conv_rows].reshape(-1).astype(f32)
    every_index = misc[:, taps + 1, :seqs].reshape(dps, n, seqs)[:, 0].astype(jnp.int32)
    gate_gain = misc[:, taps + 2, :out_rows].reshape(-1).astype(f32)

    def mine(v, size, base=0):
        return lax.dynamic_slice_in_dim(v, base + here * size, size, 0)

    up_gate = mine(up_full, hc)
    up_conv = jnp.concatenate([mine(up_full, hc, inner), up_full[2 * inner :]], 0)
    conv_w = jnp.concatenate([mine(conv_w.T, hc), conv_w.T[inner:]], 0).T
    conv_b = jnp.concatenate([mine(conv_b, hc), conv_b[inner:]], 0)
    step_bias = mine(head_step_bias, hn)
    decay_rate = -jnp.exp(mine(log_decay_rate, hn))
    skip = mine(head_skip_gain, hn)
    gate_gain = mine(gate_gain, hc)

    chosen = (adapter_index[:, None] == jnp.arange(adapters, dtype=jnp.int32)[None, :]).astype(f32)
    mask = jnp.repeat(chosen, rank, axis=1)[:, None, :]

    doc_f = docs.astype(f32)

    def same_before(k):
        return jnp.pad(doc_f, ((0, 0), (k, 0)), constant_values=-1.0)[:, :length] == doc_f

    def same_after(k):
        return jnp.pad(doc_f, ((0, 0), (0, k)), constant_values=-1.0)[:, k:] == doc_f

    blocks = doc_f.reshape(seqs, nb, BLOCK)
    prior = jnp.concatenate([blocks[:, :1, 0], blocks[:, :-1, -1]], 1)
    keep = (blocks == prior[:, :, None]).reshape(seqs, length)
    ends = (blocks == blocks[:, :, -1:]).reshape(seqs, length)
    flags = [
        same_before(1), same_before(2), same_before(3), keep, ends, doc_f,
        same_after(1), same_after(2), same_after(3),
    ]
    meta = jnp.stack([v.astype(f32) for v in flags], -1)
    meta = jnp.pad(meta, ((0, 0), (0, 0), (0, 128 - len(flags))))
    doc_rows = blocks[:, :, None, :]

    def rows8(*vs):
        return jnp.pad(jnp.stack(vs), ((0, 8 - len(vs)), (0, 0)))

    conv_rows8 = rows8(conv_w[0], conv_w[1], conv_w[2], conv_w[3], conv_b)
    head_rows = rows8(
        jnp.pad(step_bias, (0, 128 - hn)), jnp.pad(decay_rate, (0, 128 - hn))
    )
    wide_rows = rows8(jnp.repeat(skip, hd), gate_gain)
    halves = jnp.pad(
        (jnp.arange(128)[None, :] // 64 == jnp.arange(2)[:, None]).astype(bf16), ((0, 14), (0, 0))
    )
    select = (jnp.arange(hc)[:, None] // hd == jnp.arange(128)[None, :]).astype(bf16)
    mask8 = jnp.broadcast_to(mask, (seqs, 8, ranks))
    cc = conv_cols
    anywhere = pl.BlockSpec(memory_space=pl.ANY)
    params = pltpu.CompilerParams(
        dimension_semantics=("arbitrary",), vmem_limit_bytes=VMEM_BYTES
    )

    def at(w, k=0):
        return pl.BlockSpec((1, BLOCK, w), lambda b, o: (k, b, 0))

    def once(v, *block):
        block = block or v.shape
        return pl.BlockSpec(block, lambda b, o: (0,) * len(block), pipeline_mode=pl.Buffered(1))

    def of_seq(v, s0):
        k = s0 if v.shape[0] > 1 else 0
        return pl.BlockSpec(
            (1,) + v.shape[1:], lambda b, o: (k, 0, 0), pipeline_mode=pl.Buffered(1)
        )

    def one(w, dtype):
        return jax.ShapeDtypeStruct((1, length, w), dtype)

    def cost(flops, mib):
        return pl.CostEstimate(flops=int(flops), bytes_accessed=mib << 20, transcendentals=0)

    def weight_scratch(pieces, *shape):
        return [
            pltpu.VMEM(shape, bf16), pltpu.SemaphoreType.DMA((len(pieces),)),
            pltpu.SemaphoreType.DMA,
        ]

    def forward(s0, base, order, blocks, pieces, held=()):
        def part(w, k=0):
            return pl.BlockSpec((1, BLOCK, w), lambda b, o: (k, b + base, 0))

        carry_shape = jax.ShapeDtypeStruct((hc + cc // 16, 128), f32)
        whole_w = jax.ShapeDtypeStruct((width, wa_cols), bf16)
        carry_spec = once(None, *carry_shape.shape)
        more = base + 2 < nb
        inputs = [*blocks, meta, doc_rows, up_conv, conv_rows8, head_rows, mask8, halves, *pieces]
        lead = 0 if base else 1
        return pl.pallas_call(
            functools.partial(
                forward_kernel, hn=hn, hc=hc, count=len(pieces), base=base, total=nb
            ),
            grid_spec=pltpu.PrefetchScalarGridSpec(
                num_scalar_prefetch=1,
                grid=(2,),
                in_specs=[
                    *(of_seq(v, s0) for v in blocks), part(128, s0),
                    pl.BlockSpec((1, 1, 1, BLOCK), lambda b, o: (s0, b + base, 0, 0)),
                    once(up_conv), once(conv_rows8), once(head_rows), of_seq(mask8, s0), once(halves),
                    *([anywhere] * len(pieces)),
                    *([carry_spec] + [anywhere] * 7 if base else []),
                ],
                out_specs=[
                    *([] if base else [anywhere]),
                    part(width), part(128), part(cc), part(cc), part(hc),
                    pl.BlockSpec((1, 1, hc, state), lambda b, o: (0, b + base, 0, 0)), part(384),
                    *([carry_spec] if more else []),
                ],
                scratch_shapes=[
                    pltpu.VMEM((BLOCK + 8, cc), f32), pltpu.VMEM((hc, state), f32),
                    pltpu.VMEM((BLOCK, width), bf16), pltpu.VMEM((width, wa_cols), bf16),
                    pltpu.VMEM((8, width), f32), pltpu.SemaphoreType.DMA((len(pieces),)),
                    pltpu.SemaphoreType.DMA,
                ],
            ),
            out_shape=[
                *([] if base else [whole_w]),
                one(width, bf16), one(128, bf16), one(cc, bf16), one(cc, f32), one(hc, f32),
                jax.ShapeDtypeStruct((1, nb, hc, state), bf16), one(384, f32),
                *([carry_shape] if more else []),
            ],
            input_output_aliases={2 + len(inputs) + i: lead + i for i in range(7)} if base else {},
            compiler_params=params,
            name="ssm_forward",
            cost_estimate=cost(2 * length * (width * wa_cols + 3 * BLOCK * hc), 20),
        )(order, *inputs, *held)

    def gates(order, normed, rank_in, pieces):
        return pl.pallas_call(
            functools.partial(gate_kernel, hc=hc, count=len(pieces)),
            grid_spec=pltpu.PrefetchScalarGridSpec(
                num_scalar_prefetch=1,
                grid=(nb,),
                in_specs=[at(width), at(128), once(up_gate), *([anywhere] * len(pieces))],
                out_specs=[at(hc), anywhere],
                scratch_shapes=weight_scratch(pieces, width, hc + ranks),
            ),
            out_shape=[one(hc, f32), jax.ShapeDtypeStruct((width, hc + ranks), bf16)],
            compiler_params=params,
            name="gate",
            cost_estimate=cost(2 * length * width * hc, 10),
        )(order, normed, rank_in, up_gate, *pieces)

    def middle(s0, order, gate, vbc, ssm, blocks, pieces):
        return pl.pallas_call(
            functools.partial(middle_kernel, hc=hc, width=width, rank=rank, count=len(pieces)),
            grid_spec=pltpu.PrefetchScalarGridSpec(
                num_scalar_prefetch=1,
                grid=(nb,),
                in_specs=[
                    at(hc), at(cc), at(hc), *(of_seq(v, s0) for v in blocks), once(up_out),
                    once(wide_rows), of_seq(mask8, s0), *([anywhere] * len(pieces)),
                ],
                out_specs=[
                    at(hc), at(128), *(once(None, BLOCK, width) for _ in range(nb)),
                    pl.BlockSpec((1, 8 + rank, BLOCK), lambda b, o: (0, 0, b)),
                ],
                scratch_shapes=[
                    pltpu.VMEM((BLOCK, width), bf16), pltpu.VMEM((hc, width + ranks), bf16),
                    pltpu.SemaphoreType.DMA((len(pieces),)),
                ],
            ),
            out_shape=[
                one(hc, f32), one(128, bf16),
                *(jax.ShapeDtypeStruct((BLOCK, width), bf16) for _ in range(nb)),
                jax.ShapeDtypeStruct((1, 8 + rank, length), f32),
            ],
            compiler_params=params,
            name="output_side",
            cost_estimate=cost(2 * length * width * hc * 2, 15),
        )(order, gate, vbc, ssm, *blocks, up_out, wide_rows, mask8, *pieces)

    def backward(s0, q, gate, ssm, vbc, pre, tok, rm, states_low, rank_in, grad_rank_out):
        def back(w, k=0):
            return pl.BlockSpec((1, BLOCK, w), lambda b: (k, nb - 1 - b, 0))

        def whole(v):
            return pl.BlockSpec(v.shape, lambda b: (0,) * v.ndim, pipeline_mode=pl.Buffered(1))

        def back_state(shift):
            return pl.BlockSpec(
                (1, 1, hc, state), lambda b: (0, jnp.minimum(nb - 1 - b + shift, nb - 1), 0, 0)
            )

        return pl.pallas_call(
            functools.partial(backward_kernel, hn=hn, hc=hc, rank=rank),
            grid=(nb,),
            in_specs=[
                back(hc), back(hc), back(hc), back(cc), back(cc), back(384),
                pl.BlockSpec((1, 8, BLOCK), lambda b: (0, 0, nb - 1 - b)), back(128, s0),
                pl.BlockSpec((1, 1, 1, BLOCK), lambda b: (s0, nb - 1 - b, 0, 0)),
                back_state(0), back_state(1), back(128), back(128), whole(conv_rows8),
                whole(head_rows), whole(wide_rows), whole(halves), whole(select), whole(up_gate),
                whole(up_conv), pl.BlockSpec((1,) + mask8.shape[1:], lambda b: (s0, 0, 0)),
            ],
            out_specs=[
                back(hc), back(cc), back(128),
                pl.BlockSpec((1, rank, 2 * hc + cc), lambda b: (0, 0, 0)),
                pl.BlockSpec((1, rank, BLOCK), lambda b: (0, 0, nb - 1 - b)),
            ],
            out_shape=[
                one(hc, bf16), one(cc, bf16), one(128, bf16),
                jax.ShapeDtypeStruct((1, rank, 2 * hc + cc), f32),
                jax.ShapeDtypeStruct((1, rank, length), f32),
            ],
            scratch_shapes=[
                pltpu.VMEM((BLOCK + 8, cc), f32), pltpu.VMEM((hc, state), f32),
            ],
            compiler_params=params,
            name="ssm_backward",
            cost_estimate=cost(2 * length * 8 * BLOCK * hc, 25),
        )(
            q, gate, ssm, vbc, pre, tok, rm, meta, doc_rows, states_low, states_low, rank_in,
            grad_rank_out, conv_rows8, head_rows, wide_rows, halves, select, up_gate, up_conv, mask8,
        )

    def input_gradient(blocks, gp_gate, gp_conv, g_step):
        steps = blocks.shape[0]

        def of(w):
            return pl.BlockSpec((1, BLOCK, w), lambda b, o: (0, o[b], 0))

        return pl.pallas_call(
            functools.partial(input_gradient_kernel, hc=hc, cc=cc),
            grid_spec=pltpu.PrefetchScalarGridSpec(
                num_scalar_prefetch=1,
                grid=(steps,),
                in_specs=[of(hc), of(cc), of(128), once(wa), once(wb)],
                out_specs=[once(None, BLOCK, width) for _ in range(steps)],
            ),
            out_shape=[jax.ShapeDtypeStruct((BLOCK, width), bf16) for _ in range(steps)],
            compiler_params=params,
            name="input_gradient",
            cost_estimate=cost(2 * steps * BLOCK * width * (hc + cc), 10),
        )(blocks, gp_gate, gp_conv, g_step, wa, wb)

    def own_tokens(v, axis):
        return lax.dynamic_slice_in_dim(v, here * own_len, own_len, axis)

    def with_adapter(rows_of, table, s0):
        wide_rows_of = jnp.tile(rows_of, (adapters, 1)) * mask[s0, 0][:, None].astype(bf16)
        return mm("rt,dr->td", wide_rows_of, table)

    def halves_of(s0, order, blocks, pieces, held=None):
        out, whole_w = None, None
        for base in range(0, nb, 2):
            if base:
                got = forward(s0, base, order_whole, blocks, [whole_w], (out[7], *out[:7]))
            else:
                first, *got = forward(s0, 0, order, blocks, pieces)
                whole_w = first if whole_w is None else whole_w
            got = yield got, whole_w
            out, whole_w = got

    if staged:
        wa_pieces, xs[0], w_b, x1 = fence(wa_pieces, xs[0], w_b, x1)
        scan = halves_of(0, order, xs[0], wa_pieces)
        held = next(scan)
        b1, b3, b0y = rotate(w_b, 1), rotate(w_b, 3), swap(w_b, "dp", 1)
        x_far1 = swap(x1, "seq", 2)
        held, b1, b3, b0y, w_b = fence(held, b1, b3, b0y, w_b)
        held = scan.send(held)
        b2, b1y, b3y = rotate(w_b, 2), swap(b1, "dp", 1), swap(b3, "dp", 1)
        w_o = lax.ppermute(w_o, both, to_head)
        held, b2, b1y, b3y, x_far1, w_o = fence(held, b2, b1y, b3y, x_far1, w_o)
        fwd0, wa = held
        xs.append([layer_input, x_near, x_far1, swap(x_far1, "seq", 1)])
        xs[1], b2, w_o, og0, og1 = fence(xs[1], b2, w_o, output_gradient[:1], output_gradient[1:])
        scan = halves_of(1, order_whole, xs[1], [wa])
        held = next(scan)
        b2y = swap(b2, "dp", 1)
        o1, o3, o0y = rotate(w_o, 1), rotate(w_o, 3), swap(w_o, "dp", 1)
        og_far0 = swap(og0, "seq", 2)
        held, b2y, o1, o3, o0y, w_o = fence(held, b2y, o1, o3, o0y, w_o)
        held = scan.send((held[0], wa))
        o2, o1y, o3y = rotate(w_o, 2), swap(o1, "dp", 1), swap(o3, "dp", 1)
        og_near = swap(output_gradient, "seq", 1)
        held, o2, o1y, o3y, og_far0, og_near, og1 = fence(
            held, o2, o1y, o3y, og_far0, og_near, og1
        )
        fwd = [fwd0, held[0]]
        wb_pieces = [w_b, b0y, b1, b1y, b2, b2y, b3, b3y]
        gate0, wb = gates(order, fwd[0][0], fwd[0][1], wb_pieces)
        o2y = swap(o2, "dp", 1)
        og_far1 = swap(og1, "seq", 2)
        og_both0 = swap(og_far0, "seq", 1)
        gate0, wb, o2y, og_both0 = fence(gate0, wb, o2y, og_both0)
        gate1, _ = gates(order_whole, fwd[1][0], fwd[1][1], [wb])
        wo_pieces = [w_o, o0y, o1, o1y, o2, o2y, o3, o3y]
        gate1, og_far1 = fence(gate1, og_far1)
        og_both1 = swap(og_far1, "seq", 1)
        ogs = [
            [output_gradient, og_near, og_far0, og_both0],
            [output_gradient, og_near, og_far1, og_both1],
        ]
    else:
        fwd = []
        for s0 in range(seqs):
            scan = halves_of(s0, order, xs[s0], wa_pieces)
            held = next(scan)
            for _ in range(nb // 2 - 1):
                held = scan.send(held)
            fwd.append(held[0])
            wa = held[1]
        wb_pieces = [lax.all_gather(w_b, "dp", tiled=True)]
        gate0, wb = gates(order, fwd[0][0], fwd[0][1], wb_pieces)
        gate1, _ = gates(order_whole, fwd[1][0], fwd[1][1], [wb])
        wo_pieces = [lax.all_gather(w_o, "dp", tiled=True)]
        full = lax.all_gather(output_gradient, "seq", axis=1, tiled=True)
        ogs = [jnp.split(full, nb, axis=1)] * seqs
    up_out = wb[:, hc:]
    gain = wa[:, -1].astype(f32)
    gates_pre = [gate0, gate1]

    def side(s0):
        return middle(s0, order, gates_pre[s0], fwd[s0][2], fwd[s0][4], ogs[s0], wo_pieces)

    def normalisers(stats):
        inv_gated = lax.rsqrt(stats[:1] / inner + EPS)
        rm = jnp.pad(jnp.concatenate([inv_gated, stats[1:2] / inner], 0), ((0, 6), (0, 0)))[None]
        return inv_gated, rm, own_tokens((stats[8:] * inv_gated).astype(bf16), 1)

    def scan_back(s0, q, rm, grad_rank_out):
        _, rank_in, vbc, pre, ssm, states_low, tok = fwd[s0][:7]
        return backward(
            s0, q, gates_pre[s0], ssm, vbc, pre, tok, rm, states_low, rank_in, grad_rank_out
        )

    def layer_output(s0, branch, inv_gated, rank_out):
        return (
            layer_input[s0].astype(f32)
            + branch * own_tokens(inv_gated, 1).T
            + with_adapter(rank_out, up_out, s0)
        ).astype(bf16)

    def down_gradient(s0, grad_rank_in):
        return mm("rt,td->rd", grad_rank_in, fwd[s0][0][0]).astype(bf16)

    def layer_gradient(s0, partial, grad_rank_in):
        grad_normed = partial + with_adapter(
            own_tokens(grad_rank_in, 1), wa[:, cc : cc + ranks], s0
        )
        own = layer_input[s0].astype(f32)
        inv_own = lax.rsqrt(jnp.mean(own * own, -1, keepdims=True) + EPS)
        scaled_in = grad_normed * gain
        return (
            inv_own * scaled_in
            - own * inv_own**3 * jnp.mean(scaled_in * own, -1, keepdims=True)
            + output_gradient[s0].astype(f32)
        )

    if staged:
        gates_pre[1], ogs, wo_pieces = fence(gates_pre[1], ogs, wo_pieces)
        q0, gro0, *part0, stats0 = side(0)
        q0, gro0, part0, stats0 = fence(q0, gro0, part0, stats0)
        q1, gro1, *part1, stats1 = side(1)
        got = others(stats0[0])
        r3, r1 = swap(part0[3], "seq", 1), swap(part0[1], "seq", 1)
        q1, gro1, part1, stats1, got, r3, r1, part0 = fence(
            q1, gro1, part1, stats1, got, r3, r1, part0
        )
        inv0, rm0, rank_out0 = normalisers(total_of(stats0[0], got))
        mine0, away0 = near_sums(*part0, r1, r3)
        rm0, mine0, away0, stats1 = fence(rm0, mine0, away0, stats1)

        back0 = scan_back(0, q0, rm0, gro0)
        far0 = swap(away0, "seq", 2)
        got = others(stats1[0])
        r3 = swap(part1[3], "seq", 1)
        back0, far0, got, r3, part1 = fence(back0, far0, got, r3, part1)
        gp_gate, gp_conv, g_step, compact0, gri0 = back0
        output0 = layer_output(0, mine0 + far0.astype(f32), inv0, rank_out0)
        inv1, rm1, rank_out1 = normalisers(total_of(stats1[0], got))
        gri0, rm1, output0 = fence(gri0, rm1, output0)

        four = here ^ jnp.array([3, 2, 1, 0], jnp.int32)
        parts = input_gradient(four, gp_gate, gp_conv, g_step)
        got = others(gri0[0])
        r1 = swap(part1[1], "seq", 1)
        parts, got, r1 = fence(parts, got, r1)
        gri0 = total_of(gri0[0], got).astype(bf16)
        mine1, away1 = near_sums(*part1, r1, r3)
        s3, s1 = swap(parts[0], "seq", 1), swap(parts[2], "seq", 1)
        mine_g0, away_g0 = near_sums(*parts[::-1], s1, s3)
        down0 = down_gradient(0, gri0)
        mine_g0, away_g0, mine1, away1, rm1, down0 = fence(
            mine_g0, away_g0, mine1, away1, rm1, down0
        )

        back1 = scan_back(1, q1, rm1, gro1)
        far_g0 = swap(away_g0, "seq", 2)
        far1 = swap(away1, "seq", 2)
        back1, far_g0, far1 = fence(back1, far_g0, far1)
        gp_gate, gp_conv, g_step, compact1, gri1 = back1
        far = input_gradient(four[:2], gp_gate, gp_conv, g_step)
        got = others(gri1[0])
        far, got = fence(far, got)
        s3 = swap(far[0], "seq", 1)
        gri1 = total_of(gri1[0], got).astype(bf16)
        output1 = layer_output(1, mine1 + far1.astype(f32), inv1, rank_out1)
        away_g1 = (far[1].astype(f32) + s3.astype(f32)).astype(bf16)
        away_g1, output1, gri1 = fence(away_g1, output1, gri1)

        near = input_gradient(four[2:], gp_gate, gp_conv, g_step)
        far_g1 = swap(away_g1, "seq", 2)
        g_out_up = mm("srt,std->srd", jnp.stack([rank_out0, rank_out1]), output_gradient)
        split = [compact0[0], compact1[0]]
        downs = [down0, down_gradient(1, gri1)]
        grad0 = layer_gradient(0, mine_g0 + far_g0.astype(f32), gri0)
        mine_g1 = near[1].astype(f32) + swap(near[0], "seq", 1).astype(f32)
    else:
        split, downs, ranks_out, outputs, grads_in = [], [], [], [], []
        for s0 in range(seqs):
            q, gro, *parts, stats = side(s0)
            inv_gated, rm, rank_out = normalisers(lax.psum(stats[0], "seq"))
            outputs.append(layer_output(s0, scatter_plain(parts), inv_gated, rank_out))
            gp_gate, gp_conv, g_step, compacted, gri = scan_back(s0, q, rm, gro)
            gri = lax.psum(gri[0], "seq").astype(bf16)
            parts = input_gradient(jnp.arange(nb, dtype=jnp.int32), gp_gate, gp_conv, g_step)
            split.append(compacted[0])
            downs.append(down_gradient(s0, gri))
            ranks_out.append(rank_out)
            grads_in.append(layer_gradient(s0, scatter_plain(parts), gri))
        g_out_up = mm("srt,std->srd", jnp.stack(ranks_out), output_gradient)
        output = jnp.stack(outputs)
        grad_in = jnp.stack(grads_in)

    g_out_up = g_out_up.astype(bf16)
    g_in_down = jnp.stack(downs)
    split = jnp.concatenate([jnp.stack(split).astype(bf16), g_out_up], -1).reshape(seqs * rank, -1)
    split = gather_seq(split).reshape(n, seqs, rank, -1)

    def by_heads(start):
        return jnp.concatenate([split[t, :, :, start : start + hc] for t in range(n)], -1)

    def summed(start, size):
        return split[..., start : start + size].astype(f32).sum(0).astype(bf16)

    full = [
        g_in_down,
        jnp.concatenate([by_heads(0), by_heads(hc), summed(2 * hc, state2)], -1),
        by_heads(2 * hc + state2),
        summed(3 * hc + state2, width),
    ]
    widths = [v.shape[-1] // (dps * n) for v in full]
    packed = jnp.concatenate(
        [
            lax.dynamic_index_in_dim(
                v.reshape(seqs, rank, dps, n, -1), here, 3, keepdims=False
            )
            for v in full
        ],
        -1,
    ).transpose(2, 0, 1, 3)
    got = lax.all_to_all(packed, "dp", 0, 0, tiled=True).astype(f32)
    if staged:
        output = jnp.stack([output0, output1])
        grad_in = jnp.stack([grad0, layer_gradient(1, mine_g1 + far_g1.astype(f32), gri1)])
    all_chosen = (every_index[..., None] == jnp.arange(adapters)).astype(f32)
    table = jnp.einsum("dsk,dsrc->krc", all_chosen, got, precision=lax.Precision.HIGHEST)
    cuts = [sum(widths[:i]) for i in range(len(widths) + 1)]
    grads = [table[..., cuts[i] : cuts[i + 1]] for i in range(len(widths))]
    return (output, grad_in, grads[0], grads[1], grads[2], grads[3])


def solution(mesh):
    return jax.shard_map(
        per_device,
        mesh=mesh,
        in_specs=(
            P("dp", "seq", None),
            P("dp", "seq"),
            P("dp"),
            P(("dp", "seq")),
            P(("dp", "seq"), None),
            P(("dp", "seq"), None),
            P(("dp", "seq"), None),
            P(("dp", "seq")),
            P(),
            P(),
            P(),
            P(("dp", "seq")),
            P(("dp", "seq"), None),
            P(None, None, ("dp", "seq")),
            P(None, None, ("dp", "seq")),
            P(None, None, ("dp", "seq")),
            P(None, None, ("dp", "seq")),
            P("dp", "seq", None),
        ),
        out_specs=(
            P("dp", "seq", None),
            P("dp", "seq", None),
            P(None, None, ("dp", "seq")),
            P(None, None, ("dp", "seq")),
            P(None, None, ("dp", "seq")),
            P(None, None, ("dp", "seq")),
        ),
        check_vma=False,
    )
```

```python
import functools

import jax
import jax.numpy as jnp
from jax import lax
from jax.experimental import pallas as pl
from jax.experimental.pallas import tpu as pltpu
from jax.sharding import PartitionSpec as P

EPS = 1e-05
f32 = jnp.float32
bf16 = jnp.bfloat16
BLOCK = 256


def mm(form, a, b):
    return jnp.einsum(form, a, b, preferred_element_type=f32)


LOG2E = 1.4426950408889634
VMEM_BYTES = 66_000_000


def dot_nn(a, b):
    return lax.dot_general(a, b, (((1,), (0,)), ((), ())), preferred_element_type=f32)


def dot_nt(a, b):
    return lax.dot_general(a, b, (((1,), (1,)), ((), ())), preferred_element_type=f32)


def dot_tn(a, b):
    return lax.dot_general(a, b, (((0,), (0,)), ((), ())), preferred_element_type=f32)


def dot_exact(a, b):
    return lax.dot_general(
        a, b, (((1,), (0,)), ((), ())), preferred_element_type=f32, precision=lax.Precision.HIGHEST
    )


def sigmoid(v):
    return 0.5 * jnp.tanh(0.5 * v) + 0.5


def spread_pair(cols, j):
    rows = cols.shape[0]
    lane = lax.broadcasted_iota(jnp.int32, (rows, 128), 1)
    return jnp.where(lane < 64, cols[:, 2 * j : 2 * j + 1], cols[:, 2 * j + 1 : 2 * j + 2])


def spread_all(cols, pairs):
    return jnp.concatenate([spread_pair(cols, j) for j in range(pairs)], 1)


def per_head(v, select):
    hi = v.astype(bf16)
    lo = (v - hi.astype(f32)).astype(bf16)
    return dot_nn(hi, select) + dot_nn(lo, select)


def by_rank(t, rank):
    out = t[:rank]
    for k in range(rank, 128, rank):
        out = out + t[k : k + rank]
    return out


def fold(v, rank):
    return by_rank(v.T, rank)


def shards(pieces, size):
    return [p.at[k : k + size] for p in pieces for k in range(0, p.shape[0], size)]


def assemble(order_ref, base, pieces, size, target, sems):
    copies = []
    for i, piece in enumerate(shards(pieces, size)):
        at = pl.multiple_of(order_ref[base + i] * size, 16)
        copies.append(pltpu.make_async_copy(piece, target.at[pl.ds(at, size)], sems.at[i]))
    for copy in copies:
        copy.start()
    for copy in copies:
        copy.wait()


def choose(order_ref, b, blocks, target):
    for i, block in enumerate(blocks):

        @pl.when(order_ref[b] == i)
        def _(block=block):
            target[...] = block[0]


def forward_kernel(order_ref, *refs, hn, hc, count, size, keep):
    (x0, x1, x2, x3, meta_ref, doc_ref, up_ref, conv_ref, head_ref, mask_ref, half_ref) = refs[:11]
    pieces = refs[11 : 11 + count]
    normed_ref, rank_ref, vbc_ref, pre_ref, ssm_ref, state_ref, tok_ref, *rest = refs[11 + count :]
    if keep:
        full_ref, rest = rest[0], rest[1:]
    buf, carry, x_buf, wa_ref, gain_ref, sems, full_sem = rest
    pairs = hn // 2
    cc = hc + 256
    b = pl.program_id(0)

    @pl.when(b == 0)
    def _():
        assemble(order_ref, 4, pieces, size, wa_ref, sems)
        if keep:
            pltpu.make_async_copy(wa_ref, full_ref, full_sem).start()
        gain_ref[...] = wa_ref[:, cc + 128 :].astype(f32).T[120:, :]
        carry[...] = jnp.zeros_like(carry)
        buf[0:8, :] = jnp.zeros((8, cc), f32)

    choose(order_ref, b, (x0, x1, x2, x3), x_buf)
    x = x_buf[...].astype(f32)
    inv = lax.rsqrt(jnp.mean(x * x, -1, keepdims=True) + EPS)
    normed = (x * inv * gain_ref[7:8, :]).astype(bf16)
    normed_ref[0] = normed
    pa = dot_nn(normed, wa_ref[...])
    rank = (pa[:, cc : cc + 128] * mask_ref[0, 0:1, :]).astype(bf16)
    rank_ref[0] = rank
    conv_in = (pa[:, :cc] + dot_nt(rank, up_ref[...])).astype(bf16).astype(f32)
    buf[8:, :] = conv_in
    meta = meta_ref[0]
    pre = conv_ref[4:5, :] + conv_ref[3:4, :] * conv_in
    for k in (1, 2, 3):
        pre = pre + conv_ref[3 - k : 4 - k, :] * (buf[8 - k : 8 - k + BLOCK, :] * meta[:, k - 1 : k])
    buf[0:8, :] = buf[BLOCK : BLOCK + 8, :]
    pre_ref[0] = pre
    vbc = (pre * sigmoid(pre)).astype(bf16)
    vbc_ref[0] = vbc
    values = vbc[:, :hc]
    in_state = vbc[:, hc : hc + 128]
    out_state = vbc[:, hc + 128 :]
    arg = pa[:, cc + 128 : cc + 256] + head_ref[0:1, :]
    dt = jnp.maximum(arg, 0.0) + jnp.log1p(jnp.exp(-jnp.abs(arg)))
    row = lax.broadcasted_iota(jnp.int32, (BLOCK, BLOCK), 0)
    col = lax.broadcasted_iota(jnp.int32, (BLOCK, BLOCK), 1)
    cum = dot_exact((row >= col).astype(f32), dt * head_ref[1:2, :])
    tok_ref[0, :, 0:128] = dt
    tok_ref[0, :, 128:256] = cum
    tok_ref[0, :, 256:384] = arg
    left = cum * LOG2E
    right = (left - jnp.log(jnp.maximum(dt, 1e-37)) * LOG2E).T
    ok = (row >= col) & (meta[:, 5:6] == doc_ref[0, 0])
    bias = jnp.where(ok, 0.0, -1e30)
    contact = dot_nt(out_state, in_state)
    entry = jnp.exp(cum) * meta[:, 3:4]
    weight = jnp.exp(cum[BLOCK - 1 :, :] - cum) * dt * meta[:, 4:5]
    state = carry[...]
    state_low = state.astype(bf16)
    state_ref[0, 0] = state_low
    readout = dot_nt(out_state, state_low)
    half = BLOCK // 2
    scaled = []
    for j in range(pairs):
        at = slice(128 * j, 128 * j + 128)
        v = values[:, at]
        ys = []
        for r0, c1 in ((0, half), (half, BLOCK)):
            ws = []
            for h in (2 * j, 2 * j + 1):
                e = jnp.exp2(
                    (left[r0 : r0 + half, h : h + 1] - right[h : h + 1, :c1])
                    + bias[r0 : r0 + half, :c1]
                )
                ws.append((contact[r0 : r0 + half, :c1] * e).astype(bf16))
            vv = jnp.concatenate([v[:c1] * half_ref[0:1, :], v[:c1] * half_ref[1:2, :]], 0)
            ys.append(dot_nn(jnp.concatenate(ws, 1), vv))
        y = jnp.concatenate(ys, 0)
        ssm_ref[0, :, at] = y + readout[:, at] * spread_pair(entry, j)
        scaled.append((v.astype(f32) * spread_pair(weight, j)).astype(bf16))
    local = dot_tn(jnp.concatenate(scaled, 1), in_state)
    passing = entry[BLOCK - 1 :, :]
    for h in range(hn):
        at = slice(64 * h, 64 * h + 64)
        carry[at, :] = passing[:, h : h + 1] * state[at] + local[at]

    if keep:

        @pl.when(b == pl.num_programs(0) - 1)
        def _():
            pltpu.make_async_copy(wa_ref, full_ref, full_sem).wait()


def route(order_ref, b, value, near_ref, pair_ref, far_ref):
    for k, target in enumerate(
        (near_ref, pair_ref.at[0:BLOCK], far_ref, pair_ref.at[BLOCK : 2 * BLOCK])
    ):

        @pl.when(order_ref[b] == k)
        def _(target=target):
            target[...] = value


def assemble_both(order_ref, base, pieces, rows, out_rows, wb_ref, wo_ref, sems):
    part = wb_ref.shape[1]
    copies = []
    for i, piece in enumerate(shards(pieces, rows + 2 * out_rows)):
        slot = order_ref[base + i]
        to = pl.ds(pl.multiple_of(slot * rows, 16), rows)
        to_out = pl.ds(pl.multiple_of(slot * out_rows, 16), out_rows)
        rest = wo_ref.shape[1] - part
        moves = (
            (piece.at[0:rows], wb_ref.at[to]),
            (piece.at[rows : rows + out_rows], wo_ref.at[to_out, 0:part]),
            (piece.at[rows + out_rows :, 0:rest], wo_ref.at[to_out, part : part + rest]),
        )
        for j, (source, target) in enumerate(moves):
            copies.append(pltpu.make_async_copy(source, target, sems.at[3 * i + j]))
    for copy in copies:
        copy.start()
    for copy in copies:
        copy.wait()


def middle_kernel(order_ref, *refs, hc, width, rank, count, keep, merged):
    (
        normed_ref, rank_ref, vbc_ref, ssm_ref, og0, og1, og2, og3, up_ref, row_ref, mask_ref,
    ) = refs[:11]
    gate_pieces = refs[11 : 11 + count]
    after_gate = 11 + count
    out_pieces = () if merged else refs[after_gate : after_gate + count]
    first_out = after_gate + len(out_pieces)
    g_ref, q_ref, gro_ref, near_ref, pair_ref, far_ref, stat_ref, *rest = refs[first_out:]
    if keep:
        wb_full, wo_full, rest = rest[0], rest[1], rest[2:]
    og_buf, wb_ref, wo_ref, sems, more_sems, full_sems = rest
    b = pl.program_id(0)

    def keeping():
        return (
            pltpu.make_async_copy(wb_ref, wb_full, full_sems.at[0]),
            pltpu.make_async_copy(wo_ref, wo_full, full_sems.at[1]),
        )

    @pl.when(b == 0)
    def _():
        if merged:
            assemble_both(order_ref, 4, gate_pieces, *merged, wb_ref, wo_ref, sems)
        else:
            assemble(order_ref, 4, gate_pieces, wb_ref.shape[0], wb_ref, sems)
            assemble(order_ref, 4, out_pieces, wo_ref.shape[0], wo_ref, more_sems)
        if keep:
            for copy in keeping():
                copy.start()

    choose(order_ref, b, (og0, og1, og2, og3), og_buf)
    gate = dot_nn(normed_ref[0], wb_ref[:, :hc]) + dot_nt(rank_ref[0], up_ref[...])
    g_ref[0] = gate
    mixed = ssm_ref[0] + row_ref[0:1, :] * vbc_ref[0, :, :hc].astype(f32)
    gated = mixed * (gate * sigmoid(gate))
    og = og_buf[...]
    gro = (dot_nn(og, wb_ref[:, hc:]) * mask_ref[0, 0:1, :]).astype(bf16)
    gro_ref[0] = gro
    q = dot_nt(og, wo_ref[:, :width]) + dot_nt(gro, wo_ref[:, width : width + 128])
    q = q * row_ref[1:2, :]
    q_ref[0] = q
    lane = lax.broadcasted_iota(jnp.int32, (BLOCK, 128), 1)
    s0 = jnp.sum(gated * gated, -1, keepdims=True)
    s1 = jnp.sum(q * gated, -1, keepdims=True)
    stat_ref[0, 0:8, :] = jnp.where(lane == 0, s0, s1).T[:8]
    low = (gated * row_ref[1:2, :]).astype(bf16)
    route(order_ref, b, dot_nn(low, wo_ref[:, :width]).astype(bf16), near_ref, pair_ref, far_ref)
    stat_ref[0, 8:, :] = fold(dot_nn(low, wo_ref[:, width : width + 128]) * mask_ref[0, 0:1, :], rank)

    if keep:

        @pl.when(b == pl.num_programs(0) - 1)
        def _():
            for copy in keeping():
                copy.wait()


def backward_kernel(
    order_ref, q_ref, g_ref, ssm_ref, vbc_ref, pre_ref, tok_ref, rm_ref, meta_ref, doc_ref, state_ref, next_ref,
    rank_ref, gro_ref, conv_ref, head_ref, row_ref, half_ref, select_ref, upg_ref, upc_ref, mask_ref,
    wa_ref, wb_ref,
    near_ref, pair_ref, far_ref, grads_ref, gri_ref,
    buf, carry,
    *, hn, hc, rank,
):
    pairs = hn // 2
    cc = hc + 256
    first = pl.program_id(0) == 0

    @pl.when(first)
    def _():
        carry[...] = jnp.zeros_like(carry)
        buf[BLOCK:, :] = jnp.zeros((8, cc), f32)
        grads_ref[...] = jnp.zeros_like(grads_ref)

    rm = jnp.concatenate([rm_ref[0]] * 16, 0).T
    inv = rm[:, 0:1]
    mean = rm[:, 1:2]
    meta = meta_ref[0]
    gate = g_ref[0]
    ssm = ssm_ref[0]
    q = q_ref[0]
    vbc = vbc_ref[0]
    values = vbc[:, :hc]
    values_f = values.astype(f32)
    in_state = vbc[:, hc : hc + 128]
    out_state = vbc[:, hc + 128 :]
    skip = row_ref[0:1, :]
    mixed = ssm + skip * values_f
    sg = sigmoid(gate)
    act = gate * sg
    gated = mixed * act
    gated_r = gated * inv
    grad_gated = inv * (q - gated_r * (inv * mean))
    gated_low = (gated_r * row_ref[1:2, :]).astype(bf16)
    grads_ref[0, :, hc + cc :] = grads_ref[0, :, hc + cc :] + by_rank(
        dot_tn(gro_ref[0], gated_low), rank
    )
    grad_mixed = grad_gated * act
    gp_gate = (grad_gated * mixed * (sg + act * (1.0 - sg))).astype(bf16)
    gsum = grad_mixed.astype(bf16)
    gsum_f = gsum.astype(f32)

    dt = tok_ref[0, :, 0:128]
    cum = tok_ref[0, :, 128:256]
    arg = tok_ref[0, :, 256:384]
    scaled_cum = cum * LOG2E
    down = scaled_cum - jnp.log(jnp.maximum(dt, 1e-37)) * LOG2E
    across = scaled_cum.T
    row = lax.broadcasted_iota(jnp.int32, (BLOCK, BLOCK), 0)
    col = lax.broadcasted_iota(jnp.int32, (BLOCK, BLOCK), 1)
    ok = (col >= row) & (meta[:, 5:6] == doc_ref[0, 0])
    bias = jnp.where(ok, 0.0, -1e30)
    contact = dot_nt(in_state, out_state)
    entry = jnp.exp(cum) * meta[:, 3:4]
    weight = jnp.exp(cum[BLOCK - 1 :, :] - cum) * dt * meta[:, 4:5]
    later = carry[...]
    later_low = later.astype(bf16)
    grad_scaled = dot_nt(in_state, later_low)
    weight_wide = spread_all(weight, pairs)
    entry_wide = spread_all(entry, pairs)
    scaled = (values_f * weight_wide).astype(bf16)
    weighted = (gsum_f * entry_wide).astype(bf16)
    half = BLOCK // 2
    g_con = [jnp.zeros((half, BLOCK), f32), jnp.zeros((half, half), f32)]
    g_val = []
    for j in range(pairs):
        at = slice(128 * j, 128 * j + 128)
        v = values[:, at]
        gs = gsum[:, at]
        tops = []
        for i, (r0, c0) in enumerate(((0, 0), (half, half))):
            ws = []
            for side in (0, 1):
                h = 2 * j + side
                gw = dot_nt(v[r0 : r0 + half] * half_ref[side : side + 1, :], gs[c0:])
                e = jnp.exp2(
                    (across[h : h + 1, c0:] - down[r0 : r0 + half, h : h + 1])
                    + bias[r0 : r0 + half, c0:]
                )
                ws.append((contact[r0 : r0 + half, c0:] * e).astype(bf16))
                g_con[i] = g_con[i] + gw * e
            gg = jnp.concatenate([gs[c0:] * half_ref[0:1, :], gs[c0:] * half_ref[1:2, :]], 0)
            tops.append(dot_nn(jnp.concatenate(ws, 1), gg))
        g_val.append(jnp.concatenate(tops, 0))
    g_val = jnp.concatenate(g_val, 1) + grad_scaled * weight_wide
    con_low = jnp.concatenate(
        [g_con[0], jnp.concatenate([jnp.zeros((half, half), f32), g_con[1]], 1)], 0
    ).astype(bf16)
    g_in = dot_nn(con_low, out_state) + dot_nn(scaled, later_low)
    g_out = dot_tn(con_low, in_state) + dot_nn(weighted, state_ref[0, 0])
    select = select_ref[...]
    spent = per_head(values_f * g_val, select)
    gained = per_head(gsum_f * ssm, select)
    ends = later * next_ref[0, 0].astype(f32)
    parts = [jnp.sum(ends[64 * h : 64 * h + 64], 0, keepdims=True) for h in range(hn)]
    parts.append(jnp.zeros((128 - hn, 128), f32))
    last = jnp.sum(jnp.concatenate(parts, 0).T, 0, keepdims=True)
    where_last = lax.broadcasted_iota(jnp.int32, (BLOCK, 128), 0) == BLOCK - 1
    grad_cum = gained - spent + jnp.where(where_last, last, 0.0)
    grad_log = dot_exact((col >= row).astype(f32), grad_cum)
    sig = sigmoid(arg)
    g_step = (
        spent * (sig / jnp.maximum(dt, 1e-37)) + head_ref[1:2, :] * grad_log * sig
    ).astype(bf16)
    passing = entry[BLOCK - 1 :, :]
    direct = dot_tn(weighted, out_state)
    for h in range(hn):
        at = slice(64 * h, 64 * h + 64)
        carry[at, :] = passing[:, h : h + 1] * later[at] + direct[at]

    pre = pre_ref[0]
    sp = sigmoid(pre)
    grad_out = jnp.concatenate([skip * grad_mixed + g_val, g_in, g_out], 1)
    grad_pre = grad_out * (sp + pre * sp * (1.0 - sp))
    buf[:BLOCK, :] = grad_pre
    total = conv_ref[3:4, :] * grad_pre
    for k in (1, 2, 3):
        total = total + conv_ref[3 - k : 4 - k, :] * (buf[k : k + BLOCK, :] * meta[:, 5 + k : 6 + k])
    buf[BLOCK:, :] = grad_pre[:8]
    gp_conv = total.astype(bf16)
    rows = rank_ref[0]
    grads_ref[0, :, :hc] = grads_ref[0, :, :hc] + by_rank(dot_tn(rows, gp_gate), rank)
    grads_ref[0, :, hc : hc + cc] = grads_ref[0, :, hc : hc + cc] + by_rank(
        dot_tn(rows, gp_conv), rank
    )
    gri_ref[0] = fold(
        (dot_nn(gp_gate, upg_ref[...]) + dot_nn(gp_conv, upc_ref[...])) * mask_ref[0, 0:1, :], rank
    )
    part = (
        dot_nt(gp_gate, wb_ref[:, :hc])
        + dot_nt(gp_conv, wa_ref[:, :cc])
        + dot_nt(g_step, wa_ref[:, cc + 128 :])
    ).astype(bf16)
    route(order_ref, pl.num_programs(0) - 1 - pl.program_id(0), part, near_ref, pair_ref, far_ref)


def pack_weights_kernel(
    ip_ref, sp_ref, idn_ref, iup_ref, odn_ref, oup_ref, op_ref, cw_ref, cb_ref, idx_ref, gg_ref, tail_ref,
    a_ref, b_ref, o_ref, small_ref,
    turn, misc,
    *, n, hn, hc, inner, planes,
):
    rows = ip_ref.shape[0]
    ranks = idn_ref.shape[0]
    up_rows = iup_ref.shape[1]

    def turned(ref):
        turn[...] = jnp.zeros_like(turn)
        turn[:, : ref.shape[1]] = ref[...].astype(f32)
        return turn[...].T

    down = turned(idn_ref)[:rows].astype(bf16)
    late = turned(oup_ref)[:rows].astype(bf16)
    step = jnp.concatenate([sp_ref[...].astype(f32), jnp.zeros((rows, 128 - n * hn), f32)], 1)
    lane = lax.broadcasted_iota(jnp.int32, (rows, 128), 1)
    chunk = hc // planes
    heads = hn // planes

    def columns(base, t, target, to):
        for p in range(0, planes, 2):
            got = []
            for q in (p, p + 1):
                start = base + (q * n + t) * chunk
                low = start // 128 * 128
                v = ip_ref[:, low : low + 256].astype(f32)
                got.append(pltpu.roll(v, 256 - (start - low), 1) if start > low else v)
            second = pltpu.roll(got[1], 64, 1)
            at = p * chunk
            target[to, at : at + 128] = got[0][:, :128].astype(bf16)
            target[to, at + 128 : at + 256] = jnp.where(
                lane < 64, got[0][:, 128:], second[:, :128]
            ).astype(bf16)
            target[to, at + 256 : at + 384] = second[:, 128:].astype(bf16)

    for t in range(n):
        to = slice(t * rows, (t + 1) * rows)
        columns(inner, t, a_ref, to)
        a_ref[to, hc : hc + 256] = ip_ref[:, 2 * inner :]
        a_ref[to, hc + 256 : hc + 256 + ranks] = down
        last = tail_ref[...]
        for p in range(planes):
            shift = (p * heads - (p * n + t) * heads) % 128
            mine = pltpu.roll(step, shift, 1) if shift else step
            last = jnp.where((lane >= p * heads) & (lane < (p + 1) * heads), mine, last)
        a_ref[to, hc + 256 + ranks :] = last.astype(bf16)
        columns(0, t, b_ref, to)
        b_ref[to, hc:] = late
    out_rows, width = op_ref.shape
    part = o_ref.shape[1]
    o_ref[:out_rows, :] = op_ref[:, :part]
    o_ref[out_rows:, : width - part] = op_ref[:, part:]
    o_ref[out_rows:, width - part : width - part + ranks] = turned(odn_ref)[:out_rows].astype(bf16)
    o_ref[out_rows:, width - part + ranks :] = jnp.zeros(
        (out_rows, 2 * part - width - ranks), bf16
    )
    keep = -(-up_rows // 16) * 16
    small_ref[:keep, :] = turned(iup_ref)[:keep].astype(bf16)
    turn[...] = jnp.zeros_like(turn)
    turn[: cw_ref.shape[0], : cw_ref.shape[1]] = cw_ref[...].astype(f32)
    misc[...] = jnp.zeros_like(misc)
    misc[0:8, :] = turn[:, 0:128].T[0:8]
    misc[4:5, : cb_ref.shape[1]] = cb_ref[...].astype(f32)
    misc[5:6, : idx_ref.shape[1]] = idx_ref[...].astype(f32)
    misc[6:7, : gg_ref.shape[1]] = gg_ref[...].astype(f32)
    small_ref[keep:, :] = misc[...].astype(bf16)


def pack_grads_kernel(
    order_ref, g0, g1, g2, g3, down_ref, out_ref, up, middle, total, *, n, hc, inner, width, widths, starts,
    planes,
):
    chunk = hc // planes
    lane = lax.broadcasted_iota(jnp.int32, (out_ref.shape[1], 128), 1)

    def place(g, source, target, base, t):
        for p in range(planes):
            low = (source + p * chunk) // 128 * 128
            v = g[:, low : low + 256].astype(f32)
            off = source + p * chunk - low
            v = pltpu.roll(v, 256 - off, 1) if off else v
            to = base + (p * n + t) * chunk
            if to % 128 == 0:
                target[:, to : to + chunk] = v[:, :chunk]
            else:
                v = pltpu.roll(v, 64, 1)
                here = slice(to - 64, to + 64)
                target[:, here] = jnp.where(lane < 64, target[:, here], v[:, :128])
                target[:, to + 64 : to + 192] = v[:, 128:]

    for t in range(n):
        for i, g in enumerate((g0, g1, g2, g3)):

            @pl.when(order_ref[t] == i)
            def _(t=t, g=g):
                place(g, 0, up, 0, t)
                place(g, hc, up, inner, t)
                place(g, 2 * hc + 256, middle, 0, t)

    def summed(at):
        first = g0[:, at].astype(f32) + g1[:, at].astype(f32)
        return first + (g2[:, at].astype(f32) + g3[:, at].astype(f32))

    up[:, 2 * inner : 2 * inner + 256] = summed(slice(2 * hc, 2 * hc + 256))
    total[:, :width] = summed(slice(3 * hc + 256, 3 * hc + 256 + width))
    sources = (None, up, middle, total)
    for t in range(n):

        @pl.when(order_ref[0] == t)
        def _(t=t):
            for d in range(out_ref.shape[0]):
                for ref, at, w in zip(sources, starts, widths):
                    start = (d * n + t) * w
                    low = start // 128 * 128
                    span = -(-w // 128) * 128
                    if ref is None:
                        window = down_ref[:, low : low + span + 128].astype(f32)
                    else:
                        window = ref[:, low : low + span + 128]
                    if start > low:
                        window = pltpu.roll(window, span + 128 - (start - low), 1)
                    out_ref[d, :, at : at + span] = window[:, :span].astype(bf16)


def swap(v, axis, bit):
    size = lax.axis_size(axis)
    return lax.ppermute(v, axis, [(i, i ^ bit) for i in range(size)])


def put(pieces):
    rows = pieces[0][0].shape[0]
    out = jnp.zeros((len(pieces) * rows, pieces[0][0].shape[1]), pieces[0][0].dtype)
    for piece, slot in pieces:
        out = lax.dynamic_update_slice_in_dim(out, piece, slot * rows, 0)
    return out


def rotate(v, r):
    size = lax.axis_size("dp")
    return lax.ppermute(v, "dp", [(i, (i + 2 * r) % size) for i in range(size)])


def after(v, *others):
    return lax.optimization_barrier((v, others))[0]


def fence(*values):
    return lax.optimization_barrier(values)


def others(v):
    return [swap(v, "seq", k) for k in (1, 2, 3)]


def total_of(v, got):
    return (v + got[0]) + (got[1] + got[2])


def across(far, pair):
    return (far.astype(f32) + pair[BLOCK:].astype(f32)).astype(bf16)


def own_sum(near, pair, far):
    return near.astype(f32) + pair[:BLOCK].astype(f32) + far.astype(f32)


def scatter_plain(near, pair, far):
    v = jnp.concatenate([near, pair[:BLOCK], far, pair[BLOCK:]], 0).astype(f32)
    return lax.psum_scatter(v, "seq", scatter_dimension=0, tiled=True)


def per_device(
    layer_input,
    document_index,
    adapter_index,
    input_norm_gain,
    input_projection,
    step_projection,
    convolution_weight,
    convolution_bias,
    head_step_bias,
    log_decay_rate,
    head_skip_gain,
    gated_norm_gain,
    output_projection,
    adapter_input_down,
    adapter_input_up,
    adapter_output_down,
    adapter_output_up,
    output_gradient,
):
    both = ("dp", "seq")
    dps, n = lax.axis_size("dp"), lax.axis_size("seq")
    here = lax.axis_index("seq")
    seqs, own_len, width = layer_input.shape
    adapters, rank, _ = adapter_input_down.shape
    ranks = adapters * rank
    heads = head_step_bias.shape[0]
    inner = output_projection.shape[0] * dps * n
    cols = input_projection.shape[1]
    state2 = cols - 2 * inner
    state = state2 // 2
    taps = convolution_weight.shape[1]
    hn = heads // n
    hc = inner // n
    hd = inner // heads
    length = own_len * n
    nb = length // BLOCK

    staged = n == 4 and dps == 8
    rows = input_projection.shape[0]
    conv_cols = hc + state2
    wa_cols = conv_cols + ranks + 128
    doc_cols = -(-seqs * own_len // rows)
    doc_block = document_index.astype(bf16).reshape(-1)
    doc_block = jnp.pad(doc_block, (0, rows * doc_cols - doc_block.shape[0])).reshape(rows, -1)
    tail = jnp.concatenate([doc_block, input_norm_gain[:, None]], 1)
    up_rows = adapter_input_up.shape[2]
    up_keep = -(-up_rows // 16) * 16
    conv_rows = convolution_weight.shape[0]
    wide = -(-conv_rows // 128) * 128
    misc_rows = 16
    small_rows = up_keep + misc_rows * wide // 128
    out_rows = output_projection.shape[0]
    planes = dps // 2 if staged else 1
    if staged:
        to_head = [
            (8 * z + 2 * t + y, 8 * z + 4 * y + t)
            for z in range(planes) for y in range(2) for t in range(n)
        ]
    else:
        to_head = [(dps * s + d, n * d + s) for d in range(dps) for s in range(n)]
    tables = [
        v.reshape(ranks, -1)
        for v in (adapter_input_down, adapter_input_up, adapter_output_down, adapter_output_up)
    ]
    if staged:
        tail = jnp.pad(tail.astype(f32), ((0, 0), (127 - doc_cols, 0)))
        payload, late_payload, w_o, small = pl.pallas_call(
            functools.partial(
                pack_weights_kernel, n=n, hn=hn, hc=hc, inner=inner, planes=planes
            ),
            out_shape=[
                jax.ShapeDtypeStruct((n * rows, wa_cols), bf16),
                jax.ShapeDtypeStruct((n * rows, hc + ranks), bf16),
                jax.ShapeDtypeStruct((2 * out_rows, hc + ranks), bf16),
                jax.ShapeDtypeStruct((small_rows, 128), bf16),
            ],
            scratch_shapes=[pltpu.VMEM((128, 256), f32), pltpu.VMEM((misc_rows, 128), f32)],
            name="pack_weights",
        )(
            input_projection, step_projection, *tables[:2], *tables[2:], output_projection,
            convolution_weight, convolution_bias[None], adapter_index[None], gated_norm_gain[None], tail,
        )
    else:
        gap = jnp.zeros((rows, 127 - hn - doc_cols), bf16)
        payload = jnp.concatenate(
            [
                jnp.concatenate(
                    [
                        input_projection[:, inner + t * hc : inner + (t + 1) * hc],
                        input_projection[:, 2 * inner :],
                        tables[0].T,
                        step_projection[:, t * hn : (t + 1) * hn],
                        gap,
                        tail,
                    ],
                    1,
                )
                for t in range(n)
            ],
            0,
        )
        late_payload = jnp.concatenate(
            [
                jnp.concatenate([input_projection[:, t * hc : (t + 1) * hc], tables[3].T], 1)
                for t in range(n)
            ],
            0,
        )
        w_o = jnp.concatenate([output_projection, tables[2].T], 1)

        def as_row(v):
            return jnp.pad(v, ((0, 0), (0, wide - v.shape[1])))

        misc = jnp.concatenate(
            [
                as_row(convolution_weight.T),
                as_row(convolution_bias[None]),
                as_row(adapter_index.astype(bf16)[None]),
                as_row(gated_norm_gain[None]),
            ],
            0,
        )
        misc = jnp.pad(misc, ((0, misc_rows - misc.shape[0]), (0, 0)))
        small = jnp.concatenate(
            [jnp.pad(tables[1].T, ((0, up_keep - up_rows), (0, 0))), misc.reshape(-1, 128)], 0
        )
    w_a = lax.all_to_all(payload, "seq", 0, 0, tiled=True)

    if staged:
        d = lax.axis_index("dp")
        y, z = d % 2, d // 2
        w_o = lax.ppermute(w_o, both, to_head)
        small_y = swap(small, "dp", 1)
        pair = put([(small, y), (small_y, 1 - y)])
        four = put([(pair, z % 2), (swap(pair, "dp", 2), 1 - z % 2)])
        x_near = swap(layer_input, "seq", 1)
        w_a, late_payload, four, x_near, w_o = fence(w_a, late_payload, four, x_near, w_o)
        a1, a3, a0y = rotate(w_a, 1), rotate(w_a, 3), swap(w_a, "dp", 1)
        small = put([(four, z // 2), (swap(four, "dp", 4), 1 - z // 2)])
        w_b = lax.all_to_all(late_payload, "seq", 0, 0, tiled=True)
        small_far = swap(small, "seq", 2)
        a1, a3, a0y, w_a, w_b, small, small_far, x0, x1, og0, og1 = fence(
            a1, a3, a0y, w_a, w_b, small, small_far, layer_input[:1], layer_input[1:],
            output_gradient[:1], output_gradient[1:],
        )
        a13y = swap(jnp.concatenate([a1, a3]), "dp", 1)
        a2 = rotate(w_a, 2)
        x_far0 = swap(x0, "seq", 2)
        beside = swap(jnp.concatenate([small, small_far]), "seq", 1)
        w_bo = jnp.concatenate([w_b, w_o])
        half_rows = small.shape[0]
        small = put(
            [
                (small, here), (beside[:half_rows], here ^ 1), (small_far, here ^ 2),
                (beside[half_rows:], here ^ 3),
            ]
        )
        at = [2 * lax.rem(z + 4 - r, 4) + y for r in range(4)]
        slots = [at[0], at[0] ^ 1, at[1], at[3], at[1] ^ 1, at[3] ^ 1, at[2], at[2] ^ 1]
        slots = jnp.stack(slots).astype(jnp.int32)
        x_order = jnp.arange(4, dtype=jnp.int32) ^ here
    else:
        w_b = lax.all_to_all(late_payload, "seq", 0, 0, tiled=True)
        w_o = lax.ppermute(w_o, both, to_head)
        small = lax.all_gather(lax.all_gather(small, "dp", tiled=True), "seq", tiled=True)
        wa_pieces = [lax.all_gather(w_a, "dp", tiled=True)]
        slots = jnp.zeros((1,), jnp.int32)
        x_order = jnp.arange(nb, dtype=jnp.int32)
        xs = [jnp.split(lax.all_gather(layer_input, "seq", axis=1, tiled=True), nb, axis=1)] * seqs
    docs = w_a[:, wa_cols - 1 - doc_cols : wa_cols - 1].reshape(n, -1)[:, : seqs * own_len]
    docs = jnp.moveaxis(docs.reshape(n, seqs, own_len), 0, 1).reshape(seqs, length)
    order = jnp.concatenate([x_order, slots])
    order_whole = jnp.concatenate([x_order, jnp.zeros((1,), jnp.int32)])

    small = small.reshape(n, dps, small_rows, 128)
    small = jnp.moveaxis(small, 0, 1).reshape(dps * n, small_rows, 128)
    up_full = small[:, :up_rows].reshape(cols, ranks)
    misc = small[:, up_keep:].reshape(dps * n, misc_rows, wide)
    conv_w = jnp.moveaxis(misc[:, :taps, :conv_rows], 1, 0).reshape(taps, -1).astype(f32)
    conv_b = misc[:, taps, :conv_rows].reshape(-1).astype(f32)
    every_index = misc[:, taps + 1, :seqs].reshape(dps, n, seqs)[:, 0].astype(jnp.int32)
    gate_gain = misc[:, taps + 2, :out_rows].reshape(-1).astype(f32)

    def mine(v):
        v = v.reshape(planes, n, v.shape[0] // (planes * n), *v.shape[1:])
        v = lax.dynamic_index_in_dim(v, here, 1, keepdims=False)
        return v.reshape(-1, *v.shape[2:])

    up_gate = mine(up_full[:inner])
    up_conv = jnp.concatenate([mine(up_full[inner : 2 * inner]), up_full[2 * inner :]], 0)
    conv_w = jnp.concatenate([mine(conv_w.T[:inner]), conv_w.T[inner:]], 0).T
    conv_b = jnp.concatenate([mine(conv_b[:inner]), conv_b[inner:]], 0)
    step_bias = mine(head_step_bias)
    decay_rate = -jnp.exp(mine(log_decay_rate))
    skip = mine(head_skip_gain)
    gate_gain = mine(gate_gain)

    chosen = (adapter_index[:, None] == jnp.arange(adapters, dtype=jnp.int32)[None, :]).astype(f32)
    mask = jnp.repeat(chosen, rank, axis=1)[:, None, :]

    doc_f = docs.astype(f32)

    def same_before(k):
        return jnp.pad(doc_f, ((0, 0), (k, 0)), constant_values=-1.0)[:, :length] == doc_f

    def same_after(k):
        return jnp.pad(doc_f, ((0, 0), (0, k)), constant_values=-1.0)[:, k:] == doc_f

    blocks = doc_f.reshape(seqs, nb, BLOCK)
    prior = jnp.concatenate([blocks[:, :1, 0], blocks[:, :-1, -1]], 1)
    keep = (blocks == prior[:, :, None]).reshape(seqs, length)
    ends = (blocks == blocks[:, :, -1:]).reshape(seqs, length)
    flags = [
        same_before(1), same_before(2), same_before(3), keep, ends, doc_f,
        same_after(1), same_after(2), same_after(3),
    ]
    meta = jnp.stack([v.astype(f32) for v in flags], -1)
    meta = jnp.pad(meta, ((0, 0), (0, 0), (0, 128 - len(flags))))
    doc_rows = blocks[:, :, None, :]

    def rows8(*vs):
        return jnp.pad(jnp.stack(vs), ((0, 8 - len(vs)), (0, 0)))

    conv_rows8 = rows8(conv_w[0], conv_w[1], conv_w[2], conv_w[3], conv_b)
    head_rows = rows8(
        jnp.pad(step_bias, (0, 128 - hn)), jnp.pad(decay_rate, (0, 128 - hn))
    )
    wide_rows = rows8(jnp.repeat(skip, hd), gate_gain)
    halves = jnp.pad(
        (jnp.arange(128)[None, :] // 64 == jnp.arange(2)[:, None]).astype(bf16), ((0, 14), (0, 0))
    )
    select = (jnp.arange(hc)[:, None] // hd == jnp.arange(128)[None, :]).astype(bf16)
    mask8 = jnp.broadcast_to(mask, (seqs, 8, ranks))
    cc = conv_cols
    anywhere = pl.BlockSpec(memory_space=pl.ANY)
    params = pltpu.CompilerParams(
        dimension_semantics=("arbitrary",), vmem_limit_bytes=VMEM_BYTES
    )

    def at(w, k=0):
        return pl.BlockSpec((1, BLOCK, w), lambda b, o: (k, b, 0))

    def once(v, *block):
        block = block or v.shape
        return pl.BlockSpec(block, lambda b, o: (0,) * len(block), pipeline_mode=pl.Buffered(1))

    def of_seq(v, s0):
        k = s0 if v.shape[0] > 1 else 0
        return pl.BlockSpec(
            (1,) + v.shape[1:], lambda b, o: (k, 0, 0), pipeline_mode=pl.Buffered(1)
        )

    def one(w, dtype):
        return jax.ShapeDtypeStruct((1, length, w), dtype)

    def cost(flops, mib):
        return pl.CostEstimate(flops=int(flops), bytes_accessed=mib << 20, transcendentals=0)

    def parts_specs():
        return [once(None, BLOCK, width), once(None, 2 * BLOCK, width), once(None, BLOCK, width)]

    parts_shapes = [
        jax.ShapeDtypeStruct((k * BLOCK, width), bf16) for k in (1, 2, 1)
    ]

    def forward(s0, order, blocks, pieces, keep):
        whole_w = jax.ShapeDtypeStruct((width, wa_cols), bf16)
        size = n * rows if len(pieces) > 1 else width
        total = sum(v.shape[0] for v in pieces) // size
        return pl.pallas_call(
            functools.partial(
                forward_kernel, hn=hn, hc=hc, count=len(pieces), size=size, keep=keep
            ),
            grid_spec=pltpu.PrefetchScalarGridSpec(
                num_scalar_prefetch=1,
                grid=(nb,),
                in_specs=[
                    *(of_seq(v, s0) for v in blocks), at(128, s0),
                    pl.BlockSpec((1, 1, 1, BLOCK), lambda b, o: (s0, b, 0, 0)),
                    once(up_conv), once(conv_rows8), once(head_rows), of_seq(mask8, s0), once(halves),
                    *([anywhere] * len(pieces)),
                ],
                out_specs=[
                    at(width), at(128), at(cc), at(cc), at(hc),
                    pl.BlockSpec((1, 1, hc, state), lambda b, o: (0, b, 0, 0)), at(384),
                    *([anywhere] if keep else []),
                ],
                scratch_shapes=[
                    pltpu.VMEM((BLOCK + 8, cc), f32), pltpu.VMEM((hc, state), f32),
                    pltpu.VMEM((BLOCK, width), bf16), pltpu.VMEM((width, wa_cols), bf16),
                    pltpu.VMEM((8, width), f32), pltpu.SemaphoreType.DMA((total,)),
                    pltpu.SemaphoreType.DMA,
                ],
            ),
            out_shape=[
                one(width, bf16), one(128, bf16), one(cc, bf16), one(cc, f32), one(hc, f32),
                jax.ShapeDtypeStruct((1, nb, hc, state), bf16), one(384, f32),
                *([whole_w] if keep else []),
            ],
            compiler_params=params,
            name="ssm_forward",
            cost_estimate=cost(2 * length * (width * wa_cols + 3 * BLOCK * hc), 20),
        )(order, *blocks, meta, doc_rows, up_conv, conv_rows8, head_rows, mask8, halves, *pieces)

    def middle(s0, order, scanned, blocks, gate_pieces, out_pieces, keep):
        normed, rank_in, vbc, _, ssm = scanned[:5]
        count = len(gate_pieces)
        merged = () if out_pieces else (n * rows, out_rows)
        wb_shape, wo_shape = (width, hc + ranks), (hc, width + ranks)
        return pl.pallas_call(
            functools.partial(
                middle_kernel, hc=hc, width=width, rank=rank, count=count, keep=keep,
                merged=merged,
            ),
            grid_spec=pltpu.PrefetchScalarGridSpec(
                num_scalar_prefetch=1,
                grid=(nb,),
                in_specs=[
                    at(width), at(128), at(cc), at(hc), *(of_seq(v, s0) for v in blocks),
                    once(up_gate), once(wide_rows), of_seq(mask8, s0), *([anywhere] * (count + len(out_pieces))),
                ],
                out_specs=[
                    at(hc), at(hc), at(128), *parts_specs(),
                    pl.BlockSpec((1, 8 + rank, BLOCK), lambda b, o: (0, 0, b)),
                    *([anywhere] * 2 if keep else []),
                ],
                scratch_shapes=[
                    pltpu.VMEM((BLOCK, width), bf16), pltpu.VMEM(wb_shape, bf16),
                    pltpu.VMEM(wo_shape, bf16), pltpu.SemaphoreType.DMA((3 * dps,)),
                    pltpu.SemaphoreType.DMA((count,)), pltpu.SemaphoreType.DMA((2,)),
                ],
            ),
            out_shape=[
                one(hc, f32), one(hc, f32), one(128, bf16), *parts_shapes,
                jax.ShapeDtypeStruct((1, 8 + rank, length), f32),
                *([jax.ShapeDtypeStruct(v, bf16) for v in (wb_shape, wo_shape)] if keep else []),
            ],
            compiler_params=params,
            name="output_side",
            cost_estimate=cost(2 * length * width * hc * 3, 25),
        )(
            order, normed, rank_in, vbc, ssm, *blocks, up_gate, wide_rows, mask8, *gate_pieces,
            *out_pieces,
        )

    def backward(s0, scanned, gate, q, rm, grad_rank_out):
        _, rank_in, vbc, pre, ssm, states_low, tok = scanned[:7]

        def back(w, k=0):
            return pl.BlockSpec((1, BLOCK, w), lambda b, o: (k, nb - 1 - b, 0))

        def back_state(shift):
            return pl.BlockSpec(
                (1, 1, hc, state), lambda b, o: (0, jnp.minimum(nb - 1 - b + shift, nb - 1), 0, 0)
            )

        return pl.pallas_call(
            functools.partial(backward_kernel, hn=hn, hc=hc, rank=rank),
            grid_spec=pltpu.PrefetchScalarGridSpec(
                num_scalar_prefetch=1,
                grid=(nb,),
                in_specs=[
                    back(hc), back(hc), back(hc), back(cc), back(cc), back(384),
                    pl.BlockSpec((1, 8, BLOCK), lambda b, o: (0, 0, nb - 1 - b)), back(128, s0),
                    pl.BlockSpec((1, 1, 1, BLOCK), lambda b, o: (s0, nb - 1 - b, 0, 0)),
                    back_state(0), back_state(1), back(128), back(128), once(conv_rows8),
                    once(head_rows), once(wide_rows), once(halves), once(select), once(up_gate),
                    once(up_conv), of_seq(mask8, s0), once(wa), once(wb),
                ],
                out_specs=[
                    *parts_specs(), once(None, 1, rank, 2 * hc + cc),
                    pl.BlockSpec((1, rank, BLOCK), lambda b, o: (0, 0, nb - 1 - b)),
                ],
                scratch_shapes=[
                    pltpu.VMEM((BLOCK + 8, cc), f32), pltpu.VMEM((hc, state), f32),
                ],
            ),
            out_shape=[
                *parts_shapes, jax.ShapeDtypeStruct((1, rank, 2 * hc + cc), f32),
                jax.ShapeDtypeStruct((1, rank, length), f32),
            ],
            compiler_params=params,
            name="ssm_backward",
            cost_estimate=cost(2 * length * (8 * BLOCK * hc + width * (hc + cc)), 30),
        )(
            x_order, q, gate, ssm, vbc, pre, tok, rm, meta, doc_rows, states_low, states_low, rank_in,
            grad_rank_out, conv_rows8, head_rows, wide_rows, halves, select, up_gate, up_conv, mask8,
            wa, wb,
        )

    def own_tokens(v, axis):
        return lax.dynamic_slice_in_dim(v, here * own_len, own_len, axis)

    def with_adapter(rows_of, table, s0):
        wide_rows_of = jnp.tile(rows_of, (adapters, 1)) * mask[s0, 0][:, None].astype(bf16)
        return mm("rt,dr->td", wide_rows_of, table)

    if staged:
        ready = (
            order, up_conv, up_gate, conv_rows8, head_rows, meta, doc_rows, mask8, halves, select,
            wide_rows, w_bo, order_whole, every_index,
        )
        a2, a13y, x_far0, x1, ready = fence(a2, a13y, x_far0, x1, ready)
        (
            order, up_conv, up_gate, conv_rows8, head_rows, meta, doc_rows, mask8, halves, select,
            wide_rows, w_bo, order_whole, every_index,
        ) = ready
        a2y = swap(a2, "dp", 1)
        x_both0 = swap(x_far0, "seq", 1)
        b1, b3 = rotate(w_bo, 1), rotate(w_bo, 3)
        x_far1 = swap(x1, "seq", 2)
        wa_pieces = [w_a, a0y, a1, a3, a13y, a2, a2y]
        xs = [[layer_input, x_near, x_far0, x_both0]]
        wa_pieces, xs[0], w_bo = fence(wa_pieces, xs[0], w_bo)
        *fwd0, wa = forward(0, order, xs[0], wa_pieces, True)
        b0y = swap(w_bo, "dp", 1)
        fwd0, wa, b1, b3, b0y, w_bo, x_far1 = fence(fwd0, wa, b1, b3, b0y, w_bo, x_far1)
        x_both1 = swap(x_far1, "seq", 1)
        x_both1, w_bo, og0, og1, og = fence(x_both1, w_bo, og0, og1, output_gradient)
        fwd1 = forward(1, order_whole, [layer_input, x_near, x_far1, x_both1], [wa], False)
        b1y, b3y = swap(b1, "dp", 1), swap(b3, "dp", 1)
        b2 = rotate(w_bo, 2)
        og_far0 = swap(og0, "seq", 2)
        og_near = swap(og, "seq", 1)
        fwd1, b1y, b3y, b2, og_far0, og_near, w_bo, og1 = fence(
            fwd1, b1y, b3y, b2, og_far0, og_near, w_bo, og1
        )
        b2y = swap(b2, "dp", 1)
        og_both0 = swap(og_far0, "seq", 1)
        fwd = [fwd0, fwd1]
        wb_pieces = [w_bo, b0y, b1, b3, b1y, b3y, b2, b2y]
        wo_pieces = []
        ogs = [[output_gradient, og_near, og_far0, og_both0]]
        wb_pieces, ogs[0], og1 = fence(wb_pieces, ogs[0], og1)
    else:
        fwd = [forward(0, order, xs[0], wa_pieces, True)]
        wa = fwd[0][-1]
        fwd += [forward(s0, order_whole, xs[s0], [wa], False) for s0 in range(1, seqs)]
        wb_pieces = [lax.all_gather(w_b, "dp", tiled=True)]
        wo_pieces = [lax.all_gather(w_o, "dp", tiled=True)]
        full = lax.all_gather(output_gradient, "seq", axis=1, tiled=True)
        ogs = [jnp.split(full, nb, axis=1)] * seqs
    gain = wa[:, -1].astype(f32)

    def normalisers(stats):
        inv_gated = lax.rsqrt(stats[:1] / inner + EPS)
        rm = jnp.pad(jnp.concatenate([inv_gated, stats[1:2] / inner], 0), ((0, 6), (0, 0)))[None]
        return inv_gated, rm, own_tokens((stats[8:] * inv_gated).astype(bf16), 1)

    def layer_output(s0, branch, inv_gated, rank_out):
        return (
            layer_input[s0].astype(f32)
            + branch * own_tokens(inv_gated, 1).T
            + with_adapter(rank_out, up_out, s0)
        ).astype(bf16)

    def down_gradient(s0, grad_rank_in):
        return mm("rt,td->rd", grad_rank_in, fwd[s0][0][0]).astype(bf16)

    def layer_gradient(s0, partial, grad_rank_in):
        grad_normed = partial + with_adapter(
            own_tokens(grad_rank_in, 1), down_in, s0
        )
        own = layer_input[s0].astype(f32)
        inv_own = lax.rsqrt(jnp.mean(own * own, -1, keepdims=True) + EPS)
        scaled_in = grad_normed * gain
        return (
            inv_own * scaled_in
            - own * inv_own**3 * jnp.mean(scaled_in * own, -1, keepdims=True)
            + output_gradient[s0].astype(f32)
        )

    *side0, wb, wo = middle(0, order, fwd[0], ogs[0], wb_pieces, wo_pieces, True)
    up_out = wb[:, hc:]
    down_in = wa[:, cc : cc + ranks]
    if staged:
        og_far1 = swap(og1, "seq", 2)
        side0, wb, wo, og_far1 = fence(side0, wb, wo, og_far1)
        ogs.append([output_gradient, og_near, og_far1, swap(og_far1, "seq", 1)])
        ogs[1], side0, wb, wo, up_out, down_in, gain = fence(
            ogs[1], side0, wb, wo, up_out, down_in, gain
        )
        gate0, q0, gro0, near0, pair0, far0, stats0 = side0
        side1 = middle(1, order_whole, fwd[1], ogs[1], [wb], [wo], False)
        got = others(stats0[0])
        pair0 = swap(pair0, "seq", 1)
        side1, got, pair0, far0 = fence(side1, got, pair0, far0)
        gate1, q1, gro1, near1, pair1, far1, stats1 = side1
        inv0, rm0, rank_out0 = normalisers(total_of(stats0[0], got))
        rm0, away, stats1, pair1 = fence(rm0, across(far0, pair0), stats1, pair1)

        back0 = backward(0, fwd[0], gate0, q0, rm0, gro0)
        away = swap(away, "seq", 2)
        got = others(stats1[0])
        pair1 = swap(pair1, "seq", 1)
        back0, away, got, pair1, far1 = fence(back0, away, got, pair1, far1)
        near_g0, pair_g0, far_g0, compact0, gri0 = back0
        pair_g0 = swap(pair_g0, "seq", 1)
        away0 = away
        inv1, rm1, rank_out1 = normalisers(total_of(stats1[0], got))
        rm1, away, gri0, away_g, away0, rank_out0, rank_out1 = fence(
            rm1, across(far1, pair1), gri0, across(far_g0, pair_g0), away0, rank_out0, rank_out1
        )

        back1 = backward(1, fwd[1], gate1, q1, rm1, gro1)
        away = swap(away, "seq", 2)
        away_g = swap(away_g, "seq", 2)
        got = others(gri0[0])
        back1, away, away_g, got, away0, rank_out0, rank_out1, near0, pair0, inv0 = fence(
            back1, away, away_g, got, away0, rank_out0, rank_out1, near0, pair0, inv0
        )
        near_g1, pair_g1, far_g1, compact1, gri1 = back1
        pair_g1 = swap(pair_g1, "seq", 1)
        got1 = others(gri1[0])
        g_out_up = mm("srt,std->srd", jnp.stack([rank_out0, rank_out1]), output_gradient)
        split = jnp.concatenate(
            [
                jnp.concatenate([compact0[0], compact1[0]]).astype(bf16),
                g_out_up.astype(bf16).reshape(seqs * rank, width),
            ],
            1,
        )
        away_g1, split, got1 = fence(across(far_g1, pair_g1), split, got1)
        away_g1 = swap(away_g1, "seq", 2)
        split_far = swap(split, "seq", 2)
        split_near = swap(split, "seq", 1)
        split_both = swap(split_far, "seq", 1)
        gri0 = total_of(gri0[0], got).astype(bf16)
        gri1 = total_of(gri1[0], got1).astype(bf16)
        downs = jnp.concatenate([down_gradient(0, gri0), down_gradient(1, gri1)])
        output0 = layer_output(0, own_sum(near0, pair0, away0), inv0, rank_out0)
        output1 = layer_output(1, own_sum(near1, pair1, away), inv1, rank_out1)
        grad0 = layer_gradient(0, own_sum(near_g0, pair_g0, away_g), gri0)
        grads_of_seq = [split, split_near, split_far, split_both]
        grads_order = x_order
    else:
        splits, downs, ranks_out, outputs, grads_in = [], [], [], [], []
        for s0 in range(seqs):
            if s0:
                side0 = middle(s0, order_whole, fwd[s0], ogs[s0], [wb], [wo], False)
            gate, q, gro, *parts, stats = side0
            inv_gated, rm, rank_out = normalisers(lax.psum(stats[0], "seq"))
            outputs.append(layer_output(s0, scatter_plain(*parts), inv_gated, rank_out))
            *parts, compacted, gri = backward(s0, fwd[s0], gate, q, rm, gro)
            gri = lax.psum(gri[0], "seq").astype(bf16)
            splits.append(compacted[0].astype(bf16))
            downs.append(down_gradient(s0, gri))
            ranks_out.append(rank_out)
            grads_in.append(layer_gradient(s0, scatter_plain(*parts), gri))
        g_out_up = mm("srt,std->srd", jnp.stack(ranks_out), output_gradient).astype(bf16)
        output = jnp.stack(outputs)
        grad_in = jnp.stack(grads_in)
        downs = jnp.concatenate(downs)
        split = jnp.concatenate(
            [jnp.concatenate(splits), g_out_up.reshape(seqs * rank, width)], 1
        )
        grads_of_seq = jnp.split(lax.all_gather(split, "seq", axis=0, tiled=True), n)

    widths = [v // (dps * n) for v in (width, cols, inner, width)]
    starts, lanes = [], 0
    for v in widths:
        starts.append(lanes)
        lanes += -(-v // 128) * 128
    pack_rows = seqs * rank
    if staged:
        packed = pl.pallas_call(
            functools.partial(
                pack_grads_kernel, n=n, hc=hc, inner=inner, width=width, widths=widths,
                starts=starts, planes=planes,
            ),
            in_specs=[
                pl.BlockSpec(memory_space=pltpu.SMEM),
                *[pl.BlockSpec(memory_space=pltpu.VMEM)] * 5,
            ],
            out_specs=pl.BlockSpec(memory_space=pltpu.VMEM),
            out_shape=jax.ShapeDtypeStruct((dps, pack_rows, lanes), bf16),
            scratch_shapes=[
                pltpu.VMEM((pack_rows, cols + 256), f32), pltpu.VMEM((pack_rows, inner + 256), f32),
                pltpu.VMEM((pack_rows, width + 256), f32),
            ],
            name="pack_grads",
        )(
            grads_order,
            *grads_of_seq, jnp.pad(downs, ((0, 0), (0, 256))),
        )
    else:
        pieces = jnp.stack(grads_of_seq)

        def by_heads(start):
            return jnp.concatenate([pieces[t, :, start : start + hc] for t in range(n)], -1)

        def summed(start, size):
            return pieces[..., start : start + size].astype(f32).sum(0).astype(bf16)

        full = [
            downs,
            jnp.concatenate([by_heads(0), by_heads(hc), summed(2 * hc, state2)], -1),
            by_heads(2 * hc + state2),
            summed(3 * hc + state2, width),
        ]
        packed = jnp.zeros((dps, pack_rows, lanes), bf16)
        for v, start, w in zip(full, starts, widths):
            v = lax.dynamic_index_in_dim(
                v.reshape(pack_rows, dps, n, w), here, 2, keepdims=False
            )
            packed = packed.at[:, :, start : start + w].set(v.transpose(1, 0, 2))
    got = lax.all_to_all(packed, "dp", 0, 0, tiled=True)
    if staged:
        grad1 = layer_gradient(1, own_sum(near_g1, pair_g1, away_g1), gri1)
        output = jnp.stack([output0, output1])
        grad_in = jnp.stack([grad0, grad1])
    all_chosen = (every_index[..., None] == jnp.arange(adapters)).astype(bf16)
    table = mm("dsk,dsrc->krc", all_chosen, got.reshape(dps, seqs, rank, lanes))
    grads = [table[..., start : start + w] for start, w in zip(starts, widths)]
    return (output, grad_in, grads[0], grads[1], grads[2], grads[3])


def solution(mesh):
    return jax.shard_map(
        per_device,
        mesh=mesh,
        in_specs=(
            P("dp", "seq", None),
            P("dp", "seq"),
            P("dp"),
            P(("dp", "seq")),
            P(("dp", "seq"), None),
            P(("dp", "seq"), None),
            P(("dp", "seq"), None),
            P(("dp", "seq")),
            P(),
            P(),
            P(),
            P(("dp", "seq")),
            P(("dp", "seq"), None),
            P(None, None, ("dp", "seq")),
            P(None, None, ("dp", "seq")),
            P(None, None, ("dp", "seq")),
            P(None, None, ("dp", "seq")),
            P("dp", "seq", None),
        ),
        out_specs=(
            P("dp", "seq", None),
            P("dp", "seq", None),
            P(None, None, ("dp", "seq")),
            P(None, None, ("dp", "seq")),
            P(None, None, ("dp", "seq")),
            P(None, None, ("dp", "seq")),
        ),
        check_vma=False,
    )
```

```python
import functools

import jax
import jax.numpy as jnp
from jax import lax
from jax.experimental import pallas as pl
from jax.experimental.pallas import tpu as pltpu
from jax.sharding import PartitionSpec as P

EPS = 1e-05
f32 = jnp.float32
bf16 = jnp.bfloat16
BLOCK = 256


def mm(form, a, b):
    return jnp.einsum(form, a, b, preferred_element_type=f32)


LOG2E = 1.4426950408889634
VMEM_BYTES = 66_000_000


def dot_nn(a, b):
    return lax.dot_general(a, b, (((1,), (0,)), ((), ())), preferred_element_type=f32)


def dot_nt(a, b):
    return lax.dot_general(a, b, (((1,), (1,)), ((), ())), preferred_element_type=f32)


def dot_tn(a, b):
    return lax.dot_general(a, b, (((0,), (0,)), ((), ())), preferred_element_type=f32)


def dot_exact(chosen, v):
    hi = v.astype(bf16)
    rest = v - hi.astype(f32)
    mid = rest.astype(bf16)
    lo = (rest - mid.astype(f32)).astype(bf16)
    return dot_nn(chosen, hi) + (dot_nn(chosen, mid) + dot_nn(chosen, lo))


def sigmoid(v):
    return 0.5 * jnp.tanh(0.5 * v) + 0.5


def spread_pair(cols, j):
    rows = cols.shape[0]
    lane = lax.broadcasted_iota(jnp.int32, (rows, 128), 1)
    return jnp.where(lane < 64, cols[:, 2 * j : 2 * j + 1], cols[:, 2 * j + 1 : 2 * j + 2])


def spread_all(cols, pairs):
    return jnp.concatenate([spread_pair(cols, j) for j in range(pairs)], 1)


def per_head(v, select):
    hi = v.astype(bf16)
    lo = (v - hi.astype(f32)).astype(bf16)
    return dot_nn(hi, select) + dot_nn(lo, select)


def by_rank(t, rank):
    out = t[:rank]
    for k in range(rank, 128, rank):
        out = out + t[k : k + rank]
    return out


def fold(v, rank):
    return by_rank(v.T, rank)


def shards(pieces, size):
    return [p.at[k : k + size] for p in pieces for k in range(0, p.shape[0], size)]


def assemble(order_ref, base, pieces, size, target, sems):
    copies = []
    for i, piece in enumerate(shards(pieces, size)):
        at = pl.multiple_of(order_ref[base + i] * size, 16)
        copies.append(pltpu.make_async_copy(piece, target.at[pl.ds(at, size)], sems.at[i]))
    for copy in copies:
        copy.start()
    for copy in copies:
        copy.wait()


def fetch(order_ref, b, blocks, s0, target, sem):
    for i, block in enumerate(blocks):

        @pl.when(order_ref[b] == i)
        def _(block=block):
            row = s0 if block.shape[0] > 1 else 0
            pltpu.make_async_copy(block.at[row], target, sem).start()


def arrived(blocks, target, sem):
    pltpu.make_async_copy(blocks[0].at[0], target, sem).wait()


def forward_kernel(order_ref, *refs, hn, hc, count, size, s0, keep):
    (x0, x1, x2, x3, meta_ref, doc_ref, up_ref, conv_ref, head_ref, mask_ref, half_ref) = refs[:11]
    pieces = refs[11 : 11 + count]
    normed_ref, rank_ref, vbc_ref, pre_ref, ssm_ref, state_ref, tok_ref, *rest = refs[11 + count :]
    if keep:
        full_ref, rest = rest[0], rest[1:]
    buf, carry, x_buf, wa_ref, gain_ref, pa_buf, normed_buf, sems, full_sem, x_sems = rest
    pairs = hn // 2
    cc = hc + 256
    b = pl.program_id(0)

    xs = (x0, x1, x2, x3)

    @pl.when(b == 0)
    def _():
        for k in (0, 1):
            fetch(order_ref, k, xs, s0, x_buf.at[k], x_sems.at[k])
        assemble(order_ref, 4, pieces, size, wa_ref, sems)
        if keep:
            pltpu.make_async_copy(wa_ref, full_ref, full_sem).start()
        gain_ref[...] = wa_ref[:, cc + 128 :].astype(f32).T[120:, :]
        carry[...] = jnp.zeros_like(carry)
        buf[0:8, :] = jnp.zeros((8, cc), f32)

    blocks = pl.num_programs(0)
    now, later = lax.rem(b, 2), lax.rem(b + 1, 2)
    chunks = wa_ref.shape[1] // 128
    chunks = chunks // 2 if chunks % 2 == 0 else chunks
    span = wa_ref.shape[1] // chunks

    def normalise(slot):
        x = x_buf[slot].astype(f32)
        inv = lax.rsqrt(jnp.mean(x * x, -1, keepdims=True) + EPS)
        normed_buf[slot] = (x * inv * gain_ref[7:8, :]).astype(bf16)

    def project(slot, c):
        at = slice(span * c, span * c + span)
        pa_buf[slot, :, at] = dot_nn(normed_buf[slot], wa_ref[:, at])

    @pl.when(b == 0)
    def _():
        arrived(xs, x_buf.at[0], x_sems.at[0])
        normalise(0)
        for c in range(chunks):
            project(0, c)

    @pl.when(b + 2 < blocks)
    def _():
        fetch(order_ref, b + 2, xs, s0, x_buf.at[now], x_sems.at[now])

    @pl.when(b + 1 < blocks)
    def _():
        arrived(xs, x_buf.at[later], x_sems.at[later])

    normalise(later)
    normed_ref[0] = normed_buf[now]
    rank = (pa_buf[now, :, cc : cc + 128] * mask_ref[0, 0:1, :]).astype(bf16)
    rank_ref[0] = rank
    conv_in = (pa_buf[now, :, :cc] + dot_nt(rank, up_ref[...])).astype(bf16).astype(f32)
    buf[8:, :] = conv_in
    meta = meta_ref[0]
    pre = conv_ref[4:5, :] + conv_ref[3:4, :] * conv_in
    for k in (1, 2, 3):
        pre = pre + conv_ref[3 - k : 4 - k, :] * (buf[8 - k : 8 - k + BLOCK, :] * meta[:, k - 1 : k])
    buf[0:8, :] = buf[BLOCK : BLOCK + 8, :]
    pre_ref[0] = pre
    vbc = (pre * sigmoid(pre)).astype(bf16)
    vbc_ref[0] = vbc
    values = vbc[:, :hc]
    in_state = vbc[:, hc : hc + 128]
    out_state = vbc[:, hc + 128 :]
    arg = pa_buf[now, :, cc + 128 : cc + 256] + head_ref[0:1, :]
    dt = jnp.maximum(arg, 0.0) + jnp.log1p(jnp.exp(-jnp.abs(arg)))
    row = lax.broadcasted_iota(jnp.int32, (BLOCK, BLOCK), 0)
    col = lax.broadcasted_iota(jnp.int32, (BLOCK, BLOCK), 1)
    cum = dot_exact((row >= col).astype(f32).astype(bf16), dt * head_ref[1:2, :])
    tok_ref[0, :, 0:128] = dt
    tok_ref[0, :, 128:256] = cum
    tok_ref[0, :, 256:384] = arg
    left = cum * LOG2E
    right = (left - jnp.log(jnp.maximum(dt, 1e-37)) * LOG2E).T
    ok = (row >= col) & (meta[:, 5:6] == doc_ref[0, 0])
    bias = jnp.where(ok, 0.0, -1e30)
    contact = dot_nt(out_state, in_state)
    entry = jnp.exp(cum) * meta[:, 3:4]
    weight = jnp.exp(cum[BLOCK - 1 :, :] - cum) * dt * meta[:, 4:5]
    state = carry[...]
    state_low = state.astype(bf16)
    state_ref[0, 0] = state_low
    readout = dot_nt(out_state, state_low)
    half = BLOCK // 2
    scaled = []
    for j in range(pairs):
        for c in range(j * chunks // pairs, (j + 1) * chunks // pairs):
            project(later, c)
        at = slice(128 * j, 128 * j + 128)
        v = values[:, at]
        ys = []
        for r0, c1 in ((0, half), (half, BLOCK)):
            ws = []
            for h in (2 * j, 2 * j + 1):
                e = jnp.exp2(
                    (left[r0 : r0 + half, h : h + 1] - right[h : h + 1, :c1])
                    + bias[r0 : r0 + half, :c1]
                )
                ws.append((contact[r0 : r0 + half, :c1] * e).astype(bf16))
            vv = jnp.concatenate([v[:c1] * half_ref[0:1, :], v[:c1] * half_ref[1:2, :]], 0)
            ys.append(dot_nn(jnp.concatenate(ws, 1), vv))
        y = jnp.concatenate(ys, 0)
        ssm_ref[0, :, at] = y + readout[:, at] * spread_pair(entry, j)
        scaled.append((v.astype(f32) * spread_pair(weight, j)).astype(bf16))
    local = dot_tn(jnp.concatenate(scaled, 1), in_state)
    passing = entry[BLOCK - 1 :, :]
    for h in range(hn):
        at = slice(64 * h, 64 * h + 64)
        carry[at, :] = passing[:, h : h + 1] * state[at] + local[at]

    if keep:

        @pl.when(b == pl.num_programs(0) - 1)
        def _():
            pltpu.make_async_copy(wa_ref, full_ref, full_sem).wait()


def route(order_ref, b, value, near_ref, pair_ref, far_ref):
    for k, target in enumerate(
        (near_ref, pair_ref.at[0:BLOCK], far_ref, pair_ref.at[BLOCK : 2 * BLOCK])
    ):

        @pl.when(order_ref[b] == k)
        def _(target=target):
            target[...] = value


def assemble_both(order_ref, base, pieces, rows, out_rows, wb_ref, wo_ref, sems):
    part = wb_ref.shape[1]
    copies = []
    for i, piece in enumerate(shards(pieces, rows + 2 * out_rows)):
        slot = order_ref[base + i]
        to = pl.ds(pl.multiple_of(slot * rows, 16), rows)
        to_out = pl.ds(pl.multiple_of(slot * out_rows, 16), out_rows)
        rest = wo_ref.shape[1] - part
        moves = (
            (piece.at[0:rows], wb_ref.at[to]),
            (piece.at[rows : rows + out_rows], wo_ref.at[to_out, 0:part]),
            (piece.at[rows + out_rows :, 0:rest], wo_ref.at[to_out, part : part + rest]),
        )
        for j, (source, target) in enumerate(moves):
            copies.append(pltpu.make_async_copy(source, target, sems.at[3 * i + j]))
    return copies


def middle_kernel(order_ref, *refs, hc, width, rank, count, keep, merged, s0):
    (
        normed_ref, rank_ref, vbc_ref, ssm_ref, og0, og1, og2, og3, up_ref, row_ref, mask_ref,
    ) = refs[:11]
    gate_pieces = refs[11 : 11 + count]
    after_gate = 11 + count
    out_pieces = () if merged else refs[after_gate : after_gate + count]
    first_out = after_gate + len(out_pieces)
    g_ref, q_ref, gro_ref, near_ref, pair_ref, far_ref, stat_ref, *rest = refs[first_out:]
    if keep:
        wb_full, wo_full, rest = rest[0], rest[1], rest[2:]
    og_buf, wb_ref, wo_ref, sems, more_sems, full_sems, og_sems = rest
    ogs = (og0, og1, og2, og3)
    b = pl.program_id(0)

    def keeping():
        return (
            pltpu.make_async_copy(wb_ref, wb_full, full_sems.at[0]),
            pltpu.make_async_copy(wo_ref, wo_full, full_sems.at[1]),
        )

    now, later = lax.rem(b, 2), lax.rem(b + 1, 2)
    if merged:
        copies = assemble_both(order_ref, 4, gate_pieces, *merged, wb_ref, wo_ref, sems)
        gate_copies = copies[::3]
        out_copies = [c for i, c in enumerate(copies) if i % 3]
    else:
        gate_copies = [pltpu.make_async_copy(gate_pieces[0], wb_ref, sems.at[0])]
        out_copies = [pltpu.make_async_copy(out_pieces[0], wo_ref, more_sems.at[0])]

    @pl.when(b == 0)
    def _():
        for copy in gate_copies:
            copy.start()
        fetch(order_ref, 0, ogs, s0, og_buf.at[0], og_sems.at[0])
        for copy in out_copies:
            copy.start()
        for copy in gate_copies:
            copy.wait()

    @pl.when(b + 1 < pl.num_programs(0))
    def _():
        fetch(order_ref, b + 1, ogs, s0, og_buf.at[later], og_sems.at[later])

    gate = dot_nn(normed_ref[0], wb_ref[:, :hc]) + dot_nt(rank_ref[0], up_ref[...])
    g_ref[0] = gate

    @pl.when(b == 0)
    def _():
        for copy in out_copies:
            copy.wait()
        if keep:
            for copy in keeping():
                copy.start()

    arrived(ogs, og_buf.at[now], og_sems.at[now])
    mixed = ssm_ref[0] + row_ref[0:1, :] * vbc_ref[0, :, :hc].astype(f32)
    gated = mixed * (gate * sigmoid(gate))
    og = og_buf[now]
    gro = (dot_nn(og, wb_ref[:, hc:]) * mask_ref[0, 0:1, :]).astype(bf16)
    gro_ref[0] = gro
    q = dot_nt(og, wo_ref[:, :width]) + dot_nt(gro, wo_ref[:, width : width + 128])
    q = q * row_ref[1:2, :]
    q_ref[0] = q
    lane = lax.broadcasted_iota(jnp.int32, (BLOCK, 128), 1)
    s0 = jnp.sum(gated * gated, -1, keepdims=True)
    s1 = jnp.sum(q * gated, -1, keepdims=True)
    stat_ref[0, 0:8, :] = jnp.where(lane == 0, s0, s1).T[:8]
    low = (gated * row_ref[1:2, :]).astype(bf16)
    route(order_ref, b, dot_nn(low, wo_ref[:, :width]).astype(bf16), near_ref, pair_ref, far_ref)
    stat_ref[0, 8:, :] = fold(dot_nn(low, wo_ref[:, width : width + 128]) * mask_ref[0, 0:1, :], rank)

    if keep:

        @pl.when(b == pl.num_programs(0) - 1)
        def _():
            for copy in keeping():
                copy.wait()


def backward_kernel(
    order_ref, q_ref, g_ref, ssm_ref, vbc_ref, pre_ref, tok_ref, rm_ref, meta_ref, doc_ref, state_ref, next_ref,
    rank_ref, gro_ref, conv_ref, head_ref, row_ref, half_ref, select_ref, upg_ref, upc_ref, mask_ref,
    wa_ref, wb_ref,
    near_ref, pair_ref, far_ref, grads_ref, gri_ref,
    buf, carry, held_gate, held_conv, held_step, part_buf,
    *, hn, hc, rank,
):
    pairs = hn // 2
    step = pl.program_id(0)
    blocks = pl.num_programs(0)
    chunks = part_buf.shape[1] // 256

    def product(c):
        rows = slice(256 * c, 256 * c + 256)
        part_buf[:, rows] = (
            dot_nt(held_gate[...], wb_ref[rows, :hc])
            + dot_nt(held_conv[...], wa_ref[rows, :cc])
            + dot_nt(held_step[...], wa_ref[rows, cc + 128 :])
        ).astype(bf16)

    cc = hc + 256
    first = pl.program_id(0) == 0

    @pl.when(first)
    def _():
        carry[...] = jnp.zeros_like(carry)
        buf[BLOCK:, :] = jnp.zeros((8, cc), f32)
        grads_ref[...] = jnp.zeros_like(grads_ref)

    rm = jnp.concatenate([rm_ref[0]] * 16, 0).T
    inv = rm[:, 0:1]
    mean = rm[:, 1:2]
    meta = meta_ref[0]
    gate = g_ref[0]
    ssm = ssm_ref[0]
    q = q_ref[0]
    vbc = vbc_ref[0]
    values = vbc[:, :hc]
    values_f = values.astype(f32)
    in_state = vbc[:, hc : hc + 128]
    out_state = vbc[:, hc + 128 :]
    skip = row_ref[0:1, :]
    mixed = ssm + skip * values_f
    sg = sigmoid(gate)
    act = gate * sg
    gated = mixed * act
    gated_r = gated * inv
    grad_gated = inv * (q - gated_r * (inv * mean))
    gated_low = (gated_r * row_ref[1:2, :]).astype(bf16)
    grads_ref[0, :, hc + cc :] = grads_ref[0, :, hc + cc :] + by_rank(
        dot_tn(gro_ref[0], gated_low), rank
    )
    grad_mixed = grad_gated * act
    gp_gate = (grad_gated * mixed * (sg + act * (1.0 - sg))).astype(bf16)
    gsum = grad_mixed.astype(bf16)
    gsum_f = gsum.astype(f32)

    dt = tok_ref[0, :, 0:128]
    cum = tok_ref[0, :, 128:256]
    arg = tok_ref[0, :, 256:384]
    scaled_cum = cum * LOG2E
    down = scaled_cum - jnp.log(jnp.maximum(dt, 1e-37)) * LOG2E
    across = scaled_cum.T
    row = lax.broadcasted_iota(jnp.int32, (BLOCK, BLOCK), 0)
    col = lax.broadcasted_iota(jnp.int32, (BLOCK, BLOCK), 1)
    ok = (col >= row) & (meta[:, 5:6] == doc_ref[0, 0])
    bias = jnp.where(ok, 0.0, -1e30)
    contact = dot_nt(in_state, out_state)
    entry = jnp.exp(cum) * meta[:, 3:4]
    weight = jnp.exp(cum[BLOCK - 1 :, :] - cum) * dt * meta[:, 4:5]
    later = carry[...]
    later_low = later.astype(bf16)
    grad_scaled = dot_nt(in_state, later_low)
    weight_wide = spread_all(weight, pairs)
    entry_wide = spread_all(entry, pairs)
    scaled = (values_f * weight_wide).astype(bf16)
    weighted = (gsum_f * entry_wide).astype(bf16)
    half = BLOCK // 2
    g_con = [jnp.zeros((half, BLOCK), f32), jnp.zeros((half, half), f32)]
    g_val = []
    for j in range(pairs):
        for c in range(j * chunks // pairs, (j + 1) * chunks // pairs):
            product(c)
        at = slice(128 * j, 128 * j + 128)
        v = values[:, at]
        gs = gsum[:, at]
        tops = []
        for i, (r0, c0) in enumerate(((0, 0), (half, half))):
            ws = []
            for side in (0, 1):
                h = 2 * j + side
                gw = dot_nt(v[r0 : r0 + half] * half_ref[side : side + 1, :], gs[c0:])
                e = jnp.exp2(
                    (across[h : h + 1, c0:] - down[r0 : r0 + half, h : h + 1])
                    + bias[r0 : r0 + half, c0:]
                )
                ws.append((contact[r0 : r0 + half, c0:] * e).astype(bf16))
                g_con[i] = g_con[i] + gw * e
            gg = jnp.concatenate([gs[c0:] * half_ref[0:1, :], gs[c0:] * half_ref[1:2, :]], 0)
            tops.append(dot_nn(jnp.concatenate(ws, 1), gg))
        g_val.append(jnp.concatenate(tops, 0))
    g_val = jnp.concatenate(g_val, 1) + grad_scaled * weight_wide
    con_low = jnp.concatenate(
        [g_con[0], jnp.concatenate([jnp.zeros((half, half), f32), g_con[1]], 1)], 0
    ).astype(bf16)
    g_in = dot_nn(con_low, out_state) + dot_nn(scaled, later_low)
    g_out = dot_tn(con_low, in_state) + dot_nn(weighted, state_ref[0, 0])
    select = select_ref[...]
    spent = per_head(values_f * g_val, select)
    gained = per_head(gsum_f * ssm, select)
    ends = later * next_ref[0, 0].astype(f32)
    parts = [jnp.sum(ends[64 * h : 64 * h + 64], 0, keepdims=True) for h in range(hn)]
    parts.append(jnp.zeros((128 - hn, 128), f32))
    last = jnp.sum(jnp.concatenate(parts, 0).T, 0, keepdims=True)
    where_last = lax.broadcasted_iota(jnp.int32, (BLOCK, 128), 0) == BLOCK - 1
    grad_cum = gained - spent + jnp.where(where_last, last, 0.0)
    grad_log = dot_exact((col >= row).astype(f32).astype(bf16), grad_cum)
    sig = sigmoid(arg)
    g_step = (
        spent * (sig / jnp.maximum(dt, 1e-37)) + head_ref[1:2, :] * grad_log * sig
    ).astype(bf16)
    passing = entry[BLOCK - 1 :, :]
    direct = dot_tn(weighted, out_state)
    for h in range(hn):
        at = slice(64 * h, 64 * h + 64)
        carry[at, :] = passing[:, h : h + 1] * later[at] + direct[at]

    pre = pre_ref[0]
    sp = sigmoid(pre)
    grad_out = jnp.concatenate([skip * grad_mixed + g_val, g_in, g_out], 1)
    grad_pre = grad_out * (sp + pre * sp * (1.0 - sp))
    buf[:BLOCK, :] = grad_pre
    total = conv_ref[3:4, :] * grad_pre
    for k in (1, 2, 3):
        total = total + conv_ref[3 - k : 4 - k, :] * (buf[k : k + BLOCK, :] * meta[:, 5 + k : 6 + k])
    buf[BLOCK:, :] = grad_pre[:8]
    gp_conv = total.astype(bf16)
    rows = rank_ref[0]
    grads_ref[0, :, :hc] = grads_ref[0, :, :hc] + by_rank(dot_tn(rows, gp_gate), rank)
    grads_ref[0, :, hc : hc + cc] = grads_ref[0, :, hc : hc + cc] + by_rank(
        dot_tn(rows, gp_conv), rank
    )
    gri_ref[0] = fold(
        (dot_nn(gp_gate, upg_ref[...]) + dot_nn(gp_conv, upc_ref[...])) * mask_ref[0, 0:1, :], rank
    )

    @pl.when(step > 0)
    def _():
        route(order_ref, blocks - step, part_buf[...], near_ref, pair_ref, far_ref)

    held_gate[...] = gp_gate
    held_conv[...] = gp_conv
    held_step[...] = g_step

    @pl.when(step == blocks - 1)
    def _():
        for c in range(chunks):
            product(c)
        route(order_ref, 0, part_buf[...], near_ref, pair_ref, far_ref)


def pack_weights_kernel(
    ip_ref, sp_ref, idn_ref, iup_ref, odn_ref, oup_ref, op_ref, cw_ref, cb_ref, idx_ref, gg_ref, tail_ref,
    a_ref, o_ref, small_ref,
    turn, misc,
    *, n, hn, hc, inner, planes,
):
    rows = ip_ref.shape[0]
    ranks = idn_ref.shape[0]
    up_rows = iup_ref.shape[1]

    def turned(ref):
        turn[...] = jnp.zeros_like(turn)
        turn[:, : ref.shape[1]] = ref[...].astype(f32)
        return turn[...].T

    down = turned(idn_ref)[:rows].astype(bf16)
    late = turned(oup_ref)[:rows].astype(bf16)
    step = jnp.concatenate([sp_ref[...].astype(f32), jnp.zeros((rows, 128 - n * hn), f32)], 1)
    lane = lax.broadcasted_iota(jnp.int32, (rows, 128), 1)
    chunk = hc // planes
    heads = hn // planes

    b_at = hc + 256 + ranks + 128

    def columns(base, t, to, at0):
        for p in range(0, planes, 2):
            got = []
            for q in (p, p + 1):
                start = base + (q * n + t) * chunk
                low = start // 128 * 128
                v = ip_ref[:, low : low + 256].astype(f32)
                got.append(pltpu.roll(v, 256 - (start - low), 1) if start > low else v)
            second = pltpu.roll(got[1], 64, 1)
            at = at0 + p * chunk
            a_ref[to, at : at + 128] = got[0][:, :128].astype(bf16)
            a_ref[to, at + 128 : at + 256] = jnp.where(
                lane < 64, got[0][:, 128:], second[:, :128]
            ).astype(bf16)
            a_ref[to, at + 256 : at + 384] = second[:, 128:].astype(bf16)

    for t in range(n):
        to = slice(t * rows, (t + 1) * rows)
        columns(inner, t, to, 0)
        a_ref[to, hc : hc + 256] = ip_ref[:, 2 * inner :]
        a_ref[to, hc + 256 : hc + 256 + ranks] = down
        last = tail_ref[...]
        for p in range(planes):
            shift = (p * heads - (p * n + t) * heads) % 128
            mine = pltpu.roll(step, shift, 1) if shift else step
            last = jnp.where((lane >= p * heads) & (lane < (p + 1) * heads), mine, last)
        a_ref[to, hc + 256 + ranks : b_at] = last.astype(bf16)
        columns(0, t, to, b_at)
        a_ref[to, b_at + hc :] = late
    out_rows, width = op_ref.shape
    part = o_ref.shape[1]
    o_ref[:out_rows, :] = op_ref[:, :part]
    o_ref[out_rows:, : width - part] = op_ref[:, part:]
    o_ref[out_rows:, width - part : width - part + ranks] = turned(odn_ref)[:out_rows].astype(bf16)
    o_ref[out_rows:, width - part + ranks :] = jnp.zeros(
        (out_rows, 2 * part - width - ranks), bf16
    )
    keep = -(-up_rows // 16) * 16
    small_ref[:keep, :] = turned(iup_ref)[:keep].astype(bf16)
    misc[...] = jnp.zeros_like(misc)
    misc[0:4, : cw_ref.shape[1]] = cw_ref[...].astype(f32)
    misc[4:5, : cb_ref.shape[1]] = cb_ref[...].astype(f32)
    misc[5:6, : idx_ref.shape[1]] = idx_ref[...].astype(f32)
    misc[6:7, : gg_ref.shape[1]] = gg_ref[...].astype(f32)
    small_ref[keep:, :] = misc[...].astype(bf16)


def unpack_kernel(
    order_ref, own_ref, far_ref, beside_ref,
    up_gate_ref, up_conv_ref, conv_ref, gain_ref, index_ref,
    held, up, conv, gains,
    *, n, planes, up_rows, rows, inner, hc, conv_rows, out_rows,
):
    size = own_ref.shape[0]
    sources = (own_ref, beside_ref.at[0:size], far_ref, beside_ref.at[size : 2 * size])
    for t in range(n):
        for i, source in enumerate(sources):

            @pl.when(order_ref[t] == i)
            def _(t=t, source=source):
                held[t] = source[...]

    conv[...] = jnp.zeros_like(conv)
    gains[...] = jnp.zeros_like(gains)
    keep = -(-up_rows // 16) * 16

    def add(target, v, start):
        low = start // 128 * 128
        v = jnp.concatenate([v, jnp.zeros_like(v)], 1)
        v = pltpu.roll(v, start - low, 1) if start > low else v
        target[:, low : low + 256] = target[:, low : low + 256] + v

    for t in range(n):
        for y in range(2):
            for z in range(planes):
                owner = (2 * z + y) * n + t
                base = (y * planes + z) * rows
                up[up_rows * owner : up_rows * (owner + 1), :] = held[
                    t, base : base + up_rows, :
                ].astype(f32)
                misc = held[t, base + keep : base + keep + 16, :].astype(f32)[:8]
                add(conv, misc, conv_rows * owner)
                add(gains, misc, out_rows * owner)
                index_ref[owner : owner + 1, :] = misc[5:6]
    here = order_ref[0]
    chunk = hc // planes
    for p in range(planes):
        start = pl.multiple_of((p * n + here) * chunk, 8)
        to = slice(p * chunk, (p + 1) * chunk)
        up_gate_ref[to, :] = up[pl.ds(start, chunk), :].astype(bf16)
        up_conv_ref[to, :] = up[pl.ds(inner + start, chunk), :].astype(bf16)
    up_conv_ref[hc:, :] = up[2 * inner :, :].astype(bf16)
    conv_ref[:, hc:] = conv[:, inner : inner + 256]
    lane = lax.broadcasted_iota(jnp.int32, (8, 128), 1)

    def select(source, target, t):
        for p in range(0, planes, 2):
            got = []
            for q in (p, p + 1):
                start = (q * n + t) * chunk
                low = start // 128 * 128
                v = source[:, low : low + 256]
                got.append(pltpu.roll(v, 256 - (start - low), 1) if start > low else v)
            second = pltpu.roll(got[1], 64, 1)
            at = p * chunk
            target[:, at : at + 128] = got[0][:, :128]
            target[:, at + 128 : at + 256] = jnp.where(lane < 64, got[0][:, 128:], second[:, :128])
            target[:, at + 256 : at + 384] = second[:, 128:]

    for t in range(n):

        @pl.when(here == t)
        def _(t=t):
            select(conv, conv_ref, t)
            select(gains, gain_ref, t)


def final_kernel(*refs, held):
    near_ref, pair_ref, far_ref, rows_ref, down_ref, x_ref, og_ref, gain_ref = refs[:8]
    out_ref = refs[8 + held]
    wide = rows_ref[...].T.astype(bf16)
    grad = near_ref[...].astype(f32) + pair_ref[...].astype(f32) + far_ref[0].astype(f32)
    grad = grad + dot_nt(wide, down_ref[...])
    x = x_ref[0].astype(f32)
    inv = lax.rsqrt(jnp.mean(x * x, -1, keepdims=True) + EPS)
    scaled = grad * gain_ref[0:1, :]
    mean = jnp.mean(scaled * x, -1, keepdims=True)
    out_ref[0] = inv * (scaled - x * (inv * inv * mean)) + og_ref[0].astype(f32)


def pack_grads_kernel(
    order_ref, g0, g1, g2, g3, down_ref, out_ref, up, middle, total, *, n, hc, inner, width, widths, starts,
    planes,
):
    chunk = hc // planes
    lane = lax.broadcasted_iota(jnp.int32, (out_ref.shape[1], 128), 1)

    def place(g, source, target, base, t):
        for p in range(planes):
            low = (source + p * chunk) // 128 * 128
            v = g[:, low : low + 256].astype(f32)
            off = source + p * chunk - low
            v = pltpu.roll(v, 256 - off, 1) if off else v
            to = base + (p * n + t) * chunk
            if to % 128 == 0:
                target[:, to : to + chunk] = v[:, :chunk]
            else:
                v = pltpu.roll(v, 64, 1)
                here = slice(to - 64, to + 64)
                target[:, here] = jnp.where(lane < 64, target[:, here], v[:, :128])
                target[:, to + 64 : to + 192] = v[:, 128:]

    for t in range(n):
        for i, g in enumerate((g0, g1, g2, g3)):

            @pl.when(order_ref[t] == i)
            def _(t=t, g=g):
                place(g, 0, up, 0, t)
                place(g, hc, up, inner, t)
                place(g, 2 * hc + 256, middle, 0, t)

    def summed(at):
        first = g0[:, at].astype(f32) + g1[:, at].astype(f32)
        return first + (g2[:, at].astype(f32) + g3[:, at].astype(f32))

    up[:, 2 * inner : 2 * inner + 256] = summed(slice(2 * hc, 2 * hc + 256))
    total[:, :width] = summed(slice(3 * hc + 256, 3 * hc + 256 + width))
    sources = (None, up, middle, total)
    for t in range(n):

        @pl.when(order_ref[0] == t)
        def _(t=t):
            for d in range(out_ref.shape[0]):
                for ref, at, w in zip(sources, starts, widths):
                    start = (d * n + t) * w
                    low = start // 128 * 128
                    span = -(-w // 128) * 128
                    if ref is None:
                        window = down_ref[:, low : low + span + 128].astype(f32)
                    else:
                        window = ref[:, low : low + span + 128]
                    if start > low:
                        window = pltpu.roll(window, span + 128 - (start - low), 1)
                    out_ref[d, :, at : at + span] = window[:, :span].astype(bf16)


def swap(v, axis, bit):
    size = lax.axis_size(axis)
    return lax.ppermute(v, axis, [(i, i ^ bit) for i in range(size)])


def put(pieces):
    rows = pieces[0][0].shape[0]
    out = jnp.zeros((len(pieces) * rows, pieces[0][0].shape[1]), pieces[0][0].dtype)
    for piece, slot in pieces:
        out = lax.dynamic_update_slice_in_dim(out, piece, slot * rows, 0)
    return out


def rotate(v, r):
    size = lax.axis_size("dp")
    return lax.ppermute(v, "dp", [(i, (i + 2 * r) % size) for i in range(size)])


def after(v, *others):
    return lax.optimization_barrier((v, others))[0]


def fence(*values):
    return lax.optimization_barrier(values)


def others(v):
    return [swap(v, "seq", k) for k in (1, 2, 3)]


def total_of(v, got):
    return (v + got[0]) + (got[1] + got[2])


def across(far, pair):
    return (far.astype(f32) + pair[BLOCK:].astype(f32)).astype(bf16)


def own_sum(near, pair, far):
    return near.astype(f32) + pair[:BLOCK].astype(f32) + far.astype(f32)


def scatter_plain(near, pair, far):
    v = jnp.concatenate([near, pair[:BLOCK], far, pair[BLOCK:]], 0).astype(f32)
    return lax.psum_scatter(v, "seq", scatter_dimension=0, tiled=True)


def per_device(
    layer_input,
    document_index,
    adapter_index,
    input_norm_gain,
    input_projection,
    step_projection,
    convolution_weight,
    convolution_bias,
    head_step_bias,
    log_decay_rate,
    head_skip_gain,
    gated_norm_gain,
    output_projection,
    adapter_input_down,
    adapter_input_up,
    adapter_output_down,
    adapter_output_up,
    output_gradient,
):
    both = ("dp", "seq")
    dps, n = lax.axis_size("dp"), lax.axis_size("seq")
    here = lax.axis_index("seq")
    seqs, own_len, width = layer_input.shape
    adapters, rank, _ = adapter_input_down.shape
    ranks = adapters * rank
    heads = head_step_bias.shape[0]
    inner = output_projection.shape[0] * dps * n
    cols = input_projection.shape[1]
    state2 = cols - 2 * inner
    state = state2 // 2
    taps = convolution_weight.shape[1]
    hn = heads // n
    hc = inner // n
    hd = inner // heads
    length = own_len * n
    nb = length // BLOCK

    staged = n == 4 and dps == 8
    rows = input_projection.shape[0]
    conv_cols = hc + state2
    wa_cols = conv_cols + ranks + 128
    doc_cols = -(-seqs * own_len // rows)
    doc_block = document_index.astype(bf16).reshape(-1)
    doc_block = jnp.pad(doc_block, (0, rows * doc_cols - doc_block.shape[0])).reshape(rows, -1)
    tail = jnp.concatenate([doc_block, input_norm_gain[:, None]], 1)
    up_rows = adapter_input_up.shape[2]
    up_keep = -(-up_rows // 16) * 16
    conv_rows = convolution_weight.shape[0]
    wide = -(-conv_rows // 128) * 128
    misc_rows = 16
    small_rows = up_keep + misc_rows * wide // 128
    out_rows = output_projection.shape[0]
    planes = dps // 2 if staged else 1
    if staged:
        to_head = [
            (8 * z + 2 * t + y, 8 * z + 4 * y + t)
            for z in range(planes) for y in range(2) for t in range(n)
        ]
    else:
        to_head = [(dps * s + d, n * d + s) for d in range(dps) for s in range(n)]
    tables = [
        v.reshape(ranks, -1)
        for v in (adapter_input_down, adapter_input_up, adapter_output_down, adapter_output_up)
    ]
    if staged:
        tail = jnp.pad(tail.astype(f32), ((0, 0), (127 - doc_cols, 0)))
        payload, w_o, small = pl.pallas_call(
            functools.partial(
                pack_weights_kernel, n=n, hn=hn, hc=hc, inner=inner, planes=planes
            ),
            out_shape=[
                jax.ShapeDtypeStruct((n * rows, wa_cols + hc + ranks), bf16),
                jax.ShapeDtypeStruct((2 * out_rows, hc + ranks), bf16),
                jax.ShapeDtypeStruct((small_rows, 128), bf16),
            ],
            scratch_shapes=[pltpu.VMEM((128, 256), f32), pltpu.VMEM((misc_rows, 128), f32)],
            name="pack_weights",
        )(
            input_projection, step_projection, *tables[:2], *tables[2:], output_projection,
            convolution_weight.T, convolution_bias[None], adapter_index[None], gated_norm_gain[None], tail,
        )
    else:
        gap = jnp.zeros((rows, 127 - hn - doc_cols), bf16)
        payload = jnp.concatenate(
            [
                jnp.concatenate(
                    [
                        input_projection[:, inner + t * hc : inner + (t + 1) * hc],
                        input_projection[:, 2 * inner :],
                        tables[0].T,
                        step_projection[:, t * hn : (t + 1) * hn],
                        gap,
                        tail,
                    ],
                    1,
                )
                for t in range(n)
            ],
            0,
        )
        late_payload = jnp.concatenate(
            [
                jnp.concatenate([input_projection[:, t * hc : (t + 1) * hc], tables[3].T], 1)
                for t in range(n)
            ],
            0,
        )
        w_o = jnp.concatenate([output_projection, tables[2].T], 1)

        def as_row(v):
            return jnp.pad(v, ((0, 0), (0, wide - v.shape[1])))

        misc = jnp.concatenate(
            [
                as_row(convolution_weight.T),
                as_row(convolution_bias[None]),
                as_row(adapter_index.astype(bf16)[None]),
                as_row(gated_norm_gain[None]),
            ],
            0,
        )
        misc = jnp.pad(misc, ((0, misc_rows - misc.shape[0]), (0, 0)))
        small = jnp.concatenate(
            [jnp.pad(tables[1].T, ((0, up_keep - up_rows), (0, 0))), misc.reshape(-1, 128)], 0
        )
    w_a = lax.all_to_all(payload, "seq", 0, 0, tiled=True)

    if staged:
        d = lax.axis_index("dp")
        y, z = d % 2, d // 2
        w_o = lax.ppermute(w_o, both, to_head)
        turned = [rotate(small, r) for r in (1, 2, 3)]
        w_a, small, turned, w_o = fence(w_a, small, turned, w_o)
        w_a, w_b = w_a[:, :wa_cols], w_a[:, wa_cols:]
        small = put([(small, z)] + [(v, lax.rem(z + 3 - r, 4)) for r, v in enumerate(turned)])
        a1, a3, a0y = rotate(w_a, 1), rotate(w_a, 3), swap(w_a, "dp", 1)
        small_y = swap(small, "dp", 1)
        x0 = after(layer_input, w_a)[:1]
        x_far0 = swap(x0, "seq", 2)
        x1, og = after(layer_input, w_a)[1:], after(output_gradient, w_a)
        og0, og1 = og[:1], og[1:]
        at = [2 * lax.rem(z + 4 - r, 4) + y for r in range(4)]
        slots = [at[0], at[0] ^ 1, at[1], at[3], at[1] ^ 1, at[3] ^ 1, at[2], at[2] ^ 1]
        slots = jnp.stack(slots).astype(jnp.int32)
        x_order = jnp.arange(4, dtype=jnp.int32) ^ here
    else:
        w_b = lax.all_to_all(late_payload, "seq", 0, 0, tiled=True)
        w_o = lax.ppermute(w_o, both, to_head)
        small = lax.all_gather(lax.all_gather(small, "dp", tiled=True), "seq", tiled=True)
        small = jnp.moveaxis(small.reshape(n, dps, small_rows, 128), 0, 1)
        wa_pieces = [lax.all_gather(w_a, "dp", tiled=True)]
        slots = jnp.zeros((1,), jnp.int32)
        x_order = jnp.arange(nb, dtype=jnp.int32)
        xs = [jnp.split(lax.all_gather(layer_input, "seq", axis=1, tiled=True), nb, axis=1)] * seqs
    docs = w_a[:, wa_cols - 1 - doc_cols : wa_cols - 1].reshape(n, -1)[:, : seqs * own_len]
    docs = jnp.moveaxis(docs.reshape(n, seqs, own_len), 0, 1).reshape(seqs, length)
    order = jnp.concatenate([x_order, slots])
    order_whole = jnp.concatenate([x_order, jnp.zeros((1,), jnp.int32)])

    def mine(v):
        v = v.reshape(planes, n, v.shape[0] // (planes * n), *v.shape[1:])
        v = lax.dynamic_index_in_dim(v, here, 1, keepdims=False)
        return v.reshape(-1, *v.shape[2:])

    if not staged:
        small = small.reshape(dps * n, small_rows, 128)
        up_full = small[:, :up_rows].reshape(cols, ranks)
        misc = small[:, up_keep:].reshape(dps * n, misc_rows, wide)
        conv_w = jnp.moveaxis(misc[:, :taps, :conv_rows], 1, 0).reshape(taps, -1).astype(f32)
        conv_b = misc[:, taps, :conv_rows].reshape(-1).astype(f32)
        every_index = misc[:, taps + 1, :seqs].reshape(dps, n, seqs)[:, 0].astype(jnp.int32)
        gate_gain = misc[:, taps + 2, :out_rows].reshape(-1).astype(f32)

        up_gate = mine(up_full[:inner])
        up_conv = jnp.concatenate([mine(up_full[inner : 2 * inner]), up_full[2 * inner :]], 0)
        conv_w = jnp.concatenate([mine(conv_w.T[:inner]), conv_w.T[inner:]], 0).T
        conv_b = jnp.concatenate([mine(conv_b[:inner]), conv_b[inner:]], 0)
    step_bias = mine(head_step_bias)
    decay_rate = -jnp.exp(mine(log_decay_rate))
    skip = mine(head_skip_gain)
    gate_gain = None if staged else mine(gate_gain)

    chosen = (adapter_index[:, None] == jnp.arange(adapters, dtype=jnp.int32)[None, :]).astype(f32)
    mask = jnp.repeat(chosen, rank, axis=1)[:, None, :]

    doc_f = docs.astype(f32)

    def same_before(k):
        return jnp.pad(doc_f, ((0, 0), (k, 0)), constant_values=-1.0)[:, :length] == doc_f

    def same_after(k):
        return jnp.pad(doc_f, ((0, 0), (0, k)), constant_values=-1.0)[:, k:] == doc_f

    blocks = doc_f.reshape(seqs, nb, BLOCK)
    prior = jnp.concatenate([blocks[:, :1, 0], blocks[:, :-1, -1]], 1)
    keep = (blocks == prior[:, :, None]).reshape(seqs, length)
    ends = (blocks == blocks[:, :, -1:]).reshape(seqs, length)
    flags = [
        same_before(1), same_before(2), same_before(3), keep, ends, doc_f,
        same_after(1), same_after(2), same_after(3),
    ]
    meta = jnp.stack([v.astype(f32) for v in flags], -1)
    meta = jnp.pad(meta, ((0, 0), (0, 0), (0, 128 - len(flags))))
    doc_rows = blocks[:, :, None, :]

    def rows8(*vs):
        return jnp.pad(jnp.stack(vs), ((0, 8 - len(vs)), (0, 0)))

    if not staged:
        conv_rows8 = rows8(conv_w[0], conv_w[1], conv_w[2], conv_w[3], conv_b)
        wide_rows = rows8(jnp.repeat(skip, hd), gate_gain)
    head_rows = rows8(
        jnp.pad(step_bias, (0, 128 - hn)), jnp.pad(decay_rate, (0, 128 - hn))
    )
    halves = jnp.pad(
        (jnp.arange(128)[None, :] // 64 == jnp.arange(2)[:, None]).astype(bf16), ((0, 14), (0, 0))
    )
    select = (jnp.arange(hc)[:, None] // hd == jnp.arange(128)[None, :]).astype(bf16)
    mask8 = jnp.broadcast_to(mask, (seqs, 8, ranks))
    cc = conv_cols
    anywhere = pl.BlockSpec(memory_space=pl.ANY)
    params = pltpu.CompilerParams(
        dimension_semantics=("arbitrary",), vmem_limit_bytes=VMEM_BYTES
    )

    def at(w, k=0):
        return pl.BlockSpec((1, BLOCK, w), lambda b, o: (k, b, 0))

    def once(v, *block):
        block = block or v.shape
        return pl.BlockSpec(block, lambda b, o: (0,) * len(block), pipeline_mode=pl.Buffered(1))

    def of_seq(v, s0):
        k = s0 if v.shape[0] > 1 else 0
        return pl.BlockSpec(
            (1,) + v.shape[1:], lambda b, o: (k, 0, 0), pipeline_mode=pl.Buffered(1)
        )

    def one(w, dtype):
        return jax.ShapeDtypeStruct((1, length, w), dtype)

    def cost(flops, mib):
        return pl.CostEstimate(flops=int(flops), bytes_accessed=mib << 20, transcendentals=0)

    def parts_specs():
        return [once(None, BLOCK, width), once(None, 2 * BLOCK, width), once(None, BLOCK, width)]

    parts_shapes = [
        jax.ShapeDtypeStruct((k * BLOCK, width), bf16) for k in (1, 2, 1)
    ]

    def forward(s0, order, blocks, pieces, keep):
        whole_w = jax.ShapeDtypeStruct((width, wa_cols), bf16)
        size = n * rows if len(pieces) > 1 else width
        total = sum(v.shape[0] for v in pieces) // size
        return pl.pallas_call(
            functools.partial(
                forward_kernel, hn=hn, hc=hc, count=len(pieces), size=size, s0=s0, keep=keep
            ),
            grid_spec=pltpu.PrefetchScalarGridSpec(
                num_scalar_prefetch=1,
                grid=(nb,),
                in_specs=[
                    *([anywhere] * len(blocks)), at(128, s0),
                    pl.BlockSpec((1, 1, 1, BLOCK), lambda b, o: (s0, b, 0, 0)),
                    once(up_conv), once(conv_rows8), once(head_rows), of_seq(mask8, s0), once(halves),
                    *([anywhere] * len(pieces)),
                ],
                out_specs=[
                    at(width), at(128), at(cc), at(cc), at(hc),
                    pl.BlockSpec((1, 1, hc, state), lambda b, o: (0, b, 0, 0)), at(384),
                    *([anywhere] if keep else []),
                ],
                scratch_shapes=[
                    pltpu.VMEM((BLOCK + 8, cc), f32), pltpu.VMEM((hc, state), f32),
                    pltpu.VMEM((2, BLOCK, width), bf16), pltpu.VMEM((width, wa_cols), bf16),
                    pltpu.VMEM((8, width), f32), pltpu.VMEM((2, BLOCK, wa_cols), f32),
                    pltpu.VMEM((2, BLOCK, width), bf16), pltpu.SemaphoreType.DMA((total,)),
                    pltpu.SemaphoreType.DMA, pltpu.SemaphoreType.DMA((2,)),
                ],
            ),
            out_shape=[
                one(width, bf16), one(128, bf16), one(cc, bf16), one(cc, f32), one(hc, f32),
                jax.ShapeDtypeStruct((1, nb, hc, state), bf16), one(384, f32),
                *([whole_w] if keep else []),
            ],
            compiler_params=params,
            name="ssm_forward",
            cost_estimate=cost(2 * length * (width * wa_cols + 3 * BLOCK * hc), 20),
        )(order, *blocks, meta, doc_rows, up_conv, conv_rows8, head_rows, mask8, halves, *pieces)

    def middle(s0, order, scanned, blocks, gate_pieces, out_pieces, keep):
        normed, rank_in, vbc, _, ssm = scanned[:5]
        count = len(gate_pieces)
        merged = () if out_pieces else (n * rows, out_rows)
        wb_shape, wo_shape = (width, hc + ranks), (hc, width + ranks)
        return pl.pallas_call(
            functools.partial(
                middle_kernel, hc=hc, width=width, rank=rank, count=count, keep=keep,
                merged=merged, s0=s0,
            ),
            grid_spec=pltpu.PrefetchScalarGridSpec(
                num_scalar_prefetch=1,
                grid=(nb,),
                in_specs=[
                    at(width), at(128), at(cc), at(hc), *([anywhere] * len(blocks)),
                    once(up_gate), once(wide_rows), of_seq(mask8, s0), *([anywhere] * (count + len(out_pieces))),
                ],
                out_specs=[
                    at(hc), at(hc), at(128), *parts_specs(),
                    pl.BlockSpec((1, 8 + rank, BLOCK), lambda b, o: (0, 0, b)),
                    *([anywhere] * 2 if keep else []),
                ],
                scratch_shapes=[
                    pltpu.VMEM((2, BLOCK, width), bf16), pltpu.VMEM(wb_shape, bf16),
                    pltpu.VMEM(wo_shape, bf16), pltpu.SemaphoreType.DMA((3 * dps,)),
                    pltpu.SemaphoreType.DMA((count,)), pltpu.SemaphoreType.DMA((2,)),
                    pltpu.SemaphoreType.DMA((2,)),
                ],
            ),
            out_shape=[
                one(hc, f32), one(hc, f32), one(128, bf16), *parts_shapes,
                jax.ShapeDtypeStruct((1, 8 + rank, length), f32),
                *([jax.ShapeDtypeStruct(v, bf16) for v in (wb_shape, wo_shape)] if keep else []),
            ],
            compiler_params=params,
            name="output_side",
            cost_estimate=cost(2 * length * width * hc * 3, 25),
        )(
            order, normed, rank_in, vbc, ssm, *blocks, up_gate, wide_rows, mask8, *gate_pieces,
            *out_pieces,
        )

    def backward(s0, scanned, gate, q, rm, grad_rank_out):
        _, rank_in, vbc, pre, ssm, states_low, tok = scanned[:7]

        def back(w, k=0):
            return pl.BlockSpec((1, BLOCK, w), lambda b, o: (k, nb - 1 - b, 0))

        def back_state(shift):
            return pl.BlockSpec(
                (1, 1, hc, state), lambda b, o: (0, jnp.minimum(nb - 1 - b + shift, nb - 1), 0, 0)
            )

        return pl.pallas_call(
            functools.partial(backward_kernel, hn=hn, hc=hc, rank=rank),
            grid_spec=pltpu.PrefetchScalarGridSpec(
                num_scalar_prefetch=1,
                grid=(nb,),
                in_specs=[
                    back(hc), back(hc), back(hc), back(cc), back(cc), back(384),
                    pl.BlockSpec((1, 8, BLOCK), lambda b, o: (0, 0, nb - 1 - b)), back(128, s0),
                    pl.BlockSpec((1, 1, 1, BLOCK), lambda b, o: (s0, nb - 1 - b, 0, 0)),
                    back_state(0), back_state(1), back(128), back(128), once(conv_rows8),
                    once(head_rows), once(wide_rows), once(halves), once(select), once(up_gate),
                    once(up_conv), of_seq(mask8, s0), once(wa), once(wb),
                ],
                out_specs=[
                    *parts_specs(), once(None, 1, rank, 2 * hc + cc),
                    pl.BlockSpec((1, rank, BLOCK), lambda b, o: (0, 0, nb - 1 - b)),
                ],
                scratch_shapes=[
                    pltpu.VMEM((BLOCK + 8, cc), f32), pltpu.VMEM((hc, state), f32),
                    pltpu.VMEM((BLOCK, hc), bf16), pltpu.VMEM((BLOCK, cc), bf16),
                    pltpu.VMEM((BLOCK, 128), bf16), pltpu.VMEM((BLOCK, width), bf16),
                ],
            ),
            out_shape=[
                *parts_shapes, jax.ShapeDtypeStruct((1, rank, 2 * hc + cc), f32),
                jax.ShapeDtypeStruct((1, rank, length), f32),
            ],
            compiler_params=params,
            name="ssm_backward",
            cost_estimate=cost(2 * length * (8 * BLOCK * hc + width * (hc + cc)), 30),
        )(
            x_order, q, gate, ssm, vbc, pre, tok, rm, meta, doc_rows, states_low, states_low, rank_in,
            grad_rank_out, conv_rows8, head_rows, wide_rows, halves, select, up_gate, up_conv, mask8,
            wa, wb,
        )

    def own_tokens(v, axis):
        return lax.dynamic_slice_in_dim(v, here * own_len, own_len, axis)

    def with_adapter(rows_of, table, s0):
        wide_rows_of = jnp.tile(rows_of, (adapters, 1)) * mask[s0, 0][:, None].astype(bf16)
        return mm("rt,dr->td", wide_rows_of, table)

    if staged:
        ready = (head_rows, meta, doc_rows, mask8, halves, select, order, order_whole, x1, og0, og1)
        a1, a3, a0y, w_a, small, small_y, x_far0, w_b, w_o, ready = fence(
            a1, a3, a0y, w_a, small, small_y, x_far0, w_b, w_o, ready
        )
        head_rows, meta, doc_rows, mask8, halves, select, order, order_whole, x1, og0, og1 = ready
        a13y = swap(jnp.concatenate([a1, a3]), "dp", 1)
        a2 = rotate(w_a, 2)
        small = put([(small, y), (small_y, 1 - y)])
        small_far = swap(small, "seq", 2)
        x_both0 = swap(x_far0, "seq", 1)
        x_near = swap(after(layer_input, w_a), "seq", 1)
        w_bo = jnp.concatenate([w_b, w_o])
        a2, a13y, small, small_far, x_both0, x_near, w_bo, x1 = fence(
            a2, a13y, small, small_far, x_both0, x_near, w_bo, x1
        )
        a2y = swap(a2, "dp", 1)
        beside = swap(jnp.concatenate([small, small_far]), "seq", 1)
        b1, b3 = rotate(w_bo, 1), rotate(w_bo, 3)
        x_far1 = swap(x1, "seq", 2)
        up_gate, up_conv, conv_rows8, gains, index_rows = pl.pallas_call(
            functools.partial(
                unpack_kernel, n=n, planes=planes, up_rows=up_rows, rows=small_rows, inner=inner,
                hc=hc, conv_rows=conv_rows, out_rows=out_rows,
            ),
            in_specs=[
                pl.BlockSpec(memory_space=pltpu.SMEM),
                *[pl.BlockSpec(memory_space=pltpu.VMEM)] * 3,
            ],
            out_specs=[pl.BlockSpec(memory_space=pltpu.VMEM)] * 5,
            out_shape=[
                jax.ShapeDtypeStruct((hc, ranks), bf16), jax.ShapeDtypeStruct((cc, ranks), bf16),
                jax.ShapeDtypeStruct((8, cc), f32), jax.ShapeDtypeStruct((8, hc), f32),
                jax.ShapeDtypeStruct((dps * n, 128), f32),
            ],
            scratch_shapes=[
                pltpu.VMEM((n, *small.shape), bf16), pltpu.VMEM((cols, ranks), f32),
                pltpu.VMEM((8, inner + state2 + 256), f32), pltpu.VMEM((8, inner + 256), f32),
            ],
            compiler_params=pltpu.CompilerParams(vmem_limit_bytes=VMEM_BYTES),
            name="unpack_small",
        )(x_order, small, small_far, beside)
        every_index = index_rows.reshape(dps, n, 128)[:, 0, :seqs].astype(jnp.int32)
        wide_rows = rows8(jnp.repeat(skip, hd), gains[6])
        wa_pieces = [w_a, a0y, a1, a3, a13y, a2, a2y]
        xs = [[layer_input, x_near, x_far0, x_both0]]
        wa_pieces, xs[0], w_bo, up_conv, up_gate, conv_rows8 = fence(
            wa_pieces, xs[0], w_bo, up_conv, up_gate, conv_rows8
        )
        *fwd0, wa = forward(0, order, xs[0], wa_pieces, True)
        b0y, b2 = swap(w_bo, "dp", 1), rotate(w_bo, 2)
        fwd0, wa, b1, b3, b0y, w_bo, x_far1 = fence(fwd0, wa, b1, b3, b0y, w_bo, x_far1)
        x_both1 = swap(x_far1, "seq", 1)
        x_both1, w_bo, og0, og1, og = fence(x_both1, w_bo, og0, og1, output_gradient)
        fwd1 = forward(1, order_whole, [layer_input, x_near, x_far1, x_both1], [wa], False)
        b1y, b3y = swap(b1, "dp", 1), swap(b3, "dp", 1)
        og_far0 = swap(og0, "seq", 2)
        og_near = swap(og, "seq", 1)
        fwd1, b1y, b3y, b2, og_far0, og_near, w_bo, og1 = fence(
            fwd1, b1y, b3y, b2, og_far0, og_near, w_bo, og1
        )
        b2y = swap(b2, "dp", 1)
        og_both0 = swap(og_far0, "seq", 1)
        fwd = [fwd0, fwd1]
        wb_pieces = [w_bo, b0y, b1, b3, b1y, b3y, b2, b2y]
        wo_pieces = []
        ogs = [[output_gradient, og_near, og_far0, og_both0]]
        wb_pieces, ogs[0], og1 = fence(wb_pieces, ogs[0], og1)
    else:
        fwd = [forward(0, order, xs[0], wa_pieces, True)]
        wa = fwd[0][-1]
        fwd += [forward(s0, order_whole, xs[s0], [wa], False) for s0 in range(1, seqs)]
        wb_pieces = [lax.all_gather(w_b, "dp", tiled=True)]
        wo_pieces = [lax.all_gather(w_o, "dp", tiled=True)]
        full = lax.all_gather(output_gradient, "seq", axis=1, tiled=True)
        ogs = [jnp.split(full, nb, axis=1)] * seqs
    gain = wa[:, -1].astype(f32)
    gain_rows = jnp.broadcast_to(gain[None], (8, width))

    def normalisers(stats):
        inv_gated = lax.rsqrt(stats[:1] / inner + EPS)
        rm = jnp.pad(jnp.concatenate([inv_gated, stats[1:2] / inner], 0), ((0, 6), (0, 0)))[None]
        return inv_gated, rm, own_tokens((stats[8:] * inv_gated).astype(bf16), 1)

    def layer_output(s0, branch, inv_gated, rank_out):
        return (
            layer_input[s0].astype(f32)
            + branch * own_tokens(inv_gated, 1).T
            + with_adapter(rank_out, up_out, s0)
        ).astype(bf16)

    def down_gradient(s0, grad_rank_in):
        return mm("rt,td->rd", grad_rank_in, fwd[s0][0][0]).astype(bf16)

    def layer_gradient(s0, partial, grad_rank_in):
        grad_normed = partial + with_adapter(
            own_tokens(grad_rank_in, 1), down_in, s0
        )
        own = layer_input[s0].astype(f32)
        inv_own = lax.rsqrt(jnp.mean(own * own, -1, keepdims=True) + EPS)
        scaled_in = grad_normed * gain
        return (
            inv_own * scaled_in
            - own * inv_own**3 * jnp.mean(scaled_in * own, -1, keepdims=True)
            + output_gradient[s0].astype(f32)
        )

    def final_gradient(s0, near, pair, far, grad_rank_in, earlier):
        rows_of = jnp.tile(own_tokens(grad_rank_in, 1).astype(f32), (adapters, 1)) * mask[s0, 0][:, None]

        tile_rows = 128
        mine_of_seq = pl.BlockSpec((1, tile_rows, width), lambda i: (s0, i, 0))
        by_rows = pl.BlockSpec((tile_rows, width), lambda i: (i, 0))

        def full(*block):
            return pl.BlockSpec(block, lambda i: (0,) * len(block))

        ins = [near, pair, far[None], rows_of, down_in, layer_input, output_gradient, gain_rows]
        specs = [
            by_rows, by_rows, pl.BlockSpec((1, tile_rows, width), lambda i: (0, i, 0)),
            pl.BlockSpec((ranks, tile_rows), lambda i: (0, i)), full(width, ranks), mine_of_seq,
            mine_of_seq, full(8, width),
        ]
        if earlier is not None:
            ins.append(earlier)
            specs.append(anywhere)
        return pl.pallas_call(
            functools.partial(final_kernel, held=len(ins) - 8),
            grid=(own_len // tile_rows,),
            in_specs=specs,
            out_specs=mine_of_seq,
            out_shape=jax.ShapeDtypeStruct((seqs, own_len, width), f32),
            input_output_aliases={8: 0} if earlier is not None else {},
            compiler_params=params,
            name="final_gradient",
            cost_estimate=cost(2 * BLOCK * width * ranks, 5),
        )(*ins)

    *side0, wb, wo = middle(0, order, fwd[0], ogs[0], wb_pieces, wo_pieces, True)
    up_out = wb[:, hc:]
    down_in = wa[:, cc : cc + ranks]
    if staged:
        og_far1 = swap(og1, "seq", 2)
        side0, wb, wo, og_far1 = fence(side0, wb, wo, og_far1)
        ogs.append([output_gradient, og_near, og_far1, swap(og_far1, "seq", 1)])
        ogs[1], side0, wb, wo, up_out, down_in, gain_rows = fence(
            ogs[1], side0, wb, wo, up_out, down_in, gain_rows
        )
        gate0, q0, gro0, near0, pair0, far0, stats0 = side0
        side1 = middle(1, order_whole, fwd[1], ogs[1], [wb], [wo], False)
        got = others(stats0[0])
        pair0 = swap(pair0, "seq", 1)
        side1, got, pair0, far0 = fence(side1, got, pair0, far0)
        gate1, q1, gro1, near1, pair1, far1, stats1 = side1
        inv0, rm0, rank_out0 = normalisers(total_of(stats0[0], got))
        rm0, away, stats1, pair1 = fence(rm0, across(far0, pair0), stats1, pair1)

        back0 = backward(0, fwd[0], gate0, q0, rm0, gro0)
        away = swap(away, "seq", 2)
        got = others(stats1[0])
        pair1 = swap(pair1, "seq", 1)
        back0, away, got, pair1, far1 = fence(back0, away, got, pair1, far1)
        near_g0, pair_g0, far_g0, compact0, gri0 = back0
        pair_g0 = swap(pair_g0, "seq", 1)
        away0 = away
        inv1, rm1, rank_out1 = normalisers(total_of(stats1[0], got))
        rm1, away, gri0, away_g, away0, rank_out0, rank_out1 = fence(
            rm1, across(far1, pair1), gri0, across(far_g0, pair_g0), away0, rank_out0, rank_out1
        )

        back1 = backward(1, fwd[1], gate1, q1, rm1, gro1)
        away = swap(away, "seq", 2)
        away_g = swap(away_g, "seq", 2)
        got = others(gri0[0])
        back1, away, away_g, got, away0, rank_out0, rank_out1, near0, pair0, inv0 = fence(
            back1, away, away_g, got, away0, rank_out0, rank_out1, near0, pair0, inv0
        )
        near_g1, pair_g1, far_g1, compact1, gri1 = back1
        pair_g1 = swap(pair_g1, "seq", 1)
        got1 = others(gri1[0])
        g_out_up = mm("srt,std->srd", jnp.stack([rank_out0, rank_out1]), output_gradient)
        split = jnp.concatenate(
            [
                jnp.concatenate([compact0[0], compact1[0]]).astype(bf16),
                g_out_up.astype(bf16).reshape(seqs * rank, width),
            ],
            1,
        )
        away_g1, split, got1, got, gri0, near0, pair0, near1, pair1, near_g0, pair_g0, down_in = fence(
            across(far_g1, pair_g1), split, got1, got, gri0, near0, pair0, near1, pair1, near_g0,
            pair_g0, down_in,
        )
        away_g1 = swap(away_g1, "seq", 2)
        split_far = swap(split, "seq", 2)
        split_near = swap(split, "seq", 1)
        split_both = swap(split_far, "seq", 1)
        gri0 = total_of(gri0[0], got).astype(bf16)
        gri1 = total_of(gri1[0], got1).astype(bf16)
        downs = jnp.concatenate([down_gradient(0, gri0), down_gradient(1, gri1)])
        grad0 = final_gradient(0, near_g0, pair_g0, away_g, gri0, None)
        output0 = layer_output(0, own_sum(near0, pair0, away0), inv0, rank_out0)
        output1 = layer_output(1, own_sum(near1, pair1, away), inv1, rank_out1)
        grads_of_seq = [split, split_near, split_far, split_both]
        grads_order = x_order
    else:
        splits, downs, ranks_out, outputs, grads_in = [], [], [], [], []
        for s0 in range(seqs):
            if s0:
                side0 = middle(s0, order_whole, fwd[s0], ogs[s0], [wb], [wo], False)
            gate, q, gro, *parts, stats = side0
            inv_gated, rm, rank_out = normalisers(lax.psum(stats[0], "seq"))
            outputs.append(layer_output(s0, scatter_plain(*parts), inv_gated, rank_out))
            *parts, compacted, gri = backward(s0, fwd[s0], gate, q, rm, gro)
            gri = lax.psum(gri[0], "seq").astype(bf16)
            splits.append(compacted[0].astype(bf16))
            downs.append(down_gradient(s0, gri))
            ranks_out.append(rank_out)
            grads_in.append(layer_gradient(s0, scatter_plain(*parts), gri))
        g_out_up = mm("srt,std->srd", jnp.stack(ranks_out), output_gradient).astype(bf16)
        output = jnp.stack(outputs)
        grad_in = jnp.stack(grads_in)
        downs = jnp.concatenate(downs)
        split = jnp.concatenate(
            [jnp.concatenate(splits), g_out_up.reshape(seqs * rank, width)], 1
        )
        grads_of_seq = jnp.split(lax.all_gather(split, "seq", axis=0, tiled=True), n)

    widths = [v // (dps * n) for v in (width, cols, inner, width)]
    starts, lanes = [], 0
    for v in widths:
        starts.append(lanes)
        lanes += -(-v // 128) * 128
    pack_rows = seqs * rank
    if staged:
        packed = pl.pallas_call(
            functools.partial(
                pack_grads_kernel, n=n, hc=hc, inner=inner, width=width, widths=widths,
                starts=starts, planes=planes,
            ),
            in_specs=[
                pl.BlockSpec(memory_space=pltpu.SMEM),
                *[pl.BlockSpec(memory_space=pltpu.VMEM)] * 5,
            ],
            out_specs=pl.BlockSpec(memory_space=pltpu.VMEM),
            out_shape=jax.ShapeDtypeStruct((dps, pack_rows, lanes), bf16),
            scratch_shapes=[
                pltpu.VMEM((pack_rows, cols + 256), f32), pltpu.VMEM((pack_rows, inner + 256), f32),
                pltpu.VMEM((pack_rows, width + 256), f32),
            ],
            name="pack_grads",
        )(
            grads_order,
            *grads_of_seq, jnp.pad(downs, ((0, 0), (0, 256))),
        )
    else:
        pieces = jnp.stack(grads_of_seq)

        def by_heads(start):
            return jnp.concatenate([pieces[t, :, start : start + hc] for t in range(n)], -1)

        def summed(start, size):
            return pieces[..., start : start + size].astype(f32).sum(0).astype(bf16)

        full = [
            downs,
            jnp.concatenate([by_heads(0), by_heads(hc), summed(2 * hc, state2)], -1),
            by_heads(2 * hc + state2),
            summed(3 * hc + state2, width),
        ]
        packed = jnp.zeros((dps, pack_rows, lanes), bf16)
        for v, start, w in zip(full, starts, widths):
            v = lax.dynamic_index_in_dim(
                v.reshape(pack_rows, dps, n, w), here, 2, keepdims=False
            )
            packed = packed.at[:, :, start : start + w].set(v.transpose(1, 0, 2))
    got = lax.all_to_all(packed, "dp", 0, 0, tiled=True)
    if staged:
        output = jnp.stack([output0, output1])
    all_chosen = (every_index[..., None] == jnp.arange(adapters)).astype(bf16)
    table = mm("dsk,dsrc->krc", all_chosen, got.reshape(dps, seqs, rank, lanes))
    grads = [table[..., start : start + w] for start, w in zip(starts, widths)]
    if staged:
        grad0, output, away_g1, near_g1, pair_g1 = fence(grad0, output, away_g1, near_g1, pair_g1)
        grad_in = final_gradient(1, near_g1, pair_g1, away_g1, gri1, grad0)
    return (output, grad_in, grads[0], grads[1], grads[2], grads[3])


def solution(mesh):
    return jax.shard_map(
        per_device,
        mesh=mesh,
        in_specs=(
            P("dp", "seq", None),
            P("dp", "seq"),
            P("dp"),
            P(("dp", "seq")),
            P(("dp", "seq"), None),
            P(("dp", "seq"), None),
            P(("dp", "seq"), None),
            P(("dp", "seq")),
            P(),
            P(),
            P(),
            P(("dp", "seq")),
            P(("dp", "seq"), None),
            P(None, None, ("dp", "seq")),
            P(None, None, ("dp", "seq")),
            P(None, None, ("dp", "seq")),
            P(None, None, ("dp", "seq")),
            P("dp", "seq", None),
        ),
        out_specs=(
            P("dp", "seq", None),
            P("dp", "seq", None),
            P(None, None, ("dp", "seq")),
            P(None, None, ("dp", "seq")),
            P(None, None, ("dp", "seq")),
            P(None, None, ("dp", "seq")),
        ),
        check_vma=False,
    )
```

```python
import functools

import jax
import jax.numpy as jnp
from jax import lax
from jax.experimental import pallas as pl
from jax.experimental.pallas import tpu as pltpu
from jax.sharding import PartitionSpec as P

EPS = 1e-05
f32 = jnp.float32
bf16 = jnp.bfloat16
BLOCK = 256


def mm(form, a, b):
    return jnp.einsum(form, a, b, preferred_element_type=f32)


LOG2E = 1.4426950408889634
VMEM_BYTES = 66_000_000


def dot_nn(a, b):
    return lax.dot_general(a, b, (((1,), (0,)), ((), ())), preferred_element_type=f32)


def dot_nt(a, b):
    return lax.dot_general(a, b, (((1,), (1,)), ((), ())), preferred_element_type=f32)


def dot_tn(a, b):
    return lax.dot_general(a, b, (((0,), (0,)), ((), ())), preferred_element_type=f32)


def dot_exact(chosen, v):
    hi = v.astype(bf16)
    rest = v - hi.astype(f32)
    mid = rest.astype(bf16)
    lo = (rest - mid.astype(f32)).astype(bf16)
    return dot_nn(chosen, hi) + (dot_nn(chosen, mid) + dot_nn(chosen, lo))


def sigmoid(v):
    return 0.5 * jnp.tanh(0.5 * v) + 0.5


def spread_pair(cols, j):
    rows = cols.shape[0]
    lane = lax.broadcasted_iota(jnp.int32, (rows, 128), 1)
    return jnp.where(lane < 64, cols[:, 2 * j : 2 * j + 1], cols[:, 2 * j + 1 : 2 * j + 2])


def spread_all(cols, pairs):
    return jnp.concatenate([spread_pair(cols, j) for j in range(pairs)], 1)


def per_head(v, select):
    return dot_nn(v.astype(bf16), select)


def chunks_at(slot, slots, chunks):
    return [c for c in range(chunks) if c * slots // chunks == slot]


def by_rank(t, rank):
    out = t[:rank]
    for k in range(rank, 128, rank):
        out = out + t[k : k + rank]
    return out


def fold(v, rank):
    return by_rank(v.T, rank)


def shards(pieces, size):
    return [p.at[k : k + size] for p in pieces for k in range(0, p.shape[0], size)]


def assemble(order_ref, base, pieces, size, target, sems):
    copies = []
    for i, piece in enumerate(shards(pieces, size)):
        at = pl.multiple_of(order_ref[base + i] * size, 16)
        copies.append(pltpu.make_async_copy(piece, target.at[pl.ds(at, size)], sems.at[i]))
    for copy in copies:
        copy.start()
    for copy in copies:
        copy.wait()


def fetch(order_ref, b, blocks, s0, target, sem):
    for i, block in enumerate(blocks):

        @pl.when(order_ref[b] == i)
        def _(block=block):
            row = s0 if block.shape[0] > 1 else 0
            pltpu.make_async_copy(block.at[row], target, sem).start()


def arrived(blocks, target, sem):
    pltpu.make_async_copy(blocks[0].at[0], target, sem).wait()


def forward_kernel(order_ref, *refs, hn, hc, count, size, s0, keep):
    (x0, x1, x2, x3, meta_ref, doc_ref, up_ref, conv_ref, head_ref, mask_ref, half_ref) = refs[:11]
    pieces = refs[11 : 11 + count]
    normed_ref, rank_ref, vbc_ref, pre_ref, ssm_ref, state_ref, tok_ref, *rest = refs[11 + count :]
    if keep:
        full_ref, down_ref, gain_out, *rest = rest
    buf, carry, x_buf, wa_ref, gain_ref, pa_buf, normed_buf, sems, full_sem, x_sems = rest
    pairs = hn // 2
    cc = hc + 256
    b = pl.program_id(0)

    xs = (x0, x1, x2, x3)

    @pl.when(b == 0)
    def _():
        for k in (0, 1):
            fetch(order_ref, k, xs, s0, x_buf.at[k], x_sems.at[k])
        assemble(order_ref, 4, pieces, size, wa_ref, sems)
        if keep:
            pltpu.make_async_copy(wa_ref, full_ref, full_sem).start()
        gain_ref[...] = wa_ref[:, cc + 128 :].astype(f32).T[120:, :]
        if keep:
            down_ref[...] = wa_ref[:, cc : cc + 128]
            gain_out[...] = jnp.broadcast_to(gain_ref[7:8, :], gain_out.shape)
        carry[...] = jnp.zeros_like(carry)
        buf[0:8, :] = jnp.zeros((8, cc), f32)

    blocks = pl.num_programs(0)
    now, later = lax.rem(b, 2), lax.rem(b + 1, 2)
    chunks = wa_ref.shape[1] // 128
    chunks = chunks // 2 if chunks % 2 == 0 else chunks
    span = wa_ref.shape[1] // chunks

    def normalise(slot):
        x = x_buf[slot].astype(f32)
        inv = lax.rsqrt(jnp.mean(x * x, -1, keepdims=True) + EPS)
        normed_buf[slot] = (x * inv * gain_ref[7:8, :]).astype(bf16)

    def project(slot, c):
        at = slice(span * c, span * c + span)
        pa_buf[slot, :, at] = dot_nn(normed_buf[slot], wa_ref[:, at])

    @pl.when(b == 0)
    def _():
        arrived(xs, x_buf.at[0], x_sems.at[0])
        normalise(0)
        for c in range(chunks):
            project(0, c)

    @pl.when(b + 2 < blocks)
    def _():
        fetch(order_ref, b + 2, xs, s0, x_buf.at[now], x_sems.at[now])

    @pl.when(b + 1 < blocks)
    def _():
        arrived(xs, x_buf.at[later], x_sems.at[later])

    normalise(later)
    normed_ref[0] = normed_buf[now]
    rank = (pa_buf[now, :, cc : cc + 128] * mask_ref[0, 0:1, :]).astype(bf16)
    rank_ref[0] = rank
    conv_in = (pa_buf[now, :, :cc] + dot_nt(rank, up_ref[...])).astype(bf16).astype(f32)
    buf[8:, :] = conv_in
    meta = meta_ref[0]
    pre = conv_ref[4:5, :] + conv_ref[3:4, :] * conv_in
    for k in (1, 2, 3):
        pre = pre + conv_ref[3 - k : 4 - k, :] * (buf[8 - k : 8 - k + BLOCK, :] * meta[:, k - 1 : k])
    buf[0:8, :] = buf[BLOCK : BLOCK + 8, :]
    pre_ref[0] = pre
    vbc = (pre * sigmoid(pre)).astype(bf16)
    vbc_ref[0] = vbc
    values = vbc[:, :hc]
    in_state = vbc[:, hc : hc + 128]
    out_state = vbc[:, hc + 128 :]
    arg = pa_buf[now, :, cc + 128 : cc + 256] + head_ref[0:1, :]
    dt = jnp.maximum(arg, 0.0) + jnp.log1p(jnp.exp(-jnp.abs(arg)))
    row = lax.broadcasted_iota(jnp.int32, (BLOCK, BLOCK), 0)
    col = lax.broadcasted_iota(jnp.int32, (BLOCK, BLOCK), 1)
    cum = dot_exact((row >= col).astype(f32).astype(bf16), dt * head_ref[1:2, :])
    tok_ref[0, :, 0:128] = dt
    tok_ref[0, :, 128:256] = cum
    tok_ref[0, :, 256:384] = arg
    left = cum * LOG2E
    right = (left - jnp.log(jnp.maximum(dt, 1e-37)) * LOG2E).T
    ok = (row >= col) & (meta[:, 5:6] == doc_ref[0, 0])
    bias = jnp.where(ok, 0.0, -1e30)
    contact = dot_nt(out_state, in_state)
    entry = jnp.exp(cum) * meta[:, 3:4]
    weight = jnp.exp(cum[BLOCK - 1 :, :] - cum) * dt * meta[:, 4:5]
    state = carry[...]
    state_low = state.astype(bf16)
    state_ref[0, 0] = state_low
    readout = dot_nt(out_state, state_low)
    half = BLOCK // 2
    scaled = []
    for j in range(pairs):
        for c in range(j * chunks // pairs, (j + 1) * chunks // pairs):
            project(later, c)
        at = slice(128 * j, 128 * j + 128)
        v = values[:, at]
        ys = []
        for r0, c1 in ((0, half), (half, BLOCK)):
            ws = []
            for h in (2 * j, 2 * j + 1):
                e = jnp.exp2(
                    (left[r0 : r0 + half, h : h + 1] - right[h : h + 1, :c1])
                    + bias[r0 : r0 + half, :c1]
                )
                ws.append((contact[r0 : r0 + half, :c1] * e).astype(bf16))
            vv = jnp.concatenate([v[:c1] * half_ref[0:1, :], v[:c1] * half_ref[1:2, :]], 0)
            ys.append(dot_nn(jnp.concatenate(ws, 1), vv))
        y = jnp.concatenate(ys, 0)
        ssm_ref[0, :, at] = y + readout[:, at] * spread_pair(entry, j)
        scaled.append((v.astype(f32) * spread_pair(weight, j)).astype(bf16))
    local = dot_tn(jnp.concatenate(scaled, 1), in_state)
    passing = entry[BLOCK - 1 :, :]
    for h in range(hn):
        at = slice(64 * h, 64 * h + 64)
        carry[at, :] = passing[:, h : h + 1] * state[at] + local[at]

    if keep:

        @pl.when(b == pl.num_programs(0) - 1)
        def _():
            pltpu.make_async_copy(wa_ref, full_ref, full_sem).wait()


def route(order_ref, b, value, near_ref, pair_ref, far_ref):
    for k, target in enumerate(
        (near_ref, pair_ref.at[0:BLOCK], far_ref, pair_ref.at[BLOCK : 2 * BLOCK])
    ):

        @pl.when(order_ref[b] == k)
        def _(target=target):
            target[...] = value


def assemble_both(order_ref, base, pieces, rows, out_rows, wb_ref, wo_ref, sems):
    part = wb_ref.shape[1]
    copies = []
    for i, piece in enumerate(shards(pieces, rows + 2 * out_rows)):
        slot = order_ref[base + i]
        to = pl.ds(pl.multiple_of(slot * rows, 16), rows)
        to_out = pl.ds(pl.multiple_of(slot * out_rows, 16), out_rows)
        rest = wo_ref.shape[1] - part
        moves = (
            (piece.at[0:rows], wb_ref.at[to]),
            (piece.at[rows : rows + out_rows], wo_ref.at[to_out, 0:part]),
            (piece.at[rows + out_rows :, 0:rest], wo_ref.at[to_out, part : part + rest]),
        )
        for j, (source, target) in enumerate(moves):
            copies.append(pltpu.make_async_copy(source, target, sems.at[3 * i + j]))
    return copies


def middle_kernel(order_ref, *refs, hc, width, rank, count, keep, merged, s0):
    (
        normed_ref, rank_ref, vbc_ref, ssm_ref, og0, og1, og2, og3, up_ref, row_ref, mask_ref,
    ) = refs[:11]
    gate_pieces = refs[11 : 11 + count]
    after_gate = 11 + count
    out_pieces = () if merged else refs[after_gate : after_gate + count]
    first_out = after_gate + len(out_pieces)
    g_ref, q_ref, gro_ref, near_ref, pair_ref, far_ref, stat_ref, *rest = refs[first_out:]
    if keep:
        wb_full, wo_full, up_out_ref, *rest = rest
    og_buf, wb_ref, wo_ref, sems, more_sems, full_sems, og_sems = rest
    ogs = (og0, og1, og2, og3)
    b = pl.program_id(0)

    def keeping():
        return (
            pltpu.make_async_copy(wb_ref, wb_full, full_sems.at[0]),
            pltpu.make_async_copy(wo_ref, wo_full, full_sems.at[1]),
        )

    now, later = lax.rem(b, 2), lax.rem(b + 1, 2)
    if merged:
        copies = assemble_both(order_ref, 4, gate_pieces, *merged, wb_ref, wo_ref, sems)
        gate_copies = copies[::3]
        out_copies = [c for i, c in enumerate(copies) if i % 3]
    else:
        gate_copies = [pltpu.make_async_copy(gate_pieces[0], wb_ref, sems.at[0])]
        out_copies = [pltpu.make_async_copy(out_pieces[0], wo_ref, more_sems.at[0])]

    @pl.when(b == 0)
    def _():
        for copy in gate_copies:
            copy.start()
        fetch(order_ref, 0, ogs, s0, og_buf.at[0], og_sems.at[0])
        for copy in out_copies:
            copy.start()
        for copy in gate_copies:
            copy.wait()

    @pl.when(b + 1 < pl.num_programs(0))
    def _():
        fetch(order_ref, b + 1, ogs, s0, og_buf.at[later], og_sems.at[later])

    gate = dot_nn(normed_ref[0], wb_ref[:, :hc]) + dot_nt(rank_ref[0], up_ref[...])
    g_ref[0] = gate

    @pl.when(b == 0)
    def _():
        for copy in out_copies:
            copy.wait()
        if keep:
            up_out_ref[...] = wb_ref[:, hc:]
            for copy in keeping():
                copy.start()

    arrived(ogs, og_buf.at[now], og_sems.at[now])
    mixed = ssm_ref[0] + row_ref[0:1, :] * vbc_ref[0, :, :hc].astype(f32)
    gated = mixed * (gate * sigmoid(gate))
    og = og_buf[now]
    gro = (dot_nn(og, wb_ref[:, hc:]) * mask_ref[0, 0:1, :]).astype(bf16)
    gro_ref[0] = gro
    q = dot_nt(og, wo_ref[:, :width]) + dot_nt(gro, wo_ref[:, width : width + 128])
    q = q * row_ref[1:2, :]
    q_ref[0] = q
    lane = lax.broadcasted_iota(jnp.int32, (BLOCK, 128), 1)
    s0 = jnp.sum(gated * gated, -1, keepdims=True)
    s1 = jnp.sum(q * gated, -1, keepdims=True)
    stat_ref[0, 0:8, :] = jnp.where(lane == 0, s0, s1).T[:8]
    low = (gated * row_ref[1:2, :]).astype(bf16)
    route(order_ref, b, dot_nn(low, wo_ref[:, :width]).astype(bf16), near_ref, pair_ref, far_ref)
    stat_ref[0, 8:, :] = fold(dot_nn(low, wo_ref[:, width : width + 128]) * mask_ref[0, 0:1, :], rank)

    if keep:

        @pl.when(b == pl.num_programs(0) - 1)
        def _():
            for copy in keeping():
                copy.wait()


def backward_kernel(
    order_ref, q_ref, g_ref, ssm_ref, vbc_ref, pre_ref, tok_ref, rm_ref, meta_ref, doc_ref, state_ref, next_ref,
    rank_ref, gro_ref, conv_ref, head_ref, row_ref, half_ref, select_ref, upg_ref, upc_ref, mask_ref,
    wa_ref, wb_ref,
    near_ref, pair_ref, far_ref, grads_ref, gri_ref,
    buf, carry, held_gate, held_conv, held_step, part_buf,
    *, hn, hc, rank,
):
    pairs = hn // 2
    step = pl.program_id(0)
    blocks = pl.num_programs(0)
    chunks = part_buf.shape[1] // 256

    def product(c):
        rows = slice(256 * c, 256 * c + 256)
        part_buf[:, rows] = (
            dot_nt(held_gate[...], wb_ref[rows, :hc])
            + dot_nt(held_conv[...], wa_ref[rows, :cc])
            + dot_nt(held_step[...], wa_ref[rows, cc + 128 :])
        ).astype(bf16)

    cc = hc + 256
    first = pl.program_id(0) == 0

    @pl.when(first)
    def _():
        carry[...] = jnp.zeros_like(carry)
        buf[BLOCK:, :] = jnp.zeros((8, cc), f32)
        grads_ref[...] = jnp.zeros_like(grads_ref)

    slots = 3 + (pairs + 1) // 2

    def beside(slot):
        for c in chunks_at(slot, slots, chunks):
            product(c)

    beside(0)
    rm = jnp.concatenate([rm_ref[0]] * 16, 0).T
    inv = rm[:, 0:1]
    mean = rm[:, 1:2]
    meta = meta_ref[0]
    gate = g_ref[0]
    ssm = ssm_ref[0]
    q = q_ref[0]
    vbc = vbc_ref[0]
    values = vbc[:, :hc]
    values_f = values.astype(f32)
    in_state = vbc[:, hc : hc + 128]
    out_state = vbc[:, hc + 128 :]
    skip = row_ref[0:1, :]
    mixed = ssm + skip * values_f
    sg = sigmoid(gate)
    act = gate * sg
    gated = mixed * act
    gated_r = gated * inv
    grad_gated = inv * (q - gated_r * (inv * mean))
    gated_low = (gated_r * row_ref[1:2, :]).astype(bf16)
    grads_ref[0, :, hc + cc :] = grads_ref[0, :, hc + cc :] + by_rank(
        dot_tn(gro_ref[0], gated_low), rank
    )
    grad_mixed = grad_gated * act
    gp_gate = (grad_gated * mixed * (sg + act * (1.0 - sg))).astype(bf16)
    gsum = grad_mixed.astype(bf16)
    gsum_f = gsum.astype(f32)

    beside(1)
    dt = tok_ref[0, :, 0:128]
    cum = tok_ref[0, :, 128:256]
    arg = tok_ref[0, :, 256:384]
    scaled_cum = cum * LOG2E
    down = scaled_cum - jnp.log(jnp.maximum(dt, 1e-37)) * LOG2E
    across = scaled_cum.T
    row = lax.broadcasted_iota(jnp.int32, (BLOCK, BLOCK), 0)
    col = lax.broadcasted_iota(jnp.int32, (BLOCK, BLOCK), 1)
    ok = (col >= row) & (meta[:, 5:6] == doc_ref[0, 0])
    bias = jnp.where(ok, 0.0, -1e30)
    contact = dot_nt(in_state, out_state)
    entry = jnp.exp(cum) * meta[:, 3:4]
    weight = jnp.exp(cum[BLOCK - 1 :, :] - cum) * dt * meta[:, 4:5]
    later = carry[...]
    later_low = later.astype(bf16)
    grad_scaled = dot_nt(in_state, later_low)
    weight_wide = spread_all(weight, pairs)
    entry_wide = spread_all(entry, pairs)
    scaled = (values_f * weight_wide).astype(bf16)
    weighted = (gsum_f * entry_wide).astype(bf16)
    half = BLOCK // 2
    g_con = [jnp.zeros((half, BLOCK), f32), jnp.zeros((half, half), f32)]
    g_val = []
    for j in range(pairs):
        if j % 2 == 0:
            beside(2 + j // 2)
        at = slice(128 * j, 128 * j + 128)
        v = values[:, at]
        gs = gsum[:, at]
        tops = []
        for i, (r0, c0) in enumerate(((0, 0), (half, half))):
            ws = []
            for side in (0, 1):
                h = 2 * j + side
                gw = dot_nt(v[r0 : r0 + half] * half_ref[side : side + 1, :], gs[c0:])
                e = jnp.exp2(
                    (across[h : h + 1, c0:] - down[r0 : r0 + half, h : h + 1])
                    + bias[r0 : r0 + half, c0:]
                )
                ws.append((contact[r0 : r0 + half, c0:] * e).astype(bf16))
                g_con[i] = g_con[i] + gw * e
            gg = jnp.concatenate([gs[c0:] * half_ref[0:1, :], gs[c0:] * half_ref[1:2, :]], 0)
            tops.append(dot_nn(jnp.concatenate(ws, 1), gg))
        g_val.append(jnp.concatenate(tops, 0))
    g_val = jnp.concatenate(g_val, 1) + grad_scaled * weight_wide
    con_low = jnp.concatenate(
        [g_con[0], jnp.concatenate([jnp.zeros((half, half), f32), g_con[1]], 1)], 0
    ).astype(bf16)
    g_in = dot_nn(con_low, out_state) + dot_nn(scaled, later_low)
    g_out = dot_tn(con_low, in_state) + dot_nn(weighted, state_ref[0, 0])
    select = select_ref[...]
    spent = per_head(values_f * g_val, select)
    gained = per_head(gsum_f * ssm, select)
    ends = later * next_ref[0, 0].astype(f32)
    parts = [jnp.sum(ends[64 * h : 64 * h + 64], 0, keepdims=True) for h in range(hn)]
    parts.append(jnp.zeros((128 - hn, 128), f32))
    last = jnp.sum(jnp.concatenate(parts, 0).T, 0, keepdims=True)
    where_last = lax.broadcasted_iota(jnp.int32, (BLOCK, 128), 0) == BLOCK - 1
    grad_cum = gained - spent + jnp.where(where_last, last, 0.0)
    grad_log = dot_exact((col >= row).astype(f32).astype(bf16), grad_cum)
    sig = sigmoid(arg)
    g_step = (
        spent * (sig / jnp.maximum(dt, 1e-37)) + head_ref[1:2, :] * grad_log * sig
    ).astype(bf16)
    passing = entry[BLOCK - 1 :, :]
    direct = dot_tn(weighted, out_state)
    for h in range(hn):
        at = slice(64 * h, 64 * h + 64)
        carry[at, :] = passing[:, h : h + 1] * later[at] + direct[at]

    beside(slots - 1)
    pre = pre_ref[0]
    sp = sigmoid(pre)
    grad_out = jnp.concatenate([skip * grad_mixed + g_val, g_in, g_out], 1)
    grad_pre = grad_out * (sp + pre * sp * (1.0 - sp))
    buf[:BLOCK, :] = grad_pre
    total = conv_ref[3:4, :] * grad_pre
    for k in (1, 2, 3):
        total = total + conv_ref[3 - k : 4 - k, :] * (buf[k : k + BLOCK, :] * meta[:, 5 + k : 6 + k])
    buf[BLOCK:, :] = grad_pre[:8]
    gp_conv = total.astype(bf16)
    rows = rank_ref[0]
    grads_ref[0, :, :hc] = grads_ref[0, :, :hc] + by_rank(dot_tn(rows, gp_gate), rank)
    grads_ref[0, :, hc : hc + cc] = grads_ref[0, :, hc : hc + cc] + by_rank(
        dot_tn(rows, gp_conv), rank
    )
    gri_ref[0] = fold(
        (dot_nn(gp_gate, upg_ref[...]) + dot_nn(gp_conv, upc_ref[...])) * mask_ref[0, 0:1, :], rank
    )

    @pl.when(step > 0)
    def _():
        route(order_ref, blocks - step, part_buf[...], near_ref, pair_ref, far_ref)

    held_gate[...] = gp_gate
    held_conv[...] = gp_conv
    held_step[...] = g_step

    @pl.when(step == blocks - 1)
    def _():
        for c in range(chunks):
            product(c)
        route(order_ref, 0, part_buf[...], near_ref, pair_ref, far_ref)


def pack_weights_kernel(
    ip_ref, sp_ref, idn_ref, iup_ref, odn_ref, oup_ref, op_ref, cw_ref, cb_ref, idx_ref, gg_ref, tail_ref,
    a_ref, o_ref, small_ref,
    turn, misc,
    *, n, hn, hc, inner, planes,
):
    rows = ip_ref.shape[0]
    ranks = idn_ref.shape[0]
    up_rows = iup_ref.shape[1]

    def turned(ref):
        turn[...] = jnp.zeros_like(turn)
        turn[:, : ref.shape[1]] = ref[...].astype(f32)
        return turn[...].T

    down = turned(idn_ref)[:rows].astype(bf16)
    late = turned(oup_ref)[:rows].astype(bf16)
    step = jnp.concatenate([sp_ref[...].astype(f32), jnp.zeros((rows, 128 - n * hn), f32)], 1)
    lane = lax.broadcasted_iota(jnp.int32, (rows, 128), 1)
    chunk = hc // planes
    heads = hn // planes

    b_at = hc + 256 + ranks + 128

    def columns(base, t, to, at0):
        for p in range(0, planes, 2):
            got = []
            for q in (p, p + 1):
                start = base + (q * n + t) * chunk
                low = start // 128 * 128
                v = ip_ref[:, low : low + 256].astype(f32)
                got.append(pltpu.roll(v, 256 - (start - low), 1) if start > low else v)
            second = pltpu.roll(got[1], 64, 1)
            at = at0 + p * chunk
            a_ref[to, at : at + 128] = got[0][:, :128].astype(bf16)
            a_ref[to, at + 128 : at + 256] = jnp.where(
                lane < 64, got[0][:, 128:], second[:, :128]
            ).astype(bf16)
            a_ref[to, at + 256 : at + 384] = second[:, 128:].astype(bf16)

    for t in range(n):
        to = slice(t * rows, (t + 1) * rows)
        columns(inner, t, to, 0)
        a_ref[to, hc : hc + 256] = ip_ref[:, 2 * inner :]
        a_ref[to, hc + 256 : hc + 256 + ranks] = down
        last = tail_ref[...]
        for p in range(planes):
            shift = (p * heads - (p * n + t) * heads) % 128
            mine = pltpu.roll(step, shift, 1) if shift else step
            last = jnp.where((lane >= p * heads) & (lane < (p + 1) * heads), mine, last)
        a_ref[to, hc + 256 + ranks : b_at] = last.astype(bf16)
        columns(0, t, to, b_at)
        a_ref[to, b_at + hc :] = late
    out_rows, width = op_ref.shape
    part = o_ref.shape[1]
    o_ref[:out_rows, :] = op_ref[:, :part]
    o_ref[out_rows:, : width - part] = op_ref[:, part:]
    o_ref[out_rows:, width - part : width - part + ranks] = turned(odn_ref)[:out_rows].astype(bf16)
    o_ref[out_rows:, width - part + ranks :] = jnp.zeros(
        (out_rows, 2 * part - width - ranks), bf16
    )
    keep = -(-up_rows // 16) * 16
    small_ref[:keep, :] = turned(iup_ref)[:keep].astype(bf16)
    misc[...] = jnp.zeros_like(misc)
    misc[0:4, : cw_ref.shape[1]] = cw_ref[...].astype(f32)
    misc[4:5, : cb_ref.shape[1]] = cb_ref[...].astype(f32)
    misc[5:6, : idx_ref.shape[1]] = idx_ref[...].astype(f32)
    misc[6:7, : gg_ref.shape[1]] = gg_ref[...].astype(f32)
    small_ref[keep:, :] = misc[...].astype(bf16)


def unpack_kernel(
    order_ref, own_ref, far_ref, beside_ref,
    up_gate_ref, up_conv_ref, conv_ref, gain_ref, index_ref,
    held, up, conv, gains,
    *, n, planes, up_rows, rows, inner, hc, conv_rows, out_rows,
):
    size = own_ref.shape[0]
    sources = (own_ref, beside_ref.at[0:size], far_ref, beside_ref.at[size : 2 * size])
    for t in range(n):
        for i, source in enumerate(sources):

            @pl.when(order_ref[t] == i)
            def _(t=t, source=source):
                held[t] = source[...]

    conv[...] = jnp.zeros_like(conv)
    gains[...] = jnp.zeros_like(gains)
    keep = -(-up_rows // 16) * 16

    def add(target, v, start):
        low = start // 128 * 128
        v = jnp.concatenate([v, jnp.zeros_like(v)], 1)
        v = pltpu.roll(v, start - low, 1) if start > low else v
        target[:, low : low + 256] = target[:, low : low + 256] + v

    for t in range(n):
        for y in range(2):
            for z in range(planes):
                owner = (2 * z + y) * n + t
                base = (y * planes + z) * rows
                up[up_rows * owner : up_rows * (owner + 1), :] = held[
                    t, base : base + up_rows, :
                ].astype(f32)
                misc = held[t, base + keep : base + keep + 16, :].astype(f32)[:8]
                add(conv, misc, conv_rows * owner)
                add(gains, misc, out_rows * owner)
                index_ref[owner : owner + 1, :] = misc[5:6]
    here = order_ref[0]
    chunk = hc // planes
    for p in range(planes):
        start = pl.multiple_of((p * n + here) * chunk, 8)
        to = slice(p * chunk, (p + 1) * chunk)
        up_gate_ref[to, :] = up[pl.ds(start, chunk), :].astype(bf16)
        up_conv_ref[to, :] = up[pl.ds(inner + start, chunk), :].astype(bf16)
    up_conv_ref[hc:, :] = up[2 * inner :, :].astype(bf16)
    conv_ref[:, hc:] = conv[:, inner : inner + 256]
    lane = lax.broadcasted_iota(jnp.int32, (8, 128), 1)

    def select(source, target, t):
        for p in range(0, planes, 2):
            got = []
            for q in (p, p + 1):
                start = (q * n + t) * chunk
                low = start // 128 * 128
                v = source[:, low : low + 256]
                got.append(pltpu.roll(v, 256 - (start - low), 1) if start > low else v)
            second = pltpu.roll(got[1], 64, 1)
            at = p * chunk
            target[:, at : at + 128] = got[0][:, :128]
            target[:, at + 128 : at + 256] = jnp.where(lane < 64, got[0][:, 128:], second[:, :128])
            target[:, at + 256 : at + 384] = second[:, 128:]

    for t in range(n):

        @pl.when(here == t)
        def _(t=t):
            select(conv, conv_ref, t)
            select(gains, gain_ref, t)


def owners_kernel(chosen_ref, got_ref, *outs, rank, starts):
    sources, rows, _ = got_ref.shape
    for k in range(outs[0].shape[0]):
        total = None
        for d in range(sources):
            for b in range(rows // rank):
                term = chosen_ref[d * (rows // rank) + b, k] * got_ref[
                    d, b * rank : (b + 1) * rank, :
                ].astype(f32)
                total = term if total is None else total + term
        for out, start in zip(outs, starts):
            out[k] = total[:, start : start + out.shape[2]]


def final_kernel(*refs, held):
    near_ref, pair_ref, far_ref, rows_ref, down_ref, x_ref, og_ref, gain_ref = refs[:8]
    out_ref = refs[8 + held]
    wide = rows_ref[...].T.astype(bf16)
    grad = near_ref[...].astype(f32) + pair_ref[...].astype(f32) + far_ref[0].astype(f32)
    grad = grad + dot_nt(wide, down_ref[...])
    x = x_ref[0].astype(f32)
    inv = lax.rsqrt(jnp.mean(x * x, -1, keepdims=True) + EPS)
    scaled = grad * gain_ref[0:1, :]
    mean = jnp.mean(scaled * x, -1, keepdims=True)
    out_ref[0] = inv * (scaled - x * (inv * inv * mean)) + og_ref[0].astype(f32)


def pack_grads_kernel(
    order_ref, g0, g1, g2, g3, down_ref, out_ref, up, middle, total, *, n, hc, inner, width, widths, starts,
    planes,
):
    chunk = hc // planes
    lane = lax.broadcasted_iota(jnp.int32, (out_ref.shape[1], 128), 1)

    def place(g, source, target, base, t):
        for p in range(planes):
            low = (source + p * chunk) // 128 * 128
            v = g[:, low : low + 256].astype(f32)
            off = source + p * chunk - low
            v = pltpu.roll(v, 256 - off, 1) if off else v
            to = base + (p * n + t) * chunk
            if to % 128 == 0:
                target[:, to : to + chunk] = v[:, :chunk]
            else:
                v = pltpu.roll(v, 64, 1)
                here = slice(to - 64, to + 64)
                target[:, here] = jnp.where(lane < 64, target[:, here], v[:, :128])
                target[:, to + 64 : to + 192] = v[:, 128:]

    for t in range(n):
        for i, g in enumerate((g0, g1, g2, g3)):

            @pl.when(order_ref[t] == i)
            def _(t=t, g=g):
                place(g, 0, up, 0, t)
                place(g, hc, up, inner, t)
                place(g, 2 * hc + 256, middle, 0, t)

    def summed(at):
        first = g0[:, at].astype(f32) + g1[:, at].astype(f32)
        return first + (g2[:, at].astype(f32) + g3[:, at].astype(f32))

    up[:, 2 * inner : 2 * inner + 256] = summed(slice(2 * hc, 2 * hc + 256))
    total[:, :width] = summed(slice(3 * hc + 256, 3 * hc + 256 + width))
    sources = (None, up, middle, total)
    for t in range(n):

        @pl.when(order_ref[0] == t)
        def _(t=t):
            for d in range(out_ref.shape[0]):
                for ref, at, w in zip(sources, starts, widths):
                    start = (d * n + t) * w
                    low = start // 128 * 128
                    span = -(-w // 128) * 128
                    if ref is None:
                        window = down_ref[:, low : low + span + 128].astype(f32)
                    else:
                        window = ref[:, low : low + span + 128]
                    if start > low:
                        window = pltpu.roll(window, span + 128 - (start - low), 1)
                    out_ref[d, :, at : at + span] = window[:, :span].astype(bf16)


def swap(v, axis, bit):
    size = lax.axis_size(axis)
    return lax.ppermute(v, axis, [(i, i ^ bit) for i in range(size)])


def put(pieces):
    rows = pieces[0][0].shape[0]
    out = jnp.zeros((len(pieces) * rows, pieces[0][0].shape[1]), pieces[0][0].dtype)
    for piece, slot in pieces:
        out = lax.dynamic_update_slice_in_dim(out, piece, slot * rows, 0)
    return out


def rotate(v, r):
    size = lax.axis_size("dp")
    return lax.ppermute(v, "dp", [(i, (i + 2 * r) % size) for i in range(size)])


def after(v, *others):
    return lax.optimization_barrier((v, others))[0]


def fence(*values):
    return lax.optimization_barrier(values)


def others(v):
    return [swap(v, "seq", k) for k in (1, 2, 3)]


def total_of(v, got):
    return (v + got[0]) + (got[1] + got[2])


def across(far, pair):
    return (far.astype(f32) + pair[BLOCK:].astype(f32)).astype(bf16)


def own_sum(near, pair, far):
    return near.astype(f32) + pair[:BLOCK].astype(f32) + far.astype(f32)


def scatter_plain(near, pair, far):
    v = jnp.concatenate([near, pair[:BLOCK], far, pair[BLOCK:]], 0).astype(f32)
    return lax.psum_scatter(v, "seq", scatter_dimension=0, tiled=True)


def per_device(
    layer_input,
    document_index,
    adapter_index,
    input_norm_gain,
    input_projection,
    step_projection,
    convolution_weight,
    convolution_bias,
    head_step_bias,
    log_decay_rate,
    head_skip_gain,
    gated_norm_gain,
    output_projection,
    adapter_input_down,
    adapter_input_up,
    adapter_output_down,
    adapter_output_up,
    output_gradient,
):
    both = ("dp", "seq")
    dps, n = lax.axis_size("dp"), lax.axis_size("seq")
    here = lax.axis_index("seq")
    seqs, own_len, width = layer_input.shape
    adapters, rank, _ = adapter_input_down.shape
    ranks = adapters * rank
    heads = head_step_bias.shape[0]
    inner = output_projection.shape[0] * dps * n
    cols = input_projection.shape[1]
    state2 = cols - 2 * inner
    state = state2 // 2
    taps = convolution_weight.shape[1]
    hn = heads // n
    hc = inner // n
    hd = inner // heads
    length = own_len * n
    nb = length // BLOCK

    staged = n == 4 and dps == 8
    rows = input_projection.shape[0]
    conv_cols = hc + state2
    wa_cols = conv_cols + ranks + 128
    doc_cols = -(-seqs * own_len // rows)
    doc_block = document_index.astype(bf16).reshape(-1)
    doc_block = jnp.pad(doc_block, (0, rows * doc_cols - doc_block.shape[0])).reshape(rows, -1)
    tail = jnp.concatenate([doc_block, input_norm_gain[:, None]], 1)
    up_rows = adapter_input_up.shape[2]
    up_keep = -(-up_rows // 16) * 16
    conv_rows = convolution_weight.shape[0]
    wide = -(-conv_rows // 128) * 128
    misc_rows = 16
    small_rows = up_keep + misc_rows * wide // 128
    out_rows = output_projection.shape[0]
    planes = dps // 2 if staged else 1
    if staged:
        to_head = [
            (8 * z + 2 * t + y, 8 * z + 4 * y + t)
            for z in range(planes) for y in range(2) for t in range(n)
        ]
    else:
        to_head = [(dps * s + d, n * d + s) for d in range(dps) for s in range(n)]
    tables = [
        v.reshape(ranks, -1)
        for v in (adapter_input_down, adapter_input_up, adapter_output_down, adapter_output_up)
    ]
    if staged:
        tail = jnp.pad(tail.astype(f32), ((0, 0), (127 - doc_cols, 0)))
        payload, w_o, small = pl.pallas_call(
            functools.partial(
                pack_weights_kernel, n=n, hn=hn, hc=hc, inner=inner, planes=planes
            ),
            out_shape=[
                jax.ShapeDtypeStruct((n * rows, wa_cols + hc + ranks), bf16),
                jax.ShapeDtypeStruct((2 * out_rows, hc + ranks), bf16),
                jax.ShapeDtypeStruct((small_rows, 128), bf16),
            ],
            scratch_shapes=[pltpu.VMEM((128, 256), f32), pltpu.VMEM((misc_rows, 128), f32)],
            name="pack_weights",
        )(
            input_projection, step_projection, *tables[:2], *tables[2:], output_projection,
            convolution_weight.T, convolution_bias[None], adapter_index[None], gated_norm_gain[None], tail,
        )
    else:
        gap = jnp.zeros((rows, 127 - hn - doc_cols), bf16)
        payload = jnp.concatenate(
            [
                jnp.concatenate(
                    [
                        input_projection[:, inner + t * hc : inner + (t + 1) * hc],
                        input_projection[:, 2 * inner :],
                        tables[0].T,
                        step_projection[:, t * hn : (t + 1) * hn],
                        gap,
                        tail,
                    ],
                    1,
                )
                for t in range(n)
            ],
            0,
        )
        late_payload = jnp.concatenate(
            [
                jnp.concatenate([input_projection[:, t * hc : (t + 1) * hc], tables[3].T], 1)
                for t in range(n)
            ],
            0,
        )
        w_o = jnp.concatenate([output_projection, tables[2].T], 1)

        def as_row(v):
            return jnp.pad(v, ((0, 0), (0, wide - v.shape[1])))

        misc = jnp.concatenate(
            [
                as_row(convolution_weight.T),
                as_row(convolution_bias[None]),
                as_row(adapter_index.astype(bf16)[None]),
                as_row(gated_norm_gain[None]),
            ],
            0,
        )
        misc = jnp.pad(misc, ((0, misc_rows - misc.shape[0]), (0, 0)))
        small = jnp.concatenate(
            [jnp.pad(tables[1].T, ((0, up_keep - up_rows), (0, 0))), misc.reshape(-1, 128)], 0
        )
    w_a = lax.all_to_all(payload, "seq", 0, 0, tiled=True)

    if staged:
        d = lax.axis_index("dp")
        y, z = d % 2, d // 2
        w_o = lax.ppermute(w_o, both, to_head)
        turned = [rotate(small, r) for r in (1, 2, 3)]
        w_a, small, turned, w_o = fence(w_a, small, turned, w_o)
        w_a, w_b = w_a[:, :wa_cols], w_a[:, wa_cols:]
        small = put([(small, z)] + [(v, lax.rem(z + 3 - r, 4)) for r, v in enumerate(turned)])
        a1, a3, a0y = rotate(w_a, 1), rotate(w_a, 3), swap(w_a, "dp", 1)
        small_y = swap(small, "dp", 1)
        x0 = after(layer_input, w_a)[:1]
        x_far0 = swap(x0, "seq", 2)
        x1, og = after(layer_input, w_a)[1:], after(output_gradient, w_a)
        og0, og1 = og[:1], og[1:]
        at = [2 * lax.rem(z + 4 - r, 4) + y for r in range(4)]
        slots = [at[0], at[0] ^ 1, at[1], at[3], at[1] ^ 1, at[3] ^ 1, at[2], at[2] ^ 1]
        slots = jnp.stack(slots).astype(jnp.int32)
        x_order = jnp.arange(4, dtype=jnp.int32) ^ here
    else:
        w_b = lax.all_to_all(late_payload, "seq", 0, 0, tiled=True)
        w_o = lax.ppermute(w_o, both, to_head)
        small = lax.all_gather(lax.all_gather(small, "dp", tiled=True), "seq", tiled=True)
        small = jnp.moveaxis(small.reshape(n, dps, small_rows, 128), 0, 1)
        wa_pieces = [lax.all_gather(w_a, "dp", tiled=True)]
        slots = jnp.zeros((1,), jnp.int32)
        x_order = jnp.arange(nb, dtype=jnp.int32)
        xs = [jnp.split(lax.all_gather(layer_input, "seq", axis=1, tiled=True), nb, axis=1)] * seqs
    docs = w_a[:, wa_cols - 1 - doc_cols : wa_cols - 1].reshape(n, -1)[:, : seqs * own_len]
    docs = jnp.moveaxis(docs.reshape(n, seqs, own_len), 0, 1).reshape(seqs, length)
    order = jnp.concatenate([x_order, slots])
    order_whole = jnp.concatenate([x_order, jnp.zeros((1,), jnp.int32)])

    def mine(v):
        v = v.reshape(planes, n, v.shape[0] // (planes * n), *v.shape[1:])
        v = lax.dynamic_index_in_dim(v, here, 1, keepdims=False)
        return v.reshape(-1, *v.shape[2:])

    if not staged:
        small = small.reshape(dps * n, small_rows, 128)
        up_full = small[:, :up_rows].reshape(cols, ranks)
        misc = small[:, up_keep:].reshape(dps * n, misc_rows, wide)
        conv_w = jnp.moveaxis(misc[:, :taps, :conv_rows], 1, 0).reshape(taps, -1).astype(f32)
        conv_b = misc[:, taps, :conv_rows].reshape(-1).astype(f32)
        every_index = misc[:, taps + 1, :seqs].reshape(dps, n, seqs)[:, 0].astype(jnp.int32)
        gate_gain = misc[:, taps + 2, :out_rows].reshape(-1).astype(f32)

        up_gate = mine(up_full[:inner])
        up_conv = jnp.concatenate([mine(up_full[inner : 2 * inner]), up_full[2 * inner :]], 0)
        conv_w = jnp.concatenate([mine(conv_w.T[:inner]), conv_w.T[inner:]], 0).T
        conv_b = jnp.concatenate([mine(conv_b[:inner]), conv_b[inner:]], 0)
    step_bias = mine(head_step_bias)
    decay_rate = -jnp.exp(mine(log_decay_rate))
    skip = mine(head_skip_gain)
    gate_gain = None if staged else mine(gate_gain)

    chosen = (adapter_index[:, None] == jnp.arange(adapters, dtype=jnp.int32)[None, :]).astype(f32)
    mask = jnp.repeat(chosen, rank, axis=1)[:, None, :]

    doc_f = docs.astype(f32)

    def same_before(k):
        return jnp.pad(doc_f, ((0, 0), (k, 0)), constant_values=-1.0)[:, :length] == doc_f

    def same_after(k):
        return jnp.pad(doc_f, ((0, 0), (0, k)), constant_values=-1.0)[:, k:] == doc_f

    blocks = doc_f.reshape(seqs, nb, BLOCK)
    prior = jnp.concatenate([blocks[:, :1, 0], blocks[:, :-1, -1]], 1)
    keep = (blocks == prior[:, :, None]).reshape(seqs, length)
    ends = (blocks == blocks[:, :, -1:]).reshape(seqs, length)
    flags = [
        same_before(1), same_before(2), same_before(3), keep, ends, doc_f,
        same_after(1), same_after(2), same_after(3),
    ]
    meta = jnp.stack([v.astype(f32) for v in flags], -1)
    meta = jnp.pad(meta, ((0, 0), (0, 0), (0, 128 - len(flags))))
    doc_rows = blocks[:, :, None, :]

    def rows8(*vs):
        return jnp.pad(jnp.stack(vs), ((0, 8 - len(vs)), (0, 0)))

    if not staged:
        conv_rows8 = rows8(conv_w[0], conv_w[1], conv_w[2], conv_w[3], conv_b)
        wide_rows = rows8(jnp.repeat(skip, hd), gate_gain)
    head_rows = rows8(
        jnp.pad(step_bias, (0, 128 - hn)), jnp.pad(decay_rate, (0, 128 - hn))
    )
    halves = jnp.pad(
        (jnp.arange(128)[None, :] // 64 == jnp.arange(2)[:, None]).astype(bf16), ((0, 14), (0, 0))
    )
    select = (jnp.arange(hc)[:, None] // hd == jnp.arange(128)[None, :]).astype(bf16)
    mask8 = jnp.broadcast_to(mask, (seqs, 8, ranks))
    cc = conv_cols
    anywhere = pl.BlockSpec(memory_space=pl.ANY)
    params = pltpu.CompilerParams(
        dimension_semantics=("arbitrary",), vmem_limit_bytes=VMEM_BYTES
    )

    def at(w, k=0):
        return pl.BlockSpec((1, BLOCK, w), lambda b, o: (k, b, 0))

    def once(v, *block):
        block = block or v.shape
        return pl.BlockSpec(block, lambda b, o: (0,) * len(block), pipeline_mode=pl.Buffered(1))

    def of_seq(v, s0):
        k = s0 if v.shape[0] > 1 else 0
        return pl.BlockSpec(
            (1,) + v.shape[1:], lambda b, o: (k, 0, 0), pipeline_mode=pl.Buffered(1)
        )

    def one(w, dtype):
        return jax.ShapeDtypeStruct((1, length, w), dtype)

    def cost(flops, mib):
        return pl.CostEstimate(flops=int(flops), bytes_accessed=mib << 20, transcendentals=0)

    def parts_specs():
        return [once(None, BLOCK, width), once(None, 2 * BLOCK, width), once(None, BLOCK, width)]

    parts_shapes = [
        jax.ShapeDtypeStruct((k * BLOCK, width), bf16) for k in (1, 2, 1)
    ]

    def forward(s0, order, blocks, pieces, keep):
        whole_w = jax.ShapeDtypeStruct((width, wa_cols), bf16)
        size = n * rows if len(pieces) > 1 else width
        total = sum(v.shape[0] for v in pieces) // size
        return pl.pallas_call(
            functools.partial(
                forward_kernel, hn=hn, hc=hc, count=len(pieces), size=size, s0=s0, keep=keep
            ),
            grid_spec=pltpu.PrefetchScalarGridSpec(
                num_scalar_prefetch=1,
                grid=(nb,),
                in_specs=[
                    *([anywhere] * len(blocks)), at(128, s0),
                    pl.BlockSpec((1, 1, 1, BLOCK), lambda b, o: (s0, b, 0, 0)),
                    once(up_conv), once(conv_rows8), once(head_rows), of_seq(mask8, s0), once(halves),
                    *([anywhere] * len(pieces)),
                ],
                out_specs=[
                    at(width), at(128), at(cc), at(cc), at(hc),
                    pl.BlockSpec((1, 1, hc, state), lambda b, o: (0, b, 0, 0)), at(384),
                    *([anywhere, once(None, width, 128), once(None, 8, width)] if keep else []),
                ],
                scratch_shapes=[
                    pltpu.VMEM((BLOCK + 8, cc), f32), pltpu.VMEM((hc, state), f32),
                    pltpu.VMEM((2, BLOCK, width), bf16), pltpu.VMEM((width, wa_cols), bf16),
                    pltpu.VMEM((8, width), f32), pltpu.VMEM((2, BLOCK, wa_cols), f32),
                    pltpu.VMEM((2, BLOCK, width), bf16), pltpu.SemaphoreType.DMA((total,)),
                    pltpu.SemaphoreType.DMA, pltpu.SemaphoreType.DMA((2,)),
                ],
            ),
            out_shape=[
                one(width, bf16), one(128, bf16), one(cc, bf16), one(cc, f32), one(hc, f32),
                jax.ShapeDtypeStruct((1, nb, hc, state), bf16), one(384, f32),
                *(
                    [
                        whole_w, jax.ShapeDtypeStruct((width, 128), bf16),
                        jax.ShapeDtypeStruct((8, width), f32),
                    ]
                    if keep
                    else []
                ),
            ],
            compiler_params=params,
            name="ssm_forward",
            cost_estimate=cost(2 * length * (width * wa_cols + 3 * BLOCK * hc), 20),
        )(order, *blocks, meta, doc_rows, up_conv, conv_rows8, head_rows, mask8, halves, *pieces)

    def middle(s0, order, scanned, blocks, gate_pieces, out_pieces, keep):
        normed, rank_in, vbc, _, ssm = scanned[:5]
        count = len(gate_pieces)
        merged = () if out_pieces else (n * rows, out_rows)
        wb_shape, wo_shape = (width, hc + ranks), (hc, width + ranks)
        return pl.pallas_call(
            functools.partial(
                middle_kernel, hc=hc, width=width, rank=rank, count=count, keep=keep,
                merged=merged, s0=s0,
            ),
            grid_spec=pltpu.PrefetchScalarGridSpec(
                num_scalar_prefetch=1,
                grid=(nb,),
                in_specs=[
                    at(width), at(128), at(cc), at(hc), *([anywhere] * len(blocks)),
                    once(up_gate), once(wide_rows), of_seq(mask8, s0), *([anywhere] * (count + len(out_pieces))),
                ],
                out_specs=[
                    at(hc), at(hc), at(128), *parts_specs(),
                    pl.BlockSpec((1, 8 + rank, BLOCK), lambda b, o: (0, 0, b)),
                    *([anywhere, anywhere, once(None, width, 128)] if keep else []),
                ],
                scratch_shapes=[
                    pltpu.VMEM((2, BLOCK, width), bf16), pltpu.VMEM(wb_shape, bf16),
                    pltpu.VMEM(wo_shape, bf16), pltpu.SemaphoreType.DMA((3 * dps,)),
                    pltpu.SemaphoreType.DMA((count,)), pltpu.SemaphoreType.DMA((2,)),
                    pltpu.SemaphoreType.DMA((2,)),
                ],
            ),
            out_shape=[
                one(hc, f32), one(hc, f32), one(128, bf16), *parts_shapes,
                jax.ShapeDtypeStruct((1, 8 + rank, length), f32),
                *(
                    [jax.ShapeDtypeStruct(v, bf16) for v in (wb_shape, wo_shape, (width, 128))]
                    if keep
                    else []
                ),
            ],
            compiler_params=params,
            name="output_side",
            cost_estimate=cost(2 * length * width * hc * 3, 25),
        )(
            order, normed, rank_in, vbc, ssm, *blocks, up_gate, wide_rows, mask8, *gate_pieces,
            *out_pieces,
        )

    def backward(s0, scanned, gate, q, rm, grad_rank_out):
        _, rank_in, vbc, pre, ssm, states_low, tok = scanned[:7]

        def back(w, k=0):
            return pl.BlockSpec((1, BLOCK, w), lambda b, o: (k, nb - 1 - b, 0))

        def back_state(shift):
            return pl.BlockSpec(
                (1, 1, hc, state), lambda b, o: (0, jnp.minimum(nb - 1 - b + shift, nb - 1), 0, 0)
            )

        return pl.pallas_call(
            functools.partial(backward_kernel, hn=hn, hc=hc, rank=rank),
            grid_spec=pltpu.PrefetchScalarGridSpec(
                num_scalar_prefetch=1,
                grid=(nb,),
                in_specs=[
                    back(hc), back(hc), back(hc), back(cc), back(cc), back(384),
                    pl.BlockSpec((1, 8, BLOCK), lambda b, o: (0, 0, nb - 1 - b)), back(128, s0),
                    pl.BlockSpec((1, 1, 1, BLOCK), lambda b, o: (s0, nb - 1 - b, 0, 0)),
                    back_state(0), back_state(1), back(128), back(128), once(conv_rows8),
                    once(head_rows), once(wide_rows), once(halves), once(select), once(up_gate),
                    once(up_conv), of_seq(mask8, s0), once(wa), once(wb),
                ],
                out_specs=[
                    *parts_specs(), once(None, 1, rank, 2 * hc + cc),
                    pl.BlockSpec((1, rank, BLOCK), lambda b, o: (0, 0, nb - 1 - b)),
                ],
                scratch_shapes=[
                    pltpu.VMEM((BLOCK + 8, cc), f32), pltpu.VMEM((hc, state), f32),
                    pltpu.VMEM((BLOCK, hc), bf16), pltpu.VMEM((BLOCK, cc), bf16),
                    pltpu.VMEM((BLOCK, 128), bf16), pltpu.VMEM((BLOCK, width), bf16),
                ],
            ),
            out_shape=[
                *parts_shapes, jax.ShapeDtypeStruct((1, rank, 2 * hc + cc), f32),
                jax.ShapeDtypeStruct((1, rank, length), f32),
            ],
            compiler_params=params,
            name="ssm_backward",
            cost_estimate=cost(2 * length * (8 * BLOCK * hc + width * (hc + cc)), 30),
        )(
            x_order, q, gate, ssm, vbc, pre, tok, rm, meta, doc_rows, states_low, states_low, rank_in,
            grad_rank_out, conv_rows8, head_rows, wide_rows, halves, select, up_gate, up_conv, mask8,
            wa, wb,
        )

    def own_tokens(v, axis):
        return lax.dynamic_slice_in_dim(v, here * own_len, own_len, axis)

    def with_adapter(rows_of, table, s0):
        wide_rows_of = jnp.tile(rows_of, (adapters, 1)) * mask[s0, 0][:, None].astype(bf16)
        return mm("rt,dr->td", wide_rows_of, table)

    if staged:
        ready = (head_rows, meta, doc_rows, mask8, halves, select, order, order_whole, x1, og0, og1)
        a1, a3, a0y, w_a, small, small_y, x_far0, w_b, w_o, ready = fence(
            a1, a3, a0y, w_a, small, small_y, x_far0, w_b, w_o, ready
        )
        head_rows, meta, doc_rows, mask8, halves, select, order, order_whole, x1, og0, og1 = ready
        a13y = swap(jnp.concatenate([a1, a3]), "dp", 1)
        a2 = rotate(w_a, 2)
        small = put([(small, y), (small_y, 1 - y)])
        small_far = swap(small, "seq", 2)
        x_both0 = swap(x_far0, "seq", 1)
        x_near = swap(after(layer_input, w_a), "seq", 1)
        w_bo = jnp.concatenate([w_b, w_o])
        a2, a13y, small, small_far, x_both0, x_near, w_bo, x1 = fence(
            a2, a13y, small, small_far, x_both0, x_near, w_bo, x1
        )
        a2y = swap(a2, "dp", 1)
        beside = swap(jnp.concatenate([small, small_far]), "seq", 1)
        b1, b3 = rotate(w_bo, 1), rotate(w_bo, 3)
        x_far1 = swap(x1, "seq", 2)
        up_gate, up_conv, conv_rows8, gains, index_rows = pl.pallas_call(
            functools.partial(
                unpack_kernel, n=n, planes=planes, up_rows=up_rows, rows=small_rows, inner=inner,
                hc=hc, conv_rows=conv_rows, out_rows=out_rows,
            ),
            in_specs=[
                pl.BlockSpec(memory_space=pltpu.SMEM),
                *[pl.BlockSpec(memory_space=pltpu.VMEM)] * 3,
            ],
            out_specs=[pl.BlockSpec(memory_space=pltpu.VMEM)] * 5,
            out_shape=[
                jax.ShapeDtypeStruct((hc, ranks), bf16), jax.ShapeDtypeStruct((cc, ranks), bf16),
                jax.ShapeDtypeStruct((8, cc), f32), jax.ShapeDtypeStruct((8, hc), f32),
                jax.ShapeDtypeStruct((dps * n, 128), f32),
            ],
            scratch_shapes=[
                pltpu.VMEM((n, *small.shape), bf16), pltpu.VMEM((cols, ranks), f32),
                pltpu.VMEM((8, inner + state2 + 256), f32), pltpu.VMEM((8, inner + 256), f32),
            ],
            compiler_params=pltpu.CompilerParams(vmem_limit_bytes=VMEM_BYTES),
            name="unpack_small",
        )(x_order, small, small_far, beside)
        every_index = index_rows.reshape(dps, n, 128)[:, 0, :seqs].astype(jnp.int32)
        wide_rows = rows8(jnp.repeat(skip, hd), gains[6])
        wa_pieces = [w_a, a0y, a1, a3, a13y, a2, a2y]
        xs = [[layer_input, x_near, x_far0, x_both0]]
        wa_pieces, xs[0], w_bo, up_conv, up_gate, conv_rows8 = fence(
            wa_pieces, xs[0], w_bo, up_conv, up_gate, conv_rows8
        )
        *fwd0, wa, down_in, gain_rows = forward(0, order, xs[0], wa_pieces, True)
        b0y, b2 = swap(w_bo, "dp", 1), rotate(w_bo, 2)
        fwd0, wa, b1, b3, b0y, w_bo, x_far1 = fence(fwd0, wa, b1, b3, b0y, w_bo, x_far1)
        x_both1 = swap(x_far1, "seq", 1)
        x_both1, w_bo, og0, og1, og = fence(x_both1, w_bo, og0, og1, output_gradient)
        fwd1 = forward(1, order_whole, [layer_input, x_near, x_far1, x_both1], [wa], False)
        b1y, b3y = swap(b1, "dp", 1), swap(b3, "dp", 1)
        og_far0 = swap(og0, "seq", 2)
        og_near = swap(og, "seq", 1)
        fwd1, b1y, b3y, b2, og_far0, og_near, w_bo, og1 = fence(
            fwd1, b1y, b3y, b2, og_far0, og_near, w_bo, og1
        )
        b2y = swap(b2, "dp", 1)
        og_both0 = swap(og_far0, "seq", 1)
        og_far1 = swap(og1, "seq", 2)
        fwd = [fwd0, fwd1]
        wb_pieces = [w_bo, b0y, b1, b3, b1y, b3y, b2, b2y]
        wo_pieces = []
        ogs = [[output_gradient, og_near, og_far0, og_both0]]
        wb_pieces, ogs[0], og_far1 = fence(wb_pieces, ogs[0], og_far1)
        og_both1 = swap(og_far1, "seq", 1)
    else:
        *fwd0, wa, down_in, gain_rows = forward(0, order, xs[0], wa_pieces, True)
        fwd = [fwd0]
        fwd += [forward(s0, order_whole, xs[s0], [wa], False) for s0 in range(1, seqs)]
        wb_pieces = [lax.all_gather(w_b, "dp", tiled=True)]
        wo_pieces = [lax.all_gather(w_o, "dp", tiled=True)]
        full = lax.all_gather(output_gradient, "seq", axis=1, tiled=True)
        ogs = [jnp.split(full, nb, axis=1)] * seqs

    def normalisers(stats):
        inv_gated = lax.rsqrt(stats[:1] / inner + EPS)
        rm = jnp.pad(jnp.concatenate([inv_gated, stats[1:2] / inner], 0), ((0, 6), (0, 0)))[None]
        return inv_gated, rm, own_tokens((stats[8:] * inv_gated).astype(bf16), 1)

    def layer_output(s0, branch, inv_gated, rank_out):
        return (
            layer_input[s0].astype(f32)
            + branch * own_tokens(inv_gated, 1).T
            + with_adapter(rank_out, up_out, s0)
        ).astype(bf16)

    def down_gradient(s0, grad_rank_in):
        return mm("rt,td->rd", grad_rank_in, fwd[s0][0][0]).astype(bf16)

    def layer_gradient(s0, partial, grad_rank_in):
        grad_normed = partial + with_adapter(
            own_tokens(grad_rank_in, 1), down_in, s0
        )
        own = layer_input[s0].astype(f32)
        inv_own = lax.rsqrt(jnp.mean(own * own, -1, keepdims=True) + EPS)
        scaled_in = grad_normed * gain_rows[0]
        return (
            inv_own * scaled_in
            - own * inv_own**3 * jnp.mean(scaled_in * own, -1, keepdims=True)
            + output_gradient[s0].astype(f32)
        )

    def final_gradient(s0, near, pair, far, grad_rank_in, earlier):
        rows_of = jnp.tile(own_tokens(grad_rank_in, 1).astype(f32), (adapters, 1)) * mask[s0, 0][:, None]

        tile_rows = 128
        mine_of_seq = pl.BlockSpec((1, tile_rows, width), lambda i: (s0, i, 0))
        by_rows = pl.BlockSpec((tile_rows, width), lambda i: (i, 0))

        def full(*block):
            return pl.BlockSpec(block, lambda i: (0,) * len(block))

        ins = [near, pair, far[None], rows_of, down_in, layer_input, output_gradient, gain_rows]
        specs = [
            by_rows, by_rows, pl.BlockSpec((1, tile_rows, width), lambda i: (0, i, 0)),
            pl.BlockSpec((ranks, tile_rows), lambda i: (0, i)), full(width, ranks), mine_of_seq,
            mine_of_seq, full(8, width),
        ]
        if earlier is not None:
            ins.append(earlier)
            specs.append(anywhere)
        return pl.pallas_call(
            functools.partial(final_kernel, held=len(ins) - 8),
            grid=(own_len // tile_rows,),
            in_specs=specs,
            out_specs=mine_of_seq,
            out_shape=jax.ShapeDtypeStruct((seqs, own_len, width), f32),
            input_output_aliases={8: 0} if earlier is not None else {},
            compiler_params=params,
            name="final_gradient",
            cost_estimate=cost(2 * BLOCK * width * ranks, 5),
        )(*ins)

    *side0, wb, wo, up_out = middle(0, order, fwd[0], ogs[0], wb_pieces, wo_pieces, True)
    if staged:
        side0, wb, wo, og_both1 = fence(side0, wb, wo, og_both1)
        ogs.append([output_gradient, og_near, og_far1, og_both1])
        gate0, q0, gro0, near0, pair0, far0, stats0 = side0
        side1 = middle(1, order_whole, fwd[1], ogs[1], [wb], [wo], False)
        got = others(stats0[0])
        pair0 = swap(pair0, "seq", 1)
        side1, got, pair0, far0 = fence(side1, got, pair0, far0)
        gate1, q1, gro1, near1, pair1, far1, stats1 = side1
        inv0, rm0, rank_out0 = normalisers(total_of(stats0[0], got))
        rm0, away, stats1, pair1 = fence(rm0, across(far0, pair0), stats1, pair1)

        back0 = backward(0, fwd[0], gate0, q0, rm0, gro0)
        away = swap(away, "seq", 2)
        got = others(stats1[0])
        pair1 = swap(pair1, "seq", 1)
        back0, away, got, pair1, far1 = fence(back0, away, got, pair1, far1)
        near_g0, pair_g0, far_g0, compact0, gri0 = back0
        pair_g0 = swap(pair_g0, "seq", 1)
        away0 = away
        inv1, rm1, rank_out1 = normalisers(total_of(stats1[0], got))
        rm1, away, gri0, away_g, away0, rank_out0, rank_out1 = fence(
            rm1, across(far1, pair1), gri0, across(far_g0, pair_g0), away0, rank_out0, rank_out1
        )

        back1 = backward(1, fwd[1], gate1, q1, rm1, gro1)
        away = swap(away, "seq", 2)
        away_g = swap(away_g, "seq", 2)
        got = others(gri0[0])
        back1, away, away_g, got, away0, rank_out0, rank_out1, near0, pair0, inv0 = fence(
            back1, away, away_g, got, away0, rank_out0, rank_out1, near0, pair0, inv0
        )
        near_g1, pair_g1, far_g1, compact1, gri1 = back1
        pair_g1 = swap(pair_g1, "seq", 1)
        got1 = others(gri1[0])
        g_out_up = mm("srt,std->srd", jnp.stack([rank_out0, rank_out1]), output_gradient)
        split = jnp.concatenate(
            [
                jnp.concatenate([compact0[0], compact1[0]]).astype(bf16),
                g_out_up.astype(bf16).reshape(seqs * rank, width),
            ],
            1,
        )
        away_g1, split, got1, got, gri0, near0, pair0, near1, pair1, near_g0, pair_g0, down_in = fence(
            across(far_g1, pair_g1), split, got1, got, gri0, near0, pair0, near1, pair1, near_g0,
            pair_g0, down_in,
        )
        away_g1 = swap(away_g1, "seq", 2)
        split_far = swap(split, "seq", 2)
        split_near = swap(split, "seq", 1)
        split_both = swap(split_far, "seq", 1)
        gri0 = total_of(gri0[0], got).astype(bf16)
        gri1 = total_of(gri1[0], got1).astype(bf16)
        downs = jnp.concatenate([down_gradient(0, gri0), down_gradient(1, gri1)])
        grad0 = final_gradient(0, near_g0, pair_g0, away_g, gri0, None)
        output0 = layer_output(0, own_sum(near0, pair0, away0), inv0, rank_out0)
        output1 = layer_output(1, own_sum(near1, pair1, away), inv1, rank_out1)
        grads_of_seq = [split, split_near, split_far, split_both]
        grads_order = x_order
    else:
        splits, downs, ranks_out, outputs, grads_in = [], [], [], [], []
        for s0 in range(seqs):
            if s0:
                side0 = middle(s0, order_whole, fwd[s0], ogs[s0], [wb], [wo], False)
            gate, q, gro, *parts, stats = side0
            inv_gated, rm, rank_out = normalisers(lax.psum(stats[0], "seq"))
            outputs.append(layer_output(s0, scatter_plain(*parts), inv_gated, rank_out))
            *parts, compacted, gri = backward(s0, fwd[s0], gate, q, rm, gro)
            gri = lax.psum(gri[0], "seq").astype(bf16)
            splits.append(compacted[0].astype(bf16))
            downs.append(down_gradient(s0, gri))
            ranks_out.append(rank_out)
            grads_in.append(layer_gradient(s0, scatter_plain(*parts), gri))
        g_out_up = mm("srt,std->srd", jnp.stack(ranks_out), output_gradient).astype(bf16)
        output = jnp.stack(outputs)
        grad_in = jnp.stack(grads_in)
        downs = jnp.concatenate(downs)
        split = jnp.concatenate(
            [jnp.concatenate(splits), g_out_up.reshape(seqs * rank, width)], 1
        )
        grads_of_seq = jnp.split(lax.all_gather(split, "seq", axis=0, tiled=True), n)

    widths = [v // (dps * n) for v in (width, cols, inner, width)]
    starts, lanes = [], 0
    for v in widths:
        starts.append(lanes)
        lanes += -(-v // 128) * 128
    pack_rows = seqs * rank
    if staged:
        packed = pl.pallas_call(
            functools.partial(
                pack_grads_kernel, n=n, hc=hc, inner=inner, width=width, widths=widths,
                starts=starts, planes=planes,
            ),
            in_specs=[
                pl.BlockSpec(memory_space=pltpu.SMEM),
                *[pl.BlockSpec(memory_space=pltpu.VMEM)] * 5,
            ],
            out_specs=pl.BlockSpec(memory_space=pltpu.VMEM),
            out_shape=jax.ShapeDtypeStruct((dps, pack_rows, lanes), bf16),
            scratch_shapes=[
                pltpu.VMEM((pack_rows, cols + 256), f32), pltpu.VMEM((pack_rows, inner + 256), f32),
                pltpu.VMEM((pack_rows, width + 256), f32),
            ],
            name="pack_grads",
        )(
            grads_order,
            *grads_of_seq, jnp.pad(downs, ((0, 0), (0, 256))),
        )
    else:
        pieces = jnp.stack(grads_of_seq)

        def by_heads(start):
            return jnp.concatenate([pieces[t, :, start : start + hc] for t in range(n)], -1)

        def summed(start, size):
            return pieces[..., start : start + size].astype(f32).sum(0).astype(bf16)

        full = [
            downs,
            jnp.concatenate([by_heads(0), by_heads(hc), summed(2 * hc, state2)], -1),
            by_heads(2 * hc + state2),
            summed(3 * hc + state2, width),
        ]
        packed = jnp.zeros((dps, pack_rows, lanes), bf16)
        for v, start, w in zip(full, starts, widths):
            v = lax.dynamic_index_in_dim(
                v.reshape(pack_rows, dps, n, w), here, 2, keepdims=False
            )
            packed = packed.at[:, :, start : start + w].set(v.transpose(1, 0, 2))
    got = lax.all_to_all(packed, "dp", 0, 0, tiled=True)
    if staged:
        output = jnp.stack([output0, output1])
    all_chosen = every_index[..., None] == jnp.arange(adapters)
    if staged:
        grads = pl.pallas_call(
            functools.partial(owners_kernel, rank=rank, starts=starts),
            in_specs=[
                pl.BlockSpec(memory_space=pltpu.SMEM), pl.BlockSpec(memory_space=pltpu.VMEM)
            ],
            out_specs=[pl.BlockSpec(memory_space=pltpu.VMEM)] * len(widths),
            out_shape=[jax.ShapeDtypeStruct((adapters, rank, w), f32) for w in widths],
            name="owners_sum",
        )(all_chosen.astype(f32).reshape(-1, adapters), got)
    else:
        table = mm(
            "dsk,dsrc->krc", all_chosen.astype(bf16), got.reshape(dps, seqs, rank, lanes)
        )
        grads = [table[..., start : start + w] for start, w in zip(starts, widths)]
    if staged:
        grad0, output, away_g1, near_g1, pair_g1 = fence(grad0, output, away_g1, near_g1, pair_g1)
        grad_in = final_gradient(1, near_g1, pair_g1, away_g1, gri1, grad0)
    return (output, grad_in, grads[0], grads[1], grads[2], grads[3])


def solution(mesh):
    return jax.shard_map(
        per_device,
        mesh=mesh,
        in_specs=(
            P("dp", "seq", None),
            P("dp", "seq"),
            P("dp"),
            P(("dp", "seq")),
            P(("dp", "seq"), None),
            P(("dp", "seq"), None),
            P(("dp", "seq"), None),
            P(("dp", "seq")),
            P(),
            P(),
            P(),
            P(("dp", "seq")),
            P(("dp", "seq"), None),
            P(None, None, ("dp", "seq")),
            P(None, None, ("dp", "seq")),
            P(None, None, ("dp", "seq")),
            P(None, None, ("dp", "seq")),
            P("dp", "seq", None),
        ),
        out_specs=(
            P("dp", "seq", None),
            P("dp", "seq", None),
            P(None, None, ("dp", "seq")),
            P(None, None, ("dp", "seq")),
            P(None, None, ("dp", "seq")),
            P(None, None, ("dp", "seq")),
        ),
        check_vma=False,
    )
```

```python
import functools

import jax
import jax.numpy as jnp
from jax import lax
from jax.experimental import pallas as pl
from jax.experimental.pallas import tpu as pltpu
from jax.sharding import PartitionSpec as P

EPS = 1e-05
f32 = jnp.float32
bf16 = jnp.bfloat16
BLOCK = 256


def mm(form, a, b):
    return jnp.einsum(form, a, b, preferred_element_type=f32)


LOG2E = 1.4426950408889634
VMEM_BYTES = 66_000_000


def dot_nn(a, b):
    return lax.dot_general(a, b, (((1,), (0,)), ((), ())), preferred_element_type=f32)


def dot_nt(a, b):
    return lax.dot_general(a, b, (((1,), (1,)), ((), ())), preferred_element_type=f32)


def dot_tn(a, b):
    return lax.dot_general(a, b, (((0,), (0,)), ((), ())), preferred_element_type=f32)


def dot_exact(chosen, v):
    hi = v.astype(bf16)
    rest = v - hi.astype(f32)
    mid = rest.astype(bf16)
    lo = (rest - mid.astype(f32)).astype(bf16)
    return dot_nn(chosen, hi) + (dot_nn(chosen, mid) + dot_nn(chosen, lo))


def sigmoid(v):
    return 0.5 * jnp.tanh(0.5 * v) + 0.5


def spread_pair(cols, j):
    rows = cols.shape[0]
    lane = lax.broadcasted_iota(jnp.int32, (rows, 128), 1)
    return jnp.where(lane < 64, cols[:, 2 * j : 2 * j + 1], cols[:, 2 * j + 1 : 2 * j + 2])


def spread_all(cols, pairs):
    return jnp.concatenate([spread_pair(cols, j) for j in range(pairs)], 1)


def per_head(v, select):
    return dot_nn(v.astype(bf16), select)


def chunks_at(slot, slots, chunks):
    return [c for c in range(chunks) if c * slots // chunks == slot]


def by_rank(t, rank):
    out = t[:rank]
    for k in range(rank, 128, rank):
        out = out + t[k : k + rank]
    return out


def fold(v, rank):
    return by_rank(v.T, rank)


def shards(pieces, size):
    return [p.at[k : k + size] for p in pieces for k in range(0, p.shape[0], size)]


def assemble(order_ref, base, pieces, size, target, sems):
    copies = []
    for i, piece in enumerate(shards(pieces, size)):
        at = pl.multiple_of(order_ref[base + i] * size, 16)
        copies.append(pltpu.make_async_copy(piece, target.at[pl.ds(at, size)], sems.at[i]))
    for copy in copies:
        copy.start()
    for copy in copies:
        copy.wait()


def fetch(order_ref, b, blocks, s0, target, sem):
    for i, block in enumerate(blocks):

        @pl.when(order_ref[b] == i)
        def _(block=block):
            row = s0 if block.shape[0] > 1 else 0
            pltpu.make_async_copy(block.at[row], target, sem).start()


def arrived(blocks, target, sem):
    pltpu.make_async_copy(blocks[0].at[0], target, sem).wait()


def forward_kernel(order_ref, *refs, hn, hc, count, size, s0, keep):
    (x0, x1, x2, x3, meta_ref, doc_ref, up_ref, conv_ref, head_ref, mask_ref, half_ref) = refs[:11]
    pieces = refs[11 : 11 + count]
    normed_ref, rank_ref, vbc_ref, pre_ref, ssm_ref, state_ref, tok_ref, *rest = refs[11 + count :]
    if keep:
        full_ref, down_ref, gain_out, *rest = rest
    buf, carry, x_buf, wa_ref, gain_ref, pa_buf, normed_buf, sems, full_sem, x_sems = rest
    pairs = hn // 2
    cc = hc + 256
    b = pl.program_id(0)

    xs = (x0, x1, x2, x3)

    @pl.when(b == 0)
    def _():
        for k in (0, 1):
            fetch(order_ref, k, xs, s0, x_buf.at[k], x_sems.at[k])
        assemble(order_ref, 4, pieces, size, wa_ref, sems)
        if keep:
            pltpu.make_async_copy(wa_ref, full_ref, full_sem).start()
        gain_ref[...] = wa_ref[:, cc + 128 :].astype(f32).T[120:, :]
        if keep:
            down_ref[...] = wa_ref[:, cc : cc + 128]
            gain_out[...] = jnp.broadcast_to(gain_ref[7:8, :], gain_out.shape)
        carry[...] = jnp.zeros_like(carry)
        buf[0:8, :] = jnp.zeros((8, cc), f32)

    blocks = pl.num_programs(0)
    now, later = lax.rem(b, 2), lax.rem(b + 1, 2)
    chunks = wa_ref.shape[1] // 128
    chunks = chunks // 2 if chunks % 2 == 0 else chunks
    span = wa_ref.shape[1] // chunks

    def normalise(slot):
        x = x_buf[slot].astype(f32)
        inv = lax.rsqrt(jnp.mean(x * x, -1, keepdims=True) + EPS)
        normed_buf[slot] = (x * inv * gain_ref[7:8, :]).astype(bf16)

    def project(slot, c):
        at = slice(span * c, span * c + span)
        pa_buf[slot, :, at] = dot_nn(normed_buf[slot], wa_ref[:, at])

    @pl.when(b == 0)
    def _():
        arrived(xs, x_buf.at[0], x_sems.at[0])
        normalise(0)
        for c in range(chunks):
            project(0, c)

    @pl.when(b + 2 < blocks)
    def _():
        fetch(order_ref, b + 2, xs, s0, x_buf.at[now], x_sems.at[now])

    @pl.when(b + 1 < blocks)
    def _():
        arrived(xs, x_buf.at[later], x_sems.at[later])

    normalise(later)
    normed_ref[0] = normed_buf[now]
    rank = (pa_buf[now, :, cc : cc + 128] * mask_ref[0, 0:1, :]).astype(bf16)
    rank_ref[0] = rank
    conv_in = (pa_buf[now, :, :cc] + dot_nt(rank, up_ref[...])).astype(bf16).astype(f32)
    buf[8:, :] = conv_in
    meta = meta_ref[0]
    pre = conv_ref[4:5, :] + conv_ref[3:4, :] * conv_in
    for k in (1, 2, 3):
        pre = pre + conv_ref[3 - k : 4 - k, :] * (buf[8 - k : 8 - k + BLOCK, :] * meta[:, k - 1 : k])
    buf[0:8, :] = buf[BLOCK : BLOCK + 8, :]
    pre_ref[0] = pre
    vbc = (pre * sigmoid(pre)).astype(bf16)
    vbc_ref[0] = vbc
    values = vbc[:, :hc]
    in_state = vbc[:, hc : hc + 128]
    out_state = vbc[:, hc + 128 :]
    arg = pa_buf[now, :, cc + 128 : cc + 256] + head_ref[0:1, :]
    dt = jnp.maximum(arg, 0.0) + jnp.log1p(jnp.exp(-jnp.abs(arg)))
    row = lax.broadcasted_iota(jnp.int32, (BLOCK, BLOCK), 0)
    col = lax.broadcasted_iota(jnp.int32, (BLOCK, BLOCK), 1)
    cum = dot_exact((row >= col).astype(f32).astype(bf16), dt * head_ref[1:2, :])
    tok_ref[0, :, 0:128] = dt
    tok_ref[0, :, 128:256] = cum
    tok_ref[0, :, 256:384] = arg
    left = cum * LOG2E
    right = (left - jnp.log(jnp.maximum(dt, 1e-37)) * LOG2E).T
    ok = (row >= col) & (meta[:, 5:6] == doc_ref[0, 0])
    bias = jnp.where(ok, 0.0, -1e30)
    contact = dot_nt(out_state, in_state)
    entry = jnp.exp(cum) * meta[:, 3:4]
    weight = jnp.exp(cum[BLOCK - 1 :, :] - cum) * dt * meta[:, 4:5]
    state = carry[...]
    state_low = state.astype(bf16)
    state_ref[0, 0] = state_low
    readout = dot_nt(out_state, state_low)
    half = BLOCK // 2
    scaled = []
    for j in range(pairs):
        for c in range(j * chunks // pairs, (j + 1) * chunks // pairs):
            project(later, c)
        at = slice(128 * j, 128 * j + 128)
        v = values[:, at]
        ys = []
        for r0, c1 in ((0, half), (half, BLOCK)):
            ws = []
            for h in (2 * j, 2 * j + 1):
                e = jnp.exp2(
                    (left[r0 : r0 + half, h : h + 1] - right[h : h + 1, :c1])
                    + bias[r0 : r0 + half, :c1]
                )
                ws.append((contact[r0 : r0 + half, :c1] * e).astype(bf16))
            vv = jnp.concatenate([v[:c1] * half_ref[0:1, :], v[:c1] * half_ref[1:2, :]], 0)
            ys.append(dot_nn(jnp.concatenate(ws, 1), vv))
        y = jnp.concatenate(ys, 0)
        ssm_ref[0, :, at] = y + readout[:, at] * spread_pair(entry, j)
        scaled.append((v.astype(f32) * spread_pair(weight, j)).astype(bf16))
    local = dot_tn(jnp.concatenate(scaled, 1), in_state)
    passing = entry[BLOCK - 1 :, :]
    for h in range(hn):
        at = slice(64 * h, 64 * h + 64)
        carry[at, :] = passing[:, h : h + 1] * state[at] + local[at]

    if keep:

        @pl.when(b == pl.num_programs(0) - 1)
        def _():
            pltpu.make_async_copy(wa_ref, full_ref, full_sem).wait()


def route(order_ref, b, value, near_ref, pair_ref, far_ref):
    for k, target in enumerate(
        (near_ref, pair_ref.at[0:BLOCK], far_ref, pair_ref.at[BLOCK : 2 * BLOCK])
    ):

        @pl.when(order_ref[b] == k)
        def _(target=target):
            target[...] = value


def assemble_both(order_ref, base, pieces, rows, out_rows, wb_ref, wo_ref, sems):
    part = wb_ref.shape[1]
    copies = []
    for i, piece in enumerate(shards(pieces, rows + 2 * out_rows)):
        slot = order_ref[base + i]
        to = pl.ds(pl.multiple_of(slot * rows, 16), rows)
        to_out = pl.ds(pl.multiple_of(slot * out_rows, 16), out_rows)
        rest = wo_ref.shape[1] - part
        moves = (
            (piece.at[0:rows], wb_ref.at[to]),
            (piece.at[rows : rows + out_rows], wo_ref.at[to_out, 0:part]),
            (piece.at[rows + out_rows :, 0:rest], wo_ref.at[to_out, part : part + rest]),
        )
        for j, (source, target) in enumerate(moves):
            copies.append(pltpu.make_async_copy(source, target, sems.at[3 * i + j]))
    return copies


def middle_kernel(order_ref, *refs, hc, width, rank, count, keep, merged, s0):
    (
        normed_ref, rank_ref, vbc_ref, ssm_ref, og0, og1, og2, og3, up_ref, row_ref, mask_ref,
    ) = refs[:11]
    gate_pieces = refs[11 : 11 + count]
    after_gate = 11 + count
    out_pieces = () if merged else refs[after_gate : after_gate + count]
    first_out = after_gate + len(out_pieces)
    g_ref, q_ref, gro_ref, near_ref, pair_ref, far_ref, stat_ref, *rest = refs[first_out:]
    if keep:
        wb_full, wo_full, up_out_ref, *rest = rest
    og_buf, wb_ref, wo_ref, sems, more_sems, full_sems, og_sems = rest
    ogs = (og0, og1, og2, og3)
    b = pl.program_id(0)

    def keeping():
        return (
            pltpu.make_async_copy(wb_ref, wb_full, full_sems.at[0]),
            pltpu.make_async_copy(wo_ref, wo_full, full_sems.at[1]),
        )

    now, later = lax.rem(b, 2), lax.rem(b + 1, 2)
    if merged:
        copies = assemble_both(order_ref, 4, gate_pieces, *merged, wb_ref, wo_ref, sems)
        gate_copies = copies[::3]
        out_copies = [c for i, c in enumerate(copies) if i % 3]
    else:
        gate_copies = [pltpu.make_async_copy(gate_pieces[0], wb_ref, sems.at[0])]
        out_copies = [pltpu.make_async_copy(out_pieces[0], wo_ref, more_sems.at[0])]

    @pl.when(b == 0)
    def _():
        for copy in gate_copies:
            copy.start()
        fetch(order_ref, 0, ogs, s0, og_buf.at[0], og_sems.at[0])
        for copy in out_copies:
            copy.start()
        for copy in gate_copies:
            copy.wait()

    @pl.when(b + 1 < pl.num_programs(0))
    def _():
        fetch(order_ref, b + 1, ogs, s0, og_buf.at[later], og_sems.at[later])

    gate = dot_nn(normed_ref[0], wb_ref[:, :hc]) + dot_nt(rank_ref[0], up_ref[...])
    g_ref[0] = gate

    @pl.when(b == 0)
    def _():
        for copy in out_copies:
            copy.wait()
        if keep:
            up_out_ref[...] = wb_ref[:, hc:]
            for copy in keeping():
                copy.start()

    arrived(ogs, og_buf.at[now], og_sems.at[now])
    mixed = ssm_ref[0] + row_ref[0:1, :] * vbc_ref[0, :, :hc].astype(f32)
    gated = mixed * (gate * sigmoid(gate))
    og = og_buf[now]
    gro = (dot_nn(og, wb_ref[:, hc:]) * mask_ref[0, 0:1, :]).astype(bf16)
    gro_ref[0] = gro
    q = dot_nt(og, wo_ref[:, :width]) + dot_nt(gro, wo_ref[:, width : width + 128])
    q = q * row_ref[1:2, :]
    q_ref[0] = q
    lane = lax.broadcasted_iota(jnp.int32, (BLOCK, 128), 1)
    s0 = jnp.sum(gated * gated, -1, keepdims=True)
    s1 = jnp.sum(q * gated, -1, keepdims=True)
    stat_ref[0, 0:8, :] = jnp.where(lane == 0, s0, s1).T[:8]
    low = (gated * row_ref[1:2, :]).astype(bf16)
    route(order_ref, b, dot_nn(low, wo_ref[:, :width]).astype(bf16), near_ref, pair_ref, far_ref)
    stat_ref[0, 8:, :] = fold(dot_nn(low, wo_ref[:, width : width + 128]) * mask_ref[0, 0:1, :], rank)

    if keep:

        @pl.when(b == pl.num_programs(0) - 1)
        def _():
            for copy in keeping():
                copy.wait()


def backward_kernel(
    order_ref, q_ref, g_ref, ssm_ref, vbc_ref, pre_ref, tok_ref, rm_ref, meta_ref, doc_ref, state_ref, next_ref,
    rank_ref, gro_ref, conv_ref, head_ref, row_ref, half_ref, select_ref, upg_ref, upc_ref, mask_ref,
    wa_ref, wb_ref,
    near_ref, pair_ref, far_ref, grads_ref, gri_ref,
    buf, carry, held_gate, held_conv, held_step, part_buf,
    *, hn, hc, rank,
):
    pairs = hn // 2
    step = pl.program_id(0)
    blocks = pl.num_programs(0)
    chunks = part_buf.shape[1] // 256

    def product(c):
        rows = slice(256 * c, 256 * c + 256)
        part_buf[:, rows] = (
            dot_nt(held_gate[...], wb_ref[rows, :hc])
            + dot_nt(held_conv[...], wa_ref[rows, :cc])
            + dot_nt(held_step[...], wa_ref[rows, cc + 128 :])
        ).astype(bf16)

    cc = hc + 256
    first = pl.program_id(0) == 0

    @pl.when(first)
    def _():
        carry[...] = jnp.zeros_like(carry)
        buf[BLOCK:, :] = jnp.zeros((8, cc), f32)
        grads_ref[...] = jnp.zeros_like(grads_ref)

    slots = 3 + (pairs + 1) // 2

    def beside(slot):
        for c in chunks_at(slot, slots, chunks):
            product(c)

    beside(0)
    rm = jnp.concatenate([rm_ref[0]] * 16, 0).T
    inv = rm[:, 0:1]
    mean = rm[:, 1:2]
    meta = meta_ref[0]
    gate = g_ref[0]
    ssm = ssm_ref[0]
    q = q_ref[0]
    vbc = vbc_ref[0]
    values = vbc[:, :hc]
    values_f = values.astype(f32)
    in_state = vbc[:, hc : hc + 128]
    out_state = vbc[:, hc + 128 :]
    skip = row_ref[0:1, :]
    mixed = ssm + skip * values_f
    sg = sigmoid(gate)
    act = gate * sg
    gated = mixed * act
    gated_r = gated * inv
    grad_gated = inv * (q - gated_r * (inv * mean))
    gated_low = (gated_r * row_ref[1:2, :]).astype(bf16)
    grads_ref[0, :, hc + cc :] = grads_ref[0, :, hc + cc :] + by_rank(
        dot_tn(gro_ref[0], gated_low), rank
    )
    grad_mixed = grad_gated * act
    gp_gate = (grad_gated * mixed * (sg + act * (1.0 - sg))).astype(bf16)
    gsum = grad_mixed.astype(bf16)
    gsum_f = gsum.astype(f32)

    beside(1)
    dt = tok_ref[0, :, 0:128]
    cum = tok_ref[0, :, 128:256]
    arg = tok_ref[0, :, 256:384]
    scaled_cum = cum * LOG2E
    down = scaled_cum - jnp.log(jnp.maximum(dt, 1e-37)) * LOG2E
    across = scaled_cum.T
    row = lax.broadcasted_iota(jnp.int32, (BLOCK, BLOCK), 0)
    col = lax.broadcasted_iota(jnp.int32, (BLOCK, BLOCK), 1)
    ok = (col >= row) & (meta[:, 5:6] == doc_ref[0, 0])
    bias = jnp.where(ok, 0.0, -1e30)
    contact = dot_nt(in_state, out_state)
    entry = jnp.exp(cum) * meta[:, 3:4]
    weight = jnp.exp(cum[BLOCK - 1 :, :] - cum) * dt * meta[:, 4:5]
    later = carry[...]
    later_low = later.astype(bf16)
    grad_scaled = dot_nt(in_state, later_low)
    weight_wide = spread_all(weight, pairs)
    entry_wide = spread_all(entry, pairs)
    scaled = (values_f * weight_wide).astype(bf16)
    weighted = (gsum_f * entry_wide).astype(bf16)
    half = BLOCK // 2
    g_con = [jnp.zeros((half, BLOCK), f32), jnp.zeros((half, half), f32)]
    g_val = []
    for j in range(pairs):
        if j % 2 == 0:
            beside(2 + j // 2)
        at = slice(128 * j, 128 * j + 128)
        v = values[:, at]
        gs = gsum[:, at]
        tops = []
        for i, (r0, c0) in enumerate(((0, 0), (half, half))):
            ws = []
            for side in (0, 1):
                h = 2 * j + side
                gw = dot_nt(v[r0 : r0 + half] * half_ref[side : side + 1, :], gs[c0:])
                e = jnp.exp2(
                    (across[h : h + 1, c0:] - down[r0 : r0 + half, h : h + 1])
                    + bias[r0 : r0 + half, c0:]
                )
                ws.append((contact[r0 : r0 + half, c0:] * e).astype(bf16))
                g_con[i] = g_con[i] + gw * e
            gg = jnp.concatenate([gs[c0:] * half_ref[0:1, :], gs[c0:] * half_ref[1:2, :]], 0)
            tops.append(dot_nn(jnp.concatenate(ws, 1), gg))
        g_val.append(jnp.concatenate(tops, 0))
    g_val = jnp.concatenate(g_val, 1) + grad_scaled * weight_wide
    con_low = jnp.concatenate(
        [g_con[0], jnp.concatenate([jnp.zeros((half, half), f32), g_con[1]], 1)], 0
    ).astype(bf16)
    g_in = dot_nn(con_low, out_state) + dot_nn(scaled, later_low)
    g_out = dot_tn(con_low, in_state) + dot_nn(weighted, state_ref[0, 0])
    select = select_ref[...]
    spent = per_head(values_f * g_val, select)
    gained = per_head(gsum_f * ssm, select)
    ends = later * next_ref[0, 0].astype(f32)
    parts = [jnp.sum(ends[64 * h : 64 * h + 64], 0, keepdims=True) for h in range(hn)]
    parts.append(jnp.zeros((128 - hn, 128), f32))
    last = jnp.sum(jnp.concatenate(parts, 0).T, 0, keepdims=True)
    where_last = lax.broadcasted_iota(jnp.int32, (BLOCK, 128), 0) == BLOCK - 1
    grad_cum = gained - spent + jnp.where(where_last, last, 0.0)
    grad_log = dot_exact((col >= row).astype(f32).astype(bf16), grad_cum)
    sig = sigmoid(arg)
    g_step = (
        spent * (sig / jnp.maximum(dt, 1e-37)) + head_ref[1:2, :] * grad_log * sig
    ).astype(bf16)
    passing = entry[BLOCK - 1 :, :]
    direct = dot_tn(weighted, out_state)
    for h in range(hn):
        at = slice(64 * h, 64 * h + 64)
        carry[at, :] = passing[:, h : h + 1] * later[at] + direct[at]

    beside(slots - 1)
    pre = pre_ref[0]
    sp = sigmoid(pre)
    grad_out = jnp.concatenate([skip * grad_mixed + g_val, g_in, g_out], 1)
    grad_pre = grad_out * (sp + pre * sp * (1.0 - sp))
    buf[:BLOCK, :] = grad_pre
    total = conv_ref[3:4, :] * grad_pre
    for k in (1, 2, 3):
        total = total + conv_ref[3 - k : 4 - k, :] * (buf[k : k + BLOCK, :] * meta[:, 5 + k : 6 + k])
    buf[BLOCK:, :] = grad_pre[:8]
    gp_conv = total.astype(bf16)
    rows = rank_ref[0]
    grads_ref[0, :, :hc] = grads_ref[0, :, :hc] + by_rank(dot_tn(rows, gp_gate), rank)
    grads_ref[0, :, hc : hc + cc] = grads_ref[0, :, hc : hc + cc] + by_rank(
        dot_tn(rows, gp_conv), rank
    )
    gri_ref[0] = fold(
        (dot_nn(gp_gate, upg_ref[...]) + dot_nn(gp_conv, upc_ref[...])) * mask_ref[0, 0:1, :], rank
    )

    @pl.when(step > 0)
    def _():
        route(order_ref, blocks - step, part_buf[...], near_ref, pair_ref, far_ref)

    held_gate[...] = gp_gate
    held_conv[...] = gp_conv
    held_step[...] = g_step

    @pl.when(step == blocks - 1)
    def _():
        for c in range(chunks):
            product(c)
        route(order_ref, 0, part_buf[...], near_ref, pair_ref, far_ref)


def pack_weights_kernel(
    ip_ref, sp_ref, idn_ref, iup_ref, odn_ref, oup_ref, op_ref, cw_ref, cb_ref, idx_ref, gg_ref, tail_ref,
    a_ref, o_ref, small_ref,
    turn, misc,
    *, n, hn, hc, inner, planes,
):
    rows = ip_ref.shape[0]
    ranks = idn_ref.shape[0]
    up_rows = iup_ref.shape[1]

    def turned(ref):
        turn[...] = jnp.zeros_like(turn)
        turn[:, : ref.shape[1]] = ref[...].astype(f32)
        return turn[...].T

    down = turned(idn_ref)[:rows].astype(bf16)
    late = turned(oup_ref)[:rows].astype(bf16)
    step = jnp.concatenate([sp_ref[...].astype(f32), jnp.zeros((rows, 128 - n * hn), f32)], 1)
    lane = lax.broadcasted_iota(jnp.int32, (rows, 128), 1)
    chunk = hc // planes
    heads = hn // planes

    b_at = hc + 256 + ranks + 128

    def columns(base, t, to, at0):
        for p in range(0, planes, 2):
            got = []
            for q in (p, p + 1):
                start = base + (q * n + t) * chunk
                low = start // 128 * 128
                v = ip_ref[:, low : low + 256].astype(f32)
                got.append(pltpu.roll(v, 256 - (start - low), 1) if start > low else v)
            second = pltpu.roll(got[1], 64, 1)
            at = at0 + p * chunk
            a_ref[to, at : at + 128] = got[0][:, :128].astype(bf16)
            a_ref[to, at + 128 : at + 256] = jnp.where(
                lane < 64, got[0][:, 128:], second[:, :128]
            ).astype(bf16)
            a_ref[to, at + 256 : at + 384] = second[:, 128:].astype(bf16)

    for t in range(n):
        to = slice(t * rows, (t + 1) * rows)
        columns(inner, t, to, 0)
        a_ref[to, hc : hc + 256] = ip_ref[:, 2 * inner :]
        a_ref[to, hc + 256 : hc + 256 + ranks] = down
        last = tail_ref[...]
        for p in range(planes):
            shift = (p * heads - (p * n + t) * heads) % 128
            mine = pltpu.roll(step, shift, 1) if shift else step
            last = jnp.where((lane >= p * heads) & (lane < (p + 1) * heads), mine, last)
        a_ref[to, hc + 256 + ranks : b_at] = last.astype(bf16)
        columns(0, t, to, b_at)
        a_ref[to, b_at + hc :] = late
    out_rows, width = op_ref.shape
    part = o_ref.shape[1]
    o_ref[:out_rows, :] = op_ref[:, :part]
    o_ref[out_rows:, : width - part] = op_ref[:, part:]
    o_ref[out_rows:, width - part : width - part + ranks] = turned(odn_ref)[:out_rows].astype(bf16)
    o_ref[out_rows:, width - part + ranks :] = jnp.zeros(
        (out_rows, 2 * part - width - ranks), bf16
    )
    keep = -(-up_rows // 16) * 16
    small_ref[:keep, :] = turned(iup_ref)[:keep].astype(bf16)
    misc[...] = jnp.zeros_like(misc)
    misc[0:4, : cw_ref.shape[1]] = cw_ref[...].astype(f32)
    misc[4:5, : cb_ref.shape[1]] = cb_ref[...].astype(f32)
    misc[5:6, : idx_ref.shape[1]] = idx_ref[...].astype(f32)
    misc[6:7, : gg_ref.shape[1]] = gg_ref[...].astype(f32)
    small_ref[keep:, :] = misc[...].astype(bf16)


def unpack_kernel(
    order_ref, own_ref, far_ref, beside_ref,
    up_gate_ref, up_conv_ref, conv_ref, gain_ref, index_ref,
    held, up, conv, gains,
    *, n, planes, up_rows, rows, inner, hc, conv_rows, out_rows,
):
    size = own_ref.shape[0]
    sources = (own_ref, beside_ref.at[0:size], far_ref, beside_ref.at[size : 2 * size])
    for t in range(n):
        for i, source in enumerate(sources):

            @pl.when(order_ref[t] == i)
            def _(t=t, source=source):
                held[t] = source[...]

    conv[...] = jnp.zeros_like(conv)
    gains[...] = jnp.zeros_like(gains)
    keep = -(-up_rows // 16) * 16

    def add(target, v, start):
        low = start // 128 * 128
        v = jnp.concatenate([v, jnp.zeros_like(v)], 1)
        v = pltpu.roll(v, start - low, 1) if start > low else v
        target[:, low : low + 256] = target[:, low : low + 256] + v

    for t in range(n):
        for y in range(2):
            for z in range(planes):
                owner = (2 * z + y) * n + t
                base = (y * planes + z) * rows
                up[up_rows * owner : up_rows * (owner + 1), :] = held[
                    t, base : base + up_rows, :
                ].astype(f32)
                misc = held[t, base + keep : base + keep + 16, :].astype(f32)[:8]
                add(conv, misc, conv_rows * owner)
                add(gains, misc, out_rows * owner)
                index_ref[owner : owner + 1, :] = misc[5:6]
    here = order_ref[0]
    chunk = hc // planes
    for p in range(planes):
        start = pl.multiple_of((p * n + here) * chunk, 8)
        to = slice(p * chunk, (p + 1) * chunk)
        up_gate_ref[to, :] = up[pl.ds(start, chunk), :].astype(bf16)
        up_conv_ref[to, :] = up[pl.ds(inner + start, chunk), :].astype(bf16)
    up_conv_ref[hc:, :] = up[2 * inner :, :].astype(bf16)
    conv_ref[:, hc:] = conv[:, inner : inner + 256]
    lane = lax.broadcasted_iota(jnp.int32, (8, 128), 1)

    def select(source, target, t):
        for p in range(0, planes, 2):
            got = []
            for q in (p, p + 1):
                start = (q * n + t) * chunk
                low = start // 128 * 128
                v = source[:, low : low + 256]
                got.append(pltpu.roll(v, 256 - (start - low), 1) if start > low else v)
            second = pltpu.roll(got[1], 64, 1)
            at = p * chunk
            target[:, at : at + 128] = got[0][:, :128]
            target[:, at + 128 : at + 256] = jnp.where(lane < 64, got[0][:, 128:], second[:, :128])
            target[:, at + 256 : at + 384] = second[:, 128:]

    for t in range(n):

        @pl.when(here == t)
        def _(t=t):
            select(conv, conv_ref, t)
            select(gains, gain_ref, t)


def owners_kernel(chosen_ref, got_ref, *outs, rank, starts):
    sources, rows, _ = got_ref.shape
    for k in range(outs[0].shape[0]):
        total = None
        for d in range(sources):
            for b in range(rows // rank):
                term = chosen_ref[d * (rows // rank) + b, k] * got_ref[
                    d, b * rank : (b + 1) * rank, :
                ].astype(f32)
                total = term if total is None else total + term
        for out, start in zip(outs, starts):
            out[k] = total[:, start : start + out.shape[2]]


def final_kernel(*refs, held):
    near_ref, pair_ref, far_ref, rows_ref, down_ref, x_ref, og_ref, gain_ref = refs[:8]
    out_ref = refs[8 + held]
    wide = rows_ref[...].T.astype(bf16)
    grad = near_ref[...].astype(f32) + pair_ref[...].astype(f32) + far_ref[0].astype(f32)
    grad = grad + dot_nt(wide, down_ref[...])
    x = x_ref[0].astype(f32)
    inv = lax.rsqrt(jnp.mean(x * x, -1, keepdims=True) + EPS)
    scaled = grad * gain_ref[0:1, :]
    mean = jnp.mean(scaled * x, -1, keepdims=True)
    out_ref[0] = inv * (scaled - x * (inv * inv * mean)) + og_ref[0].astype(f32)


def pack_grads_kernel(
    order_ref, g0, g1, g2, g3, down_ref, out_ref, up, middle, total, *, n, hc, inner, width, widths, starts,
    planes,
):
    chunk = hc // planes
    lane = lax.broadcasted_iota(jnp.int32, (out_ref.shape[1], 128), 1)

    def place(g, source, target, base, t):
        for p in range(planes):
            low = (source + p * chunk) // 128 * 128
            v = g[:, low : low + 256].astype(f32)
            off = source + p * chunk - low
            v = pltpu.roll(v, 256 - off, 1) if off else v
            to = base + (p * n + t) * chunk
            if to % 128 == 0:
                target[:, to : to + chunk] = v[:, :chunk]
            else:
                v = pltpu.roll(v, 64, 1)
                here = slice(to - 64, to + 64)
                target[:, here] = jnp.where(lane < 64, target[:, here], v[:, :128])
                target[:, to + 64 : to + 192] = v[:, 128:]

    for t in range(n):
        for i, g in enumerate((g0, g1, g2, g3)):

            @pl.when(order_ref[t] == i)
            def _(t=t, g=g):
                place(g, 0, up, 0, t)
                place(g, hc, up, inner, t)
                place(g, 2 * hc + 256, middle, 0, t)

    def summed(at):
        first = g0[:, at].astype(f32) + g1[:, at].astype(f32)
        return first + (g2[:, at].astype(f32) + g3[:, at].astype(f32))

    up[:, 2 * inner : 2 * inner + 256] = summed(slice(2 * hc, 2 * hc + 256))
    total[:, :width] = summed(slice(3 * hc + 256, 3 * hc + 256 + width))
    sources = (None, up, middle, total)
    for t in range(n):

        @pl.when(order_ref[0] == t)
        def _(t=t):
            for d in range(out_ref.shape[0]):
                for ref, at, w in zip(sources, starts, widths):
                    start = (d * n + t) * w
                    low = start // 128 * 128
                    span = -(-w // 128) * 128
                    if ref is None:
                        window = down_ref[:, low : low + span + 128].astype(f32)
                    else:
                        window = ref[:, low : low + span + 128]
                    if start > low:
                        window = pltpu.roll(window, span + 128 - (start - low), 1)
                    out_ref[d, :, at : at + span] = window[:, :span].astype(bf16)


def swap(v, axis, bit):
    size = lax.axis_size(axis)
    return lax.ppermute(v, axis, [(i, i ^ bit) for i in range(size)])


def put(pieces):
    rows = pieces[0][0].shape[0]
    out = jnp.zeros((len(pieces) * rows, pieces[0][0].shape[1]), pieces[0][0].dtype)
    for piece, slot in pieces:
        out = lax.dynamic_update_slice_in_dim(out, piece, slot * rows, 0)
    return out


def rotate(v, r):
    size = lax.axis_size("dp")
    return lax.ppermute(v, "dp", [(i, (i + 2 * r) % size) for i in range(size)])


def after(v, *others):
    return lax.optimization_barrier((v, others))[0]


def fence(*values):
    return lax.optimization_barrier(values)


def others(v):
    return [swap(v, "seq", k) for k in (1, 2, 3)]


def total_of(v, got):
    return (v + got[0]) + (got[1] + got[2])


def across(far, pair):
    return (far.astype(f32) + pair[BLOCK:].astype(f32)).astype(bf16)


def own_sum(near, pair, far):
    return near.astype(f32) + pair[:BLOCK].astype(f32) + far.astype(f32)


def scatter_plain(near, pair, far):
    v = jnp.concatenate([near, pair[:BLOCK], far, pair[BLOCK:]], 0).astype(f32)
    return lax.psum_scatter(v, "seq", scatter_dimension=0, tiled=True)


def per_device(
    layer_input,
    document_index,
    adapter_index,
    input_norm_gain,
    input_projection,
    step_projection,
    convolution_weight,
    convolution_bias,
    head_step_bias,
    log_decay_rate,
    head_skip_gain,
    gated_norm_gain,
    output_projection,
    adapter_input_down,
    adapter_input_up,
    adapter_output_down,
    adapter_output_up,
    output_gradient,
):
    both = ("dp", "seq")
    dps, n = lax.axis_size("dp"), lax.axis_size("seq")
    here = lax.axis_index("seq")
    seqs, own_len, width = layer_input.shape
    adapters, rank, _ = adapter_input_down.shape
    ranks = adapters * rank
    heads = head_step_bias.shape[0]
    inner = output_projection.shape[0] * dps * n
    cols = input_projection.shape[1]
    state2 = cols - 2 * inner
    state = state2 // 2
    taps = convolution_weight.shape[1]
    hn = heads // n
    hc = inner // n
    hd = inner // heads
    length = own_len * n
    nb = length // BLOCK

    staged = n == 4 and dps == 8
    rows = input_projection.shape[0]
    conv_cols = hc + state2
    wa_cols = conv_cols + ranks + 128
    doc_cols = -(-seqs * own_len // rows)
    doc_block = document_index.astype(bf16).reshape(-1)
    doc_block = jnp.pad(doc_block, (0, rows * doc_cols - doc_block.shape[0])).reshape(rows, -1)
    tail = jnp.concatenate([doc_block, input_norm_gain[:, None]], 1)
    up_rows = adapter_input_up.shape[2]
    up_keep = -(-up_rows // 16) * 16
    conv_rows = convolution_weight.shape[0]
    wide = -(-conv_rows // 128) * 128
    misc_rows = 16
    small_rows = up_keep + misc_rows * wide // 128
    out_rows = output_projection.shape[0]
    planes = dps // 2 if staged else 1
    if staged:
        to_head = [
            (8 * z + 2 * t + y, 8 * z + 4 * y + t)
            for z in range(planes) for y in range(2) for t in range(n)
        ]
    else:
        to_head = [(dps * s + d, n * d + s) for d in range(dps) for s in range(n)]
    tables = [
        v.reshape(ranks, -1)
        for v in (adapter_input_down, adapter_input_up, adapter_output_down, adapter_output_up)
    ]
    if staged:
        tail = jnp.pad(tail.astype(f32), ((0, 0), (127 - doc_cols, 0)))
        payload, w_o, small = pl.pallas_call(
            functools.partial(
                pack_weights_kernel, n=n, hn=hn, hc=hc, inner=inner, planes=planes
            ),
            out_shape=[
                jax.ShapeDtypeStruct((n * rows, wa_cols + hc + ranks), bf16),
                jax.ShapeDtypeStruct((2 * out_rows, hc + ranks), bf16),
                jax.ShapeDtypeStruct((small_rows, 128), bf16),
            ],
            scratch_shapes=[pltpu.VMEM((128, 256), f32), pltpu.VMEM((misc_rows, 128), f32)],
            name="pack_weights",
        )(
            input_projection, step_projection, *tables[:2], *tables[2:], output_projection,
            convolution_weight.T, convolution_bias[None], adapter_index[None], gated_norm_gain[None], tail,
        )
    else:
        gap = jnp.zeros((rows, 127 - hn - doc_cols), bf16)
        payload = jnp.concatenate(
            [
                jnp.concatenate(
                    [
                        input_projection[:, inner + t * hc : inner + (t + 1) * hc],
                        input_projection[:, 2 * inner :],
                        tables[0].T,
                        step_projection[:, t * hn : (t + 1) * hn],
                        gap,
                        tail,
                    ],
                    1,
                )
                for t in range(n)
            ],
            0,
        )
        late_payload = jnp.concatenate(
            [
                jnp.concatenate([input_projection[:, t * hc : (t + 1) * hc], tables[3].T], 1)
                for t in range(n)
            ],
            0,
        )
        w_o = jnp.concatenate([output_projection, tables[2].T], 1)

        def as_row(v):
            return jnp.pad(v, ((0, 0), (0, wide - v.shape[1])))

        misc = jnp.concatenate(
            [
                as_row(convolution_weight.T),
                as_row(convolution_bias[None]),
                as_row(adapter_index.astype(bf16)[None]),
                as_row(gated_norm_gain[None]),
            ],
            0,
        )
        misc = jnp.pad(misc, ((0, misc_rows - misc.shape[0]), (0, 0)))
        small = jnp.concatenate(
            [jnp.pad(tables[1].T, ((0, up_keep - up_rows), (0, 0))), misc.reshape(-1, 128)], 0
        )
    w_a = lax.all_to_all(payload, "seq", 0, 0, tiled=True)

    if staged:
        d = lax.axis_index("dp")
        y, z = d % 2, d // 2
        w_o = lax.ppermute(w_o, both, to_head)
        turned = [rotate(small, r) for r in (1, 2, 3)]
        x_near = swap(layer_input, "seq", 1)
        w_a, small, turned, w_o, x_near = fence(w_a, small, turned, w_o, x_near)
        w_a, w_b = w_a[:, :wa_cols], w_a[:, wa_cols:]
        small = put([(small, z)] + [(v, lax.rem(z + 3 - r, 4)) for r, v in enumerate(turned)])
        a1, a3, a0y = rotate(w_a, 1), rotate(w_a, 3), swap(w_a, "dp", 1)
        small_y = swap(small, "dp", 1)
        x0 = after(layer_input, w_a)[:1]
        x_far0 = swap(x0, "seq", 2)
        x1, og = after(layer_input, w_a)[1:], after(output_gradient, w_a)
        og0, og1 = og[:1], og[1:]
        at = [2 * lax.rem(z + 4 - r, 4) + y for r in range(4)]
        slots = [at[0], at[0] ^ 1, at[1], at[3], at[1] ^ 1, at[3] ^ 1, at[2], at[2] ^ 1]
        slots = jnp.stack(slots).astype(jnp.int32)
        x_order = jnp.arange(4, dtype=jnp.int32) ^ here
    else:
        w_b = lax.all_to_all(late_payload, "seq", 0, 0, tiled=True)
        w_o = lax.ppermute(w_o, both, to_head)
        small = lax.all_gather(lax.all_gather(small, "dp", tiled=True), "seq", tiled=True)
        small = jnp.moveaxis(small.reshape(n, dps, small_rows, 128), 0, 1)
        wa_pieces = [lax.all_gather(w_a, "dp", tiled=True)]
        slots = jnp.zeros((1,), jnp.int32)
        x_order = jnp.arange(nb, dtype=jnp.int32)
        xs = [jnp.split(lax.all_gather(layer_input, "seq", axis=1, tiled=True), nb, axis=1)] * seqs
    docs = w_a[:, wa_cols - 1 - doc_cols : wa_cols - 1].reshape(n, -1)[:, : seqs * own_len]
    docs = jnp.moveaxis(docs.reshape(n, seqs, own_len), 0, 1).reshape(seqs, length)
    order = jnp.concatenate([x_order, slots])
    order_in = jnp.concatenate([x_order, jnp.stack([2 * slots, 2 * slots + 1], 1).reshape(-1)])
    order_whole = jnp.concatenate([x_order, jnp.zeros((1,), jnp.int32)])

    def mine(v):
        v = v.reshape(planes, n, v.shape[0] // (planes * n), *v.shape[1:])
        v = lax.dynamic_index_in_dim(v, here, 1, keepdims=False)
        return v.reshape(-1, *v.shape[2:])

    if not staged:
        small = small.reshape(dps * n, small_rows, 128)
        up_full = small[:, :up_rows].reshape(cols, ranks)
        misc = small[:, up_keep:].reshape(dps * n, misc_rows, wide)
        conv_w = jnp.moveaxis(misc[:, :taps, :conv_rows], 1, 0).reshape(taps, -1).astype(f32)
        conv_b = misc[:, taps, :conv_rows].reshape(-1).astype(f32)
        every_index = misc[:, taps + 1, :seqs].reshape(dps, n, seqs)[:, 0].astype(jnp.int32)
        gate_gain = misc[:, taps + 2, :out_rows].reshape(-1).astype(f32)

        up_gate = mine(up_full[:inner])
        up_conv = jnp.concatenate([mine(up_full[inner : 2 * inner]), up_full[2 * inner :]], 0)
        conv_w = jnp.concatenate([mine(conv_w.T[:inner]), conv_w.T[inner:]], 0).T
        conv_b = jnp.concatenate([mine(conv_b[:inner]), conv_b[inner:]], 0)
    step_bias = mine(head_step_bias)
    decay_rate = -jnp.exp(mine(log_decay_rate))
    skip = mine(head_skip_gain)
    gate_gain = None if staged else mine(gate_gain)

    chosen = (adapter_index[:, None] == jnp.arange(adapters, dtype=jnp.int32)[None, :]).astype(f32)
    mask = jnp.repeat(chosen, rank, axis=1)[:, None, :]

    doc_f = docs.astype(f32)

    def same_before(k):
        return jnp.pad(doc_f, ((0, 0), (k, 0)), constant_values=-1.0)[:, :length] == doc_f

    def same_after(k):
        return jnp.pad(doc_f, ((0, 0), (0, k)), constant_values=-1.0)[:, k:] == doc_f

    blocks = doc_f.reshape(seqs, nb, BLOCK)
    prior = jnp.concatenate([blocks[:, :1, 0], blocks[:, :-1, -1]], 1)
    keep = (blocks == prior[:, :, None]).reshape(seqs, length)
    ends = (blocks == blocks[:, :, -1:]).reshape(seqs, length)
    flags = [
        same_before(1), same_before(2), same_before(3), keep, ends, doc_f,
        same_after(1), same_after(2), same_after(3),
    ]
    meta = jnp.stack([v.astype(f32) for v in flags], -1)
    meta = jnp.pad(meta, ((0, 0), (0, 0), (0, 128 - len(flags))))
    doc_rows = blocks[:, :, None, :]

    def rows8(*vs):
        return jnp.pad(jnp.stack(vs), ((0, 8 - len(vs)), (0, 0)))

    if not staged:
        conv_rows8 = rows8(conv_w[0], conv_w[1], conv_w[2], conv_w[3], conv_b)
        wide_rows = rows8(jnp.repeat(skip, hd), gate_gain)
    head_rows = rows8(
        jnp.pad(step_bias, (0, 128 - hn)), jnp.pad(decay_rate, (0, 128 - hn))
    )
    halves = jnp.pad(
        (jnp.arange(128)[None, :] // 64 == jnp.arange(2)[:, None]).astype(bf16), ((0, 14), (0, 0))
    )
    select = (jnp.arange(hc)[:, None] // hd == jnp.arange(128)[None, :]).astype(bf16)
    mask8 = jnp.broadcast_to(mask, (seqs, 8, ranks))
    cc = conv_cols
    anywhere = pl.BlockSpec(memory_space=pl.ANY)
    params = pltpu.CompilerParams(
        dimension_semantics=("arbitrary",), vmem_limit_bytes=VMEM_BYTES
    )

    def at(w, k=0):
        return pl.BlockSpec((1, BLOCK, w), lambda b, o: (k, b, 0))

    def once(v, *block):
        block = block or v.shape
        return pl.BlockSpec(block, lambda b, o: (0,) * len(block), pipeline_mode=pl.Buffered(1))

    def of_seq(v, s0):
        k = s0 if v.shape[0] > 1 else 0
        return pl.BlockSpec(
            (1,) + v.shape[1:], lambda b, o: (k, 0, 0), pipeline_mode=pl.Buffered(1)
        )

    def one(w, dtype):
        return jax.ShapeDtypeStruct((1, length, w), dtype)

    def cost(flops, mib):
        return pl.CostEstimate(flops=int(flops), bytes_accessed=mib << 20, transcendentals=0)

    def parts_specs():
        return [once(None, BLOCK, width), once(None, 2 * BLOCK, width), once(None, BLOCK, width)]

    parts_shapes = [
        jax.ShapeDtypeStruct((k * BLOCK, width), bf16) for k in (1, 2, 1)
    ]

    def forward(s0, order, blocks, pieces, keep):
        whole_w = jax.ShapeDtypeStruct((width, wa_cols), bf16)
        size = n * rows // 2 if len(pieces) > 1 else width
        total = sum(v.shape[0] for v in pieces) // size
        return pl.pallas_call(
            functools.partial(
                forward_kernel, hn=hn, hc=hc, count=len(pieces), size=size, s0=s0, keep=keep
            ),
            grid_spec=pltpu.PrefetchScalarGridSpec(
                num_scalar_prefetch=1,
                grid=(nb,),
                in_specs=[
                    *([anywhere] * len(blocks)), at(128, s0),
                    pl.BlockSpec((1, 1, 1, BLOCK), lambda b, o: (s0, b, 0, 0)),
                    once(up_conv), once(conv_rows8), once(head_rows), of_seq(mask8, s0), once(halves),
                    *([anywhere] * len(pieces)),
                ],
                out_specs=[
                    at(width), at(128), at(cc), at(cc), at(hc),
                    pl.BlockSpec((1, 1, hc, state), lambda b, o: (0, b, 0, 0)), at(384),
                    *([anywhere, once(None, width, 128), once(None, 8, width)] if keep else []),
                ],
                scratch_shapes=[
                    pltpu.VMEM((BLOCK + 8, cc), f32), pltpu.VMEM((hc, state), f32),
                    pltpu.VMEM((2, BLOCK, width), bf16), pltpu.VMEM((width, wa_cols), bf16),
                    pltpu.VMEM((8, width), f32), pltpu.VMEM((2, BLOCK, wa_cols), f32),
                    pltpu.VMEM((2, BLOCK, width), bf16), pltpu.SemaphoreType.DMA((total,)),
                    pltpu.SemaphoreType.DMA, pltpu.SemaphoreType.DMA((2,)),
                ],
            ),
            out_shape=[
                one(width, bf16), one(128, bf16), one(cc, bf16), one(cc, f32), one(hc, f32),
                jax.ShapeDtypeStruct((1, nb, hc, state), bf16), one(384, f32),
                *(
                    [
                        whole_w, jax.ShapeDtypeStruct((width, 128), bf16),
                        jax.ShapeDtypeStruct((8, width), f32),
                    ]
                    if keep
                    else []
                ),
            ],
            compiler_params=params,
            name="ssm_forward",
            cost_estimate=cost(2 * length * (width * wa_cols + 3 * BLOCK * hc), 20),
        )(order, *blocks, meta, doc_rows, up_conv, conv_rows8, head_rows, mask8, halves, *pieces)

    def middle(s0, order, scanned, blocks, gate_pieces, out_pieces, keep):
        normed, rank_in, vbc, _, ssm = scanned[:5]
        count = len(gate_pieces)
        merged = () if out_pieces else (n * rows, out_rows)
        wb_shape, wo_shape = (width, hc + ranks), (hc, width + ranks)
        return pl.pallas_call(
            functools.partial(
                middle_kernel, hc=hc, width=width, rank=rank, count=count, keep=keep,
                merged=merged, s0=s0,
            ),
            grid_spec=pltpu.PrefetchScalarGridSpec(
                num_scalar_prefetch=1,
                grid=(nb,),
                in_specs=[
                    at(width), at(128), at(cc), at(hc), *([anywhere] * len(blocks)),
                    once(up_gate), once(wide_rows), of_seq(mask8, s0), *([anywhere] * (count + len(out_pieces))),
                ],
                out_specs=[
                    at(hc), at(hc), at(128), *parts_specs(),
                    pl.BlockSpec((1, 8 + rank, BLOCK), lambda b, o: (0, 0, b)),
                    *([anywhere, anywhere, once(None, width, 128)] if keep else []),
                ],
                scratch_shapes=[
                    pltpu.VMEM((2, BLOCK, width), bf16), pltpu.VMEM(wb_shape, bf16),
                    pltpu.VMEM(wo_shape, bf16), pltpu.SemaphoreType.DMA((3 * dps,)),
                    pltpu.SemaphoreType.DMA((count,)), pltpu.SemaphoreType.DMA((2,)),
                    pltpu.SemaphoreType.DMA((2,)),
                ],
            ),
            out_shape=[
                one(hc, f32), one(hc, f32), one(128, bf16), *parts_shapes,
                jax.ShapeDtypeStruct((1, 8 + rank, length), f32),
                *(
                    [jax.ShapeDtypeStruct(v, bf16) for v in (wb_shape, wo_shape, (width, 128))]
                    if keep
                    else []
                ),
            ],
            compiler_params=params,
            name="output_side",
            cost_estimate=cost(2 * length * width * hc * 3, 25),
        )(
            order, normed, rank_in, vbc, ssm, *blocks, up_gate, wide_rows, mask8, *gate_pieces,
            *out_pieces,
        )

    def backward(s0, scanned, gate, q, rm, grad_rank_out):
        _, rank_in, vbc, pre, ssm, states_low, tok = scanned[:7]

        def back(w, k=0):
            return pl.BlockSpec((1, BLOCK, w), lambda b, o: (k, nb - 1 - b, 0))

        def back_state(shift):
            return pl.BlockSpec(
                (1, 1, hc, state), lambda b, o: (0, jnp.minimum(nb - 1 - b + shift, nb - 1), 0, 0)
            )

        return pl.pallas_call(
            functools.partial(backward_kernel, hn=hn, hc=hc, rank=rank),
            grid_spec=pltpu.PrefetchScalarGridSpec(
                num_scalar_prefetch=1,
                grid=(nb,),
                in_specs=[
                    back(hc), back(hc), back(hc), back(cc), back(cc), back(384),
                    pl.BlockSpec((1, 8, BLOCK), lambda b, o: (0, 0, nb - 1 - b)), back(128, s0),
                    pl.BlockSpec((1, 1, 1, BLOCK), lambda b, o: (s0, nb - 1 - b, 0, 0)),
                    back_state(0), back_state(1), back(128), back(128), once(conv_rows8),
                    once(head_rows), once(wide_rows), once(halves), once(select), once(up_gate),
                    once(up_conv), of_seq(mask8, s0), once(wa), once(wb),
                ],
                out_specs=[
                    *parts_specs(), once(None, 1, rank, 2 * hc + cc),
                    pl.BlockSpec((1, rank, BLOCK), lambda b, o: (0, 0, nb - 1 - b)),
                ],
                scratch_shapes=[
                    pltpu.VMEM((BLOCK + 8, cc), f32), pltpu.VMEM((hc, state), f32),
                    pltpu.VMEM((BLOCK, hc), bf16), pltpu.VMEM((BLOCK, cc), bf16),
                    pltpu.VMEM((BLOCK, 128), bf16), pltpu.VMEM((BLOCK, width), bf16),
                ],
            ),
            out_shape=[
                *parts_shapes, jax.ShapeDtypeStruct((1, rank, 2 * hc + cc), f32),
                jax.ShapeDtypeStruct((1, rank, length), f32),
            ],
            compiler_params=params,
            name="ssm_backward",
            cost_estimate=cost(2 * length * (8 * BLOCK * hc + width * (hc + cc)), 30),
        )(
            x_order, q, gate, ssm, vbc, pre, tok, rm, meta, doc_rows, states_low, states_low, rank_in,
            grad_rank_out, conv_rows8, head_rows, wide_rows, halves, select, up_gate, up_conv, mask8,
            wa, wb,
        )

    def own_tokens(v, axis):
        return lax.dynamic_slice_in_dim(v, here * own_len, own_len, axis)

    def with_adapter(rows_of, table, s0):
        wide_rows_of = jnp.tile(rows_of, (adapters, 1)) * mask[s0, 0][:, None].astype(bf16)
        return mm("rt,dr->td", wide_rows_of, table)

    if staged:
        ready = (head_rows, meta, doc_rows, mask8, halves, select, order, order_whole, order_in, x1, og0, og1)
        a1, a3, a0y, w_a, small, small_y, x_far0, w_b, w_o, ready = fence(
            a1, a3, a0y, w_a, small, small_y, x_far0, w_b, w_o, ready
        )
        (
            head_rows, meta, doc_rows, mask8, halves, select, order, order_whole, order_in, x1, og0,
            og1,
        ) = ready
        mid = n * rows // 2
        a13y = swap(jnp.concatenate([a1, a3[:mid]]), "dp", 1)
        a2, a3y = rotate(a1, 1), rotate(a0y[mid:], 3)
        small = put([(small, y), (small_y, 1 - y)])
        small_far = swap(small, "seq", 2)
        x_both0 = swap(x_far0, "seq", 1)
        w_bo = jnp.concatenate([w_b, w_o])
        a2, a13y, a3y, small, small_far, x_both0, w_bo, x1 = fence(
            a2, a13y, a3y, small, small_far, x_both0, w_bo, x1
        )
        a2y = swap(a2, "dp", 1)
        beside = swap(jnp.concatenate([small, small_far]), "seq", 1)
        b1, b3 = rotate(w_bo, 1), rotate(w_bo, 3)
        x_far1 = swap(x1, "seq", 2)
        up_gate, up_conv, conv_rows8, gains, index_rows = pl.pallas_call(
            functools.partial(
                unpack_kernel, n=n, planes=planes, up_rows=up_rows, rows=small_rows, inner=inner,
                hc=hc, conv_rows=conv_rows, out_rows=out_rows,
            ),
            in_specs=[
                pl.BlockSpec(memory_space=pltpu.SMEM),
                *[pl.BlockSpec(memory_space=pltpu.VMEM)] * 3,
            ],
            out_specs=[pl.BlockSpec(memory_space=pltpu.VMEM)] * 5,
            out_shape=[
                jax.ShapeDtypeStruct((hc, ranks), bf16), jax.ShapeDtypeStruct((cc, ranks), bf16),
                jax.ShapeDtypeStruct((8, cc), f32), jax.ShapeDtypeStruct((8, hc), f32),
                jax.ShapeDtypeStruct((dps * n, 128), f32),
            ],
            scratch_shapes=[
                pltpu.VMEM((n, *small.shape), bf16), pltpu.VMEM((cols, ranks), f32),
                pltpu.VMEM((8, inner + state2 + 256), f32), pltpu.VMEM((8, inner + 256), f32),
            ],
            compiler_params=pltpu.CompilerParams(vmem_limit_bytes=VMEM_BYTES),
            name="unpack_small",
        )(x_order, small, small_far, beside)
        every_index = index_rows.reshape(dps, n, 128)[:, 0, :seqs].astype(jnp.int32)
        wide_rows = rows8(jnp.repeat(skip, hd), gains[6])
        wa_pieces = [w_a, a0y, a1, a3, a13y, a3y, a2, a2y]
        xs = [[layer_input, x_near, x_far0, x_both0]]
        wa_pieces, xs[0], w_bo, up_conv, up_gate, conv_rows8 = fence(
            wa_pieces, xs[0], w_bo, up_conv, up_gate, conv_rows8
        )
        *fwd0, wa, down_in, gain_rows = forward(0, order_in, xs[0], wa_pieces, True)
        b0y = swap(w_bo, "dp", 1)
        fwd0, wa, b1, b3, b0y, w_bo, x_far1 = fence(fwd0, wa, b1, b3, b0y, w_bo, x_far1)
        x_both1 = swap(x_far1, "seq", 1)
        x_both1, w_bo, og0, og1, og = fence(x_both1, w_bo, og0, og1, output_gradient)
        fwd1 = forward(1, order_whole, [layer_input, x_near, x_far1, x_both1], [wa], False)
        b1y, b3y_gate = swap(b1, "dp", 1), swap(b3[: n * rows], "dp", 1)
        b2, b3y_out = rotate(b1, 1), rotate(b0y[n * rows :], 3)
        og_far0 = swap(og0, "seq", 2)
        fwd1, b1y, b3y_gate, b3y_out, b2, og_far0, og, w_bo, og1 = fence(
            fwd1, b1y, b3y_gate, b3y_out, b2, og_far0, og, w_bo, og1
        )
        og_near = swap(og, "seq", 1)
        b3y = jnp.concatenate([b3y_gate, b3y_out])
        b2y_gate, b2y_out = swap(b2[: n * rows], "dp", 1), rotate(b1y[n * rows :], 1)
        b2y = jnp.concatenate([b2y_gate, b2y_out])
        og_both0 = swap(og_far0, "seq", 1)
        og_far1 = swap(og1, "seq", 2)
        fwd = [fwd0, fwd1]
        wb_pieces = [w_bo, b0y, b1, b3, b1y, b3y, b2, b2y]
        wo_pieces = []
        ogs = [[output_gradient, og_near, og_far0, og_both0]]
        wb_pieces, ogs[0], og_far1 = fence(wb_pieces, ogs[0], og_far1)
        og_both1 = swap(og_far1, "seq", 1)
    else:
        *fwd0, wa, down_in, gain_rows = forward(0, order, xs[0], wa_pieces, True)
        fwd = [fwd0]
        fwd += [forward(s0, order_whole, xs[s0], [wa], False) for s0 in range(1, seqs)]
        wb_pieces = [lax.all_gather(w_b, "dp", tiled=True)]
        wo_pieces = [lax.all_gather(w_o, "dp", tiled=True)]
        full = lax.all_gather(output_gradient, "seq", axis=1, tiled=True)
        ogs = [jnp.split(full, nb, axis=1)] * seqs

    def normalisers(stats):
        inv_gated = lax.rsqrt(stats[:1] / inner + EPS)
        rm = jnp.pad(jnp.concatenate([inv_gated, stats[1:2] / inner], 0), ((0, 6), (0, 0)))[None]
        return inv_gated, rm, own_tokens((stats[8:] * inv_gated).astype(bf16), 1)

    def layer_output(s0, branch, inv_gated, rank_out):
        return (
            layer_input[s0].astype(f32)
            + branch * own_tokens(inv_gated, 1).T
            + with_adapter(rank_out, up_out, s0)
        ).astype(bf16)

    def down_gradient(s0, grad_rank_in):
        return mm("rt,td->rd", grad_rank_in, fwd[s0][0][0]).astype(bf16)

    def layer_gradient(s0, partial, grad_rank_in):
        grad_normed = partial + with_adapter(
            own_tokens(grad_rank_in, 1), down_in, s0
        )
        own = layer_input[s0].astype(f32)
        inv_own = lax.rsqrt(jnp.mean(own * own, -1, keepdims=True) + EPS)
        scaled_in = grad_normed * gain_rows[0]
        return (
            inv_own * scaled_in
            - own * inv_own**3 * jnp.mean(scaled_in * own, -1, keepdims=True)
            + output_gradient[s0].astype(f32)
        )

    def final_gradient(s0, near, pair, far, grad_rank_in, earlier):
        rows_of = jnp.tile(own_tokens(grad_rank_in, 1).astype(f32), (adapters, 1)) * mask[s0, 0][:, None]

        tile_rows = 128
        mine_of_seq = pl.BlockSpec((1, tile_rows, width), lambda i: (s0, i, 0))
        by_rows = pl.BlockSpec((tile_rows, width), lambda i: (i, 0))

        def full(*block):
            return pl.BlockSpec(block, lambda i: (0,) * len(block))

        ins = [near, pair, far[None], rows_of, down_in, layer_input, output_gradient, gain_rows]
        specs = [
            by_rows, by_rows, pl.BlockSpec((1, tile_rows, width), lambda i: (0, i, 0)),
            pl.BlockSpec((ranks, tile_rows), lambda i: (0, i)), full(width, ranks), mine_of_seq,
            mine_of_seq, full(8, width),
        ]
        if earlier is not None:
            ins.append(earlier)
            specs.append(anywhere)
        return pl.pallas_call(
            functools.partial(final_kernel, held=len(ins) - 8),
            grid=(own_len // tile_rows,),
            in_specs=specs,
            out_specs=mine_of_seq,
            out_shape=jax.ShapeDtypeStruct((seqs, own_len, width), f32),
            input_output_aliases={8: 0} if earlier is not None else {},
            compiler_params=params,
            name="final_gradient",
            cost_estimate=cost(2 * BLOCK * width * ranks, 5),
        )(*ins)

    *side0, wb, wo, up_out = middle(0, order, fwd[0], ogs[0], wb_pieces, wo_pieces, True)
    if staged:
        side0, wb, wo, og_both1 = fence(side0, wb, wo, og_both1)
        ogs.append([output_gradient, og_near, og_far1, og_both1])
        gate0, q0, gro0, near0, pair0, far0, stats0 = side0
        side1 = middle(1, order_whole, fwd[1], ogs[1], [wb], [wo], False)
        got = others(stats0[0])
        pair0 = swap(pair0, "seq", 1)
        side1, got, pair0, far0 = fence(side1, got, pair0, far0)
        gate1, q1, gro1, near1, pair1, far1, stats1 = side1
        inv0, rm0, rank_out0 = normalisers(total_of(stats0[0], got))
        rm0, away, stats1, pair1 = fence(rm0, across(far0, pair0), stats1, pair1)

        back0 = backward(0, fwd[0], gate0, q0, rm0, gro0)
        away = swap(away, "seq", 2)
        got = others(stats1[0])
        pair1 = swap(pair1, "seq", 1)
        back0, away, got, pair1, far1 = fence(back0, away, got, pair1, far1)
        near_g0, pair_g0, far_g0, compact0, gri0 = back0
        pair_g0 = swap(pair_g0, "seq", 1)
        away0 = away
        inv1, rm1, rank_out1 = normalisers(total_of(stats1[0], got))
        rm1, away, gri0, away_g, away0, rank_out0, rank_out1 = fence(
            rm1, across(far1, pair1), gri0, across(far_g0, pair_g0), away0, rank_out0, rank_out1
        )

        back1 = backward(1, fwd[1], gate1, q1, rm1, gro1)
        away = swap(away, "seq", 2)
        away_g = swap(away_g, "seq", 2)
        got = others(gri0[0])
        back1, away, away_g, got, away0, rank_out0, rank_out1, near0, pair0, inv0 = fence(
            back1, away, away_g, got, away0, rank_out0, rank_out1, near0, pair0, inv0
        )
        near_g1, pair_g1, far_g1, compact1, gri1 = back1
        pair_g1 = swap(pair_g1, "seq", 1)
        got1 = others(gri1[0])
        g_out_up = mm("srt,std->srd", jnp.stack([rank_out0, rank_out1]), output_gradient)
        split = jnp.concatenate(
            [
                jnp.concatenate([compact0[0], compact1[0]]).astype(bf16),
                g_out_up.astype(bf16).reshape(seqs * rank, width),
            ],
            1,
        )
        away_g1, split, got1, got, gri0, near0, pair0, near1, pair1, near_g0, pair_g0, down_in = fence(
            across(far_g1, pair_g1), split, got1, got, gri0, near0, pair0, near1, pair1, near_g0,
            pair_g0, down_in,
        )
        away_g1 = swap(away_g1, "seq", 2)
        split_far = swap(split, "seq", 2)
        split_near = swap(split, "seq", 1)
        split_both = swap(split_far, "seq", 1)
        gri0 = total_of(gri0[0], got).astype(bf16)
        gri1 = total_of(gri1[0], got1).astype(bf16)
        downs = jnp.concatenate([down_gradient(0, gri0), down_gradient(1, gri1)])
        output0 = layer_output(0, own_sum(near0, pair0, away0), inv0, rank_out0)
        output1 = layer_output(1, own_sum(near1, pair1, away), inv1, rank_out1)
        grads_of_seq = [split, split_near, split_far, split_both]
        grads_order = x_order
    else:
        splits, downs, ranks_out, outputs, grads_in = [], [], [], [], []
        for s0 in range(seqs):
            if s0:
                side0 = middle(s0, order_whole, fwd[s0], ogs[s0], [wb], [wo], False)
            gate, q, gro, *parts, stats = side0
            inv_gated, rm, rank_out = normalisers(lax.psum(stats[0], "seq"))
            outputs.append(layer_output(s0, scatter_plain(*parts), inv_gated, rank_out))
            *parts, compacted, gri = backward(s0, fwd[s0], gate, q, rm, gro)
            gri = lax.psum(gri[0], "seq").astype(bf16)
            splits.append(compacted[0].astype(bf16))
            downs.append(down_gradient(s0, gri))
            ranks_out.append(rank_out)
            grads_in.append(layer_gradient(s0, scatter_plain(*parts), gri))
        g_out_up = mm("srt,std->srd", jnp.stack(ranks_out), output_gradient).astype(bf16)
        output = jnp.stack(outputs)
        grad_in = jnp.stack(grads_in)
        downs = jnp.concatenate(downs)
        split = jnp.concatenate(
            [jnp.concatenate(splits), g_out_up.reshape(seqs * rank, width)], 1
        )
        grads_of_seq = jnp.split(lax.all_gather(split, "seq", axis=0, tiled=True), n)

    widths = [v // (dps * n) for v in (width, cols, inner, width)]
    starts, lanes = [], 0
    for v in widths:
        starts.append(lanes)
        lanes += -(-v // 128) * 128
    pack_rows = seqs * rank
    if staged:
        packed = pl.pallas_call(
            functools.partial(
                pack_grads_kernel, n=n, hc=hc, inner=inner, width=width, widths=widths,
                starts=starts, planes=planes,
            ),
            in_specs=[
                pl.BlockSpec(memory_space=pltpu.SMEM),
                *[pl.BlockSpec(memory_space=pltpu.VMEM)] * 5,
            ],
            out_specs=pl.BlockSpec(memory_space=pltpu.VMEM),
            out_shape=jax.ShapeDtypeStruct((dps, pack_rows, lanes), bf16),
            scratch_shapes=[
                pltpu.VMEM((pack_rows, cols + 256), f32), pltpu.VMEM((pack_rows, inner + 256), f32),
                pltpu.VMEM((pack_rows, width + 256), f32),
            ],
            name="pack_grads",
        )(
            grads_order,
            *grads_of_seq, jnp.pad(downs, ((0, 0), (0, 256))),
        )
    else:
        pieces = jnp.stack(grads_of_seq)

        def by_heads(start):
            return jnp.concatenate([pieces[t, :, start : start + hc] for t in range(n)], -1)

        def summed(start, size):
            return pieces[..., start : start + size].astype(f32).sum(0).astype(bf16)

        full = [
            downs,
            jnp.concatenate([by_heads(0), by_heads(hc), summed(2 * hc, state2)], -1),
            by_heads(2 * hc + state2),
            summed(3 * hc + state2, width),
        ]
        packed = jnp.zeros((dps, pack_rows, lanes), bf16)
        for v, start, w in zip(full, starts, widths):
            v = lax.dynamic_index_in_dim(
                v.reshape(pack_rows, dps, n, w), here, 2, keepdims=False
            )
            packed = packed.at[:, :, start : start + w].set(v.transpose(1, 0, 2))
    if staged:
        packed, near_g0, pair_g0, away_g, gri0 = fence(packed, near_g0, pair_g0, away_g, gri0)
        grad0 = final_gradient(0, near_g0, pair_g0, away_g, gri0, None)
    got = lax.all_to_all(packed, "dp", 0, 0, tiled=True)
    if staged:
        output = jnp.stack([output0, output1])
    all_chosen = every_index[..., None] == jnp.arange(adapters)
    if staged:
        grads = pl.pallas_call(
            functools.partial(owners_kernel, rank=rank, starts=starts),
            in_specs=[
                pl.BlockSpec(memory_space=pltpu.SMEM), pl.BlockSpec(memory_space=pltpu.VMEM)
            ],
            out_specs=[pl.BlockSpec(memory_space=pltpu.VMEM)] * len(widths),
            out_shape=[jax.ShapeDtypeStruct((adapters, rank, w), f32) for w in widths],
            name="owners_sum",
        )(all_chosen.astype(f32).reshape(-1, adapters), got)
    else:
        table = mm(
            "dsk,dsrc->krc", all_chosen.astype(bf16), got.reshape(dps, seqs, rank, lanes)
        )
        grads = [table[..., start : start + w] for start, w in zip(starts, widths)]
    if staged:
        grad0, output, away_g1, near_g1, pair_g1 = fence(grad0, output, away_g1, near_g1, pair_g1)
        grad_in = final_gradient(1, near_g1, pair_g1, away_g1, gri1, grad0)
    return (output, grad_in, grads[0], grads[1], grads[2], grads[3])


def solution(mesh):
    return jax.shard_map(
        per_device,
        mesh=mesh,
        in_specs=(
            P("dp", "seq", None),
            P("dp", "seq"),
            P("dp"),
            P(("dp", "seq")),
            P(("dp", "seq"), None),
            P(("dp", "seq"), None),
            P(("dp", "seq"), None),
            P(("dp", "seq")),
            P(),
            P(),
            P(),
            P(("dp", "seq")),
            P(("dp", "seq"), None),
            P(None, None, ("dp", "seq")),
            P(None, None, ("dp", "seq")),
            P(None, None, ("dp", "seq")),
            P(None, None, ("dp", "seq")),
            P("dp", "seq", None),
        ),
        out_specs=(
            P("dp", "seq", None),
            P("dp", "seq", None),
            P(None, None, ("dp", "seq")),
            P(None, None, ("dp", "seq")),
            P(None, None, ("dp", "seq")),
            P(None, None, ("dp", "seq")),
        ),
        check_vma=False,
    )
```

```python
import functools

import jax
import jax.numpy as jnp
from jax import lax
from jax.experimental import pallas as pl
from jax.experimental.pallas import tpu as pltpu
from jax.sharding import PartitionSpec as P

EPS = 1e-05
f32 = jnp.float32
bf16 = jnp.bfloat16
BLOCK = 256


def mm(form, a, b):
    return jnp.einsum(form, a, b, preferred_element_type=f32)


LOG2E = 1.4426950408889634
VMEM_BYTES = 66_000_000


def dot_nn(a, b):
    return lax.dot_general(a, b, (((1,), (0,)), ((), ())), preferred_element_type=f32)


def dot_nt(a, b):
    return lax.dot_general(a, b, (((1,), (1,)), ((), ())), preferred_element_type=f32)


def dot_tn(a, b):
    return lax.dot_general(a, b, (((0,), (0,)), ((), ())), preferred_element_type=f32)


def dot_exact(chosen, v):
    hi = v.astype(bf16)
    rest = v - hi.astype(f32)
    mid = rest.astype(bf16)
    lo = (rest - mid.astype(f32)).astype(bf16)
    return dot_nn(chosen, hi) + (dot_nn(chosen, mid) + dot_nn(chosen, lo))


def sigmoid(v):
    return 0.5 * jnp.tanh(0.5 * v) + 0.5


def spread_pair(cols, j):
    rows = cols.shape[0]
    lane = lax.broadcasted_iota(jnp.int32, (rows, 128), 1)
    return jnp.where(lane < 64, cols[:, 2 * j : 2 * j + 1], cols[:, 2 * j + 1 : 2 * j + 2])


def spread_all(cols, pairs):
    return jnp.concatenate([spread_pair(cols, j) for j in range(pairs)], 1)


def per_head(v, select):
    return dot_nn(v.astype(bf16), select)


def chunks_at(slot, slots, chunks):
    return [c for c in range(chunks) if c * slots // chunks == slot]


def by_rank(t, rank):
    out = t[:rank]
    for k in range(rank, 128, rank):
        out = out + t[k : k + rank]
    return out


def fold(v, rank):
    return by_rank(v.T, rank)


def shards(pieces, size):
    return [p.at[k : k + size] for p in pieces for k in range(0, p.shape[0], size)]


def assemble(order_ref, base, pieces, size, target, sems):
    copies = []
    for i, piece in enumerate(shards(pieces, size)):
        at = pl.multiple_of(order_ref[base + i] * size, 16)
        copies.append(pltpu.make_async_copy(piece, target.at[pl.ds(at, size)], sems.at[i]))
    for copy in copies:
        copy.start()
    for copy in copies:
        copy.wait()


def fetch(order_ref, b, blocks, s0, target, sem):
    for i, block in enumerate(blocks):

        @pl.when(order_ref[b] == i)
        def _(block=block):
            row = s0 if block.shape[0] > 1 else 0
            pltpu.make_async_copy(block.at[row], target, sem).start()


def arrived(blocks, target, sem):
    pltpu.make_async_copy(blocks[0].at[0], target, sem).wait()


def forward_kernel(order_ref, *refs, hn, hc, count, size, s0, keep):
    (x0, x1, x2, x3, meta_ref, doc_ref, up_ref, conv_ref, head_ref, mask_ref, half_ref) = refs[:11]
    pieces = refs[11 : 11 + count]
    normed_ref, rank_ref, vbc_ref, pre_ref, ssm_ref, state_ref, tok_ref, *rest = refs[11 + count :]
    if keep:
        full_ref, down_ref, gain_out, *rest = rest
    buf, carry, x_buf, wa_ref, gain_ref, pa_buf, normed_buf, sems, full_sem, x_sems = rest
    pairs = hn // 2
    cc = hc + 256
    b = pl.program_id(0)

    xs = (x0, x1, x2, x3)

    @pl.when(b == 0)
    def _():
        for k in (0, 1):
            fetch(order_ref, k, xs, s0, x_buf.at[k], x_sems.at[k])
        assemble(order_ref, 4, pieces, size, wa_ref, sems)
        if keep:
            pltpu.make_async_copy(wa_ref, full_ref, full_sem).start()
        gain_ref[...] = wa_ref[:, cc + 128 :].astype(f32).T[120:, :]
        if keep:
            down_ref[...] = wa_ref[:, cc : cc + 128]
            gain_out[...] = jnp.broadcast_to(gain_ref[7:8, :], gain_out.shape)
        carry[...] = jnp.zeros_like(carry)
        buf[0:8, :] = jnp.zeros((8, cc), f32)

    blocks = pl.num_programs(0)
    now, later = lax.rem(b, 2), lax.rem(b + 1, 2)
    chunks = wa_ref.shape[1] // 128
    chunks = chunks // 2 if chunks % 2 == 0 else chunks
    span = wa_ref.shape[1] // chunks

    def normalise(slot):
        x = x_buf[slot].astype(f32)
        inv = lax.rsqrt(jnp.mean(x * x, -1, keepdims=True) + EPS)
        normed_buf[slot] = (x * inv * gain_ref[7:8, :]).astype(bf16)

    def project(slot, c):
        at = slice(span * c, span * c + span)
        pa_buf[slot, :, at] = dot_nn(normed_buf[slot], wa_ref[:, at])

    @pl.when(b == 0)
    def _():
        arrived(xs, x_buf.at[0], x_sems.at[0])
        normalise(0)
        for c in range(chunks):
            project(0, c)

    @pl.when(b + 2 < blocks)
    def _():
        fetch(order_ref, b + 2, xs, s0, x_buf.at[now], x_sems.at[now])

    @pl.when(b + 1 < blocks)
    def _():
        arrived(xs, x_buf.at[later], x_sems.at[later])

    normalise(later)
    normed_ref[0] = normed_buf[now]
    rank = (pa_buf[now, :, cc : cc + 128] * mask_ref[0, 0:1, :]).astype(bf16)
    rank_ref[0] = rank
    conv_in = (pa_buf[now, :, :cc] + dot_nt(rank, up_ref[...])).astype(bf16).astype(f32)
    buf[8:, :] = conv_in
    meta = meta_ref[0]
    pre = conv_ref[4:5, :] + conv_ref[3:4, :] * conv_in
    for k in (1, 2, 3):
        pre = pre + conv_ref[3 - k : 4 - k, :] * (buf[8 - k : 8 - k + BLOCK, :] * meta[:, k - 1 : k])
    buf[0:8, :] = buf[BLOCK : BLOCK + 8, :]
    pre_ref[0] = pre
    vbc = (pre * sigmoid(pre)).astype(bf16)
    vbc_ref[0] = vbc
    values = vbc[:, :hc]
    in_state = vbc[:, hc : hc + 128]
    out_state = vbc[:, hc + 128 :]
    arg = pa_buf[now, :, cc + 128 : cc + 256] + head_ref[0:1, :]
    dt = jnp.maximum(arg, 0.0) + jnp.log1p(jnp.exp(-jnp.abs(arg)))
    row = lax.broadcasted_iota(jnp.int32, (BLOCK, BLOCK), 0)
    col = lax.broadcasted_iota(jnp.int32, (BLOCK, BLOCK), 1)
    cum = dot_exact((row >= col).astype(f32).astype(bf16), dt * head_ref[1:2, :])
    tok_ref[0, :, 0:128] = dt
    tok_ref[0, :, 128:256] = cum
    tok_ref[0, :, 256:384] = arg
    left = cum * LOG2E
    right = (left - jnp.log(jnp.maximum(dt, 1e-37)) * LOG2E).T
    ok = (row >= col) & (meta[:, 5:6] == doc_ref[0, 0])
    bias = jnp.where(ok, 0.0, -1e30)
    contact = dot_nt(out_state, in_state)
    entry = jnp.exp(cum) * meta[:, 3:4]
    weight = jnp.exp(cum[BLOCK - 1 :, :] - cum) * dt * meta[:, 4:5]
    state = carry[...]
    state_low = state.astype(bf16)
    state_ref[0, 0] = state_low
    readout = dot_nt(out_state, state_low)
    half = BLOCK // 2
    scaled = []
    for j in range(pairs):
        for c in range(j * chunks // pairs, (j + 1) * chunks // pairs):
            project(later, c)
        at = slice(128 * j, 128 * j + 128)
        v = values[:, at]
        ys = []
        for r0, c1 in ((0, half), (half, BLOCK)):
            ws = []
            for h in (2 * j, 2 * j + 1):
                e = jnp.exp2(
                    (left[r0 : r0 + half, h : h + 1] - right[h : h + 1, :c1])
                    + bias[r0 : r0 + half, :c1]
                )
                ws.append((contact[r0 : r0 + half, :c1] * e).astype(bf16))
            vv = jnp.concatenate([v[:c1] * half_ref[0:1, :], v[:c1] * half_ref[1:2, :]], 0)
            ys.append(dot_nn(jnp.concatenate(ws, 1), vv))
        y = jnp.concatenate(ys, 0)
        ssm_ref[0, :, at] = y + readout[:, at] * spread_pair(entry, j)
        scaled.append((v.astype(f32) * spread_pair(weight, j)).astype(bf16))
    local = dot_tn(jnp.concatenate(scaled, 1), in_state)
    passing = entry[BLOCK - 1 :, :]
    for h in range(hn):
        at = slice(64 * h, 64 * h + 64)
        carry[at, :] = passing[:, h : h + 1] * state[at] + local[at]

    if keep:

        @pl.when(b == pl.num_programs(0) - 1)
        def _():
            pltpu.make_async_copy(wa_ref, full_ref, full_sem).wait()


def route(order_ref, b, value, near_ref, pair_ref, far_ref):
    for k, target in enumerate(
        (near_ref, pair_ref.at[0:BLOCK], far_ref, pair_ref.at[BLOCK : 2 * BLOCK])
    ):

        @pl.when(order_ref[b] == k)
        def _(target=target):
            target[...] = value


def assemble_both(order_ref, base, pieces, rows, out_rows, wb_ref, wo_ref, sems):
    part = wb_ref.shape[1]
    copies = []
    for i, piece in enumerate(shards(pieces, rows + 2 * out_rows)):
        slot = order_ref[base + i]
        to = pl.ds(pl.multiple_of(slot * rows, 16), rows)
        to_out = pl.ds(pl.multiple_of(slot * out_rows, 16), out_rows)
        rest = wo_ref.shape[1] - part
        moves = (
            (piece.at[0:rows], wb_ref.at[to]),
            (piece.at[rows : rows + out_rows], wo_ref.at[to_out, 0:part]),
            (piece.at[rows + out_rows :, 0:rest], wo_ref.at[to_out, part : part + rest]),
        )
        for j, (source, target) in enumerate(moves):
            copies.append(pltpu.make_async_copy(source, target, sems.at[3 * i + j]))
    return copies


def middle_kernel(order_ref, *refs, hc, width, rank, count, keep, merged, s0):
    (
        normed_ref, rank_ref, vbc_ref, ssm_ref, og0, og1, og2, og3, up_ref, row_ref, mask_ref,
    ) = refs[:11]
    gate_pieces = refs[11 : 11 + count]
    after_gate = 11 + count
    out_pieces = () if merged else refs[after_gate : after_gate + count]
    first_out = after_gate + len(out_pieces)
    g_ref, q_ref, gro_ref, near_ref, pair_ref, far_ref, stat_ref, *rest = refs[first_out:]
    if keep:
        wb_full, wo_full, up_out_ref, *rest = rest
    og_buf, wb_ref, wo_ref, sems, more_sems, full_sems, og_sems = rest
    ogs = (og0, og1, og2, og3)
    b = pl.program_id(0)

    def keeping():
        return (
            pltpu.make_async_copy(wb_ref, wb_full, full_sems.at[0]),
            pltpu.make_async_copy(wo_ref, wo_full, full_sems.at[1]),
        )

    now, later = lax.rem(b, 2), lax.rem(b + 1, 2)
    if merged:
        copies = assemble_both(order_ref, 4, gate_pieces, *merged, wb_ref, wo_ref, sems)
        gate_copies = copies[::3]
        out_copies = [c for i, c in enumerate(copies) if i % 3]
    else:
        gate_copies = [pltpu.make_async_copy(gate_pieces[0], wb_ref, sems.at[0])]
        out_copies = [pltpu.make_async_copy(out_pieces[0], wo_ref, more_sems.at[0])]

    @pl.when(b == 0)
    def _():
        for copy in gate_copies:
            copy.start()
        fetch(order_ref, 0, ogs, s0, og_buf.at[0], og_sems.at[0])
        for copy in out_copies:
            copy.start()
        for copy in gate_copies:
            copy.wait()

    @pl.when(b + 1 < pl.num_programs(0))
    def _():
        fetch(order_ref, b + 1, ogs, s0, og_buf.at[later], og_sems.at[later])

    gate = dot_nn(normed_ref[0], wb_ref[:, :hc]) + dot_nt(rank_ref[0], up_ref[...])
    g_ref[0] = gate

    @pl.when(b == 0)
    def _():
        for copy in out_copies:
            copy.wait()
        if keep:
            up_out_ref[...] = wb_ref[:, hc:]
            for copy in keeping():
                copy.start()

    arrived(ogs, og_buf.at[now], og_sems.at[now])
    mixed = ssm_ref[0] + row_ref[0:1, :] * vbc_ref[0, :, :hc].astype(f32)
    gated = mixed * (gate * sigmoid(gate))
    og = og_buf[now]
    gro = (dot_nn(og, wb_ref[:, hc:]) * mask_ref[0, 0:1, :]).astype(bf16)
    gro_ref[0] = gro
    q = dot_nt(og, wo_ref[:, :width]) + dot_nt(gro, wo_ref[:, width : width + 128])
    q = q * row_ref[1:2, :]
    q_ref[0] = q
    lane = lax.broadcasted_iota(jnp.int32, (BLOCK, 128), 1)
    s0 = jnp.sum(gated * gated, -1, keepdims=True)
    s1 = jnp.sum(q * gated, -1, keepdims=True)
    stat_ref[0, 0:8, :] = jnp.where(lane == 0, s0, s1).T[:8]
    low = (gated * row_ref[1:2, :]).astype(bf16)
    route(order_ref, b, dot_nn(low, wo_ref[:, :width]).astype(bf16), near_ref, pair_ref, far_ref)
    stat_ref[0, 8:, :] = fold(dot_nn(low, wo_ref[:, width : width + 128]) * mask_ref[0, 0:1, :], rank)

    if keep:

        @pl.when(b == pl.num_programs(0) - 1)
        def _():
            for copy in keeping():
                copy.wait()


def backward_kernel(
    order_ref, q_ref, g_ref, ssm_ref, vbc_ref, pre_ref, tok_ref, rm_ref, meta_ref, doc_ref, state_ref, next_ref,
    rank_ref, gro_ref, conv_ref, head_ref, row_ref, half_ref, select_ref, upg_ref, upc_ref, mask_ref,
    wa_ref, wb_ref,
    near_ref, pair_ref, far_ref, grads_ref, gri_ref,
    buf, carry, held_gate, held_conv, held_step, part_buf,
    *, hn, hc, rank,
):
    pairs = hn // 2
    step = pl.program_id(0)
    blocks = pl.num_programs(0)
    chunks = part_buf.shape[1] // 256

    def product(c):
        rows = slice(256 * c, 256 * c + 256)
        part_buf[:, rows] = (
            dot_nt(held_gate[...], wb_ref[rows, :hc])
            + dot_nt(held_conv[...], wa_ref[rows, :cc])
            + dot_nt(held_step[...], wa_ref[rows, cc + 128 :])
        ).astype(bf16)

    cc = hc + 256
    first = pl.program_id(0) == 0

    @pl.when(first)
    def _():
        carry[...] = jnp.zeros_like(carry)
        buf[BLOCK:, :] = jnp.zeros((8, cc), f32)
        grads_ref[...] = jnp.zeros_like(grads_ref)

    slots = 3 + (pairs + 1) // 2

    def beside(slot):
        for c in chunks_at(slot, slots, chunks):
            product(c)

    beside(0)
    rm = jnp.concatenate([rm_ref[0]] * 16, 0).T
    inv = rm[:, 0:1]
    mean = rm[:, 1:2]
    meta = meta_ref[0]
    gate = g_ref[0]
    ssm = ssm_ref[0]
    q = q_ref[0]
    vbc = vbc_ref[0]
    values = vbc[:, :hc]
    values_f = values.astype(f32)
    in_state = vbc[:, hc : hc + 128]
    out_state = vbc[:, hc + 128 :]
    skip = row_ref[0:1, :]
    mixed = ssm + skip * values_f
    sg = sigmoid(gate)
    act = gate * sg
    gated = mixed * act
    gated_r = gated * inv
    grad_gated = inv * (q - gated_r * (inv * mean))
    gated_low = (gated_r * row_ref[1:2, :]).astype(bf16)
    grads_ref[0, :, hc + cc :] = grads_ref[0, :, hc + cc :] + by_rank(
        dot_tn(gro_ref[0], gated_low), rank
    )
    grad_mixed = grad_gated * act
    gp_gate = (grad_gated * mixed * (sg + act * (1.0 - sg))).astype(bf16)
    gsum = grad_mixed.astype(bf16)
    gsum_f = gsum.astype(f32)

    beside(1)
    dt = tok_ref[0, :, 0:128]
    cum = tok_ref[0, :, 128:256]
    arg = tok_ref[0, :, 256:384]
    scaled_cum = cum * LOG2E
    down = scaled_cum - jnp.log(jnp.maximum(dt, 1e-37)) * LOG2E
    across = scaled_cum.T
    row = lax.broadcasted_iota(jnp.int32, (BLOCK, BLOCK), 0)
    col = lax.broadcasted_iota(jnp.int32, (BLOCK, BLOCK), 1)
    ok = (col >= row) & (meta[:, 5:6] == doc_ref[0, 0])
    bias = jnp.where(ok, 0.0, -1e30)
    contact = dot_nt(in_state, out_state)
    entry = jnp.exp(cum) * meta[:, 3:4]
    weight = jnp.exp(cum[BLOCK - 1 :, :] - cum) * dt * meta[:, 4:5]
    later = carry[...]
    later_low = later.astype(bf16)
    grad_scaled = dot_nt(in_state, later_low)
    weight_wide = spread_all(weight, pairs)
    entry_wide = spread_all(entry, pairs)
    scaled = (values_f * weight_wide).astype(bf16)
    weighted = (gsum_f * entry_wide).astype(bf16)
    half = BLOCK // 2
    g_con = [jnp.zeros((half, BLOCK), f32), jnp.zeros((half, half), f32)]
    g_val = []
    for j in range(pairs):
        if j % 2 == 0:
            beside(2 + j // 2)
        at = slice(128 * j, 128 * j + 128)
        v = values[:, at]
        gs = gsum[:, at]
        tops = []
        for i, (r0, c0) in enumerate(((0, 0), (half, half))):
            ws = []
            for side in (0, 1):
                h = 2 * j + side
                gw = dot_nt(v[r0 : r0 + half] * half_ref[side : side + 1, :], gs[c0:])
                e = jnp.exp2(
                    (across[h : h + 1, c0:] - down[r0 : r0 + half, h : h + 1])
                    + bias[r0 : r0 + half, c0:]
                )
                ws.append((contact[r0 : r0 + half, c0:] * e).astype(bf16))
                g_con[i] = g_con[i] + gw * e
            gg = jnp.concatenate([gs[c0:] * half_ref[0:1, :], gs[c0:] * half_ref[1:2, :]], 0)
            tops.append(dot_nn(jnp.concatenate(ws, 1), gg))
        g_val.append(jnp.concatenate(tops, 0))
    g_val = jnp.concatenate(g_val, 1) + grad_scaled * weight_wide
    con_low = jnp.concatenate(
        [g_con[0], jnp.concatenate([jnp.zeros((half, half), f32), g_con[1]], 1)], 0
    ).astype(bf16)
    g_in = dot_nn(con_low, out_state) + dot_nn(scaled, later_low)
    g_out = dot_tn(con_low, in_state) + dot_nn(weighted, state_ref[0, 0])
    select = select_ref[...]
    spent = per_head(values_f * g_val, select)
    gained = per_head(gsum_f * ssm, select)
    ends = later * next_ref[0, 0].astype(f32)
    parts = [jnp.sum(ends[64 * h : 64 * h + 64], 0, keepdims=True) for h in range(hn)]
    parts.append(jnp.zeros((128 - hn, 128), f32))
    last = jnp.sum(jnp.concatenate(parts, 0).T, 0, keepdims=True)
    where_last = lax.broadcasted_iota(jnp.int32, (BLOCK, 128), 0) == BLOCK - 1
    grad_cum = gained - spent + jnp.where(where_last, last, 0.0)
    grad_log = dot_exact((col >= row).astype(f32).astype(bf16), grad_cum)
    sig = sigmoid(arg)
    g_step = (
        spent * (sig / jnp.maximum(dt, 1e-37)) + head_ref[1:2, :] * grad_log * sig
    ).astype(bf16)
    passing = entry[BLOCK - 1 :, :]
    direct = dot_tn(weighted, out_state)
    for h in range(hn):
        at = slice(64 * h, 64 * h + 64)
        carry[at, :] = passing[:, h : h + 1] * later[at] + direct[at]

    beside(slots - 1)
    pre = pre_ref[0]
    sp = sigmoid(pre)
    grad_out = jnp.concatenate([skip * grad_mixed + g_val, g_in, g_out], 1)
    grad_pre = grad_out * (sp + pre * sp * (1.0 - sp))
    buf[:BLOCK, :] = grad_pre
    total = conv_ref[3:4, :] * grad_pre
    for k in (1, 2, 3):
        total = total + conv_ref[3 - k : 4 - k, :] * (buf[k : k + BLOCK, :] * meta[:, 5 + k : 6 + k])
    buf[BLOCK:, :] = grad_pre[:8]
    gp_conv = total.astype(bf16)
    rows = rank_ref[0]
    grads_ref[0, :, :hc] = grads_ref[0, :, :hc] + by_rank(dot_tn(rows, gp_gate), rank)
    grads_ref[0, :, hc : hc + cc] = grads_ref[0, :, hc : hc + cc] + by_rank(
        dot_tn(rows, gp_conv), rank
    )
    gri_ref[0] = fold(
        (dot_nn(gp_gate, upg_ref[...]) + dot_nn(gp_conv, upc_ref[...])) * mask_ref[0, 0:1, :], rank
    )

    @pl.when(step > 0)
    def _():
        route(order_ref, blocks - step, part_buf[...], near_ref, pair_ref, far_ref)

    held_gate[...] = gp_gate
    held_conv[...] = gp_conv
    held_step[...] = g_step

    @pl.when(step == blocks - 1)
    def _():
        for c in range(chunks):
            product(c)
        route(order_ref, 0, part_buf[...], near_ref, pair_ref, far_ref)


def pack_weights_kernel(
    ip_ref, sp_ref, idn_ref, iup_ref, odn_ref, oup_ref, op_ref, cw_ref, cb_ref, idx_ref, gg_ref, tail_ref,
    a_ref, o_ref, small_ref,
    turn, misc,
    *, n, hn, hc, inner, planes,
):
    rows = ip_ref.shape[0]
    ranks = idn_ref.shape[0]
    up_rows = iup_ref.shape[1]

    def turned(ref):
        turn[...] = jnp.zeros_like(turn)
        turn[:, : ref.shape[1]] = ref[...].astype(f32)
        return turn[...].T

    down = turned(idn_ref)[:rows].astype(bf16)
    late = turned(oup_ref)[:rows].astype(bf16)
    step = jnp.concatenate([sp_ref[...].astype(f32), jnp.zeros((rows, 128 - n * hn), f32)], 1)
    lane = lax.broadcasted_iota(jnp.int32, (rows, 128), 1)
    chunk = hc // planes
    heads = hn // planes

    b_at = hc + 256 + ranks + 128

    def columns(base, t, to, at0):
        for p in range(0, planes, 2):
            got = []
            for q in (p, p + 1):
                start = base + (q * n + t) * chunk
                low = start // 128 * 128
                v = ip_ref[:, low : low + 256].astype(f32)
                got.append(pltpu.roll(v, 256 - (start - low), 1) if start > low else v)
            second = pltpu.roll(got[1], 64, 1)
            at = at0 + p * chunk
            a_ref[to, at : at + 128] = got[0][:, :128].astype(bf16)
            a_ref[to, at + 128 : at + 256] = jnp.where(
                lane < 64, got[0][:, 128:], second[:, :128]
            ).astype(bf16)
            a_ref[to, at + 256 : at + 384] = second[:, 128:].astype(bf16)

    for t in range(n):
        to = slice(t * rows, (t + 1) * rows)
        columns(inner, t, to, 0)
        a_ref[to, hc : hc + 256] = ip_ref[:, 2 * inner :]
        a_ref[to, hc + 256 : hc + 256 + ranks] = down
        last = tail_ref[...]
        for p in range(planes):
            shift = (p * heads - (p * n + t) * heads) % 128
            mine = pltpu.roll(step, shift, 1) if shift else step
            last = jnp.where((lane >= p * heads) & (lane < (p + 1) * heads), mine, last)
        a_ref[to, hc + 256 + ranks : b_at] = last.astype(bf16)
        columns(0, t, to, b_at)
        a_ref[to, b_at + hc :] = late
    out_rows, width = op_ref.shape
    part = o_ref.shape[1]
    o_ref[:out_rows, :] = op_ref[:, :part]
    o_ref[out_rows:, : width - part] = op_ref[:, part:]
    o_ref[out_rows:, width - part : width - part + ranks] = turned(odn_ref)[:out_rows].astype(bf16)
    o_ref[out_rows:, width - part + ranks :] = jnp.zeros(
        (out_rows, 2 * part - width - ranks), bf16
    )
    keep = -(-up_rows // 16) * 16
    small_ref[:keep, :] = turned(iup_ref)[:keep].astype(bf16)
    misc[...] = jnp.zeros_like(misc)
    misc[0:4, : cw_ref.shape[1]] = cw_ref[...].astype(f32)
    misc[4:5, : cb_ref.shape[1]] = cb_ref[...].astype(f32)
    misc[5:6, : idx_ref.shape[1]] = idx_ref[...].astype(f32)
    misc[6:7, : gg_ref.shape[1]] = gg_ref[...].astype(f32)
    small_ref[keep:, :] = misc[...].astype(bf16)


def unpack_kernel(
    order_ref, own_ref, far_ref, beside_ref,
    up_gate_ref, up_conv_ref, conv_ref, gain_ref, index_ref,
    held, up, conv, gains,
    *, n, planes, up_rows, rows, inner, hc, conv_rows, out_rows,
):
    size = own_ref.shape[0]
    sources = (own_ref, beside_ref.at[0:size], far_ref, beside_ref.at[size : 2 * size])
    for t in range(n):
        for i, source in enumerate(sources):

            @pl.when(order_ref[t] == i)
            def _(t=t, source=source):
                held[t] = source[...]

    conv[...] = jnp.zeros_like(conv)
    gains[...] = jnp.zeros_like(gains)
    keep = -(-up_rows // 16) * 16

    def add(target, v, start):
        low = start // 128 * 128
        v = jnp.concatenate([v, jnp.zeros_like(v)], 1)
        v = pltpu.roll(v, start - low, 1) if start > low else v
        target[:, low : low + 256] = target[:, low : low + 256] + v

    for t in range(n):
        for y in range(2):
            for z in range(planes):
                owner = (2 * z + y) * n + t
                base = (y * planes + z) * rows
                up[up_rows * owner : up_rows * (owner + 1), :] = held[
                    t, base : base + up_rows, :
                ].astype(f32)
                misc = held[t, base + keep : base + keep + 16, :].astype(f32)[:8]
                add(conv, misc, conv_rows * owner)
                add(gains, misc, out_rows * owner)
                index_ref[owner : owner + 1, :] = misc[5:6]
    here = order_ref[0]
    chunk = hc // planes
    for p in range(planes):
        start = pl.multiple_of((p * n + here) * chunk, 8)
        to = slice(p * chunk, (p + 1) * chunk)
        up_gate_ref[to, :] = up[pl.ds(start, chunk), :].astype(bf16)
        up_conv_ref[to, :] = up[pl.ds(inner + start, chunk), :].astype(bf16)
    up_conv_ref[hc:, :] = up[2 * inner :, :].astype(bf16)
    conv_ref[:, hc:] = conv[:, inner : inner + 256]
    lane = lax.broadcasted_iota(jnp.int32, (8, 128), 1)

    def select(source, target, t):
        for p in range(0, planes, 2):
            got = []
            for q in (p, p + 1):
                start = (q * n + t) * chunk
                low = start // 128 * 128
                v = source[:, low : low + 256]
                got.append(pltpu.roll(v, 256 - (start - low), 1) if start > low else v)
            second = pltpu.roll(got[1], 64, 1)
            at = p * chunk
            target[:, at : at + 128] = got[0][:, :128]
            target[:, at + 128 : at + 256] = jnp.where(lane < 64, got[0][:, 128:], second[:, :128])
            target[:, at + 256 : at + 384] = second[:, 128:]

    for t in range(n):

        @pl.when(here == t)
        def _(t=t):
            select(conv, conv_ref, t)
            select(gains, gain_ref, t)


def owners_kernel(chosen_ref, got_ref, *outs, rank, starts):
    sources, rows, _ = got_ref.shape
    for k in range(outs[0].shape[0]):
        total = None
        for d in range(sources):
            for b in range(rows // rank):
                term = chosen_ref[d * (rows // rank) + b, k] * got_ref[
                    d, b * rank : (b + 1) * rank, :
                ].astype(f32)
                total = term if total is None else total + term
        for out, start in zip(outs, starts):
            out[k] = total[:, start : start + out.shape[2]]


def final_kernel(*refs, held):
    near_ref, pair_ref, far_ref, rows_ref, down_ref, x_ref, og_ref, gain_ref = refs[:8]
    out_ref = refs[8 + held]
    wide = rows_ref[...].T.astype(bf16)
    grad = near_ref[...].astype(f32) + pair_ref[...].astype(f32) + far_ref[0].astype(f32)
    grad = grad + dot_nt(wide, down_ref[...])
    x = x_ref[0].astype(f32)
    inv = lax.rsqrt(jnp.mean(x * x, -1, keepdims=True) + EPS)
    scaled = grad * gain_ref[0:1, :]
    mean = jnp.mean(scaled * x, -1, keepdims=True)
    out_ref[0] = inv * (scaled - x * (inv * inv * mean)) + og_ref[0].astype(f32)


def pack_grads_kernel(
    order_ref, g0, g1, g2, g3, down_ref, out_ref, up, middle, total, *, n, hc, inner, width, widths, starts,
    planes,
):
    chunk = hc // planes
    lane = lax.broadcasted_iota(jnp.int32, (out_ref.shape[1], 128), 1)

    def place(g, source, target, base, t):
        for p in range(planes):
            low = (source + p * chunk) // 128 * 128
            v = g[:, low : low + 256].astype(f32)
            off = source + p * chunk - low
            v = pltpu.roll(v, 256 - off, 1) if off else v
            to = base + (p * n + t) * chunk
            if to % 128 == 0:
                target[:, to : to + chunk] = v[:, :chunk]
            else:
                v = pltpu.roll(v, 64, 1)
                here = slice(to - 64, to + 64)
                target[:, here] = jnp.where(lane < 64, target[:, here], v[:, :128])
                target[:, to + 64 : to + 192] = v[:, 128:]

    for t in range(n):
        for i, g in enumerate((g0, g1, g2, g3)):

            @pl.when(order_ref[t] == i)
            def _(t=t, g=g):
                place(g, 0, up, 0, t)
                place(g, hc, up, inner, t)
                place(g, 2 * hc + 256, middle, 0, t)

    def summed(at):
        first = g0[:, at].astype(f32) + g1[:, at].astype(f32)
        return first + (g2[:, at].astype(f32) + g3[:, at].astype(f32))

    up[:, 2 * inner : 2 * inner + 256] = summed(slice(2 * hc, 2 * hc + 256))
    total[:, :width] = summed(slice(3 * hc + 256, 3 * hc + 256 + width))
    sources = (None, up, middle, total)
    for t in range(n):

        @pl.when(order_ref[0] == t)
        def _(t=t):
            for d in range(out_ref.shape[0]):
                for ref, at, w in zip(sources, starts, widths):
                    start = (d * n + t) * w
                    low = start // 128 * 128
                    span = -(-w // 128) * 128
                    if ref is None:
                        window = down_ref[:, low : low + span + 128].astype(f32)
                    else:
                        window = ref[:, low : low + span + 128]
                    if start > low:
                        window = pltpu.roll(window, span + 128 - (start - low), 1)
                    out_ref[d, :, at : at + span] = window[:, :span].astype(bf16)


def swap(v, axis, bit):
    size = lax.axis_size(axis)
    return lax.ppermute(v, axis, [(i, i ^ bit) for i in range(size)])


def put(pieces):
    rows = pieces[0][0].shape[0]
    out = jnp.zeros((len(pieces) * rows, pieces[0][0].shape[1]), pieces[0][0].dtype)
    for piece, slot in pieces:
        out = lax.dynamic_update_slice_in_dim(out, piece, slot * rows, 0)
    return out


def rotate(v, r):
    size = lax.axis_size("dp")
    return lax.ppermute(v, "dp", [(i, (i + 2 * r) % size) for i in range(size)])


def after(v, *others):
    return lax.optimization_barrier((v, others))[0]


def fence(*values):
    return lax.optimization_barrier(values)


def others(v):
    return [swap(v, "seq", k) for k in (1, 2, 3)]


def total_of(v, got):
    return (v + got[0]) + (got[1] + got[2])


def across(far, pair):
    return (far.astype(f32) + pair[BLOCK:].astype(f32)).astype(bf16)


def own_sum(near, pair, far):
    return near.astype(f32) + pair[:BLOCK].astype(f32) + far.astype(f32)


def scatter_plain(near, pair, far):
    v = jnp.concatenate([near, pair[:BLOCK], far, pair[BLOCK:]], 0).astype(f32)
    return lax.psum_scatter(v, "seq", scatter_dimension=0, tiled=True)


def per_device(
    layer_input,
    document_index,
    adapter_index,
    input_norm_gain,
    input_projection,
    step_projection,
    convolution_weight,
    convolution_bias,
    head_step_bias,
    log_decay_rate,
    head_skip_gain,
    gated_norm_gain,
    output_projection,
    adapter_input_down,
    adapter_input_up,
    adapter_output_down,
    adapter_output_up,
    output_gradient,
):
    both = ("dp", "seq")
    dps, n = lax.axis_size("dp"), lax.axis_size("seq")
    here = lax.axis_index("seq")
    seqs, own_len, width = layer_input.shape
    adapters, rank, _ = adapter_input_down.shape
    ranks = adapters * rank
    heads = head_step_bias.shape[0]
    inner = output_projection.shape[0] * dps * n
    cols = input_projection.shape[1]
    state2 = cols - 2 * inner
    state = state2 // 2
    taps = convolution_weight.shape[1]
    hn = heads // n
    hc = inner // n
    hd = inner // heads
    length = own_len * n
    nb = length // BLOCK

    staged = n == 4 and dps == 8
    rows = input_projection.shape[0]
    conv_cols = hc + state2
    wa_cols = conv_cols + ranks + 128
    doc_cols = -(-seqs * own_len // rows)
    doc_block = document_index.astype(bf16).reshape(-1)
    doc_block = jnp.pad(doc_block, (0, rows * doc_cols - doc_block.shape[0])).reshape(rows, -1)
    tail = jnp.concatenate([doc_block, input_norm_gain[:, None]], 1)
    up_rows = adapter_input_up.shape[2]
    up_keep = -(-up_rows // 16) * 16
    conv_rows = convolution_weight.shape[0]
    wide = -(-conv_rows // 128) * 128
    misc_rows = 16
    small_rows = up_keep + misc_rows * wide // 128
    out_rows = output_projection.shape[0]
    planes = dps // 2 if staged else 1
    if staged:
        to_head = [
            (8 * z + 2 * t + y, 8 * z + 4 * y + t)
            for z in range(planes) for y in range(2) for t in range(n)
        ]
    else:
        to_head = [(dps * s + d, n * d + s) for d in range(dps) for s in range(n)]
    tables = [
        v.reshape(ranks, -1)
        for v in (adapter_input_down, adapter_input_up, adapter_output_down, adapter_output_up)
    ]
    if staged:
        tail = jnp.pad(tail.astype(f32), ((0, 0), (127 - doc_cols, 0)))
        payload, w_o, small = pl.pallas_call(
            functools.partial(
                pack_weights_kernel, n=n, hn=hn, hc=hc, inner=inner, planes=planes
            ),
            out_shape=[
                jax.ShapeDtypeStruct((n * rows, wa_cols + hc + ranks), bf16),
                jax.ShapeDtypeStruct((2 * out_rows, hc + ranks), bf16),
                jax.ShapeDtypeStruct((small_rows, 128), bf16),
            ],
            scratch_shapes=[pltpu.VMEM((128, 256), f32), pltpu.VMEM((misc_rows, 128), f32)],
            name="pack_weights",
        )(
            input_projection, step_projection, *tables[:2], *tables[2:], output_projection,
            convolution_weight.T, convolution_bias[None], adapter_index[None], gated_norm_gain[None], tail,
        )
    else:
        gap = jnp.zeros((rows, 127 - hn - doc_cols), bf16)
        payload = jnp.concatenate(
            [
                jnp.concatenate(
                    [
                        input_projection[:, inner + t * hc : inner + (t + 1) * hc],
                        input_projection[:, 2 * inner :],
                        tables[0].T,
                        step_projection[:, t * hn : (t + 1) * hn],
                        gap,
                        tail,
                    ],
                    1,
                )
                for t in range(n)
            ],
            0,
        )
        late_payload = jnp.concatenate(
            [
                jnp.concatenate([input_projection[:, t * hc : (t + 1) * hc], tables[3].T], 1)
                for t in range(n)
            ],
            0,
        )
        w_o = jnp.concatenate([output_projection, tables[2].T], 1)

        def as_row(v):
            return jnp.pad(v, ((0, 0), (0, wide - v.shape[1])))

        misc = jnp.concatenate(
            [
                as_row(convolution_weight.T),
                as_row(convolution_bias[None]),
                as_row(adapter_index.astype(bf16)[None]),
                as_row(gated_norm_gain[None]),
            ],
            0,
        )
        misc = jnp.pad(misc, ((0, misc_rows - misc.shape[0]), (0, 0)))
        small = jnp.concatenate(
            [jnp.pad(tables[1].T, ((0, up_keep - up_rows), (0, 0))), misc.reshape(-1, 128)], 0
        )
    w_a = lax.all_to_all(payload, "seq", 0, 0, tiled=True)

    if staged:
        d = lax.axis_index("dp")
        y, z = d % 2, d // 2
        w_o = lax.ppermute(w_o, both, to_head)
        turned = [rotate(small, r) for r in (1, 2, 3)]
        x_near = swap(layer_input, "seq", 1)
        w_a, small, turned, w_o, x_near = fence(w_a, small, turned, w_o, x_near)
        w_a, w_b = w_a[:, :wa_cols], w_a[:, wa_cols:]
        small = put([(small, z)] + [(v, lax.rem(z + 3 - r, 4)) for r, v in enumerate(turned)])
        a1, a3, a0y = rotate(w_a, 1), rotate(w_a, 3), swap(w_a, "dp", 1)
        small_y = swap(small, "dp", 1)
        x0 = after(layer_input, w_a)[:1]
        x_far0 = swap(x0, "seq", 2)
        x1, og = after(layer_input, w_a)[1:], after(output_gradient, w_a)
        og0, og1 = og[:1], og[1:]
        at = [2 * lax.rem(z + 4 - r, 4) + y for r in range(4)]
        slots = [at[0], at[0] ^ 1, at[1], at[3], at[1] ^ 1, at[3] ^ 1, at[2], at[2] ^ 1]
        slots = jnp.stack(slots).astype(jnp.int32)
        x_order = jnp.arange(4, dtype=jnp.int32) ^ here
    else:
        w_b = lax.all_to_all(late_payload, "seq", 0, 0, tiled=True)
        w_o = lax.ppermute(w_o, both, to_head)
        small = lax.all_gather(lax.all_gather(small, "dp", tiled=True), "seq", tiled=True)
        small = jnp.moveaxis(small.reshape(n, dps, small_rows, 128), 0, 1)
        wa_pieces = [lax.all_gather(w_a, "dp", tiled=True)]
        slots = jnp.zeros((1,), jnp.int32)
        x_order = jnp.arange(nb, dtype=jnp.int32)
        xs = [jnp.split(lax.all_gather(layer_input, "seq", axis=1, tiled=True), nb, axis=1)] * seqs
    docs = w_a[:, wa_cols - 1 - doc_cols : wa_cols - 1].reshape(n, -1)[:, : seqs * own_len]
    docs = jnp.moveaxis(docs.reshape(n, seqs, own_len), 0, 1).reshape(seqs, length)
    order = jnp.concatenate([x_order, slots])
    order_in = jnp.concatenate([x_order, jnp.stack([2 * slots, 2 * slots + 1], 1).reshape(-1)])
    order_whole = jnp.concatenate([x_order, jnp.zeros((1,), jnp.int32)])

    def mine(v):
        v = v.reshape(planes, n, v.shape[0] // (planes * n), *v.shape[1:])
        v = lax.dynamic_index_in_dim(v, here, 1, keepdims=False)
        return v.reshape(-1, *v.shape[2:])

    if not staged:
        small = small.reshape(dps * n, small_rows, 128)
        up_full = small[:, :up_rows].reshape(cols, ranks)
        misc = small[:, up_keep:].reshape(dps * n, misc_rows, wide)
        conv_w = jnp.moveaxis(misc[:, :taps, :conv_rows], 1, 0).reshape(taps, -1).astype(f32)
        conv_b = misc[:, taps, :conv_rows].reshape(-1).astype(f32)
        every_index = misc[:, taps + 1, :seqs].reshape(dps, n, seqs)[:, 0].astype(jnp.int32)
        gate_gain = misc[:, taps + 2, :out_rows].reshape(-1).astype(f32)

        up_gate = mine(up_full[:inner])
        up_conv = jnp.concatenate([mine(up_full[inner : 2 * inner]), up_full[2 * inner :]], 0)
        conv_w = jnp.concatenate([mine(conv_w.T[:inner]), conv_w.T[inner:]], 0).T
        conv_b = jnp.concatenate([mine(conv_b[:inner]), conv_b[inner:]], 0)
    step_bias = mine(head_step_bias)
    decay_rate = -jnp.exp(mine(log_decay_rate))
    skip = mine(head_skip_gain)
    gate_gain = None if staged else mine(gate_gain)

    chosen = (adapter_index[:, None] == jnp.arange(adapters, dtype=jnp.int32)[None, :]).astype(f32)
    mask = jnp.repeat(chosen, rank, axis=1)[:, None, :]

    doc_f = docs.astype(f32)

    def same_before(k):
        return jnp.pad(doc_f, ((0, 0), (k, 0)), constant_values=-1.0)[:, :length] == doc_f

    def same_after(k):
        return jnp.pad(doc_f, ((0, 0), (0, k)), constant_values=-1.0)[:, k:] == doc_f

    blocks = doc_f.reshape(seqs, nb, BLOCK)
    prior = jnp.concatenate([blocks[:, :1, 0], blocks[:, :-1, -1]], 1)
    keep = (blocks == prior[:, :, None]).reshape(seqs, length)
    ends = (blocks == blocks[:, :, -1:]).reshape(seqs, length)
    flags = [
        same_before(1), same_before(2), same_before(3), keep, ends, doc_f,
        same_after(1), same_after(2), same_after(3),
    ]
    meta = jnp.stack([v.astype(f32) for v in flags], -1)
    meta = jnp.pad(meta, ((0, 0), (0, 0), (0, 128 - len(flags))))
    doc_rows = blocks[:, :, None, :]

    def rows8(*vs):
        return jnp.pad(jnp.stack(vs), ((0, 8 - len(vs)), (0, 0)))

    if not staged:
        conv_rows8 = rows8(conv_w[0], conv_w[1], conv_w[2], conv_w[3], conv_b)
        wide_rows = rows8(jnp.repeat(skip, hd), gate_gain)
    head_rows = rows8(
        jnp.pad(step_bias, (0, 128 - hn)), jnp.pad(decay_rate, (0, 128 - hn))
    )
    halves = jnp.pad(
        (jnp.arange(128)[None, :] // 64 == jnp.arange(2)[:, None]).astype(bf16), ((0, 14), (0, 0))
    )
    select = (jnp.arange(hc)[:, None] // hd == jnp.arange(128)[None, :]).astype(bf16)
    mask8 = jnp.broadcast_to(mask, (seqs, 8, ranks))
    cc = conv_cols
    anywhere = pl.BlockSpec(memory_space=pl.ANY)
    params = pltpu.CompilerParams(
        dimension_semantics=("arbitrary",), vmem_limit_bytes=VMEM_BYTES
    )

    def at(w, k=0):
        return pl.BlockSpec((1, BLOCK, w), lambda b, o: (k, b, 0))

    def once(v, *block):
        block = block or v.shape
        return pl.BlockSpec(block, lambda b, o: (0,) * len(block), pipeline_mode=pl.Buffered(1))

    def of_seq(v, s0):
        k = s0 if v.shape[0] > 1 else 0
        return pl.BlockSpec(
            (1,) + v.shape[1:], lambda b, o: (k, 0, 0), pipeline_mode=pl.Buffered(1)
        )

    def one(w, dtype):
        return jax.ShapeDtypeStruct((1, length, w), dtype)

    def cost(flops, mib):
        return pl.CostEstimate(flops=int(flops), bytes_accessed=mib << 20, transcendentals=0)

    def parts_specs():
        return [once(None, BLOCK, width), once(None, 2 * BLOCK, width), once(None, BLOCK, width)]

    parts_shapes = [
        jax.ShapeDtypeStruct((k * BLOCK, width), bf16) for k in (1, 2, 1)
    ]

    def forward(s0, order, blocks, pieces, keep):
        whole_w = jax.ShapeDtypeStruct((width, wa_cols), bf16)
        size = n * rows // 2 if len(pieces) > 1 else width
        total = sum(v.shape[0] for v in pieces) // size
        return pl.pallas_call(
            functools.partial(
                forward_kernel, hn=hn, hc=hc, count=len(pieces), size=size, s0=s0, keep=keep
            ),
            grid_spec=pltpu.PrefetchScalarGridSpec(
                num_scalar_prefetch=1,
                grid=(nb,),
                in_specs=[
                    *([anywhere] * len(blocks)), at(128, s0),
                    pl.BlockSpec((1, 1, 1, BLOCK), lambda b, o: (s0, b, 0, 0)),
                    once(up_conv), once(conv_rows8), once(head_rows), of_seq(mask8, s0), once(halves),
                    *([anywhere] * len(pieces)),
                ],
                out_specs=[
                    at(width), at(128), at(cc), at(cc), at(hc),
                    pl.BlockSpec((1, 1, hc, state), lambda b, o: (0, b, 0, 0)), at(384),
                    *([anywhere, once(None, width, 128), once(None, 8, width)] if keep else []),
                ],
                scratch_shapes=[
                    pltpu.VMEM((BLOCK + 8, cc), f32), pltpu.VMEM((hc, state), f32),
                    pltpu.VMEM((2, BLOCK, width), bf16), pltpu.VMEM((width, wa_cols), bf16),
                    pltpu.VMEM((8, width), f32), pltpu.VMEM((2, BLOCK, wa_cols), f32),
                    pltpu.VMEM((2, BLOCK, width), bf16), pltpu.SemaphoreType.DMA((total,)),
                    pltpu.SemaphoreType.DMA, pltpu.SemaphoreType.DMA((2,)),
                ],
            ),
            out_shape=[
                one(width, bf16), one(128, bf16), one(cc, bf16), one(cc, f32), one(hc, f32),
                jax.ShapeDtypeStruct((1, nb, hc, state), bf16), one(384, f32),
                *(
                    [
                        whole_w, jax.ShapeDtypeStruct((width, 128), bf16),
                        jax.ShapeDtypeStruct((8, width), f32),
                    ]
                    if keep
                    else []
                ),
            ],
            compiler_params=params,
            name="ssm_forward",
            cost_estimate=cost(2 * length * (width * wa_cols + 3 * BLOCK * hc), 20),
        )(order, *blocks, meta, doc_rows, up_conv, conv_rows8, head_rows, mask8, halves, *pieces)

    def middle(s0, order, scanned, blocks, gate_pieces, out_pieces, keep):
        normed, rank_in, vbc, _, ssm = scanned[:5]
        count = len(gate_pieces)
        merged = () if out_pieces else (n * rows, out_rows)
        wb_shape, wo_shape = (width, hc + ranks), (hc, width + ranks)
        return pl.pallas_call(
            functools.partial(
                middle_kernel, hc=hc, width=width, rank=rank, count=count, keep=keep,
                merged=merged, s0=s0,
            ),
            grid_spec=pltpu.PrefetchScalarGridSpec(
                num_scalar_prefetch=1,
                grid=(nb,),
                in_specs=[
                    at(width), at(128), at(cc), at(hc), *([anywhere] * len(blocks)),
                    once(up_gate), once(wide_rows), of_seq(mask8, s0), *([anywhere] * (count + len(out_pieces))),
                ],
                out_specs=[
                    at(hc), at(hc), at(128), *parts_specs(),
                    pl.BlockSpec((1, 8 + rank, BLOCK), lambda b, o: (0, 0, b)),
                    *([anywhere, anywhere, once(None, width, 128)] if keep else []),
                ],
                scratch_shapes=[
                    pltpu.VMEM((2, BLOCK, width), bf16), pltpu.VMEM(wb_shape, bf16),
                    pltpu.VMEM(wo_shape, bf16), pltpu.SemaphoreType.DMA((3 * dps,)),
                    pltpu.SemaphoreType.DMA((count,)), pltpu.SemaphoreType.DMA((2,)),
                    pltpu.SemaphoreType.DMA((2,)),
                ],
            ),
            out_shape=[
                one(hc, f32), one(hc, f32), one(128, bf16), *parts_shapes,
                jax.ShapeDtypeStruct((1, 8 + rank, length), f32),
                *(
                    [jax.ShapeDtypeStruct(v, bf16) for v in (wb_shape, wo_shape, (width, 128))]
                    if keep
                    else []
                ),
            ],
            compiler_params=params,
            name="output_side",
            cost_estimate=cost(2 * length * width * hc * 3, 25),
        )(
            order, normed, rank_in, vbc, ssm, *blocks, up_gate, wide_rows, mask8, *gate_pieces,
            *out_pieces,
        )

    def backward(s0, scanned, gate, q, rm, grad_rank_out):
        _, rank_in, vbc, pre, ssm, states_low, tok = scanned[:7]

        def back(w, k=0):
            return pl.BlockSpec((1, BLOCK, w), lambda b, o: (k, nb - 1 - b, 0))

        def back_state(shift):
            return pl.BlockSpec(
                (1, 1, hc, state), lambda b, o: (0, jnp.minimum(nb - 1 - b + shift, nb - 1), 0, 0)
            )

        return pl.pallas_call(
            functools.partial(backward_kernel, hn=hn, hc=hc, rank=rank),
            grid_spec=pltpu.PrefetchScalarGridSpec(
                num_scalar_prefetch=1,
                grid=(nb,),
                in_specs=[
                    back(hc), back(hc), back(hc), back(cc), back(cc), back(384),
                    pl.BlockSpec((1, 8, BLOCK), lambda b, o: (0, 0, nb - 1 - b)), back(128, s0),
                    pl.BlockSpec((1, 1, 1, BLOCK), lambda b, o: (s0, nb - 1 - b, 0, 0)),
                    back_state(0), back_state(1), back(128), back(128), once(conv_rows8),
                    once(head_rows), once(wide_rows), once(halves), once(select), once(up_gate),
                    once(up_conv), of_seq(mask8, s0), once(wa), once(wb),
                ],
                out_specs=[
                    *parts_specs(), once(None, 1, rank, 2 * hc + cc),
                    pl.BlockSpec((1, rank, BLOCK), lambda b, o: (0, 0, nb - 1 - b)),
                ],
                scratch_shapes=[
                    pltpu.VMEM((BLOCK + 8, cc), f32), pltpu.VMEM((hc, state), f32),
                    pltpu.VMEM((BLOCK, hc), bf16), pltpu.VMEM((BLOCK, cc), bf16),
                    pltpu.VMEM((BLOCK, 128), bf16), pltpu.VMEM((BLOCK, width), bf16),
                ],
            ),
            out_shape=[
                *parts_shapes, jax.ShapeDtypeStruct((1, rank, 2 * hc + cc), f32),
                jax.ShapeDtypeStruct((1, rank, length), f32),
            ],
            compiler_params=params,
            name="ssm_backward",
            cost_estimate=cost(2 * length * (8 * BLOCK * hc + width * (hc + cc)), 30),
        )(
            x_order, q, gate, ssm, vbc, pre, tok, rm, meta, doc_rows, states_low, states_low, rank_in,
            grad_rank_out, conv_rows8, head_rows, wide_rows, halves, select, up_gate, up_conv, mask8,
            wa, wb,
        )

    def own_tokens(v, axis):
        return lax.dynamic_slice_in_dim(v, here * own_len, own_len, axis)

    def with_adapter(rows_of, table, s0):
        wide_rows_of = jnp.tile(rows_of, (adapters, 1)) * mask[s0, 0][:, None].astype(bf16)
        return mm("rt,dr->td", wide_rows_of, table)

    if staged:
        ready = (head_rows, meta, doc_rows, mask8, halves, select, order, order_whole, order_in, x1, og0, og1)
        a1, a3, a0y, w_a, small, small_y, x_far0, w_b, w_o, ready = fence(
            a1, a3, a0y, w_a, small, small_y, x_far0, w_b, w_o, ready
        )
        (
            head_rows, meta, doc_rows, mask8, halves, select, order, order_whole, order_in, x1, og0,
            og1,
        ) = ready
        mid = n * rows // 2
        a13y = swap(jnp.concatenate([a1, a3[:mid]]), "dp", 1)
        a2, a3y = rotate(a1, 1), rotate(a0y[mid:], 3)
        small = put([(small, y), (small_y, 1 - y)])
        small_far = swap(small, "seq", 2)
        x_both0 = swap(x_far0, "seq", 1)
        w_bo = jnp.concatenate([w_b, w_o])
        a2, a13y, a3y, small, small_far, x_both0, w_bo, x1 = fence(
            a2, a13y, a3y, small, small_far, x_both0, w_bo, x1
        )
        a2y = swap(a2, "dp", 1)
        beside = swap(jnp.concatenate([small, small_far]), "seq", 1)
        b1, b3 = rotate(w_bo, 1), rotate(w_bo, 3)
        x_far1 = swap(x1, "seq", 2)
        up_gate, up_conv, conv_rows8, gains, index_rows = pl.pallas_call(
            functools.partial(
                unpack_kernel, n=n, planes=planes, up_rows=up_rows, rows=small_rows, inner=inner,
                hc=hc, conv_rows=conv_rows, out_rows=out_rows,
            ),
            in_specs=[
                pl.BlockSpec(memory_space=pltpu.SMEM),
                *[pl.BlockSpec(memory_space=pltpu.VMEM)] * 3,
            ],
            out_specs=[pl.BlockSpec(memory_space=pltpu.VMEM)] * 5,
            out_shape=[
                jax.ShapeDtypeStruct((hc, ranks), bf16), jax.ShapeDtypeStruct((cc, ranks), bf16),
                jax.ShapeDtypeStruct((8, cc), f32), jax.ShapeDtypeStruct((8, hc), f32),
                jax.ShapeDtypeStruct((dps * n, 128), f32),
            ],
            scratch_shapes=[
                pltpu.VMEM((n, *small.shape), bf16), pltpu.VMEM((cols, ranks), f32),
                pltpu.VMEM((8, inner + state2 + 256), f32), pltpu.VMEM((8, inner + 256), f32),
            ],
            compiler_params=pltpu.CompilerParams(vmem_limit_bytes=VMEM_BYTES),
            name="unpack_small",
        )(x_order, small, small_far, beside)
        every_index = index_rows.reshape(dps, n, 128)[:, 0, :seqs].astype(jnp.int32)
        wide_rows = rows8(jnp.repeat(skip, hd), gains[6])
        wa_pieces = [w_a, a0y, a1, a3, a13y, a3y, a2, a2y]
        xs = [[layer_input, x_near, x_far0, x_both0]]
        wa_pieces, xs[0], w_bo, up_conv, up_gate, conv_rows8 = fence(
            wa_pieces, xs[0], w_bo, up_conv, up_gate, conv_rows8
        )
        *fwd0, wa, down_in, gain_rows = forward(0, order_in, xs[0], wa_pieces, True)
        b0y = swap(w_bo, "dp", 1)
        x_both1 = swap(x1, "seq", 3)
        fwd0, wa, b1, b3, b0y, w_bo, x_far1, x_both1 = fence(
            fwd0, wa, b1, b3, b0y, w_bo, x_far1, x_both1
        )
        w_bo, og0, og1, og = fence(w_bo, og0, og1, output_gradient)
        fwd1 = forward(1, order_whole, [layer_input, x_near, x_far1, x_both1], [wa], False)
        b1y, b3y_gate = swap(b1, "dp", 1), swap(b3[: n * rows], "dp", 1)
        b2, b3y_out = rotate(b1, 1), rotate(b0y[n * rows :], 3)
        og_far0 = swap(og0, "seq", 2)
        fwd1, b1y, b3y_gate, b3y_out, b2, og_far0, og, w_bo, og1 = fence(
            fwd1, b1y, b3y_gate, b3y_out, b2, og_far0, og, w_bo, og1
        )
        og_near = swap(og, "seq", 1)
        b3y = jnp.concatenate([b3y_gate, b3y_out])
        b2y_gate, b2y_out = swap(b2[: n * rows], "dp", 1), rotate(b1y[n * rows :], 1)
        b2y = jnp.concatenate([b2y_gate, b2y_out])
        og_both0 = swap(og_far0, "seq", 1)
        og_far1 = swap(og1, "seq", 2)
        fwd = [fwd0, fwd1]
        wb_pieces = [w_bo, b0y, b1, b3, b1y, b3y, b2, b2y]
        wo_pieces = []
        ogs = [[output_gradient, og_near, og_far0, og_both0]]
        wb_pieces, ogs[0], og_far1 = fence(wb_pieces, ogs[0], og_far1)
        og_both1 = swap(og_far1, "seq", 1)
    else:
        *fwd0, wa, down_in, gain_rows = forward(0, order, xs[0], wa_pieces, True)
        fwd = [fwd0]
        fwd += [forward(s0, order_whole, xs[s0], [wa], False) for s0 in range(1, seqs)]
        wb_pieces = [lax.all_gather(w_b, "dp", tiled=True)]
        wo_pieces = [lax.all_gather(w_o, "dp", tiled=True)]
        full = lax.all_gather(output_gradient, "seq", axis=1, tiled=True)
        ogs = [jnp.split(full, nb, axis=1)] * seqs

    def normalisers(stats):
        inv_gated = lax.rsqrt(stats[:1] / inner + EPS)
        rm = jnp.pad(jnp.concatenate([inv_gated, stats[1:2] / inner], 0), ((0, 6), (0, 0)))[None]
        return inv_gated, rm, own_tokens((stats[8:] * inv_gated).astype(bf16), 1)

    def layer_output(s0, branch, inv_gated, rank_out):
        return (
            layer_input[s0].astype(f32)
            + branch * own_tokens(inv_gated, 1).T
            + with_adapter(rank_out, up_out, s0)
        ).astype(bf16)

    def down_gradient(s0, grad_rank_in):
        return mm("rt,td->rd", grad_rank_in, fwd[s0][0][0]).astype(bf16)

    def layer_gradient(s0, partial, grad_rank_in):
        grad_normed = partial + with_adapter(
            own_tokens(grad_rank_in, 1), down_in, s0
        )
        own = layer_input[s0].astype(f32)
        inv_own = lax.rsqrt(jnp.mean(own * own, -1, keepdims=True) + EPS)
        scaled_in = grad_normed * gain_rows[0]
        return (
            inv_own * scaled_in
            - own * inv_own**3 * jnp.mean(scaled_in * own, -1, keepdims=True)
            + output_gradient[s0].astype(f32)
        )

    def final_gradient(s0, near, pair, far, grad_rank_in, earlier):
        rows_of = jnp.tile(own_tokens(grad_rank_in, 1).astype(f32), (adapters, 1)) * mask[s0, 0][:, None]

        tile_rows = 128
        mine_of_seq = pl.BlockSpec((1, tile_rows, width), lambda i: (s0, i, 0))
        by_rows = pl.BlockSpec((tile_rows, width), lambda i: (i, 0))

        def full(*block):
            return pl.BlockSpec(block, lambda i: (0,) * len(block))

        ins = [near, pair, far[None], rows_of, down_in, layer_input, output_gradient, gain_rows]
        specs = [
            by_rows, by_rows, pl.BlockSpec((1, tile_rows, width), lambda i: (0, i, 0)),
            pl.BlockSpec((ranks, tile_rows), lambda i: (0, i)), full(width, ranks), mine_of_seq,
            mine_of_seq, full(8, width),
        ]
        if earlier is not None:
            ins.append(earlier)
            specs.append(anywhere)
        return pl.pallas_call(
            functools.partial(final_kernel, held=len(ins) - 8),
            grid=(own_len // tile_rows,),
            in_specs=specs,
            out_specs=mine_of_seq,
            out_shape=jax.ShapeDtypeStruct((seqs, own_len, width), f32),
            input_output_aliases={8: 0} if earlier is not None else {},
            compiler_params=params,
            name="final_gradient",
            cost_estimate=cost(2 * BLOCK * width * ranks, 5),
        )(*ins)

    *side0, wb, wo, up_out = middle(0, order, fwd[0], ogs[0], wb_pieces, wo_pieces, True)
    if staged:
        side0, wb, wo, og_both1 = fence(side0, wb, wo, og_both1)
        ogs.append([output_gradient, og_near, og_far1, og_both1])
        gate0, q0, gro0, near0, pair0, far0, stats0 = side0
        side1 = middle(1, order_whole, fwd[1], ogs[1], [wb], [wo], False)
        got = others(stats0[0])
        pair0 = swap(pair0, "seq", 1)
        side1, got, pair0, far0 = fence(side1, got, pair0, far0)
        gate1, q1, gro1, near1, pair1, far1, stats1 = side1
        inv0, rm0, rank_out0 = normalisers(total_of(stats0[0], got))
        rm0, away, stats1, pair1 = fence(rm0, across(far0, pair0), stats1, pair1)

        back0 = backward(0, fwd[0], gate0, q0, rm0, gro0)
        away = swap(away, "seq", 2)
        got = others(stats1[0])
        pair1 = swap(pair1, "seq", 1)
        back0, away, got, pair1, far1 = fence(back0, away, got, pair1, far1)
        near_g0, pair_g0, far_g0, compact0, gri0 = back0
        pair_g0 = swap(pair_g0, "seq", 1)
        away0 = away
        inv1, rm1, rank_out1 = normalisers(total_of(stats1[0], got))
        rm1, away, gri0, away_g, away0, rank_out0, rank_out1 = fence(
            rm1, across(far1, pair1), gri0, across(far_g0, pair_g0), away0, rank_out0, rank_out1
        )

        back1 = backward(1, fwd[1], gate1, q1, rm1, gro1)
        away = swap(away, "seq", 2)
        away_g = swap(away_g, "seq", 2)
        got = others(gri0[0])
        back1, away, away_g, got, away0, rank_out0, rank_out1, near0, pair0, inv0 = fence(
            back1, away, away_g, got, away0, rank_out0, rank_out1, near0, pair0, inv0
        )
        near_g1, pair_g1, far_g1, compact1, gri1 = back1
        pair_g1 = swap(pair_g1, "seq", 1)
        got1 = others(gri1[0])
        g_out_up = mm("srt,std->srd", jnp.stack([rank_out0, rank_out1]), output_gradient)
        split = jnp.concatenate(
            [
                jnp.concatenate([compact0[0], compact1[0]]).astype(bf16),
                g_out_up.astype(bf16).reshape(seqs * rank, width),
            ],
            1,
        )
        away_g1, split, got1, got, gri0, near0, pair0, near1, pair1, near_g0, pair_g0, down_in = fence(
            across(far_g1, pair_g1), split, got1, got, gri0, near0, pair0, near1, pair1, near_g0,
            pair_g0, down_in,
        )
        away_g1 = swap(away_g1, "seq", 2)
        split_far = swap(split, "seq", 2)
        split_near = swap(split, "seq", 1)
        split_both = swap(split_far, "seq", 1)
        gri0 = total_of(gri0[0], got).astype(bf16)
        gri1 = total_of(gri1[0], got1).astype(bf16)
        downs = jnp.concatenate([down_gradient(0, gri0), down_gradient(1, gri1)])
        output0 = layer_output(0, own_sum(near0, pair0, away0), inv0, rank_out0)
        output1 = layer_output(1, own_sum(near1, pair1, away), inv1, rank_out1)
        grads_of_seq = [split, split_near, split_far, split_both]
        grads_order = x_order
    else:
        splits, downs, ranks_out, outputs, grads_in = [], [], [], [], []
        for s0 in range(seqs):
            if s0:
                side0 = middle(s0, order_whole, fwd[s0], ogs[s0], [wb], [wo], False)
            gate, q, gro, *parts, stats = side0
            inv_gated, rm, rank_out = normalisers(lax.psum(stats[0], "seq"))
            outputs.append(layer_output(s0, scatter_plain(*parts), inv_gated, rank_out))
            *parts, compacted, gri = backward(s0, fwd[s0], gate, q, rm, gro)
            gri = lax.psum(gri[0], "seq").astype(bf16)
            splits.append(compacted[0].astype(bf16))
            downs.append(down_gradient(s0, gri))
            ranks_out.append(rank_out)
            grads_in.append(layer_gradient(s0, scatter_plain(*parts), gri))
        g_out_up = mm("srt,std->srd", jnp.stack(ranks_out), output_gradient).astype(bf16)
        output = jnp.stack(outputs)
        grad_in = jnp.stack(grads_in)
        downs = jnp.concatenate(downs)
        split = jnp.concatenate(
            [jnp.concatenate(splits), g_out_up.reshape(seqs * rank, width)], 1
        )
        grads_of_seq = jnp.split(lax.all_gather(split, "seq", axis=0, tiled=True), n)

    widths = [v // (dps * n) for v in (width, cols, inner, width)]
    starts, lanes = [], 0
    for v in widths:
        starts.append(lanes)
        lanes += -(-v // 128) * 128
    pack_rows = seqs * rank
    if staged:
        packed = pl.pallas_call(
            functools.partial(
                pack_grads_kernel, n=n, hc=hc, inner=inner, width=width, widths=widths,
                starts=starts, planes=planes,
            ),
            in_specs=[
                pl.BlockSpec(memory_space=pltpu.SMEM),
                *[pl.BlockSpec(memory_space=pltpu.VMEM)] * 5,
            ],
            out_specs=pl.BlockSpec(memory_space=pltpu.VMEM),
            out_shape=jax.ShapeDtypeStruct((dps, pack_rows, lanes), bf16),
            scratch_shapes=[
                pltpu.VMEM((pack_rows, cols + 256), f32), pltpu.VMEM((pack_rows, inner + 256), f32),
                pltpu.VMEM((pack_rows, width + 256), f32),
            ],
            name="pack_grads",
        )(
            grads_order,
            *grads_of_seq, jnp.pad(downs, ((0, 0), (0, 256))),
        )
    else:
        pieces = jnp.stack(grads_of_seq)

        def by_heads(start):
            return jnp.concatenate([pieces[t, :, start : start + hc] for t in range(n)], -1)

        def summed(start, size):
            return pieces[..., start : start + size].astype(f32).sum(0).astype(bf16)

        full = [
            downs,
            jnp.concatenate([by_heads(0), by_heads(hc), summed(2 * hc, state2)], -1),
            by_heads(2 * hc + state2),
            summed(3 * hc + state2, width),
        ]
        packed = jnp.zeros((dps, pack_rows, lanes), bf16)
        for v, start, w in zip(full, starts, widths):
            v = lax.dynamic_index_in_dim(
                v.reshape(pack_rows, dps, n, w), here, 2, keepdims=False
            )
            packed = packed.at[:, :, start : start + w].set(v.transpose(1, 0, 2))
    if staged:
        packed, near_g0, pair_g0, away_g, gri0 = fence(packed, near_g0, pair_g0, away_g, gri0)
        grad0 = final_gradient(0, near_g0, pair_g0, away_g, gri0, None)
    got = lax.all_to_all(packed, "dp", 0, 0, tiled=True)
    if staged:
        output = jnp.stack([output0, output1])
    all_chosen = every_index[..., None] == jnp.arange(adapters)
    if staged:
        grads = pl.pallas_call(
            functools.partial(owners_kernel, rank=rank, starts=starts),
            in_specs=[
                pl.BlockSpec(memory_space=pltpu.SMEM), pl.BlockSpec(memory_space=pltpu.VMEM)
            ],
            out_specs=[pl.BlockSpec(memory_space=pltpu.VMEM)] * len(widths),
            out_shape=[jax.ShapeDtypeStruct((adapters, rank, w), f32) for w in widths],
            name="owners_sum",
        )(all_chosen.astype(f32).reshape(-1, adapters), got)
    else:
        table = mm(
            "dsk,dsrc->krc", all_chosen.astype(bf16), got.reshape(dps, seqs, rank, lanes)
        )
        grads = [table[..., start : start + w] for start, w in zip(starts, widths)]
    if staged:
        grad0, output, away_g1, near_g1, pair_g1 = fence(grad0, output, away_g1, near_g1, pair_g1)
        grad_in = final_gradient(1, near_g1, pair_g1, away_g1, gri1, grad0)
    return (output, grad_in, grads[0], grads[1], grads[2], grads[3])


def solution(mesh):
    return jax.shard_map(
        per_device,
        mesh=mesh,
        in_specs=(
            P("dp", "seq", None),
            P("dp", "seq"),
            P("dp"),
            P(("dp", "seq")),
            P(("dp", "seq"), None),
            P(("dp", "seq"), None),
            P(("dp", "seq"), None),
            P(("dp", "seq")),
            P(),
            P(),
            P(),
            P(("dp", "seq")),
            P(("dp", "seq"), None),
            P(None, None, ("dp", "seq")),
            P(None, None, ("dp", "seq")),
            P(None, None, ("dp", "seq")),
            P(None, None, ("dp", "seq")),
            P("dp", "seq", None),
        ),
        out_specs=(
            P("dp", "seq", None),
            P("dp", "seq", None),
            P(None, None, ("dp", "seq")),
            P(None, None, ("dp", "seq")),
            P(None, None, ("dp", "seq")),
            P(None, None, ("dp", "seq")),
        ),
        check_vma=False,
    )
```
